32 devices in a mesh: dp: 4 (over y, core), expert: 8 (over z, x).
Axes of the slice: x: 2, y: 2, z: 4, core: 2. Of those that a mesh axis runs over, the one named last changes fastest.
Arguments:
- tokens: bfloat16 [16384, 512], P(('dp', 'expert')), may hold values from -6 to 6
- remain: float32 [16384], P(('dp', 'expert')), may hold values from 0.1 to 1
- halting: int32 [16384], P(('dp', 'expert')), may hold values 0 or 1
- head_routes: int32 [16384, 4], P(('dp', 'expert')), may hold values from 0 to 23, all different within a row
- expert_routes: int32 [16384, 2], P(('dp', 'expert')), may hold values from 0 to 15, all different within a row; in each aligned block of 512 rows (0 to 511, 512 to 1023, ...) at most 128 rows name the same one
- first_gain: bfloat16 [512], replicated, may hold values from 0.25 to 1.75
- first_bias: bfloat16 [512], replicated, may hold values from -4 to 4
- query_weight: bfloat16 [512, 1536], replicated, may hold values from -0.5 to 0.5
- key_weight: bfloat16 [512, 64], replicated, may hold values from -0.25 to 0.25
- value_weight: bfloat16 [512, 64], replicated, may hold values from -0.25 to 0.25
- output_weight: bfloat16 [1536, 512], replicated, may hold values from -4 to 4
- head_router: bfloat16 [512, 24], replicated, may hold values from -0.125 to 0.125
- second_gain: bfloat16 [512], replicated, may hold values from 0.25 to 1.75
- second_bias: bfloat16 [512], replicated, may hold values from -4 to 4
- expert_router: bfloat16 [512, 16], replicated, may hold values from -0.1875 to 0.1875
- expert_in: bfloat16 [16, 512, 2048], P('expert'), may hold values from -0.25 to 0.25
- expert_out: bfloat16 [16, 2048, 512], P('expert'), may hold values from -0.1875 to 0.1875
- halt_weight: bfloat16 [512], replicated, may hold values from -0.25 to 0.25
- state_cotan: bfloat16 [16384, 512], P(('dp', 'expert')), may hold values from -6 to 6
- accum_cotan: bfloat16 [16384, 512], P(('dp', 'expert')), may hold values from -6 to 6
- remain_cotan: float32 [16384], P(('dp', 'expert')), may hold values from -6 to 6
Outputs:
- new_state: bfloat16 [16384, 512], P(('dp', 'expert'))
- accum_part: float32 [16384, 512], P(('dp', 'expert'))
- remain_left: float32 [16384], P(('dp', 'expert'))
- tokens_grad: float32 [16384, 512], P(('dp', 'expert'))
- remain_grad: float32 [16384], P(('dp', 'expert'))
- first_gain_grad: float32 [512], replicated
- first_bias_grad: float32 [512], replicated
- query_grad: float32 [512, 1536], replicated
- key_grad: float32 [512, 64], replicated
- value_grad: float32 [512, 64], replicated
- output_grad: float32 [1536, 512], replicated
- head_router_grad: float32 [512, 24], replicated
- second_gain_grad: float32 [512], replicated
- second_bias_grad: float32 [512], replicated
- expert_router_grad: float32 [512, 16], replicated
- expert_in_grad: float32 [16, 512, 2048], P('expert', None, 'dp')
- expert_out_grad: float32 [16, 2048, 512], P('expert', 'dp')
- halt_grad: float32 [512], replicated
The draws below stay inside these ranges and needn't reach their ends.
Inputs may be any that keep to these rules, and one draw needn't show every extreme that they name: `head_routes`: each row names 4 different head experts. `expert_routes`: each row names 2 different FFN experts; among the 512 rows of one device no expert is named by more than 128 rows.
All inputs are finite; a program needn't handle non-finite values. No bound on the sum of `halting` on one device may be relied on, other than what follows from the above.
Results may differ from the reference program's by a relative error of at most 0.019.
Values may be sent and summed in bfloat16 or wider, within the bound.
A program may use at most 128 MiB of HBM per device.

```python
import math
import jax
import jax.numpy as jnp
import numpy as np
from jax import lax

D = 512
HEADS = 24
HD = 64
FF = 2048
TOPA = 4
TOPF = 2
TOK_DEV = 512
EXPERTS = 16
CAP = 128
TOKENS = 16384
N_DP = 4
N_EXPERT = 8


def touch_ends(entries, stream_key, smallest, high):
    spot = [jax.random.randint(jax.random.fold_in(stream_key, axis), (), 0, length) for axis, length in enumerate(entries.shape)]
    longest = entries.shape.index(max(entries.shape))
    beside = spot[:longest] + [(spot[longest] + 1) % entries.shape[longest]] + spot[longest + 1:]
    return entries.at[tuple(spot)].set(smallest).at[tuple(beside)].set(high)


def block_levels(stream_key, dims, shards, smallest, largest):
    factor_of, own = 1.0, jax.random.fold_in(stream_key, 6)
    for axis_at, parts in shards:
        draws = jnp.exp(jax.random.uniform(jax.random.fold_in(own, axis_at), (parts,), jnp.float32, smallest / len(shards), largest / len(shards)))
        factor_of = factor_of * jnp.repeat(draws, dims[axis_at] // parts).reshape([-1 if axis == axis_at else 1 for axis in range(len(dims))])
    return factor_of


def choose_distinct(rng, rows, number_of, top, lift):
    sequence = jax.random.permutation(jax.random.fold_in(rng, 1), number_of)
    favour = sequence
    for power in range(3):
        favour = favour * favour // number_of
    favour = favour * lift // number_of
    chance = jax.random.randint(jax.random.fold_in(rng, 2), (rows, number_of), 0, 4096) + favour
    sure = jax.random.permutation(jax.random.fold_in(rng, 3), rows)[jnp.arange(number_of) % rows]
    chance = jnp.where(jnp.arange(rows)[:, None] == sure[None, :], 1 << 14, chance)
    priority = chance * number_of + jnp.arange(number_of)
    return lax.top_k(priority.astype(jnp.int32), top)[1].astype(jnp.int32)


def routed_block(rng, own, number, rows, number_of, top, most, lean):
    order = jax.random.permutation(rng, number_of)
    packed, usual = load_shares(number_of, rows * top, most, lean, True), load_shares(number_of, rows * top, most, lean, False)
    places = jnp.arange(number_of)

    def named(tallies, offset_by):
        used = int((tallies > 0).sum())
        fixed = max(1, used // 4)
        moved = fixed + (places - fixed + offset_by * (used - fixed)) % max(1, number_of - fixed)
        return jnp.zeros((number_of,), jnp.int32).at[order[jnp.where(places < fixed, places, moved)]].set(jnp.asarray(tallies, jnp.int32))

    tallies = jnp.where(number % 4 == 0, named(packed, number // 4), named(usual, number - number // 4 - 1))
    mixed = jax.random.permutation(jax.random.fold_in(own, 3), number_of)
    source_of, sink = mixed[0:number_of // 2 * 2:2], mixed[1:number_of // 2 * 2:2]
    margin = jnp.minimum(tallies[source_of] - 1, most - tallies[sink]) // 2
    margin = jnp.where((source_of == order[0]) | (sink == order[0]) | (tallies[sink] == 0), 0, jnp.maximum(margin, 0))
    moved = jax.random.randint(jax.random.fold_in(own, 4), (number_of // 2,), 0, 1 << 20) % (margin + 1)
    tallies = tallies.at[source_of].add(-moved).at[sink].add(moved)
    items = jnp.searchsorted(jnp.cumsum(tallies), jnp.arange(rows * top), side="right").astype(jnp.int32)
    grid = items.reshape(top, rows).T
    grid = grid[jax.random.permutation(jax.random.fold_in(own, 1), rows)]
    offset_by = jax.random.randint(jax.random.fold_in(own, 2), (rows, 1), 0, top)
    return jnp.take_along_axis(grid, (jnp.arange(top)[None, :] + offset_by) % top, axis=1)


def load_shares(number_of, total, bound, lean, full):
    loads = [(1 << 20) // math.isqrt(grade ** lean) + 1 for grade in range(1, number_of + 1)]
    largest = bound if full else min(bound, max(-(-total // number_of), total * loads[0] // sum(loads)))
    least = 1 if total - largest >= number_of - 1 else 0
    holding, surplus = [largest] + [least] * (number_of - 1), total - largest - least * (number_of - 1)
    while surplus > 0:
        candidates = [i for i in range(1, number_of) if holding[i] < largest] or [i for i in range(1, number_of) if holding[i] < bound]
        pool, remaining = sum([loads[i] for i in candidates]), surplus
        for i in candidates:
            extra = min(bound - holding[i], max(1, remaining * loads[i] // pool), surplus)
            holding[i] = holding[i] + extra
            surplus = surplus - extra
    return np.array(holding)


def scatter_about(stream_key, extent, scale, most, cuts=(), held_as=jnp.bfloat16):
    result = jax.random.normal(stream_key, extent, jnp.float32) * scale
    if len(cuts) > 0:
        result = block_levels(stream_key, extent, cuts, -0.22, 0.18) * result
    return jnp.clip(result, min=-most, max=most).astype(held_as)


def setup_inputs(seed: int = 0) -> dict:
    streams_of = jax.random.split(jax.random.key(seed), 22)
    tokens = scatter_about(streams_of[0], (TOKENS, D), 1.0, 6.0, ((0, 32),))
    remain = jnp.clip(jnp.exp(math.log(1.0) - 2.3025851 * jax.random.uniform(streams_of[1], (TOKENS,), jnp.float32) ** block_levels(streams_of[1], (TOKENS,), ((0, 32),), -0.2, 0.2)), 0.1, 1.0)
    halting = touch_ends((jax.random.randint(streams_of[2], (TOKENS,), 0, 4) < 3).astype(jnp.int32), jax.random.fold_in(streams_of[2], 1), 0, 1)
    head_routes = choose_distinct(streams_of[3], TOKENS, HEADS, TOPA, 0)
    expert_routes_keys = jax.random.split(jax.random.fold_in(streams_of[4], 1), TOKENS // TOK_DEV)
    expert_routes_turns = jax.random.permutation(jax.random.fold_in(streams_of[4], 3), TOKENS // TOK_DEV)
    expert_routes = jax.vmap(lambda own, number: routed_block(jax.random.fold_in(streams_of[4], 2), own, number, TOK_DEV, EXPERTS, TOPF, CAP, 2))(expert_routes_keys, expert_routes_turns).reshape((TOKENS, TOPF))
    first_gain = jnp.clip(1.0 + 0.15 * jax.random.normal(streams_of[5], (D,), jnp.float32), 0.25, 1.75).astype(jnp.bfloat16)
    first_bias = scatter_about(streams_of[6], (D,), 0.25, 4.0)
    query_weight = scatter_about(streams_of[7], (D, HEADS * HD), (D // 4) ** -0.5, 0.5)
    key_weight = scatter_about(streams_of[8], (D, HD), D ** -0.5, 0.25)
    value_weight = scatter_about(streams_of[9], (D, HD), D ** -0.5, 0.25)
    output_weight = scatter_about(streams_of[10], (HEADS * HD, D), 2 ** -0.5, 4.0)
    head_router = scatter_about(streams_of[11], (D, HEADS), (4 * D) ** -0.5, 0.125)
    second_gain = jnp.clip(1.0 + 0.15 * jax.random.normal(streams_of[12], (D,), jnp.float32), 0.25, 1.75).astype(jnp.bfloat16)
    second_bias = scatter_about(streams_of[13], (D,), 0.25, 4.0)
    expert_router = scatter_about(streams_of[14], (D, EXPERTS), (2 * D) ** -0.5, 0.1875)
    expert_in = scatter_about(streams_of[15], (EXPERTS, D, FF), D ** -0.5, 0.25, ((0, 8),))
    expert_out = scatter_about(streams_of[16], (EXPERTS, FF, D), (FF // 2) ** -0.5, 0.1875, ((0, 8),))
    halt_weight = scatter_about(streams_of[17], (D,), D ** -0.5, 0.25)
    state_cotan = scatter_about(streams_of[18], (TOKENS, D), 1.0, 6.0, ((0, 32),))
    accum_cotan = scatter_about(streams_of[19], (TOKENS, D), 1.0, 6.0, ((0, 32),))
    remain_cotan = scatter_about(streams_of[20], (TOKENS,), 1.0, 6.0, ((0, 32),), jnp.float32)
    return {"tokens": tokens, "remain": remain, "halting": halting, "head_routes": head_routes, "expert_routes": expert_routes, "first_gain": first_gain, "first_bias": first_bias, "query_weight": query_weight, "key_weight": key_weight, "value_weight": value_weight, "output_weight": output_weight, "head_router": head_router, "second_gain": second_gain, "second_bias": second_bias, "expert_router": expert_router, "expert_in": expert_in, "expert_out": expert_out, "halt_weight": halt_weight, "state_cotan": state_cotan, "accum_cotan": accum_cotan, "remain_cotan": remain_cotan}


@jax.custom_vjp
def low(v):
    return lax.optimization_barrier(v.astype(jnp.bfloat16)).astype(jnp.float32)

@jax.custom_vjp
def low_back(v):
    return v

def low_keep(v):
    return (low(v), None)

def low_pass(kept, grad):
    return (grad,)

def back_keep(v):
    return (v, None)

def back_low(kept, grad):
    return (low(grad),)
low.defvjp(low_keep, low_pass)
low_back.defvjp(back_keep, back_low)
highest = lax.Precision.HIGHEST
epsilon = 1e-05

def layer_norm(values, scales, offset):
    centre = lax.optimization_barrier(jnp.mean(values, axis=-1, keepdims=True))
    shifted = values - centre
    spread = lax.optimization_barrier(jnp.mean(shifted * shifted, axis=-1, keepdims=True))
    return shifted * lax.rsqrt(spread + epsilon) * scales + offset

def attend_group(pieces):
    queries, key_rows, value_rows = pieces
    length = key_rows.shape[1]
    raw_scores = jnp.einsum('gsah,guh->gsau', queries, key_rows, precision=highest)
    scores = low_back(raw_scores * HD ** (-0.5))
    row_pos = lax.broadcasted_iota(jnp.int32, (length, length), 0)
    col_pos = lax.broadcasted_iota(jnp.int32, (length, length), 1)
    allowed = (col_pos <= row_pos)[None, :, None, :]
    scores = jnp.where(allowed, scores, jnp.float32(-1e+30))
    attn_prob = low(jax.nn.softmax(scores, axis=-1))
    return jnp.einsum('gsau,guh->gsah', attn_prob, value_rows, precision=highest)

def expert_apply(pieces):
    rows_in, first_mat, second_mat = pieces
    pre_act = low_back(jnp.dot(rows_in, first_mat, precision=highest))
    inner_act = low(jax.nn.gelu(pre_act, approximate=False))
    return low_back(low(jnp.dot(inner_act, second_mat, precision=highest)))

def slot_targets(routes, experts, room_rows):
    flattened = routes.reshape(-1).astype(jnp.int32)
    hot_rows = (flattened[:, None] == jnp.arange(experts, dtype=jnp.int32)[None, :]).astype(jnp.int32)
    before = jnp.cumsum(hot_rows, axis=0) - hot_rows
    return (flattened * room_rows + lax.optimization_barrier(jnp.sum(hot_rows * before, axis=1))).astype(jnp.int32)

def reference(tokens, remain, halting, head_routes, expert_routes, first_gain, first_bias, query_weight, key_weight, value_weight, output_weight, head_router, second_gain, second_bias, expert_router, expert_in, expert_out, halt_weight, state_cotan, accum_cotan, remain_cotan):
    active = halting.astype(jnp.float32)
    room_rows = N_DP * N_EXPERT * CAP
    targets = slot_targets(expert_routes, EXPERTS, room_rows)
    head_hot = jax.nn.one_hot(head_routes, HEADS, dtype=jnp.float32)

    def forward(tokens_f, remain_f, first_gain_f, first_bias_f, query_f, key_f, value_f, output_f, head_router_f, second_gain_f, second_bias_f, expert_router_f, expert_in_f, expert_out_f, halt_f):
        tok_total = tokens_f.shape[0]
        attn_in = low(layer_norm(tokens_f, first_gain_f, first_bias_f))
        query_all = jnp.dot(attn_in, query_f, precision=highest).reshape(tok_total, HEADS, HD)
        query_sel = low_back(low(jnp.einsum('teh,tae->tah', query_all, head_hot, precision=highest)))
        key_rows = low_back(low(jnp.dot(attn_in, key_f, precision=highest)))
        value_rows = low_back(low(jnp.dot(attn_in, value_f, precision=highest)))
        head_logits = jnp.dot(attn_in, head_router_f, precision=highest)
        head_gate = jax.nn.softmax(jnp.take_along_axis(head_logits, head_routes, axis=1), axis=1)
        per_group = min(max(1, 4096 // TOK_DEV), N_DP * N_EXPERT)
        groups = tok_total // (per_group * TOK_DEV)
        heads_out = lax.map(jax.checkpoint(attend_group), (query_sel.reshape(groups, per_group, TOK_DEV, TOPA, HD), key_rows.reshape(groups, per_group, TOK_DEV, HD), value_rows.reshape(groups, per_group, TOK_DEV, HD)))
        heads_out = low_back(heads_out.reshape(tok_total, TOPA, HD))
        weighted = low(head_gate[:, :, None] * heads_out)
        spread_out = jnp.einsum('tah,tae->teh', weighted, head_hot, precision=highest).reshape(tok_total, HEADS * HD)
        hidden_one = tokens_f + low_back(jnp.dot(spread_out, output_f, precision=highest))
        ffn_in = low(layer_norm(hidden_one, second_gain_f, second_bias_f))
        expert_logits = jnp.dot(ffn_in, expert_router_f, precision=highest)
        expert_gate = jax.nn.softmax(jnp.take_along_axis(expert_logits, expert_routes, axis=1), axis=1)
        buffer = jnp.zeros((EXPERTS * room_rows, D), jnp.float32).at[targets].set(jnp.repeat(ffn_in, TOPF, axis=0))
        buffer = low_back(buffer.reshape(EXPERTS, room_rows, D))
        produced = lax.map(jax.checkpoint(expert_apply), (buffer, expert_in_f, expert_out_f))
        picked = produced.reshape(EXPERTS * room_rows, D)[targets].reshape(tok_total, TOPF, D)
        hidden = hidden_one + lax.optimization_barrier(jnp.sum(expert_gate[:, :, None] * picked, axis=1))
        halt_prob = jax.nn.sigmoid(jnp.dot(hidden, halt_f, precision=highest))
        halt_share = active * remain_f * halt_prob
        new_state = jnp.where(active[:, None] > 0.5, hidden, tokens_f)
        return (new_state, halt_share[:, None] * hidden, remain_f * (1.0 - active * halt_prob))
    floats = jax.tree.map(lambda member: member.astype(jnp.float32), (tokens, remain, first_gain, first_bias, query_weight, key_weight, value_weight, output_weight, head_router, second_gain, second_bias, expert_router, expert_in, expert_out, halt_weight))
    primal, pullback = jax.vjp(forward, *floats)
    grads = pullback((state_cotan.astype(jnp.float32), accum_cotan.astype(jnp.float32), remain_cotan.astype(jnp.float32)))
    return (primal[0].astype(jnp.bfloat16), primal[1], primal[2], grads[0], grads[1], grads[2], grads[3], grads[4], grads[5], grads[6], grads[7], grads[8], grads[9], grads[10], grads[11], grads[12], grads[13], grads[14])
```

```python
import functools
import math

import jax
import jax.numpy as jnp
from jax import lax
from jax.experimental import pallas as pl
from jax.experimental.pallas import tpu as pltpu
from jax.sharding import PartitionSpec as P

epsilon = 1e-05
f32 = jnp.float32
bf16 = jnp.bfloat16
MESH = pl.DeviceIdType.MESH
VMEM_LIMIT = 67043328


def dot_nn(left, right):
    return jnp.dot(left, right, preferred_element_type=f32)


def dot_nt(left, right):
    return lax.dot_general(left, right, (((1,), (1,)), ((), ())), preferred_element_type=f32)


def dot_tn(left, right):
    return lax.dot_general(left, right, (((0,), (0,)), ((), ())), preferred_element_type=f32)


def iota(shape, axis):
    return lax.broadcasted_iota(jnp.int32, shape, axis)


def norm_rows(values):
    centre = jnp.mean(values, axis=-1, keepdims=True)
    shifted = values - centre
    spread = jnp.mean(shifted * shifted, axis=-1, keepdims=True)
    inverse = lax.rsqrt(spread + epsilon)
    return shifted * inverse, inverse


def norm_back(upstream, normal, inverse, scales):
    scaled = upstream * scales
    inner = (
        scaled
        - jnp.mean(scaled, axis=-1, keepdims=True)
        - normal * jnp.mean(scaled * normal, axis=-1, keepdims=True)
    )
    return inner * inverse


def pick_heads(wide, place, odd, head_size, positions):
    pair = 2 * head_size
    kept = wide[:, :pair]
    for index in range(1, positions):
        kept = jnp.where(place == index, wide[:, index * pair : (index + 1) * pair], kept)
    return jnp.where(odd, kept[:, head_size:], kept[:, :head_size])


def place_heads(out_ref, columns, places, odds, head_size, positions):
    pair = 2 * head_size
    rows = columns[0].shape[0]
    upper = iota((rows, pair), 1) >= head_size
    doubled = [
        jnp.where(upper == odd, jnp.concatenate([column, column], axis=1), 0.0)
        for column, odd in zip(columns, odds)
    ]
    for index in range(positions):
        total = jnp.zeros((rows, pair), f32)
        for value, place in zip(doubled, places):
            total = total + jnp.where(place == index, value, 0.0)
        out_ref[:, index * pair : (index + 1) * pair] = total.astype(bf16)


def lanes_of(columns, width=128):
    rows = columns[0].shape[0]
    lane = iota((rows, width), 1)
    total = jnp.zeros((rows, width), f32)
    for index, column in enumerate(columns):
        total = jnp.where(lane == index, column, total)
    return total


def soft_columns(logits):
    peak = functools.reduce(jnp.maximum, logits)
    raised = [jnp.exp(value - peak) for value in logits]
    whole = functools.reduce(lambda a, b: a + b, raised)
    return [value / whole for value in raised]


def attend_forward(
    block_rows, tokens, head_routes, expert_routes, vectors, query_weight, key_weight, value_weight,
    output_weight, head_router, expert_router,
    attn_in_out, query_out, key_out, value_out, heads_out, spread_out, hidden_out, ffn_out, columns_out,
    slots_out, wide,
):
    rows, width = tokens.shape
    head_size = key_weight.shape[1]
    positions = query_weight.shape[1] // (2 * head_size)
    top = head_routes.shape[1]
    experts = expert_router.shape[1]
    inputs = tokens[...].astype(f32)
    normal, _ = norm_rows(inputs)
    attn_in = (normal * vectors[0:1, :] + vectors[1:2, :]).astype(bf16)
    attn_in_out[...] = attn_in
    wide[...] = dot_nn(attn_in, query_weight[...])
    keys = dot_nn(attn_in, key_weight[...]).astype(bf16)
    key_out[...] = keys
    values = dot_nn(attn_in, value_weight[...]).astype(bf16)
    value_out[...] = values
    head_logits = dot_nn(attn_in, head_router[...])
    chosen = [head_routes[:, a : a + 1] for a in range(top)]
    places = [value // 2 for value in chosen]
    odds = [value % 2 == 1 for value in chosen]
    head_lane = iota(head_logits.shape, 1)
    gates = soft_columns(
        [
            jnp.sum(jnp.where(head_lane == value, head_logits, 0.0), axis=1, keepdims=True)
            for value in chosen
        ]
    )
    for a in range(top):
        picked = pick_heads(wide, places[a], odds[a], head_size, positions)
        query_out[a] = (picked.astype(bf16).astype(f32) * head_size ** (-0.5)).astype(bf16)
    totals = [[] for _ in range(top)]
    for start in range(0, rows, block_rows):
        stop = start + block_rows
        query = jnp.concatenate([query_out[a, start:stop, :] for a in range(top)], axis=0)
        scores = dot_nt(query, key_out[0:stop, :])
        row_pos = iota((top * block_rows, block_rows), 0) % block_rows
        corner = jnp.where(
            iota((top * block_rows, block_rows), 1) <= row_pos, scores[:, start:], f32(-1e30)
        )
        if start:
            scores = jnp.concatenate([scores[:, :start], corner], axis=1)
        else:
            scores = corner
        peak = jnp.max(scores, axis=1, keepdims=True)
        raised = jnp.exp(scores - peak)
        whole = jnp.sum(raised, axis=1, keepdims=True)
        output = dot_nn(raised.astype(bf16), value_out[0:stop, :]) / whole
        log_total = peak + jnp.log(whole)
        for a in range(top):
            heads_out[a, start:stop, :] = output[a * block_rows : (a + 1) * block_rows]
            totals[a].append(log_total[a * block_rows : (a + 1) * block_rows])
    totals = [jnp.concatenate(value, axis=0) for value in totals]
    columns_out[...] = lanes_of(gates + totals)
    weighted = [
        (gates[a] * heads_out[a]).astype(bf16).astype(f32) for a in range(top)
    ]
    place_heads(spread_out, weighted, places, odds, head_size, positions)
    hidden_one = inputs + dot_nn(spread_out[...], output_weight[...])
    hidden_out[...] = hidden_one
    normal_two, _ = norm_rows(hidden_one)
    ffn_in = (normal_two * vectors[2:3, :] + vectors[3:4, :]).astype(bf16)
    ffn_out[...] = ffn_in
    expert_logits = dot_nn(ffn_in, expert_router[...])
    expert_lane = iota(expert_logits.shape, 1)
    named = [expert_routes[:, c : c + 1] for c in range(2)]
    expert_gates = soft_columns(
        [
            jnp.sum(jnp.where(expert_lane == value, expert_logits, 0.0), axis=1, keepdims=True)
            for value in named
        ]
    )
    lane = iota((rows, 128), 1)
    expert = jnp.where(lane < 2 * experts, (lane // 8) * 4 + lane % 4, -1)
    first, second = expert == named[0], expert == named[1]
    hot = jnp.where(first | second, 1.0, 0.0)
    earlier = (iota((rows, rows), 1) < iota((rows, rows), 0)).astype(f32).astype(bf16)
    before = dot_nn(earlier, hot.astype(bf16))
    slot = jnp.where(hot > 0.5, before, -1.0)
    gate = jnp.where(first, expert_gates[0], jnp.where(second, expert_gates[1], 0.0))
    turned = jnp.where(lane % 8 < 4, slot, gate).T
    slots_out[...] = turned[: 2 * experts].reshape(experts // 4, 8, rows)


def attend_backward(
    block_rows, tokens, head_routes, halting, vectors, query_weight, key_weight, value_weight, output_weight,
    head_router, expert_router, attn_in, query, keys, values, heads_out, spread_out, hidden_one, ffn_in,
    columns, grad_rows, grad_logits_t, grad_hidden, state_cotan,
    tokens_grad, query_sum, output_sum, small_sum, router_two, vector_sum, wide, narrow,
):
    rows, width = tokens.shape
    head_size = key_weight.shape[1]
    heads = head_router.shape[1]
    positions = query_weight.shape[1] // (2 * head_size)
    top = head_routes.shape[1]
    gain_one, gain_two = vectors[0:1, :], vectors[2:3, :]
    normal_two, inverse_two = norm_rows(hidden_one[...])
    logits_low = grad_logits_t[...].astype(bf16)
    grad_ffn = grad_rows[...] + lax.dot_general(
        logits_low, expert_router[...], (((0,), (1,)), ((), ())), preferred_element_type=f32
    )
    router_two[...] = dot_nn(logits_low, ffn_in[...])
    gain_two_sum = jnp.sum(grad_ffn * normal_two, axis=0, keepdims=True)
    bias_two_sum = jnp.sum(grad_ffn, axis=0, keepdims=True)
    grad_one = grad_hidden[...] + norm_back(grad_ffn, normal_two, inverse_two, gain_two)
    tokens_grad[...] = grad_one
    grad_attn = grad_one.astype(bf16)
    output_sum[...] = dot_tn(spread_out[...], grad_attn)
    wide[...] = dot_nt(grad_attn, output_weight[...])
    chosen = [head_routes[:, a : a + 1] for a in range(top)]
    places = [value // 2 for value in chosen]
    odds = [value % 2 == 1 for value in chosen]
    gates = [columns[:, a : a + 1] for a in range(top)]
    grad_gates, grad_heads = [], []
    for a in range(top):
        picked = pick_heads(wide, places[a], odds[a], head_size, positions)
        grad_gates.append(jnp.sum(picked * heads_out[a], axis=1, keepdims=True))
        grad_heads.append((gates[a] * picked).astype(bf16))
    inner = functools.reduce(lambda a, b: a + b, [g * d for g, d in zip(gates, grad_gates)])
    grad_logit = [g * (d - inner) for g, d in zip(gates, grad_gates)]
    head_lane = iota((rows, heads), 1)
    grad_hot = functools.reduce(
        lambda a, b: a + b,
        [jnp.where(head_lane == chosen[a], grad_logit[a], 0.0) for a in range(top)],
    )
    grad_keys = [jnp.zeros((block_rows, head_size), f32) for _ in range(rows // block_rows)]
    grad_values = [jnp.zeros((block_rows, head_size), f32) for _ in range(rows // block_rows)]
    grad_query = [[] for _ in range(top)]
    for start in range(0, rows, block_rows):
        stop = start + block_rows
        part = slice(start, stop)
        queries = jnp.concatenate([query[a, part, :] for a in range(top)], axis=0)
        grads = jnp.concatenate([value[part] for value in grad_heads], axis=0)
        total = jnp.concatenate([columns[part, top + a : top + a + 1] for a in range(top)], axis=0)
        scores = dot_nt(queries, keys[0:stop, :])
        row_pos = iota((top * block_rows, block_rows), 0) % block_rows
        corner = jnp.where(
            iota((top * block_rows, block_rows), 1) <= row_pos, scores[:, start:], f32(-1e30)
        )
        if start:
            scores = jnp.concatenate([scores[:, :start], corner], axis=1)
        else:
            scores = corner
        prob = jnp.exp(scores - total)
        grad_prob = dot_nt(grads, values[0:stop, :])
        row_inner = jnp.sum(prob * grad_prob, axis=1, keepdims=True)
        grad_scores = (prob * (grad_prob - row_inner)).astype(bf16)
        grad_q = (dot_nn(grad_scores, keys[0:stop, :]) * head_size ** (-0.5)).astype(bf16)
        for a in range(top):
            grad_query[a].append(grad_q[a * block_rows : (a + 1) * block_rows].astype(f32))
        step_v = dot_tn(prob.astype(bf16), grads)
        step_k = dot_tn(grad_scores, queries)
        for index in range(stop // block_rows):
            piece = slice(index * block_rows, (index + 1) * block_rows)
            grad_values[index] = grad_values[index] + step_v[piece]
            grad_keys[index] = grad_keys[index] + step_k[piece]
    grad_query = [jnp.concatenate(value, axis=0) for value in grad_query]
    place_heads(narrow, grad_query, places, odds, head_size, positions)
    grad_k = jnp.concatenate(grad_keys, axis=0).astype(bf16)
    grad_v = jnp.concatenate(grad_values, axis=0).astype(bf16)
    hot_low = grad_hot.astype(bf16)
    query_sum[...] = dot_tn(attn_in[...], narrow[...])
    small_sum[:, 0:head_size] = dot_tn(attn_in[...], grad_k)
    small_sum[:, head_size : 2 * head_size] = dot_tn(attn_in[...], grad_v)
    small_sum[:, 2 * head_size : 2 * head_size + heads] = dot_tn(attn_in[...], hot_low)
    grad_in = (
        dot_nt(narrow[...], query_weight[...])
        + dot_nt(grad_k, key_weight[...])
        + dot_nt(grad_v, value_weight[...])
        + dot_nt(hot_low, head_router[...])
    )
    normal_one, inverse_one = norm_rows(tokens[...].astype(f32))
    vector_sum[0:1, :] = jnp.sum(grad_in * normal_one, axis=0, keepdims=True)
    vector_sum[1:2, :] = jnp.sum(grad_in, axis=0, keepdims=True)
    vector_sum[2:3, :] = gain_two_sum
    vector_sum[3:4, :] = bias_two_sum
    vector_sum[4:8, :] = jnp.zeros((4, width), f32)
    tokens_grad[...] = (
        tokens_grad[...]
        + norm_back(grad_in, normal_one, inverse_one, gain_one)
        + (1.0 - halting[...].astype(f32)) * state_cotan[...].astype(f32)
    )


def expert_exchange(
    capacity, chunks,
    ffn_in, slots, tokens, hidden_one, state_cotan, accum_cotan, scalars, vectors, first_hbm, second_hbm,
    new_state, accum_part, columns_out, grad_hidden, grad_rows, grad_logits_t, halt_sum, in_terms, out_terms,
    first, second, column, gathered, grads_in, cross, act, slope, produced, crossed, grad_out, grad_crossed,
    partial, landed, staged, keys, shares, share_out,
    weight_sem, key_send, key_recv, gather_send, gather_recv, cross_send, cross_recv, back_send, back_recv,
    reduce_send, reduce_recv, share_send, share_recv, stage_sem,
):
    rows, width = ffn_in.shape
    local, _, hidden_size = first.shape
    tile = width
    tiles = hidden_size // tile
    piece = rows // chunks
    me = lax.axis_index("expert")
    z, x = me // 2, me % 2
    other = 1 - x
    low = z < 2
    middle = (z == 1) | (z == 2)
    edge = jnp.logical_not(middle)

    def real(mirrored):
        return jnp.where(low, mirrored, 3 - mirrored)

    def along(depth):
        return {"expert": depth * 2 + x}

    across = {"expert": z * 2 + other}

    def order(j):
        return real(jnp.where(middle, jnp.where(j < 2, 1 - j, j), j))

    barrier = pltpu.get_barrier_semaphore()
    for step in range(1, 4):
        pl.semaphore_signal(barrier, inc=1, device_id=along((z + step) % 4), device_id_type=MESH)
    pl.semaphore_signal(barrier, inc=1, device_id=across, device_id_type=MESH)
    loads = [
        pltpu.make_async_copy(first_hbm, first, weight_sem.at[0]),
        pltpu.make_async_copy(second_hbm, second, weight_sem.at[1]),
    ]
    for load in loads:
        load.start()
    column[0, z] = ffn_in[...]
    keys[z] = slots[z]
    pl.semaphore_wait(barrier, 4)

    def key_copy(step):
        there = (z + step) % 4
        return pltpu.make_async_remote_copy(
            src_ref=slots.at[there], dst_ref=keys.at[z], send_sem=key_send.at[step], recv_sem=key_recv.at[z],
            device_id=along(there), device_id_type=MESH,
        )

    def key_arrival(shard):
        return pltpu.make_async_remote_copy(
            src_ref=slots.at[0], dst_ref=keys.at[shard], send_sem=key_send.at[0], recv_sem=key_recv.at[shard],
            device_id=across, device_id_type=MESH,
        )

    def gather_copy(phase, source, shard, depth, index):
        return pltpu.make_async_remote_copy(
            src_ref=source, dst_ref=column.at[phase, shard], send_sem=gather_send.at[phase, index],
            recv_sem=gather_recv.at[phase, shard], device_id=along(depth), device_id_type=MESH,
        )

    def send_own(phase, source):
        @pl.when(edge)
        def _():
            gather_copy(phase, source, z, real(1), 0).start()

        @pl.when(middle)
        def _():
            gather_copy(phase, source, z, real(0), 0).start()
            gather_copy(phase, source, z, real(2), 1).start()

    def forward(phase, mirrored, target, index):
        shard = real(mirrored)
        return gather_copy(phase, column.at[phase, shard], shard, real(target), index)

    def finish_gather(phase, source):
        gather_copy(phase, source, z, real(1), 0).wait_send()

        @pl.when(middle)
        def _():
            gather_copy(phase, source, z, real(2), 1).wait_send()
            forward(phase, 0, 2, 2).wait_send()
            forward(phase, 2, 0, 3).wait_send()
            forward(phase, 3, 0, 4).wait_send()

    def await_shard(phase, mirrored):
        shard = real(mirrored)
        if phase == 0:
            key_arrival(shard).wait_recv()
        gather_copy(phase, column.at[phase, shard], shard, z, 0).wait_recv()

    def await_shards(phase, j):
        @pl.when(edge & (j > 0))
        def _():
            await_shard(phase, j)

        @pl.when(middle & (j == 1))
        def _():
            await_shard(phase, 0)
            forward(phase, 0, 2, 2).start()
            await_shard(phase, 2)
            forward(phase, 2, 0, 3).start()

        @pl.when(middle & (j == 2))
        def _():
            await_shard(phase, 3)
            forward(phase, 3, 0, 4).start()

    def experts_of(shard):
        table = keys[shard]
        found = []
        for own in (True, False):
            for r in range(local):
                here, there = (r, local + r) if own else (local + r, r)
                line = jnp.where(x == 0, table[here : here + 1], table[there : there + 1])
                gate = jnp.where(x == 0, table[4 + here : 5 + here], table[4 + there : 5 + there])
                mask = iota((capacity, rows), 0).astype(f32) == line
                found.append((mask, jnp.sum(jnp.where(mask, gate, 0.0), axis=1, keepdims=True)))
        return found

    def hot_rows(found):
        return jnp.concatenate([jnp.where(mask, 1.0, 0.0).astype(bf16) for mask, _ in found], axis=0)

    def cross_copy(phase, shard, r):
        target = gathered if phase == 0 else grads_in
        return pltpu.make_async_remote_copy(
            src_ref=cross.at[shard, r], dst_ref=target.at[4 + shard, r], send_sem=cross_send.at[phase, shard, r],
            recv_sem=cross_recv.at[phase, shard, r], device_id=across, device_id_type=MESH,
        )

    def back_copy(phase, shard, r):
        source, target = (produced, crossed) if phase == 0 else (grad_out, grad_crossed)
        return pltpu.make_async_remote_copy(
            src_ref=source.at[4 + shard, r], dst_ref=target.at[shard, r], send_sem=back_send.at[phase, shard, r],
            recv_sem=back_recv.at[phase, shard, r], device_id=across, device_id_type=MESH,
        )

    def share_copy(shard):
        return pltpu.make_async_remote_copy(
            src_ref=share_out.at[shard], dst_ref=shares.at[z], send_sem=share_send.at[shard],
            recv_sem=share_recv.at[z], device_id=along(shard), device_id_type=MESH,
        )

    def dispatch(phase, shard):
        found = experts_of(shard)
        taken = dot_nn(hot_rows(found), column[phase, shard])
        lines = []
        for index, (mask, gate) in enumerate(found):
            part = taken[index * capacity : (index + 1) * capacity]
            if phase == 1:
                part = gate * part
            r = index % local
            if index < local:
                (gathered if phase == 0 else grads_in)[shard, r] = part.astype(bf16)
            else:
                cross[shard, r] = part.astype(bf16)
                cross_copy(phase, shard, r).start()
            if phase == 1:
                value = (produced if index < local else crossed)[shard, r].astype(f32)
                inner = jnp.sum(part * value, axis=1, keepdims=True)
                lines.append(jnp.sum(jnp.where(mask, inner, 0.0), axis=0, keepdims=True))
        if phase == 1:
            own, far = lines[:local], lines[local:]
            stack = [jnp.where(x == 0, a, b) for a, b in zip(own + far, far + own)]
            share_out[shard] = jnp.concatenate(stack + [jnp.zeros((4, rows), f32)], axis=0)

            @pl.when(shard == z)
            def _():
                shares[z] = share_out[z]

            @pl.when(shard != z)
            def _():
                share_copy(shard).start()

    def expert_forward(shard):
        def one(r, carry):
            cross_copy(0, shard, r).wait_recv()
            taken = jnp.concatenate([gathered[shard, r], gathered[4 + shard, r]], axis=0)
            total = jnp.zeros((2 * capacity, width), f32)
            for n in range(tiles):
                part = slice(n * tile, (n + 1) * tile)
                pre = dot_nn(taken, first[r, :, part])
                cumulative = 0.5 * (1.0 + lax.erf(pre * (1.0 / math.sqrt(2.0))))
                density = jnp.exp(-0.5 * pre * pre) * (1.0 / math.sqrt(2.0 * math.pi))
                inner = (pre * cumulative).astype(bf16)
                steep = (cumulative + pre * density).astype(bf16)
                act[shard, r, :, part] = inner[:capacity]
                act[4 + shard, r, :, part] = inner[capacity:]
                slope[shard, r, :, part] = steep[:capacity]
                slope[4 + shard, r, :, part] = steep[capacity:]
                total = total + dot_nn(inner, second[r, part, :])
            produced[shard, r] = total[:capacity].astype(bf16)
            produced[4 + shard, r] = total[capacity:].astype(bf16)
            back_copy(0, shard, r).start()
            return carry

        lax.fori_loop(0, local, one, 0)

    def expert_backward(shard):
        def one(r, carry):
            cross_copy(1, shard, r).wait_recv()
            taken = jnp.concatenate([grads_in[shard, r], grads_in[4 + shard, r]], axis=0)
            total = jnp.zeros((2 * capacity, width), f32)
            for n in range(tiles):
                part = slice(n * tile, (n + 1) * tile)
                grad = dot_nt(taken, second[r, part, :])
                steep = jnp.concatenate([slope[shard, r, :, part], slope[4 + shard, r, :, part]], axis=0)
                grad_pre = (grad * steep.astype(f32)).astype(bf16)
                slope[shard, r, :, part] = grad_pre[:capacity]
                slope[4 + shard, r, :, part] = grad_pre[capacity:]
                total = total + dot_nt(grad_pre, first[r, :, part])
            grad_out[shard, r] = total[:capacity].astype(bf16)
            grad_out[4 + shard, r] = total[capacity:].astype(bf16)
            back_copy(1, shard, r).start()
            return carry

        lax.fori_loop(0, local, one, 0)

    def reduce_copy(phase, shard, index, chunk, depth):
        part = pl.ds(pl.multiple_of(chunk * piece, piece), piece)
        return pltpu.make_async_remote_copy(
            src_ref=partial.at[shard, part], dst_ref=landed.at[phase, index, part],
            send_sem=reduce_send.at[phase, index, chunk], recv_sem=reduce_recv.at[phase, index, chunk],
            device_id=along(depth), device_id_type=MESH,
        )

    def combine(phase, j):
        shard = order(j)
        for r in range(local):
            back_copy(phase, shard, r).wait_recv()
        found = experts_of(shard)
        if phase == 0:
            pieces = [
                gate * (produced if index < local else crossed)[shard, index % local].astype(f32)
                for index, (_, gate) in enumerate(found)
            ]
            pieces = [value.astype(bf16) for value in pieces]
        else:
            pieces = [
                (grad_out if index < local else grad_crossed)[shard, index % local]
                for index in range(2 * local)
            ]
        partial[shard] = dot_tn(hot_rows(found), jnp.concatenate(pieces, axis=0)).astype(bf16)

        @pl.when(edge & (j > 0))
        def _():
            for chunk in range(chunks):
                reduce_copy(phase, shard, j - 1, chunk, real(1)).start()

    def pass_on(phase, chunk, source, mirrored, index, depth):
        shard = real(mirrored)
        reduce_copy(phase, shard, source, chunk, z).wait_recv()
        part = pl.ds(pl.multiple_of(chunk * piece, piece), piece)
        partial[shard, part] = (
            partial[shard, part].astype(f32) + landed[phase, source, part].astype(f32)
        ).astype(bf16)
        reduce_copy(phase, shard, index, chunk, depth).start()

    def reduce_rows(phase, filler):
        def step(i, carry):
            @pl.when(middle & (i < chunks))
            def _():
                pass_on(phase, i, 1, 2, 3, real(2))

            @pl.when(middle & (i >= chunks))
            def _():
                pass_on(phase, i - chunks, 2, 3, 4, real(2))
                pass_on(phase, i - chunks, 4, 0, 0, real(0))

            filler(i)
            return carry

        lax.fori_loop(0, 2 * chunks, step, 0)

    def reduced(phase):
        for chunk in range(chunks):
            reduce_copy(phase, z, 0, chunk, z).wait_recv()
        total = partial[z].astype(f32) + landed[phase, 0].astype(f32)

        @pl.when(middle)
        def _():
            for chunk in range(chunks):
                reduce_copy(phase, z, 3, chunk, z).wait_recv()

        return total + jnp.where(middle, landed[phase, 3].astype(f32), 0.0)

    def finish_reduce(phase):
        @pl.when(edge)
        def _():
            for index in range(3):
                for chunk in range(chunks):
                    reduce_copy(phase, real(index + 1), index, chunk, real(1)).wait_send()

        @pl.when(middle)
        def _():
            for chunk in range(chunks):
                reduce_copy(phase, real(2), 3, chunk, real(2)).wait_send()
                reduce_copy(phase, real(3), 4, chunk, real(2)).wait_send()
                reduce_copy(phase, real(0), 0, chunk, real(0)).wait_send()

    def finish_cross(phase):
        for shard in range(4):
            for r in range(local):
                cross_copy(phase, shard, r).wait_send()
                back_copy(phase, shard, r).wait_send()

    def run(phase, experts):
        def step(j, carry):
            @pl.when(j >= 2)
            def _():
                combine(phase, j - 2)

            @pl.when((j >= 1) & (j <= 4))
            def _():
                experts(order(j - 1))

            @pl.when(j <= 3)
            def _():
                await_shards(phase, j)
                dispatch(phase, order(j))

            return carry

        lax.fori_loop(0, 6, step, 0)

    for step in range(1, 4):
        key_copy(step).start()
    send_own(0, ffn_in)
    for load in loads:
        load.wait()
    run(0, expert_forward)
    reduce_rows(0, lambda i: None)
    hidden = hidden_one[...] + reduced(0)
    remain, active, remain_cotan = scalars[:, 0:1], scalars[:, 1:2], scalars[:, 2:3]
    halt_vector = vectors[4:5, :]
    halt_prob = jax.nn.sigmoid(jnp.sum(hidden * halt_vector, axis=1, keepdims=True))
    halt_share = active * remain * halt_prob
    grad_accum = accum_cotan[...].astype(f32)
    grad_share = jnp.sum(grad_accum * hidden, axis=1, keepdims=True)
    grad_logit = active * remain * (grad_share - remain_cotan) * halt_prob * (1.0 - halt_prob)
    grad_here = active * state_cotan[...].astype(f32) + halt_share * grad_accum + grad_logit * halt_vector
    grad_hidden[...] = grad_here
    column[1, z] = grad_here.astype(bf16)
    send_own(1, column.at[1, z])
    new_state[...] = jnp.where(active > 0.5, hidden, tokens[...].astype(f32)).astype(bf16)
    accum_part[...] = halt_share * hidden
    columns_out[...] = lanes_of(
        [
            remain * (1.0 - active * halt_prob),
            active * halt_prob * grad_share + (1.0 - active * halt_prob) * remain_cotan,
        ]
    )
    halt_sum[...] = jnp.concatenate(
        [jnp.sum(grad_logit * hidden, axis=0, keepdims=True), jnp.zeros((7, width), f32)], axis=0
    )
    for step in range(1, 4):
        key_copy(step).wait_send()
    finish_gather(0, ffn_in)
    finish_cross(0)
    finish_reduce(0)
    run(1, expert_backward)

    def stage_in(r, n, slot):
        part = pl.ds(pl.multiple_of(n * tile, tile), tile)
        return pltpu.make_async_copy(staged.at[slot], in_terms.at[r, :, part], stage_sem.at[slot])

    def stage_out(r, n, slot):
        part = pl.ds(pl.multiple_of(n * tile, tile), tile)
        return pltpu.make_async_copy(staged.at[slot], out_terms.at[r, part, :], stage_sem.at[slot])

    def weight_terms(i):
        r, n = i // tiles, i % tiles
        part = pl.ds(pl.multiple_of(n * tile, tile), tile)
        total = local * 4 * capacity

        @pl.when(i > 0)
        def _():
            stage_in(0, 0, 0).wait()
            stage_out(0, 0, 1).wait()

        left = gathered[:, r].reshape(total, width)
        right = slope[:, r, :, part].reshape(total, tile)
        staged[0] = dot_tn(left, right).astype(bf16)
        stage_in(r, n, 0).start()
        left = act[:, r, :, part].reshape(total, tile)
        right = grads_in[:, r].reshape(total, width)
        staged[1] = dot_tn(left, right).astype(bf16)
        stage_out(r, n, 1).start()

    reduce_rows(1, weight_terms)
    stage_in(0, 0, 0).wait()
    stage_out(0, 0, 1).wait()
    for step in range(1, 4):
        shard = (z + step) % 4
        pltpu.make_async_remote_copy(
            src_ref=share_out.at[0], dst_ref=shares.at[shard], send_sem=share_send.at[0],
            recv_sem=share_recv.at[shard], device_id=across, device_id_type=MESH,
        ).wait_recv()
        share_copy(shard).wait_send()
    share = jnp.concatenate([shares[s, 0:4] for s in range(4)], axis=0)
    gate = jnp.concatenate([slots[s, 4:8] for s in range(4)], axis=0)
    grad_logits_t[...] = share - gate * jnp.sum(share, axis=0, keepdims=True)
    grad_rows[...] = reduced(1)
    finish_gather(1, column.at[1, z])
    finish_cross(1)
    finish_reduce(1)


def slot_targets(routes, experts, room_rows):
    flattened = routes.reshape(-1)
    hot_rows = (flattened[:, None] == jnp.arange(experts, dtype=jnp.int32)[None, :]).astype(jnp.int32)
    before = jnp.cumsum(hot_rows, axis=0) - hot_rows
    return flattened * room_rows + jnp.sum(hot_rows * before, axis=1)


def experts_by_all_to_all(
    capacity, tokens, remain, halting, expert_routes, halt_weight, expert_router, expert_in, expert_out,
    state_cotan, accum_cotan, remain_cotan, hidden_one, ffn_in,
):
    rows, width = tokens.shape
    experts = expert_router.shape[1]
    top = expert_routes.shape[1]
    highest = lax.Precision.HIGHEST
    inputs = tokens.astype(f32)
    active = halting.astype(f32)
    expert_logits = jnp.dot(ffn_in, expert_router, preferred_element_type=f32)
    expert_gate = jax.nn.softmax(jnp.take_along_axis(expert_logits, expert_routes, axis=1), axis=1)
    targets = slot_targets(expert_routes, experts, capacity)

    def spread(values):
        placed = jnp.zeros((experts * capacity, width), bf16).at[targets].set(values)
        return lax.all_to_all(
            placed.reshape(experts, capacity, width), "expert", split_axis=0, concat_axis=1, tiled=True
        )

    def collect(values):
        back = lax.all_to_all(values, "expert", split_axis=1, concat_axis=0, tiled=True)
        back = back.reshape(experts * capacity, width)
        return back[targets].astype(f32).reshape(rows, top, width)

    arrived = spread(jnp.repeat(ffn_in, top, axis=0))
    pre_act = jnp.einsum("erd,edf->erf", arrived, expert_in, preferred_element_type=f32)
    inner_act = jax.nn.gelu(pre_act, approximate=False).astype(bf16)
    produced = jnp.einsum("erf,efd->erd", inner_act, expert_out, preferred_element_type=f32).astype(bf16)
    picked = collect(produced)
    hidden = hidden_one + jnp.sum(expert_gate[:, :, None] * picked, axis=1)
    halt_vector = halt_weight.astype(f32)
    halt_prob = jax.nn.sigmoid(jnp.dot(hidden, halt_vector, precision=highest))
    halt_share = active * remain * halt_prob
    new_state = jnp.where(active[:, None] > 0.5, hidden, inputs).astype(bf16)
    accum_part = halt_share[:, None] * hidden
    remain_left = remain * (1.0 - active * halt_prob)
    grad_accum = accum_cotan.astype(f32)
    grad_share = jnp.sum(grad_accum * hidden, axis=1)
    grad_logit = active * remain * (grad_share - remain_cotan) * halt_prob * (1.0 - halt_prob)
    remain_grad = active * halt_prob * grad_share + (1.0 - active * halt_prob) * remain_cotan
    grad_hidden = (
        active[:, None] * state_cotan.astype(f32)
        + halt_share[:, None] * grad_accum
        + grad_logit[:, None] * halt_vector[None, :]
    )
    halt_sum = jnp.dot(grad_logit, hidden, precision=highest)
    grad_gate = jnp.sum(grad_hidden[:, None, :] * picked, axis=2)
    grad_chosen = expert_gate * (grad_gate - jnp.sum(expert_gate * grad_gate, axis=1, keepdims=True))
    expert_hot = (expert_routes[:, :, None] == jnp.arange(experts, dtype=jnp.int32)[None, None, :]).astype(f32)
    grad_logits = jnp.einsum("tk,tke->te", grad_chosen, expert_hot, precision=highest)
    grad_prod = (expert_gate[:, :, None] * grad_hidden[:, None, :]).astype(bf16)
    grad_arrived = spread(grad_prod.reshape(rows * top, width))
    grad_inner = jnp.einsum("erd,efd->erf", grad_arrived, expert_out, preferred_element_type=f32)
    cumulative = 0.5 * (1.0 + lax.erf(pre_act * (1.0 / math.sqrt(2.0))))
    density = jnp.exp(-0.5 * pre_act * pre_act) * (1.0 / math.sqrt(2.0 * math.pi))
    grad_pre = (grad_inner * (cumulative + pre_act * density)).astype(bf16)
    grad_rows = jnp.einsum("erf,edf->erd", grad_pre, expert_in, preferred_element_type=f32).astype(bf16)
    in_terms = jnp.einsum("erd,erf->edf", arrived, grad_pre, preferred_element_type=f32)
    out_terms = jnp.einsum("erf,erd->efd", inner_act, grad_arrived, preferred_element_type=f32)
    return (
        new_state, accum_part, remain_left, remain_grad, grad_hidden, jnp.sum(collect(grad_rows), axis=1),
        grad_logits.T, halt_sum, in_terms.astype(bf16), out_terms.astype(bf16),
    )


def vmem(count):
    return [pl.BlockSpec(memory_space=pltpu.VMEM)] * count


def hbm(count):
    return [pl.BlockSpec(memory_space=pl.ANY)] * count


def experts_on_lines(
    capacity, chunks, tokens, scalars, vectors, expert_in, expert_out, state_cotan, accum_cotan, hidden_one, ffn_in,
    slots,
):
    rows, width = tokens.shape
    local, _, hidden_size = expert_in.shape
    shape, buffer, flags = jax.ShapeDtypeStruct, pltpu.VMEM, pltpu.SemaphoreType.DMA
    results = pl.pallas_call(
        functools.partial(expert_exchange, capacity, chunks),
        out_shape=[
            shape((rows, width), bf16),
            shape((rows, width), f32),
            shape((rows, 128), f32),
            shape((rows, width), f32),
            shape((rows, width), f32),
            shape((8 * local, rows), f32),
            shape((8, width), f32),
            shape((local, width, hidden_size), bf16),
            shape((local, hidden_size, width), bf16),
        ],
        in_specs=vmem(8) + hbm(2),
        out_specs=vmem(7) + hbm(2),
        scratch_shapes=[
            buffer((local, width, hidden_size), bf16),
            buffer((local, hidden_size, width), bf16),
            buffer((2, 4, rows, width), bf16),
            buffer((8, local, capacity, width), bf16),
            buffer((8, local, capacity, width), bf16),
            buffer((4, local, capacity, width), bf16),
            buffer((8, local, capacity, hidden_size), bf16),
            buffer((8, local, capacity, hidden_size), bf16),
            buffer((8, local, capacity, width), bf16),
            buffer((4, local, capacity, width), bf16),
            buffer((8, local, capacity, width), bf16),
            buffer((4, local, capacity, width), bf16),
            buffer((4, rows, width), bf16),
            buffer((2, 5, rows, width), bf16),
            buffer((2, width, width), bf16),
            buffer((4, 8, rows), f32),
            buffer((4, 8, rows), f32),
            buffer((4, 8, rows), f32),
            flags((2,)),
            flags((4,)),
            flags((4,)),
            flags((2, 5)),
            flags((2, 4)),
            flags((2, 4, local)),
            flags((2, 4, local)),
            flags((2, 4, local)),
            flags((2, 4, local)),
            flags((2, 5, chunks)),
            flags((2, 5, chunks)),
            flags((4,)),
            flags((4,)),
            flags((2,)),
        ],
        compiler_params=pltpu.CompilerParams(
            vmem_limit_bytes=VMEM_LIMIT, collective_id=1, has_side_effects=True
        ),
        name="expert_exchange",
    )(ffn_in, slots, tokens, hidden_one, state_cotan, accum_cotan, scalars, vectors, expert_in, expert_out)
    new_state, accum_part, pair, grad_hidden, grad_rows, grad_logits_t, halt_sum, in_terms, out_terms = results
    return (
        new_state, accum_part, pair[:, 0], pair[:, 1], grad_hidden, grad_rows, grad_logits_t, halt_sum[0], in_terms,
        out_terms,
    )


def body(
    mesh_sizes, tokens, remain, halting, head_routes, expert_routes, first_gain, first_bias, query_weight,
    key_weight, value_weight, output_weight, head_router, second_gain, second_bias, expert_router, expert_in,
    expert_out, halt_weight, state_cotan, accum_cotan, remain_cotan,
):
    rows, width = tokens.shape
    head_size = key_weight.shape[1]
    top = head_routes.shape[1]
    wide_size = query_weight.shape[1]
    experts = expert_router.shape[1]
    heads = head_router.shape[1]
    capacity = 4 * rows // experts
    shape = jax.ShapeDtypeStruct
    vectors = jnp.stack(
        [first_gain, first_bias, second_gain, second_bias, halt_weight, halt_weight, halt_weight, halt_weight]
    ).astype(f32)
    scalars = jnp.stack([remain, halting.astype(f32), remain_cotan], axis=1)
    attn_in, query, keys, values, heads_out, spread_out, hidden_one, ffn_in, columns, slots = pl.pallas_call(
        functools.partial(attend_forward, 128),
        out_shape=[
            shape((rows, width), bf16),
            shape((top, rows, head_size), bf16),
            shape((rows, head_size), bf16),
            shape((rows, head_size), bf16),
            shape((top, rows, head_size), f32),
            shape((rows, wide_size), bf16),
            shape((rows, width), f32),
            shape((rows, width), bf16),
            shape((rows, 128), f32),
            shape((experts // 4, 8, rows), f32),
        ],
        in_specs=vmem(10),
        out_specs=vmem(10),
        scratch_shapes=[pltpu.VMEM((rows, wide_size), f32)],
        compiler_params=pltpu.CompilerParams(vmem_limit_bytes=VMEM_LIMIT),
        name="attend_forward",
    )(
        tokens, head_routes, expert_routes, vectors, query_weight, key_weight, value_weight, output_weight,
        head_router, expert_router,
    )
    if mesh_sizes == (4, 8):
        stage = experts_on_lines(
            capacity, 4, tokens, scalars, vectors, expert_in, expert_out, state_cotan, accum_cotan, hidden_one,
            ffn_in, slots,
        )
    else:
        stage = experts_by_all_to_all(
            capacity, tokens, remain, halting, expert_routes, halt_weight, expert_router, expert_in, expert_out,
            state_cotan, accum_cotan, remain_cotan, hidden_one, ffn_in,
        )
    (new_state, accum_part, remain_left, remain_grad, grad_hidden, grad_rows, grad_logits_t, halt_sum, in_terms,
     out_terms) = stage
    expert_in_grad = lax.psum_scatter(in_terms, "dp", scatter_dimension=2, tiled=True).astype(f32)
    expert_out_grad = lax.psum_scatter(out_terms, "dp", scatter_dimension=1, tiled=True).astype(f32)
    tokens_grad, query_sum, output_sum, small_sum, router_two, vector_sum = pl.pallas_call(
        functools.partial(attend_backward, 128),
        out_shape=[
            shape((rows, width), f32),
            shape((width, wide_size), f32),
            shape((wide_size, width), f32),
            shape((width, 256), f32),
            shape((experts, width), f32),
            shape((8, width), f32),
        ],
        in_specs=vmem(23),
        out_specs=vmem(6),
        scratch_shapes=[pltpu.VMEM((rows, wide_size), f32), pltpu.VMEM((rows, wide_size), bf16)],
        compiler_params=pltpu.CompilerParams(vmem_limit_bytes=VMEM_LIMIT),
        name="attend_backward",
    )(
        tokens, head_routes, halting[:, None], vectors, query_weight, key_weight, value_weight, output_weight,
        head_router, expert_router, attn_in, query, keys, values, heads_out, spread_out, hidden_one, ffn_in,
        columns, grad_rows, grad_logits_t, grad_hidden, state_cotan,
    )
    totals = lax.psum(
        (query_sum, output_sum, small_sum, router_two, vector_sum, halt_sum), ("dp", "expert")
    )
    query_grad, output_grad, small, router, vector, halt_grad = totals
    return (
        new_state,
        accum_part,
        remain_left,
        tokens_grad,
        remain_grad,
        vector[0],
        vector[1],
        query_grad,
        small[:, :head_size],
        small[:, head_size : 2 * head_size],
        output_grad,
        small[:, 2 * head_size : 2 * head_size + heads],
        vector[2],
        vector[3],
        router.T,
        expert_in_grad,
        expert_out_grad,
        halt_grad,
    )


def solution(mesh):
    in_specs = (
        P(("dp", "expert"), None),
        P(("dp", "expert")),
        P(("dp", "expert")),
        P(("dp", "expert"), None),
        P(("dp", "expert"), None),
        P(),
        P(),
        P(),
        P(),
        P(),
        P(),
        P(),
        P(),
        P(),
        P(),
        P("expert", None, None),
        P("expert", None, None),
        P(),
        P(("dp", "expert"), None),
        P(("dp", "expert"), None),
        P(("dp", "expert")),
    )
    out_specs = (
        P(("dp", "expert"), None),
        P(("dp", "expert"), None),
        P(("dp", "expert")),
        P(("dp", "expert"), None),
        P(("dp", "expert")),
        P(),
        P(),
        P(),
        P(),
        P(),
        P(),
        P(),
        P(),
        P(),
        P(),
        P("expert", None, "dp"),
        P("expert", "dp", None),
        P(),
    )
    sizes = (mesh.shape["dp"], mesh.shape["expert"])
    run = functools.partial(body, sizes)
    return jax.shard_map(run, mesh=mesh, in_specs=in_specs, out_specs=out_specs, check_vma=False)
```

```python
import functools
import math

import jax
import jax.numpy as jnp
from jax import lax
from jax.experimental import pallas as pl
from jax.experimental.pallas import tpu as pltpu
from jax.sharding import PartitionSpec as P

epsilon = 1e-05
f32 = jnp.float32
bf16 = jnp.bfloat16
MESH = pl.DeviceIdType.MESH
VMEM_LIMIT = 67043328


def dot_nn(left, right):
    return jnp.dot(left, right, preferred_element_type=f32)


def dot_nt(left, right):
    return lax.dot_general(left, right, (((1,), (1,)), ((), ())), preferred_element_type=f32)


def dot_tn(left, right):
    return lax.dot_general(left, right, (((0,), (0,)), ((), ())), preferred_element_type=f32)


def iota(shape, axis):
    return lax.broadcasted_iota(jnp.int32, shape, axis)


def norm_rows(values):
    centre = jnp.mean(values, axis=-1, keepdims=True)
    shifted = values - centre
    spread = jnp.mean(shifted * shifted, axis=-1, keepdims=True)
    inverse = lax.rsqrt(spread + epsilon)
    return shifted * inverse, inverse


def norm_back(upstream, normal, inverse, scales):
    scaled = upstream * scales
    inner = (
        scaled
        - jnp.mean(scaled, axis=-1, keepdims=True)
        - normal * jnp.mean(scaled * normal, axis=-1, keepdims=True)
    )
    return inner * inverse


def pick_heads(wide, place, odd, head_size, positions):
    pair = 2 * head_size
    kept = wide[:, :pair]
    for index in range(1, positions):
        kept = jnp.where(place == index, wide[:, index * pair : (index + 1) * pair], kept)
    return jnp.where(odd, kept[:, head_size:], kept[:, :head_size])


def place_heads(out_ref, columns, places, odds, head_size, positions):
    pair = 2 * head_size
    rows = columns[0].shape[0]
    upper = iota((rows, pair), 1) >= head_size
    doubled = [
        jnp.where(upper == odd, jnp.concatenate([column, column], axis=1), 0.0)
        for column, odd in zip(columns, odds)
    ]
    for index in range(positions):
        total = jnp.zeros((rows, pair), f32)
        for value, place in zip(doubled, places):
            total = total + jnp.where(place == index, value, 0.0)
        out_ref[:, index * pair : (index + 1) * pair] = total.astype(bf16)


def lanes_of(columns, width=128):
    rows = columns[0].shape[0]
    lane = iota((rows, width), 1)
    total = jnp.zeros((rows, width), f32)
    for index, column in enumerate(columns):
        total = jnp.where(lane == index, column, total)
    return total


def soft_columns(logits):
    peak = functools.reduce(jnp.maximum, logits)
    raised = [jnp.exp(value - peak) for value in logits]
    whole = functools.reduce(lambda a, b: a + b, raised)
    return [value / whole for value in raised]


def attend_forward(
    block_rows, tokens, head_routes, expert_routes, vectors, query_weight, key_weight, value_weight,
    output_weight, head_router, expert_router,
    attn_in_out, query_out, key_out, value_out, heads_out, spread_out, hidden_out, ffn_out, columns_out,
    slots_out, wide,
):
    rows, width = tokens.shape
    head_size = key_weight.shape[1]
    positions = query_weight.shape[1] // (2 * head_size)
    top = head_routes.shape[1]
    experts = expert_router.shape[1]
    inputs = tokens[...].astype(f32)
    normal, _ = norm_rows(inputs)
    attn_in = (normal * vectors[0:1, :] + vectors[1:2, :]).astype(bf16)
    attn_in_out[...] = attn_in
    wide[...] = dot_nn(attn_in, query_weight[...])
    keys = dot_nn(attn_in, key_weight[...]).astype(bf16)
    key_out[...] = keys
    values = dot_nn(attn_in, value_weight[...]).astype(bf16)
    value_out[...] = values
    head_logits = dot_nn(attn_in, head_router[...])
    chosen = [head_routes[:, a : a + 1] for a in range(top)]
    places = [value // 2 for value in chosen]
    odds = [value % 2 == 1 for value in chosen]
    head_lane = iota(head_logits.shape, 1)
    gates = soft_columns(
        [
            jnp.sum(jnp.where(head_lane == value, head_logits, 0.0), axis=1, keepdims=True)
            for value in chosen
        ]
    )
    for a in range(top):
        picked = pick_heads(wide, places[a], odds[a], head_size, positions)
        query_out[a] = (picked.astype(bf16).astype(f32) * head_size ** (-0.5)).astype(bf16)
    totals = [[] for _ in range(top)]
    for start in range(0, rows, block_rows):
        stop = start + block_rows
        query = jnp.concatenate([query_out[a, start:stop, :] for a in range(top)], axis=0)
        scores = dot_nt(query, key_out[0:stop, :])
        row_pos = iota((top * block_rows, block_rows), 0) % block_rows
        corner = jnp.where(
            iota((top * block_rows, block_rows), 1) <= row_pos, scores[:, start:], f32(-1e30)
        )
        if start:
            scores = jnp.concatenate([scores[:, :start], corner], axis=1)
        else:
            scores = corner
        peak = jnp.max(scores, axis=1, keepdims=True)
        raised = jnp.exp(scores - peak)
        whole = jnp.sum(raised, axis=1, keepdims=True)
        output = dot_nn(raised.astype(bf16), value_out[0:stop, :]) / whole
        log_total = peak + jnp.log(whole)
        for a in range(top):
            heads_out[a, start:stop, :] = output[a * block_rows : (a + 1) * block_rows]
            totals[a].append(log_total[a * block_rows : (a + 1) * block_rows])
    totals = [jnp.concatenate(value, axis=0) for value in totals]
    columns_out[...] = lanes_of(gates + totals)
    weighted = [
        (gates[a] * heads_out[a]).astype(bf16).astype(f32) for a in range(top)
    ]
    place_heads(spread_out, weighted, places, odds, head_size, positions)
    hidden_one = inputs + dot_nn(spread_out[...], output_weight[...])
    hidden_out[...] = hidden_one
    normal_two, _ = norm_rows(hidden_one)
    ffn_in = (normal_two * vectors[2:3, :] + vectors[3:4, :]).astype(bf16)
    ffn_out[...] = ffn_in
    expert_logits = dot_nn(ffn_in, expert_router[...])
    expert_lane = iota(expert_logits.shape, 1)
    named = [expert_routes[:, c : c + 1] for c in range(2)]
    expert_gates = soft_columns(
        [
            jnp.sum(jnp.where(expert_lane == value, expert_logits, 0.0), axis=1, keepdims=True)
            for value in named
        ]
    )
    lane = iota((rows, 128), 1)
    expert = jnp.where(lane < 2 * experts, (lane // 8) * 4 + lane % 4, -1)
    first, second = expert == named[0], expert == named[1]
    hot = jnp.where(first | second, 1.0, 0.0)
    earlier = (iota((rows, rows), 1) < iota((rows, rows), 0)).astype(f32).astype(bf16)
    before = dot_nn(earlier, hot.astype(bf16))
    slot = jnp.where(hot > 0.5, before, -1.0)
    gate = jnp.where(first, expert_gates[0], jnp.where(second, expert_gates[1], 0.0))
    turned = jnp.where(lane % 8 < 4, slot, gate).T
    slots_out[...] = turned[: 2 * experts].reshape(experts // 4, 8, rows)


def attention_back(
    block_rows, hooks, tokens, head_routes, halting, vectors, query_weight, key_weight, value_weight,
    output_weight, head_router, expert_router, attn_in, query, keys, values, heads_out, spread_out, hidden_one,
    ffn_in, columns, grad_rows, grad_logits_t, grad_hidden, state_cotan, halt_sum, tokens_grad, wide, narrow,
):
    take_output, take_query, take_small, pause = hooks
    rows, width = tokens.shape
    head_size = key_weight.shape[1]
    heads = head_router.shape[1]
    positions = query_weight.shape[1] // (2 * head_size)
    top = head_routes.shape[1]
    gain_one, gain_two = vectors[0:1, :], vectors[2:3, :]
    normal_two, inverse_two = norm_rows(hidden_one[...])
    logits_low = grad_logits_t[...].astype(bf16)
    grad_ffn = grad_rows[...] + lax.dot_general(
        logits_low, expert_router[...], (((0,), (1,)), ((), ())), preferred_element_type=f32
    )
    router_two = dot_nn(logits_low, ffn_in[...])
    gain_two_sum = jnp.sum(grad_ffn * normal_two, axis=0, keepdims=True)
    bias_two_sum = jnp.sum(grad_ffn, axis=0, keepdims=True)
    grad_one = grad_hidden[...] + norm_back(grad_ffn, normal_two, inverse_two, gain_two)
    tokens_grad[...] = grad_one
    grad_attn = grad_one.astype(bf16)
    take_output(lambda part: dot_tn(spread_out[:, part], grad_attn))
    wide[...] = dot_nt(grad_attn, output_weight[...])
    chosen = [head_routes[:, a : a + 1] for a in range(top)]
    places = [value // 2 for value in chosen]
    odds = [value % 2 == 1 for value in chosen]
    gates = [columns[:, a : a + 1] for a in range(top)]
    pause(0)
    grad_gates, grad_heads = [], []
    for a in range(top):
        picked = pick_heads(wide, places[a], odds[a], head_size, positions)
        grad_gates.append(jnp.sum(picked * heads_out[a], axis=1, keepdims=True))
        grad_heads.append((gates[a] * picked).astype(bf16))
    inner = functools.reduce(lambda a, b: a + b, [g * d for g, d in zip(gates, grad_gates)])
    grad_logit = [g * (d - inner) for g, d in zip(gates, grad_gates)]
    head_lane = iota((rows, heads), 1)
    grad_hot = functools.reduce(
        lambda a, b: a + b,
        [jnp.where(head_lane == chosen[a], grad_logit[a], 0.0) for a in range(top)],
    )
    pause(1)
    grad_keys = [jnp.zeros((block_rows, head_size), f32) for _ in range(rows // block_rows)]
    grad_values = [jnp.zeros((block_rows, head_size), f32) for _ in range(rows // block_rows)]
    grad_query = [[] for _ in range(top)]
    for start in range(0, rows, block_rows):
        stop = start + block_rows
        part = slice(start, stop)
        queries = jnp.concatenate([query[a, part, :] for a in range(top)], axis=0)
        grads = jnp.concatenate([value[part] for value in grad_heads], axis=0)
        total = jnp.concatenate([columns[part, top + a : top + a + 1] for a in range(top)], axis=0)
        scores = dot_nt(queries, keys[0:stop, :])
        row_pos = iota((top * block_rows, block_rows), 0) % block_rows
        corner = jnp.where(
            iota((top * block_rows, block_rows), 1) <= row_pos, scores[:, start:], f32(-1e30)
        )
        if start:
            scores = jnp.concatenate([scores[:, :start], corner], axis=1)
        else:
            scores = corner
        prob = jnp.exp(scores - total)
        grad_prob = dot_nt(grads, values[0:stop, :])
        row_inner = jnp.sum(prob * grad_prob, axis=1, keepdims=True)
        grad_scores = (prob * (grad_prob - row_inner)).astype(bf16)
        grad_q = (dot_nn(grad_scores, keys[0:stop, :]) * head_size ** (-0.5)).astype(bf16)
        for a in range(top):
            grad_query[a].append(grad_q[a * block_rows : (a + 1) * block_rows].astype(f32))
        step_v = dot_tn(prob.astype(bf16), grads)
        step_k = dot_tn(grad_scores, queries)
        for index in range(stop // block_rows):
            piece = slice(index * block_rows, (index + 1) * block_rows)
            grad_values[index] = grad_values[index] + step_v[piece]
            grad_keys[index] = grad_keys[index] + step_k[piece]
        pause(2 + start // block_rows)
    grad_query = [jnp.concatenate(value, axis=0) for value in grad_query]
    place_heads(narrow, grad_query, places, odds, head_size, positions)
    take_query(lambda part: dot_tn(attn_in[...], narrow[:, part]))
    grad_k = jnp.concatenate(grad_keys, axis=0).astype(bf16)
    grad_v = jnp.concatenate(grad_values, axis=0).astype(bf16)
    hot_low = grad_hot.astype(bf16)
    grad_in = (
        dot_nt(narrow[...], query_weight[...])
        + dot_nt(grad_k, key_weight[...])
        + dot_nt(grad_v, value_weight[...])
        + dot_nt(hot_low, head_router[...])
    )
    normal_one, inverse_one = norm_rows(tokens[...].astype(f32))
    take_small(
        [
            dot_tn(grad_k, attn_in[...]),
            dot_tn(grad_v, attn_in[...]),
            dot_tn(hot_low, attn_in[...]),
            router_two,
            jnp.sum(grad_in * normal_one, axis=0, keepdims=True),
            jnp.sum(grad_in, axis=0, keepdims=True),
            gain_two_sum,
            bias_two_sum,
            halt_sum[0:1, :],
        ]
    )
    tokens_grad[...] = (
        tokens_grad[...]
        + norm_back(grad_in, normal_one, inverse_one, gain_one)
        + (1.0 - halting[...].astype(f32)) * state_cotan[...].astype(f32)
    )


def stack_small(pieces, room):
    count = sum(piece.shape[0] for piece in pieces)
    width = pieces[0].shape[1]
    return jnp.concatenate(pieces + [jnp.zeros((room - count, width), f32)], axis=0)


def attend_backward(block_rows, *refs):
    inputs, (tokens_grad, query_sum, output_sum, small_sum, wide, narrow) = refs[:24], refs[24:]

    def take_output(term):
        output_sum[...] = term(slice(None))

    def take_query(term):
        query_sum[...] = term(slice(None))

    def take_small(pieces):
        small_sum[...] = stack_small(pieces, small_sum.shape[0])

    hooks = take_output, take_query, take_small, lambda point: None
    attention_back(block_rows, hooks, *inputs, tokens_grad, wide, narrow)


class SumOverAll:
    def __init__(self, number, place, send, recv, full, final, lands, lanes):
        self.number, self.place, self.send, self.recv = number, place, send, recv
        self.full, self.final, self.lands, self.lanes = full, final, lands, lanes
        self.copies = {}

    def part(self, ref, *lead):
        return ref.at[lead + (slice(None),) * (5 - len(lead)) + (self.lanes,)]

    def go(self, stage, source, target, device):
        self.copies[stage] = pltpu.make_async_remote_copy(
            src_ref=source, dst_ref=target, send_sem=self.send.at[self.number, stage],
            recv_sem=self.recv.at[self.number, stage], device_id=device, device_id_type=MESH,
        )
        self.copies[stage].start()

    def add(self, lead, landed):
        own = self.part(self.full, *lead)
        total = own[...].astype(f32)
        for value in landed:
            total = total + value[...].astype(f32)
        own[...] = total.astype(self.full.dtype)

    def step(self, stage):
        (c, x, z, y), (to_core, to_x, to_y, to_z) = self.place
        full, final = self.full, self.final
        land_core, land_x, land_z, land_y = self.lands
        if stage == 0:
            self.go(0, self.part(full, 1 - c), land_core, to_core)
        elif stage == 1:
            self.copies[0].wait_recv()
            self.add((c, 1 - x), [land_core.at[1 - x]])
            self.go(1, self.part(full, c, 1 - x), land_x, to_x)
            self.add((c, x), [land_core.at[x]])
        elif stage == 2:
            self.copies[1].wait_recv()
            for hop in (2, 1, 3):
                there = (z + hop) % 4
                self.add((c, x, there), [land_x.at[there]])
                self.go(1 + hop, self.part(full, c, x, there), land_z.at[hop - 1], to_z(hop))
            self.add((c, x, z), [land_x.at[z]])
        elif stage == 3:
            for hop in (1, 2, 3):
                self.copies[1 + hop].wait_recv()
            self.add((c, x, z, 1 - y), [land_z.at[hop, 1 - y] for hop in range(3)])
            self.go(5, self.part(full, c, x, z, 1 - y), land_y, to_y)
            self.add((c, x, z, y), [land_z.at[hop, y] for hop in range(3)])
        elif stage == 4:
            self.copies[5].wait_recv()
            total = self.part(full, c, x, z, y)[...].astype(f32) + land_y[...].astype(f32)
            own = self.part(final, c, x, z, y)
            own[...] = total.astype(final.dtype)
            self.go(6, own, own, to_y)
        elif stage == 5:
            self.copies[6].wait_recv()
            own = self.part(final, c, x, z)
            for hop in (2, 1, 3):
                self.go(6 + hop, own, own, to_z(hop))
        elif stage == 6:
            for hop in (1, 2, 3):
                self.copies[6 + hop].wait_recv()
            own = self.part(final, c, x)
            self.go(10, own, own, to_x)
        elif stage == 7:
            self.copies[10].wait_recv()
            own = self.part(final, c)
            self.go(11, own, own, to_core)
        elif stage == 8:
            self.copies[11].wait_recv()
            for copy in self.copies.values():
                copy.wait_send()


def backward_and_sums(block_rows, *refs):
    inputs, terms = refs[:24], refs[24]
    tokens_grad, output_final, query_final, small_final, terms_final = refs[25:30]
    (wide, narrow, output_full, query_full, small_full, own_terms, near_terms, far_terms, output_core, output_x,
     output_z, output_y, query_core, query_x, query_z, query_y, small_core, small_x, small_z, small_y, send, recv,
     load_sem, term_send, term_recv) = refs[30:]
    units = terms.shape[0]
    line, group = lax.axis_index("expert"), lax.axis_index("dp")
    z, x, y, c = line // 2, line % 2, group // 2, group % 2
    to_core, to_y = {"dp": y * 2 + 1 - c}, {"dp": (1 - y) * 2 + c}
    to_x = {"expert": z * 2 + 1 - x}

    def to_z(hop):
        return {"expert": (z + hop) % 4 * 2 + x}

    barrier = pltpu.get_barrier_semaphore()
    for device in (to_core, to_x, to_y, to_z(1), to_z(2), to_z(3)):
        pl.semaphore_signal(barrier, inc=1, device_id=device, device_id_type=MESH)
    far, near = (1 - y) * 2 + c, y * 2 + c
    loads = [
        [
            pltpu.make_async_copy(terms.at[u, quarter], own_terms.at[u, side], load_sem.at[u, side])
            for side, quarter in enumerate((far, near))
        ]
        for u in range(units)
    ]
    for side in range(2):
        for u in range(units):
            loads[u][side].start()
    pl.semaphore_wait(barrier, 6)

    def term_copy(u, stage):
        if stage < 2:
            quarter = ((1 - y) if stage == 0 else y) * 2 + 1 - c
            source, target, device = terms.at[u, quarter], near_terms.at[u, stage], to_core
        else:
            source, target, device = own_terms.at[u, 0], far_terms.at[u], to_y
        return pltpu.make_async_remote_copy(
            src_ref=source, dst_ref=target, send_sem=term_send.at[u, stage], recv_sem=term_recv.at[u, stage],
            device_id=device, device_id_type=MESH,
        )

    for side in range(2):
        for u in range(units):
            term_copy(u, side).start()

    def send_far(u):
        loads[u][0].wait()
        term_copy(u, 0).wait_recv()
        total = own_terms[u, 0].astype(f32) + near_terms[u, 0].astype(f32)
        own_terms[u, 0] = total.astype(bf16)
        term_copy(u, 2).start()

    def finish_near(u):
        loads[u][1].wait()
        term_copy(u, 1).wait_recv()
        term_copy(u, 2).wait_recv()
        total = own_terms[u, 1].astype(f32) + near_terms[u, 1].astype(f32) + far_terms[u].astype(f32)
        terms_final[u] = total.astype(bf16)
        for stage in range(3):
            term_copy(u, stage).wait_send()

    place = (c, x, z, y), (to_core, to_x, to_y, to_z)
    third = query_full.shape[5] // 3
    whole = slice(None)
    output_sum = SumOverAll(
        0, place, send, recv, output_full, output_final, (output_core, output_x, output_z, output_y), whole
    )
    later = [
        SumOverAll(
            1 + q, place, send, recv, query_full, query_final,
            (query_core.at[q], query_x.at[q], query_z.at[q], query_y.at[q]), pl.ds(q * third, third),
        )
        for q in range(3)
    ]
    later.append(
        SumOverAll(4, place, send, recv, small_full, small_final, (small_core, small_x, small_z, small_y), whole)
    )

    def take_output(term):
        half = output_full.shape[1:]
        size = math.prod(half[:-1])
        for index in range(2):
            value = term(slice(index * size, (index + 1) * size))
            output_full[index] = value.astype(bf16).reshape(half)
        output_sum.step(0)
        send_far(0)

    def take_query(term):
        for q in range(3):
            part = pl.ds(q * third, third)
            value = term(part).astype(bf16).reshape(query_full.shape[:5] + (third,))
            query_full[:, :, :, :, :, part] = value
            later[q].step(0)

    def take_small(pieces):
        rows = math.prod(small_full.shape[:-1])
        small_full[...] = stack_small(pieces, rows).reshape(small_full.shape)
        later[3].step(0)

    def pause(point):
        output_sum.step(point + 1)
        if 1 <= point < units:
            send_far(point)

    attention_back(block_rows, (take_output, take_query, take_small, pause), *inputs, tokens_grad, wide, narrow)
    output_sum.step(7)
    for time in range(1, 9 + len(later) - 1):
        for index, item in enumerate(later):
            if 1 <= time - index <= 8:
                item.step(time - index)
    output_sum.step(8)
    for u in range(units):
        finish_near(u)


def expert_exchange(
    capacity, chunks,
    ffn_in, slots, tokens, hidden_one, state_cotan, accum_cotan, scalars, vectors, first_hbm, second_hbm,
    new_state, accum_part, columns_out, grad_hidden, grad_rows, grad_logits_t, halt_sum, terms,
    first, second, column, gathered, grads_in, cross, act, slope, produced, crossed, grad_out, grad_crossed,
    partial, landed, staged, keys, shares, share_out,
    weight_sem, key_send, key_recv, gather_send, gather_recv, cross_send, cross_recv, back_send, back_recv,
    reduce_send, reduce_recv, share_send, share_recv, stage_sem,
):
    rows, width = ffn_in.shape
    local, _, hidden_size = first.shape
    tile = width
    tiles = hidden_size // tile
    piece = rows // chunks
    me = lax.axis_index("expert")
    z, x = me // 2, me % 2
    other = 1 - x
    low = z < 2
    middle = (z == 1) | (z == 2)
    edge = jnp.logical_not(middle)

    def real(mirrored):
        return jnp.where(low, mirrored, 3 - mirrored)

    def along(depth):
        return {"expert": depth * 2 + x}

    across = {"expert": z * 2 + other}

    def order(j):
        return real(jnp.where(middle, jnp.where(j < 2, 1 - j, j), j))

    barrier = pltpu.get_barrier_semaphore()
    for step in range(1, 4):
        pl.semaphore_signal(barrier, inc=1, device_id=along((z + step) % 4), device_id_type=MESH)
    pl.semaphore_signal(barrier, inc=1, device_id=across, device_id_type=MESH)
    loads = [
        pltpu.make_async_copy(first_hbm, first, weight_sem.at[0]),
        pltpu.make_async_copy(second_hbm, second, weight_sem.at[1]),
    ]
    for load in loads:
        load.start()
    column[0, z] = ffn_in[...]
    keys[z] = slots[z]
    pl.semaphore_wait(barrier, 4)

    def key_copy(step):
        there = (z + step) % 4
        return pltpu.make_async_remote_copy(
            src_ref=slots.at[there], dst_ref=keys.at[z], send_sem=key_send.at[step], recv_sem=key_recv.at[z],
            device_id=along(there), device_id_type=MESH,
        )

    def key_arrival(shard):
        return pltpu.make_async_remote_copy(
            src_ref=slots.at[0], dst_ref=keys.at[shard], send_sem=key_send.at[0], recv_sem=key_recv.at[shard],
            device_id=across, device_id_type=MESH,
        )

    def gather_copy(phase, source, shard, depth, index):
        return pltpu.make_async_remote_copy(
            src_ref=source, dst_ref=column.at[phase, shard], send_sem=gather_send.at[phase, index],
            recv_sem=gather_recv.at[phase, shard], device_id=along(depth), device_id_type=MESH,
        )

    def send_own(phase, source):
        @pl.when(edge)
        def _():
            gather_copy(phase, source, z, real(1), 0).start()

        @pl.when(middle)
        def _():
            gather_copy(phase, source, z, real(0), 0).start()
            gather_copy(phase, source, z, real(2), 1).start()

    def forward(phase, mirrored, target, index):
        shard = real(mirrored)
        return gather_copy(phase, column.at[phase, shard], shard, real(target), index)

    def finish_gather(phase, source):
        gather_copy(phase, source, z, real(1), 0).wait_send()

        @pl.when(middle)
        def _():
            gather_copy(phase, source, z, real(2), 1).wait_send()
            forward(phase, 0, 2, 2).wait_send()
            forward(phase, 2, 0, 3).wait_send()
            forward(phase, 3, 0, 4).wait_send()

    def await_shard(phase, mirrored):
        shard = real(mirrored)
        if phase == 0:
            key_arrival(shard).wait_recv()
        gather_copy(phase, column.at[phase, shard], shard, z, 0).wait_recv()

    def await_shards(phase, j):
        @pl.when(edge & (j > 0))
        def _():
            await_shard(phase, j)

        @pl.when(middle & (j == 1))
        def _():
            await_shard(phase, 0)
            forward(phase, 0, 2, 2).start()
            await_shard(phase, 2)
            forward(phase, 2, 0, 3).start()

        @pl.when(middle & (j == 2))
        def _():
            await_shard(phase, 3)
            forward(phase, 3, 0, 4).start()

    def experts_of(shard):
        table = keys[shard]
        found = []
        for own in (True, False):
            for r in range(local):
                here, there = (r, local + r) if own else (local + r, r)
                line = jnp.where(x == 0, table[here : here + 1], table[there : there + 1])
                gate = jnp.where(x == 0, table[4 + here : 5 + here], table[4 + there : 5 + there])
                mask = iota((capacity, rows), 0).astype(f32) == line
                found.append((mask, jnp.sum(jnp.where(mask, gate, 0.0), axis=1, keepdims=True)))
        return found

    def hot_rows(found):
        return jnp.concatenate([jnp.where(mask, 1.0, 0.0).astype(bf16) for mask, _ in found], axis=0)

    def cross_copy(phase, shard, r):
        target = gathered if phase == 0 else grads_in
        return pltpu.make_async_remote_copy(
            src_ref=cross.at[shard, r], dst_ref=target.at[4 + shard, r], send_sem=cross_send.at[phase, shard, r],
            recv_sem=cross_recv.at[phase, shard, r], device_id=across, device_id_type=MESH,
        )

    def back_copy(phase, shard, r):
        source, target = (produced, crossed) if phase == 0 else (grad_out, grad_crossed)
        return pltpu.make_async_remote_copy(
            src_ref=source.at[4 + shard, r], dst_ref=target.at[shard, r], send_sem=back_send.at[phase, shard, r],
            recv_sem=back_recv.at[phase, shard, r], device_id=across, device_id_type=MESH,
        )

    def share_copy(shard):
        return pltpu.make_async_remote_copy(
            src_ref=share_out.at[shard], dst_ref=shares.at[z], send_sem=share_send.at[shard],
            recv_sem=share_recv.at[z], device_id=along(shard), device_id_type=MESH,
        )

    def dispatch(phase, shard):
        found = experts_of(shard)
        taken = dot_nn(hot_rows(found), column[phase, shard])
        lines = []
        for index, (mask, gate) in enumerate(found):
            part = taken[index * capacity : (index + 1) * capacity]
            if phase == 1:
                part = gate * part
            r = index % local
            if index < local:
                (gathered if phase == 0 else grads_in)[shard, r] = part.astype(bf16)
            else:
                cross[shard, r] = part.astype(bf16)
                cross_copy(phase, shard, r).start()
            if phase == 1:
                value = (produced if index < local else crossed)[shard, r].astype(f32)
                inner = jnp.sum(part * value, axis=1, keepdims=True)
                lines.append(jnp.sum(jnp.where(mask, inner, 0.0), axis=0, keepdims=True))
        if phase == 1:
            own, far = lines[:local], lines[local:]
            stack = [jnp.where(x == 0, a, b) for a, b in zip(own + far, far + own)]
            share_out[shard] = jnp.concatenate(stack + [jnp.zeros((4, rows), f32)], axis=0)

            @pl.when(shard == z)
            def _():
                shares[z] = share_out[z]

            @pl.when(shard != z)
            def _():
                share_copy(shard).start()

    def expert_forward(shard):
        def one(r, carry):
            cross_copy(0, shard, r).wait_recv()
            taken = jnp.concatenate([gathered[shard, r], gathered[4 + shard, r]], axis=0)
            total = jnp.zeros((2 * capacity, width), f32)
            for n in range(tiles):
                part = slice(n * tile, (n + 1) * tile)
                pre = dot_nn(taken, first[r, :, part])
                cumulative = 0.5 * (1.0 + lax.erf(pre * (1.0 / math.sqrt(2.0))))
                density = jnp.exp(-0.5 * pre * pre) * (1.0 / math.sqrt(2.0 * math.pi))
                inner = (pre * cumulative).astype(bf16)
                steep = (cumulative + pre * density).astype(bf16)
                act[shard, r, :, part] = inner[:capacity]
                act[4 + shard, r, :, part] = inner[capacity:]
                slope[shard, r, :, part] = steep[:capacity]
                slope[4 + shard, r, :, part] = steep[capacity:]
                total = total + dot_nn(inner, second[r, part, :])
            produced[shard, r] = total[:capacity].astype(bf16)
            produced[4 + shard, r] = total[capacity:].astype(bf16)
            back_copy(0, shard, r).start()
            return carry

        lax.fori_loop(0, local, one, 0)

    def expert_backward(shard):
        def one(r, carry):
            cross_copy(1, shard, r).wait_recv()
            taken = jnp.concatenate([grads_in[shard, r], grads_in[4 + shard, r]], axis=0)
            total = jnp.zeros((2 * capacity, width), f32)
            for n in range(tiles):
                part = slice(n * tile, (n + 1) * tile)
                grad = dot_nt(taken, second[r, part, :])
                steep = jnp.concatenate([slope[shard, r, :, part], slope[4 + shard, r, :, part]], axis=0)
                grad_pre = (grad * steep.astype(f32)).astype(bf16)
                slope[shard, r, :, part] = grad_pre[:capacity]
                slope[4 + shard, r, :, part] = grad_pre[capacity:]
                total = total + dot_nt(grad_pre, first[r, :, part])
            grad_out[shard, r] = total[:capacity].astype(bf16)
            grad_out[4 + shard, r] = total[capacity:].astype(bf16)
            back_copy(1, shard, r).start()
            return carry

        lax.fori_loop(0, local, one, 0)

    def reduce_copy(phase, shard, index, chunk, depth):
        part = pl.ds(pl.multiple_of(chunk * piece, piece), piece)
        return pltpu.make_async_remote_copy(
            src_ref=partial.at[shard, part], dst_ref=landed.at[phase, index, part],
            send_sem=reduce_send.at[phase, index, chunk], recv_sem=reduce_recv.at[phase, index, chunk],
            device_id=along(depth), device_id_type=MESH,
        )

    def combine(phase, j):
        shard = order(j)
        for r in range(local):
            back_copy(phase, shard, r).wait_recv()
        found = experts_of(shard)
        if phase == 0:
            pieces = [
                gate * (produced if index < local else crossed)[shard, index % local].astype(f32)
                for index, (_, gate) in enumerate(found)
            ]
            pieces = [value.astype(bf16) for value in pieces]
        else:
            pieces = [
                (grad_out if index < local else grad_crossed)[shard, index % local]
                for index in range(2 * local)
            ]
        partial[shard] = dot_tn(hot_rows(found), jnp.concatenate(pieces, axis=0)).astype(bf16)

        @pl.when(edge & (j > 0))
        def _():
            for chunk in range(chunks):
                reduce_copy(phase, shard, j - 1, chunk, real(1)).start()

    def pass_on(phase, chunk, source, mirrored, index, depth):
        shard = real(mirrored)
        reduce_copy(phase, shard, source, chunk, z).wait_recv()
        part = pl.ds(pl.multiple_of(chunk * piece, piece), piece)
        partial[shard, part] = (
            partial[shard, part].astype(f32) + landed[phase, source, part].astype(f32)
        ).astype(bf16)
        reduce_copy(phase, shard, index, chunk, depth).start()

    def reduce_rows(phase, filler):
        def step(i, carry):
            @pl.when(middle & (i < chunks))
            def _():
                pass_on(phase, i, 1, 2, 3, real(2))

            @pl.when(middle & (i >= chunks))
            def _():
                pass_on(phase, i - chunks, 2, 3, 4, real(2))
                pass_on(phase, i - chunks, 4, 0, 0, real(0))

            filler(i)
            return carry

        lax.fori_loop(0, 2 * chunks, step, 0)

    def reduced(phase):
        for chunk in range(chunks):
            reduce_copy(phase, z, 0, chunk, z).wait_recv()
        total = partial[z].astype(f32) + landed[phase, 0].astype(f32)

        @pl.when(middle)
        def _():
            for chunk in range(chunks):
                reduce_copy(phase, z, 3, chunk, z).wait_recv()

        return total + jnp.where(middle, landed[phase, 3].astype(f32), 0.0)

    def finish_reduce(phase):
        @pl.when(edge)
        def _():
            for index in range(3):
                for chunk in range(chunks):
                    reduce_copy(phase, real(index + 1), index, chunk, real(1)).wait_send()

        @pl.when(middle)
        def _():
            for chunk in range(chunks):
                reduce_copy(phase, real(2), 3, chunk, real(2)).wait_send()
                reduce_copy(phase, real(3), 4, chunk, real(2)).wait_send()
                reduce_copy(phase, real(0), 0, chunk, real(0)).wait_send()

    def finish_cross(phase):
        for shard in range(4):
            for r in range(local):
                cross_copy(phase, shard, r).wait_send()
                back_copy(phase, shard, r).wait_send()

    def run(phase, experts):
        def step(j, carry):
            @pl.when(j >= 2)
            def _():
                combine(phase, j - 2)

            @pl.when((j >= 1) & (j <= 4))
            def _():
                experts(order(j - 1))

            @pl.when(j <= 3)
            def _():
                await_shards(phase, j)
                dispatch(phase, order(j))

            return carry

        lax.fori_loop(0, 6, step, 0)

    for step in range(1, 4):
        key_copy(step).start()
    send_own(0, ffn_in)
    for load in loads:
        load.wait()
    run(0, expert_forward)
    reduce_rows(0, lambda i: None)
    hidden = hidden_one[...] + reduced(0)
    remain, active, remain_cotan = scalars[:, 0:1], scalars[:, 1:2], scalars[:, 2:3]
    halt_vector = vectors[4:5, :]
    halt_prob = jax.nn.sigmoid(jnp.sum(hidden * halt_vector, axis=1, keepdims=True))
    halt_share = active * remain * halt_prob
    grad_accum = accum_cotan[...].astype(f32)
    grad_share = jnp.sum(grad_accum * hidden, axis=1, keepdims=True)
    grad_logit = active * remain * (grad_share - remain_cotan) * halt_prob * (1.0 - halt_prob)
    grad_here = active * state_cotan[...].astype(f32) + halt_share * grad_accum + grad_logit * halt_vector
    grad_hidden[...] = grad_here
    column[1, z] = grad_here.astype(bf16)
    send_own(1, column.at[1, z])
    new_state[...] = jnp.where(active > 0.5, hidden, tokens[...].astype(f32)).astype(bf16)
    accum_part[...] = halt_share * hidden
    columns_out[...] = lanes_of(
        [
            remain * (1.0 - active * halt_prob),
            active * halt_prob * grad_share + (1.0 - active * halt_prob) * remain_cotan,
        ]
    )
    halt_sum[...] = jnp.concatenate(
        [jnp.sum(grad_logit * hidden, axis=0, keepdims=True), jnp.zeros((7, width), f32)], axis=0
    )
    for step in range(1, 4):
        key_copy(step).wait_send()
    finish_gather(0, ffn_in)
    finish_cross(0)
    finish_reduce(0)
    run(1, expert_backward)

    def stage(unit, n, slot):
        return pltpu.make_async_copy(staged.at[slot], terms.at[unit, n], stage_sem.at[slot])

    def weight_terms(i):
        r, n = i // tiles, i % tiles
        part = pl.ds(pl.multiple_of(n * tile, tile), tile)
        total = local * 4 * capacity

        @pl.when(i > 0)
        def _():
            stage(0, 0, 0).wait()
            stage(0, 0, 1).wait()

        left = gathered[:, r].reshape(total, width)
        right = slope[:, r, :, part].reshape(total, tile)
        staged[0] = dot_tn(left, right).astype(bf16)
        stage(r, n, 0).start()
        left = act[:, r, :, part].reshape(total, tile)
        right = grads_in[:, r].reshape(total, width)
        staged[1] = dot_tn(left, right).astype(bf16)
        stage(local + r, n, 1).start()

    reduce_rows(1, weight_terms)
    stage(0, 0, 0).wait()
    stage(0, 0, 1).wait()
    for step in range(1, 4):
        shard = (z + step) % 4
        pltpu.make_async_remote_copy(
            src_ref=share_out.at[0], dst_ref=shares.at[shard], send_sem=share_send.at[0],
            recv_sem=share_recv.at[shard], device_id=across, device_id_type=MESH,
        ).wait_recv()
        share_copy(shard).wait_send()
    share = jnp.concatenate([shares[s, 0:4] for s in range(4)], axis=0)
    gate = jnp.concatenate([slots[s, 4:8] for s in range(4)], axis=0)
    grad_logits_t[...] = share - gate * jnp.sum(share, axis=0, keepdims=True)
    grad_rows[...] = reduced(1)
    finish_gather(1, column.at[1, z])
    finish_cross(1)
    finish_reduce(1)


def slot_targets(routes, experts, room_rows):
    flattened = routes.reshape(-1)
    hot_rows = (flattened[:, None] == jnp.arange(experts, dtype=jnp.int32)[None, :]).astype(jnp.int32)
    before = jnp.cumsum(hot_rows, axis=0) - hot_rows
    return flattened * room_rows + jnp.sum(hot_rows * before, axis=1)


def experts_by_all_to_all(
    capacity, tokens, remain, halting, expert_routes, halt_weight, expert_router, expert_in, expert_out,
    state_cotan, accum_cotan, remain_cotan, hidden_one, ffn_in,
):
    rows, width = tokens.shape
    experts = expert_router.shape[1]
    top = expert_routes.shape[1]
    highest = lax.Precision.HIGHEST
    inputs = tokens.astype(f32)
    active = halting.astype(f32)
    expert_logits = jnp.dot(ffn_in, expert_router, preferred_element_type=f32)
    expert_gate = jax.nn.softmax(jnp.take_along_axis(expert_logits, expert_routes, axis=1), axis=1)
    targets = slot_targets(expert_routes, experts, capacity)

    def spread(values):
        placed = jnp.zeros((experts * capacity, width), bf16).at[targets].set(values)
        return lax.all_to_all(
            placed.reshape(experts, capacity, width), "expert", split_axis=0, concat_axis=1, tiled=True
        )

    def collect(values):
        back = lax.all_to_all(values, "expert", split_axis=1, concat_axis=0, tiled=True)
        back = back.reshape(experts * capacity, width)
        return back[targets].astype(f32).reshape(rows, top, width)

    arrived = spread(jnp.repeat(ffn_in, top, axis=0))
    pre_act = jnp.einsum("erd,edf->erf", arrived, expert_in, preferred_element_type=f32)
    inner_act = jax.nn.gelu(pre_act, approximate=False).astype(bf16)
    produced = jnp.einsum("erf,efd->erd", inner_act, expert_out, preferred_element_type=f32).astype(bf16)
    picked = collect(produced)
    hidden = hidden_one + jnp.sum(expert_gate[:, :, None] * picked, axis=1)
    halt_vector = halt_weight.astype(f32)
    halt_prob = jax.nn.sigmoid(jnp.dot(hidden, halt_vector, precision=highest))
    halt_share = active * remain * halt_prob
    new_state = jnp.where(active[:, None] > 0.5, hidden, inputs).astype(bf16)
    accum_part = halt_share[:, None] * hidden
    remain_left = remain * (1.0 - active * halt_prob)
    grad_accum = accum_cotan.astype(f32)
    grad_share = jnp.sum(grad_accum * hidden, axis=1)
    grad_logit = active * remain * (grad_share - remain_cotan) * halt_prob * (1.0 - halt_prob)
    remain_grad = active * halt_prob * grad_share + (1.0 - active * halt_prob) * remain_cotan
    grad_hidden = (
        active[:, None] * state_cotan.astype(f32)
        + halt_share[:, None] * grad_accum
        + grad_logit[:, None] * halt_vector[None, :]
    )
    halt_sum = jnp.dot(grad_logit, hidden, precision=highest)
    grad_gate = jnp.sum(grad_hidden[:, None, :] * picked, axis=2)
    grad_chosen = expert_gate * (grad_gate - jnp.sum(expert_gate * grad_gate, axis=1, keepdims=True))
    expert_hot = (expert_routes[:, :, None] == jnp.arange(experts, dtype=jnp.int32)[None, None, :]).astype(f32)
    grad_logits = jnp.einsum("tk,tke->te", grad_chosen, expert_hot, precision=highest)
    grad_prod = (expert_gate[:, :, None] * grad_hidden[:, None, :]).astype(bf16)
    grad_arrived = spread(grad_prod.reshape(rows * top, width))
    grad_inner = jnp.einsum("erd,efd->erf", grad_arrived, expert_out, preferred_element_type=f32)
    cumulative = 0.5 * (1.0 + lax.erf(pre_act * (1.0 / math.sqrt(2.0))))
    density = jnp.exp(-0.5 * pre_act * pre_act) * (1.0 / math.sqrt(2.0 * math.pi))
    grad_pre = (grad_inner * (cumulative + pre_act * density)).astype(bf16)
    grad_rows = jnp.einsum("erf,edf->erd", grad_pre, expert_in, preferred_element_type=f32).astype(bf16)
    in_terms = jnp.einsum("erd,erf->edf", arrived, grad_pre, preferred_element_type=f32)
    out_terms = jnp.einsum("erf,erd->efd", inner_act, grad_arrived, preferred_element_type=f32)
    return (
        new_state, accum_part, remain_left, remain_grad, grad_hidden, jnp.sum(collect(grad_rows), axis=1),
        grad_logits.T, jnp.broadcast_to(halt_sum, (8, width)), (in_terms.astype(bf16), out_terms.astype(bf16)),
    )


def vmem(count):
    return [pl.BlockSpec(memory_space=pltpu.VMEM)] * count


def hbm(count):
    return [pl.BlockSpec(memory_space=pl.ANY)] * count


def experts_on_lines(
    capacity, chunks, tokens, scalars, vectors, expert_in, expert_out, state_cotan, accum_cotan, hidden_one, ffn_in,
    slots,
):
    rows, width = tokens.shape
    local, _, hidden_size = expert_in.shape
    shape, buffer, flags = jax.ShapeDtypeStruct, pltpu.VMEM, pltpu.SemaphoreType.DMA
    results = pl.pallas_call(
        functools.partial(expert_exchange, capacity, chunks),
        out_shape=[
            shape((rows, width), bf16),
            shape((rows, width), f32),
            shape((rows, 128), f32),
            shape((rows, width), f32),
            shape((rows, width), f32),
            shape((8 * local, rows), f32),
            shape((8, width), f32),
            shape((2 * local, hidden_size // width, width, width), bf16),
        ],
        in_specs=vmem(8) + hbm(2),
        out_specs=vmem(7) + hbm(1),
        scratch_shapes=[
            buffer((local, width, hidden_size), bf16),
            buffer((local, hidden_size, width), bf16),
            buffer((2, 4, rows, width), bf16),
            buffer((8, local, capacity, width), bf16),
            buffer((8, local, capacity, width), bf16),
            buffer((4, local, capacity, width), bf16),
            buffer((8, local, capacity, hidden_size), bf16),
            buffer((8, local, capacity, hidden_size), bf16),
            buffer((8, local, capacity, width), bf16),
            buffer((4, local, capacity, width), bf16),
            buffer((8, local, capacity, width), bf16),
            buffer((4, local, capacity, width), bf16),
            buffer((4, rows, width), bf16),
            buffer((2, 5, rows, width), bf16),
            buffer((2, width, width), bf16),
            buffer((4, 8, rows), f32),
            buffer((4, 8, rows), f32),
            buffer((4, 8, rows), f32),
            flags((2,)),
            flags((4,)),
            flags((4,)),
            flags((2, 5)),
            flags((2, 4)),
            flags((2, 4, local)),
            flags((2, 4, local)),
            flags((2, 4, local)),
            flags((2, 4, local)),
            flags((2, 5, chunks)),
            flags((2, 5, chunks)),
            flags((4,)),
            flags((4,)),
            flags((2,)),
        ],
        compiler_params=pltpu.CompilerParams(
            vmem_limit_bytes=VMEM_LIMIT, collective_id=1, has_side_effects=True
        ),
        name="expert_exchange",
    )(ffn_in, slots, tokens, hidden_one, state_cotan, accum_cotan, scalars, vectors, expert_in, expert_out)
    new_state, accum_part, pair, grad_hidden, grad_rows, grad_logits_t, halt_sum, terms = results
    return new_state, accum_part, pair[:, 0], pair[:, 1], grad_hidden, grad_rows, grad_logits_t, halt_sum, terms


def sums_on_links(operands, terms, small_rows, wides):
    rows, width = operands[0].shape
    wide_size = wides[0].shape[1]
    units = terms.shape[0]
    shape, buffer, flags = jax.ShapeDtypeStruct, pltpu.VMEM, pltpu.SemaphoreType.DMA
    split = (2, 2, 4, 2)
    block, thin, small = wide_size // 32, width // 32, small_rows // 32
    third = wide_size // 3

    def landing(size, lanes, kind, lead=()):
        return [
            buffer(lead + dims + (size, lanes), kind) for dims in ((2, 4, 2), (4, 2), (3, 2), ())
        ]

    return pl.pallas_call(
        functools.partial(backward_and_sums, 128),
        out_shape=[
            shape((rows, width), f32),
            shape(split + (block, width), bf16),
            shape(split + (thin, wide_size), bf16),
            shape(split + (small, width), f32),
            shape((units, width, width), bf16),
        ],
        in_specs=vmem(24) + hbm(1),
        out_specs=vmem(5),
        scratch_shapes=[
            *wides,
            buffer(split + (block, width), bf16),
            buffer(split + (thin, wide_size), bf16),
            buffer(split + (small, width), f32),
            buffer((units, 2, width, width), bf16),
            buffer((units, 2, width, width), bf16),
            buffer((units, width, width), bf16),
            *landing(block, width, bf16),
            *landing(thin, third, bf16, (3,)),
            *landing(small, width, f32),
            flags((5, 12)),
            flags((5, 12)),
            flags((units, 2)),
            flags((units, 3)),
            flags((units, 3)),
        ],
        compiler_params=pltpu.CompilerParams(
            vmem_limit_bytes=VMEM_LIMIT, collective_id=2, has_side_effects=True
        ),
        name="backward_and_sums",
    )(*operands, terms)


def body(
    mesh_sizes, tokens, remain, halting, head_routes, expert_routes, first_gain, first_bias, query_weight,
    key_weight, value_weight, output_weight, head_router, second_gain, second_bias, expert_router, expert_in,
    expert_out, halt_weight, state_cotan, accum_cotan, remain_cotan,
):
    rows, width = tokens.shape
    head_size = key_weight.shape[1]
    top = head_routes.shape[1]
    wide_size = query_weight.shape[1]
    experts = expert_router.shape[1]
    heads = head_router.shape[1]
    capacity = 4 * rows // experts
    shape = jax.ShapeDtypeStruct
    vectors = jnp.stack(
        [first_gain, first_bias, second_gain, second_bias, halt_weight, halt_weight, halt_weight, halt_weight]
    ).astype(f32)
    scalars = jnp.stack([remain, halting.astype(f32), remain_cotan], axis=1)
    attn_in, query, keys, values, heads_out, spread_out, hidden_one, ffn_in, columns, slots = pl.pallas_call(
        functools.partial(attend_forward, 128),
        out_shape=[
            shape((rows, width), bf16),
            shape((top, rows, head_size), bf16),
            shape((rows, head_size), bf16),
            shape((rows, head_size), bf16),
            shape((top, rows, head_size), f32),
            shape((rows, wide_size), bf16),
            shape((rows, width), f32),
            shape((rows, width), bf16),
            shape((rows, 128), f32),
            shape((experts // 4, 8, rows), f32),
        ],
        in_specs=vmem(10),
        out_specs=vmem(10),
        scratch_shapes=[pltpu.VMEM((rows, wide_size), f32)],
        compiler_params=pltpu.CompilerParams(vmem_limit_bytes=VMEM_LIMIT),
        name="attend_forward",
    )(
        tokens, head_routes, expert_routes, vectors, query_weight, key_weight, value_weight, output_weight,
        head_router, expert_router,
    )
    if mesh_sizes == (4, 8):
        stage = experts_on_lines(
            capacity, 4, tokens, scalars, vectors, expert_in, expert_out, state_cotan, accum_cotan, hidden_one,
            ffn_in, slots,
        )
    else:
        stage = experts_by_all_to_all(
            capacity, tokens, remain, halting, expert_routes, halt_weight, expert_router, expert_in, expert_out,
            state_cotan, accum_cotan, remain_cotan, hidden_one, ffn_in,
        )
    new_state, accum_part, remain_left, remain_grad, grad_hidden, grad_rows, grad_logits_t, halt_sum, terms = stage
    operands = (
        tokens, head_routes, halting[:, None], vectors, query_weight, key_weight, value_weight, output_weight,
        head_router, expert_router, attn_in, query, keys, values, heads_out, spread_out, hidden_one, ffn_in,
        columns, grad_rows, grad_logits_t, grad_hidden, state_cotan, halt_sum,
    )
    small_rows = 256
    wides = [pltpu.VMEM((rows, wide_size), f32), pltpu.VMEM((rows, wide_size), bf16)]
    if mesh_sizes == (4, 8):
        tokens_grad, output_grad, query_grad, small, expert_grads = sums_on_links(
            operands, terms, small_rows, wides
        )
        local = expert_in.shape[0]
        output_grad = output_grad.reshape(wide_size, width).astype(f32)
        query_grad = query_grad.reshape(width, wide_size).astype(f32)
        small = small.reshape(small_rows, width)
        expert_in_grad = expert_grads[:local].astype(f32)
        expert_out_grad = expert_grads[local:].astype(f32)
    else:
        in_terms, out_terms = terms
        expert_in_grad = lax.psum_scatter(in_terms, "dp", scatter_dimension=2, tiled=True).astype(f32)
        expert_out_grad = lax.psum_scatter(out_terms, "dp", scatter_dimension=1, tiled=True).astype(f32)
        small_rows = -(-(2 * head_size + heads + experts + 5) // 8) * 8
        tokens_grad, query_sum, output_sum, small_sum = pl.pallas_call(
            functools.partial(attend_backward, 128),
            out_shape=[
                shape((rows, width), f32),
                shape((width, wide_size), f32),
                shape((wide_size, width), f32),
                shape((small_rows, width), f32),
            ],
            in_specs=vmem(24),
            out_specs=vmem(4),
            scratch_shapes=wides,
            compiler_params=pltpu.CompilerParams(vmem_limit_bytes=VMEM_LIMIT),
            name="attend_backward",
        )(*operands)
        query_grad, output_grad, small = lax.psum((query_sum, output_sum, small_sum), ("dp", "expert"))
    edges = [0, head_size, 2 * head_size, 2 * head_size + heads, 2 * head_size + heads + experts]
    key_grad, value_grad, head_router_grad, expert_router_grad = [
        small[start:stop].T for start, stop in zip(edges[:-1], edges[1:])
    ]
    first_gain_grad, first_bias_grad, second_gain_grad, second_bias_grad, halt_grad = [
        small[edges[-1] + index] for index in range(5)
    ]
    return (
        new_state, accum_part, remain_left, tokens_grad, remain_grad, first_gain_grad, first_bias_grad, query_grad,
        key_grad, value_grad, output_grad, head_router_grad, second_gain_grad, second_bias_grad,
        expert_router_grad, expert_in_grad, expert_out_grad, halt_grad,
    )


def solution(mesh):
    in_specs = (
        P(("dp", "expert"), None),
        P(("dp", "expert")),
        P(("dp", "expert")),
        P(("dp", "expert"), None),
        P(("dp", "expert"), None),
        P(),
        P(),
        P(),
        P(),
        P(),
        P(),
        P(),
        P(),
        P(),
        P(),
        P("expert", None, None),
        P("expert", None, None),
        P(),
        P(("dp", "expert"), None),
        P(("dp", "expert"), None),
        P(("dp", "expert")),
    )
    out_specs = (
        P(("dp", "expert"), None),
        P(("dp", "expert"), None),
        P(("dp", "expert")),
        P(("dp", "expert"), None),
        P(("dp", "expert")),
        P(),
        P(),
        P(),
        P(),
        P(),
        P(),
        P(),
        P(),
        P(),
        P(),
        P("expert", None, "dp"),
        P("expert", "dp", None),
        P(),
    )
    sizes = (mesh.shape["dp"], mesh.shape["expert"])
    run = functools.partial(body, sizes)
    return jax.shard_map(run, mesh=mesh, in_specs=in_specs, out_specs=out_specs, check_vma=False)
```

```python
import functools
import math

import jax
import jax.numpy as jnp
from jax import lax
from jax.experimental import pallas as pl
from jax.experimental.pallas import tpu as pltpu
from jax.sharding import PartitionSpec as P

epsilon = 1e-05
f32 = jnp.float32
bf16 = jnp.bfloat16
MESH = pl.DeviceIdType.MESH
VMEM_LIMIT = 67043328


def dot_nn(left, right):
    return jnp.dot(left, right, preferred_element_type=f32)


def dot_nt(left, right):
    return lax.dot_general(left, right, (((1,), (1,)), ((), ())), preferred_element_type=f32)


def dot_tn(left, right):
    return lax.dot_general(left, right, (((0,), (0,)), ((), ())), preferred_element_type=f32)


def iota(shape, axis):
    return lax.broadcasted_iota(jnp.int32, shape, axis)


def norm_rows(values):
    centre = jnp.mean(values, axis=-1, keepdims=True)
    shifted = values - centre
    spread = jnp.mean(shifted * shifted, axis=-1, keepdims=True)
    inverse = lax.rsqrt(spread + epsilon)
    return shifted * inverse, inverse


def norm_back(upstream, normal, inverse, scales):
    scaled = upstream * scales
    inner = (
        scaled
        - jnp.mean(scaled, axis=-1, keepdims=True)
        - normal * jnp.mean(scaled * normal, axis=-1, keepdims=True)
    )
    return inner * inverse


def pick_heads(wide, place, odd, head_size, positions):
    pair = 2 * head_size
    kept = wide[:, :pair]
    for index in range(1, positions):
        kept = jnp.where(place == index, wide[:, index * pair : (index + 1) * pair], kept)
    return jnp.where(odd, kept[:, head_size:], kept[:, :head_size])


def place_heads(out_ref, columns, places, odds, head_size, positions):
    pair = 2 * head_size
    rows = columns[0].shape[0]
    upper = iota((rows, pair), 1) >= head_size
    doubled = [
        jnp.where(upper == odd, jnp.concatenate([column, column], axis=1), 0.0)
        for column, odd in zip(columns, odds)
    ]
    for index in range(positions):
        total = jnp.zeros((rows, pair), f32)
        for value, place in zip(doubled, places):
            total = total + jnp.where(place == index, value, 0.0)
        out_ref[:, index * pair : (index + 1) * pair] = total.astype(bf16)


def lanes_of(columns, width=128):
    rows = columns[0].shape[0]
    lane = iota((rows, width), 1)
    total = jnp.zeros((rows, width), f32)
    for index, column in enumerate(columns):
        total = jnp.where(lane == index, column, total)
    return total


def soft_columns(logits):
    peak = functools.reduce(jnp.maximum, logits)
    raised = [jnp.exp(value - peak) for value in logits]
    whole = functools.reduce(lambda a, b: a + b, raised)
    return [value / whole for value in raised]


def attend_forward(
    block_rows, tokens, head_routes, expert_routes, vectors, query_weight, key_weight, value_weight,
    output_weight, head_router, expert_router,
    attn_in_out, query_out, key_out, value_out, heads_out, spread_out, hidden_out, ffn_out, columns_out,
    slots_out, wide,
):
    rows, width = tokens.shape
    head_size = key_weight.shape[1]
    positions = query_weight.shape[1] // (2 * head_size)
    top = head_routes.shape[1]
    experts = expert_router.shape[1]
    inputs = tokens[...].astype(f32)
    normal, _ = norm_rows(inputs)
    attn_in = (normal * vectors[0:1, :] + vectors[1:2, :]).astype(bf16)
    attn_in_out[...] = attn_in
    wide[...] = dot_nn(attn_in, query_weight[...])
    keys = dot_nn(attn_in, key_weight[...]).astype(bf16)
    key_out[...] = keys
    values = dot_nn(attn_in, value_weight[...]).astype(bf16)
    value_out[...] = values
    head_logits = dot_nn(attn_in, head_router[...])
    chosen = [head_routes[:, a : a + 1] for a in range(top)]
    places = [value // 2 for value in chosen]
    odds = [value % 2 == 1 for value in chosen]
    head_lane = iota(head_logits.shape, 1)
    gates = soft_columns(
        [
            jnp.sum(jnp.where(head_lane == value, head_logits, 0.0), axis=1, keepdims=True)
            for value in chosen
        ]
    )
    for a in range(top):
        picked = pick_heads(wide, places[a], odds[a], head_size, positions)
        query_out[a] = (picked.astype(bf16).astype(f32) * head_size ** (-0.5)).astype(bf16)
    totals = [[] for _ in range(top)]
    for start in range(0, rows, block_rows):
        stop = start + block_rows
        query = jnp.concatenate([query_out[a, start:stop, :] for a in range(top)], axis=0)
        scores = dot_nt(query, key_out[0:stop, :])
        row_pos = iota((top * block_rows, block_rows), 0) % block_rows
        corner = jnp.where(
            iota((top * block_rows, block_rows), 1) <= row_pos, scores[:, start:], f32(-1e30)
        )
        if start:
            scores = jnp.concatenate([scores[:, :start], corner], axis=1)
        else:
            scores = corner
        peak = jnp.max(scores, axis=1, keepdims=True)
        raised = jnp.exp(scores - peak)
        whole = jnp.sum(raised, axis=1, keepdims=True)
        output = dot_nn(raised.astype(bf16), value_out[0:stop, :]) / whole
        log_total = peak + jnp.log(whole)
        for a in range(top):
            heads_out[a, start:stop, :] = output[a * block_rows : (a + 1) * block_rows]
            totals[a].append(log_total[a * block_rows : (a + 1) * block_rows])
    totals = [jnp.concatenate(value, axis=0) for value in totals]
    columns_out[...] = lanes_of(gates + totals)
    weighted = [
        (gates[a] * heads_out[a]).astype(bf16).astype(f32) for a in range(top)
    ]
    place_heads(spread_out, weighted, places, odds, head_size, positions)
    hidden_one = inputs + dot_nn(spread_out[...], output_weight[...])
    hidden_out[...] = hidden_one
    normal_two, _ = norm_rows(hidden_one)
    ffn_in = (normal_two * vectors[2:3, :] + vectors[3:4, :]).astype(bf16)
    ffn_out[...] = ffn_in
    expert_logits = dot_nn(ffn_in, expert_router[...])
    expert_lane = iota(expert_logits.shape, 1)
    named = [expert_routes[:, c : c + 1] for c in range(2)]
    expert_gates = soft_columns(
        [
            jnp.sum(jnp.where(expert_lane == value, expert_logits, 0.0), axis=1, keepdims=True)
            for value in named
        ]
    )
    lane = iota((rows, 128), 1)
    expert = jnp.where(lane < 2 * experts, (lane // 8) * 4 + lane % 4, -1)
    first, second = expert == named[0], expert == named[1]
    hot = jnp.where(first | second, 1.0, 0.0)
    earlier = (iota((rows, rows), 1) < iota((rows, rows), 0)).astype(f32).astype(bf16)
    before = dot_nn(earlier, hot.astype(bf16))
    slot = jnp.where(hot > 0.5, before, -1.0)
    gate = jnp.where(first, expert_gates[0], jnp.where(second, expert_gates[1], 0.0))
    turned = jnp.where(lane % 8 < 4, slot, gate).T
    slots_out[...] = turned[: 2 * experts].reshape(experts // 4, 8, rows)


def attention_back(
    block_rows, hooks, tokens, head_routes, halting, vectors, query_weight, key_weight, value_weight,
    output_weight, head_router, expert_router, attn_in, query, keys, values, heads_out, spread_out, hidden_one,
    ffn_in, columns, grad_rows, grad_logits_t, grad_hidden, state_cotan, halt_sum, tokens_grad, wide, narrow,
):
    take_output, take_query, take_small, pause = hooks
    rows, width = tokens.shape
    head_size = key_weight.shape[1]
    heads = head_router.shape[1]
    positions = query_weight.shape[1] // (2 * head_size)
    top = head_routes.shape[1]
    gain_one, gain_two = vectors[0:1, :], vectors[2:3, :]
    normal_two, inverse_two = norm_rows(hidden_one[...])
    logits_low = grad_logits_t[...].astype(bf16)
    grad_ffn = grad_rows[...] + lax.dot_general(
        logits_low, expert_router[...], (((0,), (1,)), ((), ())), preferred_element_type=f32
    )
    router_two = dot_nn(logits_low, ffn_in[...])
    gain_two_sum = jnp.sum(grad_ffn * normal_two, axis=0, keepdims=True)
    bias_two_sum = jnp.sum(grad_ffn, axis=0, keepdims=True)
    grad_one = grad_hidden[...] + norm_back(grad_ffn, normal_two, inverse_two, gain_two)
    tokens_grad[...] = grad_one
    grad_attn = grad_one.astype(bf16)
    take_output(lambda part: dot_tn(spread_out[:, part], grad_attn))
    pause(0)
    wide[...] = dot_nt(grad_attn, output_weight[...])
    chosen = [head_routes[:, a : a + 1] for a in range(top)]
    places = [value // 2 for value in chosen]
    odds = [value % 2 == 1 for value in chosen]
    gates = [columns[:, a : a + 1] for a in range(top)]
    pause(1)
    grad_gates, grad_heads = [], []
    for a in range(top):
        picked = pick_heads(wide, places[a], odds[a], head_size, positions)
        grad_gates.append(jnp.sum(picked * heads_out[a], axis=1, keepdims=True))
        grad_heads.append((gates[a] * picked).astype(bf16))
    inner = functools.reduce(lambda a, b: a + b, [g * d for g, d in zip(gates, grad_gates)])
    grad_logit = [g * (d - inner) for g, d in zip(gates, grad_gates)]
    head_lane = iota((rows, heads), 1)
    grad_hot = functools.reduce(
        lambda a, b: a + b,
        [jnp.where(head_lane == chosen[a], grad_logit[a], 0.0) for a in range(top)],
    )
    pause(2)
    grad_keys = [jnp.zeros((block_rows, head_size), f32) for _ in range(rows // block_rows)]
    grad_values = [jnp.zeros((block_rows, head_size), f32) for _ in range(rows // block_rows)]
    grad_query = [[] for _ in range(top)]
    for start in range(0, rows, block_rows):
        stop = start + block_rows
        part = slice(start, stop)
        queries = jnp.concatenate([query[a, part, :] for a in range(top)], axis=0)
        grads = jnp.concatenate([value[part] for value in grad_heads], axis=0)
        total = jnp.concatenate([columns[part, top + a : top + a + 1] for a in range(top)], axis=0)
        scores = dot_nt(queries, keys[0:stop, :])
        row_pos = iota((top * block_rows, block_rows), 0) % block_rows
        corner = jnp.where(
            iota((top * block_rows, block_rows), 1) <= row_pos, scores[:, start:], f32(-1e30)
        )
        if start:
            scores = jnp.concatenate([scores[:, :start], corner], axis=1)
        else:
            scores = corner
        prob = jnp.exp(scores - total)
        grad_prob = dot_nt(grads, values[0:stop, :])
        row_inner = jnp.sum(prob * grad_prob, axis=1, keepdims=True)
        grad_scores = (prob * (grad_prob - row_inner)).astype(bf16)
        grad_q = (dot_nn(grad_scores, keys[0:stop, :]) * head_size ** (-0.5)).astype(bf16)
        for a in range(top):
            grad_query[a].append(grad_q[a * block_rows : (a + 1) * block_rows].astype(f32))
        step_v = dot_tn(prob.astype(bf16), grads)
        step_k = dot_tn(grad_scores, queries)
        for index in range(stop // block_rows):
            piece = slice(index * block_rows, (index + 1) * block_rows)
            grad_values[index] = grad_values[index] + step_v[piece]
            grad_keys[index] = grad_keys[index] + step_k[piece]
        pause(3 + min(start // block_rows, 3))
    grad_query = [jnp.concatenate(value, axis=0) for value in grad_query]
    place_heads(narrow, grad_query, places, odds, head_size, positions)
    take_query(lambda part: dot_tn(attn_in[...], narrow[:, part]), pause)
    grad_k = jnp.concatenate(grad_keys, axis=0).astype(bf16)
    grad_v = jnp.concatenate(grad_values, axis=0).astype(bf16)
    hot_low = grad_hot.astype(bf16)
    grad_in = (
        dot_nt(narrow[...], query_weight[...])
        + dot_nt(grad_k, key_weight[...])
        + dot_nt(grad_v, value_weight[...])
        + dot_nt(hot_low, head_router[...])
    )
    pause(10)
    normal_one, inverse_one = norm_rows(tokens[...].astype(f32))
    take_small(
        [
            dot_tn(grad_k, attn_in[...]),
            dot_tn(grad_v, attn_in[...]),
            dot_tn(hot_low, attn_in[...]),
            router_two,
            jnp.sum(grad_in * normal_one, axis=0, keepdims=True),
            jnp.sum(grad_in, axis=0, keepdims=True),
            gain_two_sum,
            bias_two_sum,
            halt_sum[0:1, :],
        ]
    )
    tokens_grad[...] = (
        tokens_grad[...]
        + norm_back(grad_in, normal_one, inverse_one, gain_one)
        + (1.0 - halting[...].astype(f32)) * state_cotan[...].astype(f32)
    )


def stack_small(pieces, room):
    count = sum(piece.shape[0] for piece in pieces)
    width = pieces[0].shape[1]
    return jnp.concatenate(pieces + [jnp.zeros((room - count, width), f32)], axis=0)


def attend_backward(block_rows, *refs):
    inputs, (tokens_grad, query_sum, output_sum, small_sum, wide, narrow) = refs[:24], refs[24:]

    def take_output(term):
        output_sum[...] = term(slice(None))

    def take_query(term, pause):
        query_sum[...] = term(slice(None))

    def take_small(pieces):
        small_sum[...] = stack_small(pieces, small_sum.shape[0])

    hooks = take_output, take_query, take_small, lambda point: None
    attention_back(block_rows, hooks, *inputs, tokens_grad, wide, narrow)


class SumOverAll:
    def __init__(self, number, place, send, recv, full, final, lands, lanes):
        self.number, self.place, self.send, self.recv = number, place, send, recv
        self.full, self.final, self.lands, self.lanes = full, final, lands, lanes
        self.copies = {}

    def part(self, ref, *lead):
        return ref.at[lead + (slice(None),) * (5 - len(lead)) + (self.lanes,)]

    def go(self, stage, source, target, device):
        self.copies[stage] = pltpu.make_async_remote_copy(
            src_ref=source, dst_ref=target, send_sem=self.send.at[self.number, stage],
            recv_sem=self.recv.at[self.number, stage], device_id=device, device_id_type=MESH,
        )
        self.copies[stage].start()

    def add(self, lead, landed):
        own = self.part(self.full, *lead)
        total = own[...].astype(f32)
        for value in landed:
            total = total + value[...].astype(f32)
        own[...] = total.astype(self.full.dtype)

    def step(self, stage):
        (c, x, z, y), (to_core, to_x, to_y, to_z) = self.place
        full, final = self.full, self.final
        land_core, land_x, land_z, land_y = self.lands
        if stage == 0:
            self.go(0, self.part(full, 1 - c), land_core, to_core)
        elif stage == 1:
            self.copies[0].wait_recv()
            self.add((c, 1 - x), [land_core.at[1 - x]])
            self.go(1, self.part(full, c, 1 - x), land_x, to_x)
            self.add((c, x), [land_core.at[x]])
        elif stage == 2:
            self.copies[1].wait_recv()
            for hop in (2, 1, 3):
                there = (z + hop) % 4
                self.add((c, x, there), [land_x.at[there]])
                self.go(1 + hop, self.part(full, c, x, there), land_z.at[hop - 1], to_z(hop))
            self.add((c, x, z), [land_x.at[z]])
        elif stage == 3:
            for hop in (1, 2, 3):
                self.copies[1 + hop].wait_recv()
            self.add((c, x, z, 1 - y), [land_z.at[hop, 1 - y] for hop in range(3)])
            self.go(5, self.part(full, c, x, z, 1 - y), land_y, to_y)
            self.add((c, x, z, y), [land_z.at[hop, y] for hop in range(3)])
        elif stage == 4:
            self.copies[5].wait_recv()
            total = self.part(full, c, x, z, y)[...].astype(f32) + land_y[...].astype(f32)
            own = self.part(final, c, x, z, y)
            own[...] = total.astype(final.dtype)
            self.go(6, own, own, to_y)
        elif stage == 5:
            self.copies[6].wait_recv()
            own = self.part(final, c, x, z)
            for hop in (2, 1, 3):
                self.go(6 + hop, own, own, to_z(hop))
        elif stage == 6:
            for hop in (1, 2, 3):
                self.copies[6 + hop].wait_recv()
            own = self.part(final, c, x)
            self.go(10, own, own, to_x)
        elif stage == 7:
            self.copies[10].wait_recv()
            own = self.part(final, c)
            self.go(11, own, own, to_core)
        elif stage == 8:
            self.copies[11].wait_recv()
            for copy in self.copies.values():
                copy.wait_send()


POINTS = (2.5, 3.5, 5.0, 6.0, 7.5, 9.5, 12.0, 13.0, 14.0, 15.0, 16.0, 17.5)
OUTPUT_POINT, QUERY_POINTS, SMALL_POINT = 0, (7, 8, 9), 11
DELAYS = {"core": 1.0, "x": 1.7, "z": 2.4, "y": 1.7}
RATES = {"core": 600.0, "x": 48.0, "z": 50.0, "y": 46.0}
WAYS = ("core", "x", "z", "y", "y", "z", "x", "core")


def plan_steps(piece_bytes, items, far_chunks, chunk_bytes):
    sizes = [piece_bytes * part for part in (1 / 2, 1 / 4, 1 / 4, 1 / 32, 1 / 32, 1 / 4, 1 / 4, 1 / 2)]
    free = dict.fromkeys(RATES, 0.0)
    ready, plan, done = [], [[] for _ in POINTS], 0

    def send(way, size, now):
        free[way] = max(free[way], now) + size / RATES[way] / 1000
        return free[way] + DELAYS[way]

    far_ready = [send("core", chunk_bytes, 0.5) for _ in range(far_chunks)]
    sent_far = 0

    def begin(item, now):
        ready.append((send("core", sizes[0], now), item, 1))

    now = 0.0
    for point, time in enumerate(POINTS):
        now = max(now, time)
        last = point == len(POINTS) - 1
        if point == OUTPUT_POINT:
            for item in range(3):
                begin(item, now)
        if point in QUERY_POINTS:
            begin(3 + QUERY_POINTS.index(point), now)
        if point == SMALL_POINT:
            begin(6, now)
        while True:
            ready.sort()
            if sent_far < far_chunks and far_ready[sent_far] <= now and free["y"] <= now + 6.0:
                plan[point].append((-1, sent_far))
                now += 0.2
                send("y", chunk_bytes, now)
                sent_far += 1
                continue
            if ready and (last or ready[0][0] <= now):
                if last and sent_far < far_chunks and max(free["y"] - 6.0, far_ready[sent_far]) < ready[0][0]:
                    now = max(now, free["y"] - 6.0, far_ready[sent_far])
                    continue
                time, item, stage = ready.pop(0)
                now = max(now, time) + (0.3 if stage == 1 else 0.15)
                plan[point].append((item, stage))
                if stage < 8:
                    ready.append((send(WAYS[stage], sizes[stage], now), item, stage + 1))
                continue
            if last and sent_far < far_chunks:
                now = max(now, free["y"] - 6.0, far_ready[sent_far])
                continue
            break
    return plan, now


def backward_and_sums(block_rows, *refs):
    inputs, terms = refs[:24], refs[24]
    tokens_grad, output_final, query_final, small_final, terms_final = refs[25:30]
    (wide, narrow, output_full, query_full, small_full, own_terms, near_terms, far_terms, output_core, output_x,
     output_z, output_y, query_core, query_x, query_z, query_y, small_core, small_x, small_z, small_y, send, recv,
     load_sem, term_send, term_recv, near_send, near_recv) = refs[30:]
    units, width = terms.shape[0], terms.shape[3]
    line, group = lax.axis_index("expert"), lax.axis_index("dp")
    z, x, y, c = line // 2, line % 2, group // 2, group % 2
    to_core, to_y = {"dp": y * 2 + 1 - c}, {"dp": (1 - y) * 2 + c}
    to_x = {"expert": z * 2 + 1 - x}

    def to_z(hop):
        return {"expert": (z + hop) % 4 * 2 + x}

    barrier = pltpu.get_barrier_semaphore()
    for device in (to_core, to_x, to_y, to_z(1), to_z(2), to_z(3)):
        pl.semaphore_signal(barrier, inc=1, device_id=device, device_id_type=MESH)
    far, near = (1 - y) * 2 + c, y * 2 + c
    loads = [
        [
            pltpu.make_async_copy(terms.at[u, quarter], own_terms.at[u, side], load_sem.at[u, side])
            for side, quarter in enumerate((far, near))
        ]
        for u in range(units)
    ]
    for side in range(2):
        for u in range(units):
            loads[u][side].start()
    pl.semaphore_wait(barrier, 6)

    split_rows = width // 2

    def term_copy(u, half, stage):
        rows = pl.ds(half * split_rows, split_rows)
        if stage == 0:
            source = terms.at[u, (1 - y) * 2 + 1 - c, rows]
            target, device = near_terms.at[u, 0, rows], to_core
        else:
            source, target, device = own_terms.at[u, 0, rows], far_terms.at[u, rows], to_y
        return pltpu.make_async_remote_copy(
            src_ref=source, dst_ref=target, send_sem=term_send.at[u, half, stage],
            recv_sem=term_recv.at[u, half, stage], device_id=device, device_id_type=MESH,
        )

    def near_copy(u):
        return pltpu.make_async_remote_copy(
            src_ref=terms.at[u, y * 2 + 1 - c], dst_ref=near_terms.at[u, 1], send_sem=near_send.at[u],
            recv_sem=near_recv.at[u], device_id=to_core, device_id_type=MESH,
        )

    for chunk in range(2 * units):
        term_copy(chunk // 2, chunk % 2, 0).start()

    def send_far(chunk):
        u, half = chunk // 2, chunk % 2
        if half == 0:
            loads[u][0].wait()
        term_copy(u, half, 0).wait_recv()
        rows = pl.ds(half * split_rows, split_rows)
        total = own_terms[u, 0, rows].astype(f32) + near_terms[u, 0, rows].astype(f32)
        own_terms[u, 0, rows] = total.astype(bf16)
        term_copy(u, half, 1).start()

    def finish_near(u):
        loads[u][1].wait()
        near_copy(u).wait_recv()
        for half in range(2):
            term_copy(u, half, 1).wait_recv()
        total = own_terms[u, 1].astype(f32) + near_terms[u, 1].astype(f32) + far_terms[u].astype(f32)
        terms_final[u] = total.astype(bf16)
        near_copy(u).wait_send()
        for half in range(2):
            term_copy(u, half, 0).wait_send()
            term_copy(u, half, 1).wait_send()

    place = (c, x, z, y), (to_core, to_x, to_y, to_z)
    third = query_full.shape[5] // 3
    whole = slice(None)
    items = [
        SumOverAll(
            part, place, send, recv, output_full.at[part], output_final.at[part],
            (output_core.at[part], output_x.at[part], output_z.at[part], output_y.at[part]), whole,
        )
        for part in range(3)
    ] + [
        SumOverAll(
            3 + q, place, send, recv, query_full, query_final,
            (query_core.at[q], query_x.at[q], query_z.at[q], query_y.at[q]), pl.ds(q * third, third),
        )
        for q in range(3)
    ]
    items.append(
        SumOverAll(6, place, send, recv, small_full, small_final, (small_core, small_x, small_z, small_y), whole)
    )
    block_bytes = math.prod(small_full.shape) * 4
    plan, _ = plan_steps(block_bytes, len(items), 2 * units, split_rows * width * 2)

    def take_output(term):
        size = math.prod(output_full.shape[1:-1])
        for part in range(3):
            value = term(slice(part * size, (part + 1) * size))
            output_full[part] = value.astype(bf16).reshape(output_full.shape[1:])
            items[part].step(0)

    def take_query(term, pause):
        for q in range(3):
            part = pl.ds(q * third, third)
            value = term(part).astype(bf16).reshape(query_full.shape[:5] + (third,))
            query_full[:, :, :, :, :, part] = value
            items[3 + q].step(0)
            pause(QUERY_POINTS[q])

    def take_small(pieces):
        rows = math.prod(small_full.shape[:-1])
        small_full[...] = stack_small(pieces, rows).reshape(small_full.shape)
        items[6].step(0)

    def pause(point):
        for item, stage in plan[point]:
            if item < 0:
                send_far(stage)
            else:
                items[item].step(stage)

    attention_back(block_rows, (take_output, take_query, take_small, pause), *inputs, tokens_grad, wide, narrow)
    for u in range(units):
        near_copy(u).start()
    pause(SMALL_POINT)
    for u in range(units):
        finish_near(u)


def expert_exchange(
    capacity, chunks,
    ffn_in, slots, tokens, hidden_one, state_cotan, accum_cotan, scalars, vectors, first_hbm, second_hbm,
    new_state, accum_part, columns_out, grad_hidden, grad_rows, grad_logits_t, halt_sum, terms,
    first, second, column, gathered, grads_in, cross, act, slope, produced, crossed, grad_out, grad_crossed,
    partial, landed, staged, keys, shares, share_out,
    weight_sem, key_send, key_recv, gather_send, gather_recv, cross_send, cross_recv, back_send, back_recv,
    reduce_send, reduce_recv, share_send, share_recv, stage_sem,
):
    rows, width = ffn_in.shape
    local, _, hidden_size = first.shape
    tile = width
    tiles = hidden_size // tile
    piece = rows // chunks
    me = lax.axis_index("expert")
    z, x = me // 2, me % 2
    other = 1 - x
    low = z < 2
    middle = (z == 1) | (z == 2)
    edge = jnp.logical_not(middle)

    def real(mirrored):
        return jnp.where(low, mirrored, 3 - mirrored)

    def along(depth):
        return {"expert": depth * 2 + x}

    across = {"expert": z * 2 + other}

    def order(j):
        return real(jnp.where(middle, jnp.where(j < 2, 1 - j, j), j))

    barrier = pltpu.get_barrier_semaphore()
    for step in range(1, 4):
        pl.semaphore_signal(barrier, inc=1, device_id=along((z + step) % 4), device_id_type=MESH)
    pl.semaphore_signal(barrier, inc=1, device_id=across, device_id_type=MESH)
    loads = [
        pltpu.make_async_copy(first_hbm, first, weight_sem.at[0]),
        pltpu.make_async_copy(second_hbm, second, weight_sem.at[1]),
    ]
    for load in loads:
        load.start()
    column[0, z] = ffn_in[...]
    keys[z] = slots[z]
    pl.semaphore_wait(barrier, 4)

    def key_copy(step):
        there = (z + step) % 4
        return pltpu.make_async_remote_copy(
            src_ref=slots.at[there], dst_ref=keys.at[z], send_sem=key_send.at[step], recv_sem=key_recv.at[z],
            device_id=along(there), device_id_type=MESH,
        )

    def key_arrival(shard):
        return pltpu.make_async_remote_copy(
            src_ref=slots.at[0], dst_ref=keys.at[shard], send_sem=key_send.at[0], recv_sem=key_recv.at[shard],
            device_id=across, device_id_type=MESH,
        )

    def gather_copy(phase, source, shard, depth, index):
        return pltpu.make_async_remote_copy(
            src_ref=source, dst_ref=column.at[phase, shard], send_sem=gather_send.at[phase, index],
            recv_sem=gather_recv.at[phase, shard], device_id=along(depth), device_id_type=MESH,
        )

    def send_own(phase, source):
        @pl.when(edge)
        def _():
            gather_copy(phase, source, z, real(1), 0).start()

        @pl.when(middle)
        def _():
            gather_copy(phase, source, z, real(0), 0).start()
            gather_copy(phase, source, z, real(2), 1).start()

    def forward(phase, mirrored, target, index):
        shard = real(mirrored)
        return gather_copy(phase, column.at[phase, shard], shard, real(target), index)

    def finish_gather(phase, source):
        gather_copy(phase, source, z, real(1), 0).wait_send()

        @pl.when(middle)
        def _():
            gather_copy(phase, source, z, real(2), 1).wait_send()
            forward(phase, 0, 2, 2).wait_send()
            forward(phase, 2, 0, 3).wait_send()
            forward(phase, 3, 0, 4).wait_send()

    def await_shard(phase, mirrored):
        shard = real(mirrored)
        if phase == 0:
            key_arrival(shard).wait_recv()
        gather_copy(phase, column.at[phase, shard], shard, z, 0).wait_recv()

    def await_shards(phase, j):
        @pl.when(edge & (j > 0))
        def _():
            await_shard(phase, j)

        @pl.when(middle & (j == 1))
        def _():
            await_shard(phase, 0)
            forward(phase, 0, 2, 2).start()
            await_shard(phase, 2)
            forward(phase, 2, 0, 3).start()

        @pl.when(middle & (j == 2))
        def _():
            await_shard(phase, 3)
            forward(phase, 3, 0, 4).start()

    def experts_of(shard):
        table = keys[shard]
        found = []
        for own in (True, False):
            for r in range(local):
                here, there = (r, local + r) if own else (local + r, r)
                line = jnp.where(x == 0, table[here : here + 1], table[there : there + 1])
                gate = jnp.where(x == 0, table[4 + here : 5 + here], table[4 + there : 5 + there])
                mask = iota((capacity, rows), 0).astype(f32) == line
                found.append((mask, jnp.sum(jnp.where(mask, gate, 0.0), axis=1, keepdims=True)))
        return found

    def hot_rows(found):
        return jnp.concatenate([jnp.where(mask, 1.0, 0.0).astype(bf16) for mask, _ in found], axis=0)

    def cross_copy(phase, shard, r):
        target = gathered if phase == 0 else grads_in
        return pltpu.make_async_remote_copy(
            src_ref=cross.at[shard, r], dst_ref=target.at[4 + shard, r], send_sem=cross_send.at[phase, shard, r],
            recv_sem=cross_recv.at[phase, shard, r], device_id=across, device_id_type=MESH,
        )

    def back_copy(phase, shard, r):
        source, target = (produced, crossed) if phase == 0 else (grad_out, grad_crossed)
        return pltpu.make_async_remote_copy(
            src_ref=source.at[4 + shard, r], dst_ref=target.at[shard, r], send_sem=back_send.at[phase, shard, r],
            recv_sem=back_recv.at[phase, shard, r], device_id=across, device_id_type=MESH,
        )

    def share_copy(shard):
        return pltpu.make_async_remote_copy(
            src_ref=share_out.at[shard], dst_ref=shares.at[z], send_sem=share_send.at[shard],
            recv_sem=share_recv.at[z], device_id=along(shard), device_id_type=MESH,
        )

    def dispatch(phase, shard):
        found = experts_of(shard)
        taken = dot_nn(hot_rows(found), column[phase, shard])
        lines = []
        for index, (mask, gate) in enumerate(found):
            part = taken[index * capacity : (index + 1) * capacity]
            if phase == 1:
                part = gate * part
            r = index % local
            if index < local:
                (gathered if phase == 0 else grads_in)[shard, r] = part.astype(bf16)
            else:
                cross[shard, r] = part.astype(bf16)
                cross_copy(phase, shard, r).start()
            if phase == 1:
                value = (produced if index < local else crossed)[shard, r].astype(f32)
                inner = jnp.sum(part * value, axis=1, keepdims=True)
                lines.append(jnp.sum(jnp.where(mask, inner, 0.0), axis=0, keepdims=True))
        if phase == 1:
            own, far = lines[:local], lines[local:]
            stack = [jnp.where(x == 0, a, b) for a, b in zip(own + far, far + own)]
            share_out[shard] = jnp.concatenate(stack + [jnp.zeros((4, rows), f32)], axis=0)

            @pl.when(shard == z)
            def _():
                shares[z] = share_out[z]

            @pl.when(shard != z)
            def _():
                share_copy(shard).start()

    def expert_forward(shard):
        def one(r, carry):
            cross_copy(0, shard, r).wait_recv()
            taken = jnp.concatenate([gathered[shard, r], gathered[4 + shard, r]], axis=0)
            total = jnp.zeros((2 * capacity, width), f32)
            for n in range(tiles):
                part = slice(n * tile, (n + 1) * tile)
                pre = dot_nn(taken, first[r, :, part])
                cumulative = 0.5 * (1.0 + lax.erf(pre * (1.0 / math.sqrt(2.0))))
                density = jnp.exp(-0.5 * pre * pre) * (1.0 / math.sqrt(2.0 * math.pi))
                inner = (pre * cumulative).astype(bf16)
                steep = (cumulative + pre * density).astype(bf16)
                act[shard, r, :, part] = inner[:capacity]
                act[4 + shard, r, :, part] = inner[capacity:]
                slope[shard, r, :, part] = steep[:capacity]
                slope[4 + shard, r, :, part] = steep[capacity:]
                total = total + dot_nn(inner, second[r, part, :])
            produced[shard, r] = total[:capacity].astype(bf16)
            produced[4 + shard, r] = total[capacity:].astype(bf16)
            back_copy(0, shard, r).start()
            return carry

        lax.fori_loop(0, local, one, 0)

    def expert_backward(shard):
        def one(r, carry):
            cross_copy(1, shard, r).wait_recv()
            taken = jnp.concatenate([grads_in[shard, r], grads_in[4 + shard, r]], axis=0)
            total = jnp.zeros((2 * capacity, width), f32)
            for n in range(tiles):
                part = slice(n * tile, (n + 1) * tile)
                grad = dot_nt(taken, second[r, part, :])
                steep = jnp.concatenate([slope[shard, r, :, part], slope[4 + shard, r, :, part]], axis=0)
                grad_pre = (grad * steep.astype(f32)).astype(bf16)
                slope[shard, r, :, part] = grad_pre[:capacity]
                slope[4 + shard, r, :, part] = grad_pre[capacity:]
                total = total + dot_nt(grad_pre, first[r, :, part])
            grad_out[shard, r] = total[:capacity].astype(bf16)
            grad_out[4 + shard, r] = total[capacity:].astype(bf16)
            back_copy(1, shard, r).start()
            return carry

        lax.fori_loop(0, local, one, 0)

    def reduce_copy(phase, shard, index, chunk, depth):
        part = pl.ds(pl.multiple_of(chunk * piece, piece), piece)
        return pltpu.make_async_remote_copy(
            src_ref=partial.at[shard, part], dst_ref=landed.at[phase, index, part],
            send_sem=reduce_send.at[phase, index, chunk], recv_sem=reduce_recv.at[phase, index, chunk],
            device_id=along(depth), device_id_type=MESH,
        )

    def combine(phase, j):
        shard = order(j)
        for r in range(local):
            back_copy(phase, shard, r).wait_recv()
        found = experts_of(shard)
        if phase == 0:
            pieces = [
                gate * (produced if index < local else crossed)[shard, index % local].astype(f32)
                for index, (_, gate) in enumerate(found)
            ]
            pieces = [value.astype(bf16) for value in pieces]
        else:
            pieces = [
                (grad_out if index < local else grad_crossed)[shard, index % local]
                for index in range(2 * local)
            ]
        partial[shard] = dot_tn(hot_rows(found), jnp.concatenate(pieces, axis=0)).astype(bf16)

        @pl.when(edge & (j > 0))
        def _():
            for chunk in range(chunks):
                reduce_copy(phase, shard, j - 1, chunk, real(1)).start()

    def pass_on(phase, chunk, source, mirrored, index, depth):
        shard = real(mirrored)
        reduce_copy(phase, shard, source, chunk, z).wait_recv()
        part = pl.ds(pl.multiple_of(chunk * piece, piece), piece)
        partial[shard, part] = (
            partial[shard, part].astype(f32) + landed[phase, source, part].astype(f32)
        ).astype(bf16)
        reduce_copy(phase, shard, index, chunk, depth).start()

    def reduce_rows(phase, filler):
        def step(i, carry):
            @pl.when(middle & (i < chunks))
            def _():
                pass_on(phase, i, 1, 2, 3, real(2))

            @pl.when(middle & (i >= chunks))
            def _():
                pass_on(phase, i - chunks, 2, 3, 4, real(2))
                pass_on(phase, i - chunks, 4, 0, 0, real(0))

            filler(i)
            return carry

        lax.fori_loop(0, 2 * chunks, step, 0)

    def reduced(phase):
        for chunk in range(chunks):
            reduce_copy(phase, z, 0, chunk, z).wait_recv()
        total = partial[z].astype(f32) + landed[phase, 0].astype(f32)

        @pl.when(middle)
        def _():
            for chunk in range(chunks):
                reduce_copy(phase, z, 3, chunk, z).wait_recv()

        return total + jnp.where(middle, landed[phase, 3].astype(f32), 0.0)

    def finish_reduce(phase):
        @pl.when(edge)
        def _():
            for index in range(3):
                for chunk in range(chunks):
                    reduce_copy(phase, real(index + 1), index, chunk, real(1)).wait_send()

        @pl.when(middle)
        def _():
            for chunk in range(chunks):
                reduce_copy(phase, real(2), 3, chunk, real(2)).wait_send()
                reduce_copy(phase, real(3), 4, chunk, real(2)).wait_send()
                reduce_copy(phase, real(0), 0, chunk, real(0)).wait_send()

    def finish_cross(phase):
        for shard in range(4):
            for r in range(local):
                cross_copy(phase, shard, r).wait_send()
                back_copy(phase, shard, r).wait_send()

    def run(phase, experts):
        def step(j, carry):
            @pl.when(j >= 2)
            def _():
                combine(phase, j - 2)

            @pl.when((j >= 1) & (j <= 4))
            def _():
                experts(order(j - 1))

            @pl.when(j <= 3)
            def _():
                await_shards(phase, j)
                dispatch(phase, order(j))

            return carry

        lax.fori_loop(0, 6, step, 0)

    for step in range(1, 4):
        key_copy(step).start()
    send_own(0, ffn_in)
    for load in loads:
        load.wait()
    run(0, expert_forward)
    reduce_rows(0, lambda i: None)
    hidden = hidden_one[...] + reduced(0)
    remain, active, remain_cotan = scalars[:, 0:1], scalars[:, 1:2], scalars[:, 2:3]
    halt_vector = vectors[4:5, :]
    halt_prob = jax.nn.sigmoid(jnp.sum(hidden * halt_vector, axis=1, keepdims=True))
    halt_share = active * remain * halt_prob
    grad_accum = accum_cotan[...].astype(f32)
    grad_share = jnp.sum(grad_accum * hidden, axis=1, keepdims=True)
    grad_logit = active * remain * (grad_share - remain_cotan) * halt_prob * (1.0 - halt_prob)
    grad_here = active * state_cotan[...].astype(f32) + halt_share * grad_accum + grad_logit * halt_vector
    grad_hidden[...] = grad_here
    column[1, z] = grad_here.astype(bf16)
    send_own(1, column.at[1, z])
    new_state[...] = jnp.where(active > 0.5, hidden, tokens[...].astype(f32)).astype(bf16)
    accum_part[...] = halt_share * hidden
    columns_out[...] = lanes_of(
        [
            remain * (1.0 - active * halt_prob),
            active * halt_prob * grad_share + (1.0 - active * halt_prob) * remain_cotan,
        ]
    )
    halt_sum[...] = jnp.concatenate(
        [jnp.sum(grad_logit * hidden, axis=0, keepdims=True), jnp.zeros((7, width), f32)], axis=0
    )
    for step in range(1, 4):
        key_copy(step).wait_send()
    finish_gather(0, ffn_in)
    finish_cross(0)
    finish_reduce(0)
    run(1, expert_backward)

    def stage(unit, n, slot):
        return pltpu.make_async_copy(staged.at[slot], terms.at[unit, n], stage_sem.at[slot])

    def weight_terms(i):
        r, n = i // tiles, i % tiles
        part = pl.ds(pl.multiple_of(n * tile, tile), tile)
        total = local * 4 * capacity

        @pl.when(i > 0)
        def _():
            stage(0, 0, 0).wait()
            stage(0, 0, 1).wait()

        left = gathered[:, r].reshape(total, width)
        right = slope[:, r, :, part].reshape(total, tile)
        staged[0] = dot_tn(left, right).astype(bf16)
        stage(r, n, 0).start()
        left = act[:, r, :, part].reshape(total, tile)
        right = grads_in[:, r].reshape(total, width)
        staged[1] = dot_tn(left, right).astype(bf16)
        stage(local + r, n, 1).start()

    reduce_rows(1, weight_terms)
    stage(0, 0, 0).wait()
    stage(0, 0, 1).wait()
    for step in range(1, 4):
        shard = (z + step) % 4
        pltpu.make_async_remote_copy(
            src_ref=share_out.at[0], dst_ref=shares.at[shard], send_sem=share_send.at[0],
            recv_sem=share_recv.at[shard], device_id=across, device_id_type=MESH,
        ).wait_recv()
        share_copy(shard).wait_send()
    share = jnp.concatenate([shares[s, 0:4] for s in range(4)], axis=0)
    gate = jnp.concatenate([slots[s, 4:8] for s in range(4)], axis=0)
    grad_logits_t[...] = share - gate * jnp.sum(share, axis=0, keepdims=True)
    grad_rows[...] = reduced(1)
    finish_gather(1, column.at[1, z])
    finish_cross(1)
    finish_reduce(1)


def slot_targets(routes, experts, room_rows):
    flattened = routes.reshape(-1)
    hot_rows = (flattened[:, None] == jnp.arange(experts, dtype=jnp.int32)[None, :]).astype(jnp.int32)
    before = jnp.cumsum(hot_rows, axis=0) - hot_rows
    return flattened * room_rows + jnp.sum(hot_rows * before, axis=1)


def experts_by_all_to_all(
    capacity, tokens, remain, halting, expert_routes, halt_weight, expert_router, expert_in, expert_out,
    state_cotan, accum_cotan, remain_cotan, hidden_one, ffn_in,
):
    rows, width = tokens.shape
    experts = expert_router.shape[1]
    top = expert_routes.shape[1]
    highest = lax.Precision.HIGHEST
    inputs = tokens.astype(f32)
    active = halting.astype(f32)
    expert_logits = jnp.dot(ffn_in, expert_router, preferred_element_type=f32)
    expert_gate = jax.nn.softmax(jnp.take_along_axis(expert_logits, expert_routes, axis=1), axis=1)
    targets = slot_targets(expert_routes, experts, capacity)

    def spread(values):
        placed = jnp.zeros((experts * capacity, width), bf16).at[targets].set(values)
        return lax.all_to_all(
            placed.reshape(experts, capacity, width), "expert", split_axis=0, concat_axis=1, tiled=True
        )

    def collect(values):
        back = lax.all_to_all(values, "expert", split_axis=1, concat_axis=0, tiled=True)
        back = back.reshape(experts * capacity, width)
        return back[targets].astype(f32).reshape(rows, top, width)

    arrived = spread(jnp.repeat(ffn_in, top, axis=0))
    pre_act = jnp.einsum("erd,edf->erf", arrived, expert_in, preferred_element_type=f32)
    inner_act = jax.nn.gelu(pre_act, approximate=False).astype(bf16)
    produced = jnp.einsum("erf,efd->erd", inner_act, expert_out, preferred_element_type=f32).astype(bf16)
    picked = collect(produced)
    hidden = hidden_one + jnp.sum(expert_gate[:, :, None] * picked, axis=1)
    halt_vector = halt_weight.astype(f32)
    halt_prob = jax.nn.sigmoid(jnp.dot(hidden, halt_vector, precision=highest))
    halt_share = active * remain * halt_prob
    new_state = jnp.where(active[:, None] > 0.5, hidden, inputs).astype(bf16)
    accum_part = halt_share[:, None] * hidden
    remain_left = remain * (1.0 - active * halt_prob)
    grad_accum = accum_cotan.astype(f32)
    grad_share = jnp.sum(grad_accum * hidden, axis=1)
    grad_logit = active * remain * (grad_share - remain_cotan) * halt_prob * (1.0 - halt_prob)
    remain_grad = active * halt_prob * grad_share + (1.0 - active * halt_prob) * remain_cotan
    grad_hidden = (
        active[:, None] * state_cotan.astype(f32)
        + halt_share[:, None] * grad_accum
        + grad_logit[:, None] * halt_vector[None, :]
    )
    halt_sum = jnp.dot(grad_logit, hidden, precision=highest)
    grad_gate = jnp.sum(grad_hidden[:, None, :] * picked, axis=2)
    grad_chosen = expert_gate * (grad_gate - jnp.sum(expert_gate * grad_gate, axis=1, keepdims=True))
    expert_hot = (expert_routes[:, :, None] == jnp.arange(experts, dtype=jnp.int32)[None, None, :]).astype(f32)
    grad_logits = jnp.einsum("tk,tke->te", grad_chosen, expert_hot, precision=highest)
    grad_prod = (expert_gate[:, :, None] * grad_hidden[:, None, :]).astype(bf16)
    grad_arrived = spread(grad_prod.reshape(rows * top, width))
    grad_inner = jnp.einsum("erd,efd->erf", grad_arrived, expert_out, preferred_element_type=f32)
    cumulative = 0.5 * (1.0 + lax.erf(pre_act * (1.0 / math.sqrt(2.0))))
    density = jnp.exp(-0.5 * pre_act * pre_act) * (1.0 / math.sqrt(2.0 * math.pi))
    grad_pre = (grad_inner * (cumulative + pre_act * density)).astype(bf16)
    grad_rows = jnp.einsum("erf,edf->erd", grad_pre, expert_in, preferred_element_type=f32).astype(bf16)
    in_terms = jnp.einsum("erd,erf->edf", arrived, grad_pre, preferred_element_type=f32)
    out_terms = jnp.einsum("erf,erd->efd", inner_act, grad_arrived, preferred_element_type=f32)
    return (
        new_state, accum_part, remain_left, remain_grad, grad_hidden, jnp.sum(collect(grad_rows), axis=1),
        grad_logits.T, jnp.broadcast_to(halt_sum, (8, width)), (in_terms.astype(bf16), out_terms.astype(bf16)),
    )


def vmem(count):
    return [pl.BlockSpec(memory_space=pltpu.VMEM)] * count


def hbm(count):
    return [pl.BlockSpec(memory_space=pl.ANY)] * count


def experts_on_lines(
    capacity, chunks, tokens, scalars, vectors, expert_in, expert_out, state_cotan, accum_cotan, hidden_one, ffn_in,
    slots,
):
    rows, width = tokens.shape
    local, _, hidden_size = expert_in.shape
    shape, buffer, flags = jax.ShapeDtypeStruct, pltpu.VMEM, pltpu.SemaphoreType.DMA
    results = pl.pallas_call(
        functools.partial(expert_exchange, capacity, chunks),
        out_shape=[
            shape((rows, width), bf16),
            shape((rows, width), f32),
            shape((rows, 128), f32),
            shape((rows, width), f32),
            shape((rows, width), f32),
            shape((8 * local, rows), f32),
            shape((8, width), f32),
            shape((2 * local, hidden_size // width, width, width), bf16),
        ],
        in_specs=vmem(8) + hbm(2),
        out_specs=vmem(7) + hbm(1),
        scratch_shapes=[
            buffer((local, width, hidden_size), bf16),
            buffer((local, hidden_size, width), bf16),
            buffer((2, 4, rows, width), bf16),
            buffer((8, local, capacity, width), bf16),
            buffer((8, local, capacity, width), bf16),
            buffer((4, local, capacity, width), bf16),
            buffer((8, local, capacity, hidden_size), bf16),
            buffer((8, local, capacity, hidden_size), bf16),
            buffer((8, local, capacity, width), bf16),
            buffer((4, local, capacity, width), bf16),
            buffer((8, local, capacity, width), bf16),
            buffer((4, local, capacity, width), bf16),
            buffer((4, rows, width), bf16),
            buffer((2, 5, rows, width), bf16),
            buffer((2, width, width), bf16),
            buffer((4, 8, rows), f32),
            buffer((4, 8, rows), f32),
            buffer((4, 8, rows), f32),
            flags((2,)),
            flags((4,)),
            flags((4,)),
            flags((2, 5)),
            flags((2, 4)),
            flags((2, 4, local)),
            flags((2, 4, local)),
            flags((2, 4, local)),
            flags((2, 4, local)),
            flags((2, 5, chunks)),
            flags((2, 5, chunks)),
            flags((4,)),
            flags((4,)),
            flags((2,)),
        ],
        compiler_params=pltpu.CompilerParams(
            vmem_limit_bytes=VMEM_LIMIT, collective_id=1, has_side_effects=True
        ),
        name="expert_exchange",
    )(ffn_in, slots, tokens, hidden_one, state_cotan, accum_cotan, scalars, vectors, expert_in, expert_out)
    new_state, accum_part, pair, grad_hidden, grad_rows, grad_logits_t, halt_sum, terms = results
    return new_state, accum_part, pair[:, 0], pair[:, 1], grad_hidden, grad_rows, grad_logits_t, halt_sum, terms


def sums_on_links(operands, terms, small_rows, wides):
    rows, width = operands[0].shape
    wide_size = wides[0].shape[1]
    units = terms.shape[0]
    shape, buffer, flags = jax.ShapeDtypeStruct, pltpu.VMEM, pltpu.SemaphoreType.DMA
    split = (2, 2, 4, 2)
    block, thin, small = wide_size // 96, width // 32, small_rows // 32
    third = wide_size // 3

    def landing(size, lanes, kind, lead=()):
        return [
            buffer(lead + dims + (size, lanes), kind) for dims in ((2, 4, 2), (4, 2), (3, 2), ())
        ]

    return pl.pallas_call(
        functools.partial(backward_and_sums, 128),
        out_shape=[
            shape((rows, width), f32),
            shape((3,) + split + (block, width), bf16),
            shape(split + (thin, wide_size), bf16),
            shape(split + (small, width), f32),
            shape((units, width, width), bf16),
        ],
        in_specs=vmem(24) + hbm(1),
        out_specs=vmem(5),
        scratch_shapes=[
            *wides,
            buffer((3,) + split + (block, width), bf16),
            buffer(split + (thin, wide_size), bf16),
            buffer(split + (small, width), f32),
            buffer((units, 2, width, width), bf16),
            buffer((units, 2, width, width), bf16),
            buffer((units, width, width), bf16),
            *landing(block, width, bf16, (3,)),
            *landing(thin, third, bf16, (3,)),
            *landing(small, width, f32),
            flags((7, 12)),
            flags((7, 12)),
            flags((units, 2)),
            flags((units, 2, 2)),
            flags((units, 2, 2)),
            flags((units,)),
            flags((units,)),
        ],
        compiler_params=pltpu.CompilerParams(
            vmem_limit_bytes=VMEM_LIMIT, collective_id=2, has_side_effects=True
        ),
        name="backward_and_sums",
    )(*operands, terms)


def body(
    mesh_sizes, tokens, remain, halting, head_routes, expert_routes, first_gain, first_bias, query_weight,
    key_weight, value_weight, output_weight, head_router, second_gain, second_bias, expert_router, expert_in,
    expert_out, halt_weight, state_cotan, accum_cotan, remain_cotan,
):
    rows, width = tokens.shape
    head_size = key_weight.shape[1]
    top = head_routes.shape[1]
    wide_size = query_weight.shape[1]
    experts = expert_router.shape[1]
    heads = head_router.shape[1]
    capacity = 4 * rows // experts
    shape = jax.ShapeDtypeStruct
    vectors = jnp.stack(
        [first_gain, first_bias, second_gain, second_bias, halt_weight, halt_weight, halt_weight, halt_weight]
    ).astype(f32)
    scalars = jnp.stack([remain, halting.astype(f32), remain_cotan], axis=1)
    attn_in, query, keys, values, heads_out, spread_out, hidden_one, ffn_in, columns, slots = pl.pallas_call(
        functools.partial(attend_forward, 128),
        out_shape=[
            shape((rows, width), bf16),
            shape((top, rows, head_size), bf16),
            shape((rows, head_size), bf16),
            shape((rows, head_size), bf16),
            shape((top, rows, head_size), f32),
            shape((rows, wide_size), bf16),
            shape((rows, width), f32),
            shape((rows, width), bf16),
            shape((rows, 128), f32),
            shape((experts // 4, 8, rows), f32),
        ],
        in_specs=vmem(10),
        out_specs=vmem(10),
        scratch_shapes=[pltpu.VMEM((rows, wide_size), f32)],
        compiler_params=pltpu.CompilerParams(vmem_limit_bytes=VMEM_LIMIT),
        name="attend_forward",
    )(
        tokens, head_routes, expert_routes, vectors, query_weight, key_weight, value_weight, output_weight,
        head_router, expert_router,
    )
    if mesh_sizes == (4, 8):
        stage = experts_on_lines(
            capacity, 4, tokens, scalars, vectors, expert_in, expert_out, state_cotan, accum_cotan, hidden_one,
            ffn_in, slots,
        )
    else:
        stage = experts_by_all_to_all(
            capacity, tokens, remain, halting, expert_routes, halt_weight, expert_router, expert_in, expert_out,
            state_cotan, accum_cotan, remain_cotan, hidden_one, ffn_in,
        )
    new_state, accum_part, remain_left, remain_grad, grad_hidden, grad_rows, grad_logits_t, halt_sum, terms = stage
    operands = (
        tokens, head_routes, halting[:, None], vectors, query_weight, key_weight, value_weight, output_weight,
        head_router, expert_router, attn_in, query, keys, values, heads_out, spread_out, hidden_one, ffn_in,
        columns, grad_rows, grad_logits_t, grad_hidden, state_cotan, halt_sum,
    )
    small_rows = 256
    wides = [pltpu.VMEM((rows, wide_size), f32), pltpu.VMEM((rows, wide_size), bf16)]
    if mesh_sizes == (4, 8):
        tokens_grad, output_grad, query_grad, small, expert_grads = sums_on_links(
            operands, terms, small_rows, wides
        )
        local = expert_in.shape[0]
        output_grad = output_grad.reshape(wide_size, width).astype(f32)
        query_grad = query_grad.reshape(width, wide_size).astype(f32)
        small = small.reshape(small_rows, width)
        expert_in_grad = expert_grads[:local].astype(f32)
        expert_out_grad = expert_grads[local:].astype(f32)
    else:
        in_terms, out_terms = terms
        expert_in_grad = lax.psum_scatter(in_terms, "dp", scatter_dimension=2, tiled=True).astype(f32)
        expert_out_grad = lax.psum_scatter(out_terms, "dp", scatter_dimension=1, tiled=True).astype(f32)
        small_rows = -(-(2 * head_size + heads + experts + 5) // 8) * 8
        tokens_grad, query_sum, output_sum, small_sum = pl.pallas_call(
            functools.partial(attend_backward, 128),
            out_shape=[
                shape((rows, width), f32),
                shape((width, wide_size), f32),
                shape((wide_size, width), f32),
                shape((small_rows, width), f32),
            ],
            in_specs=vmem(24),
            out_specs=vmem(4),
            scratch_shapes=wides,
            compiler_params=pltpu.CompilerParams(vmem_limit_bytes=VMEM_LIMIT),
            name="attend_backward",
        )(*operands)
        query_grad, output_grad, small = lax.psum((query_sum, output_sum, small_sum), ("dp", "expert"))
    edges = [0, head_size, 2 * head_size, 2 * head_size + heads, 2 * head_size + heads + experts]
    key_grad, value_grad, head_router_grad, expert_router_grad = [
        small[start:stop].T for start, stop in zip(edges[:-1], edges[1:])
    ]
    first_gain_grad, first_bias_grad, second_gain_grad, second_bias_grad, halt_grad = [
        small[edges[-1] + index] for index in range(5)
    ]
    return (
        new_state, accum_part, remain_left, tokens_grad, remain_grad, first_gain_grad, first_bias_grad, query_grad,
        key_grad, value_grad, output_grad, head_router_grad, second_gain_grad, second_bias_grad,
        expert_router_grad, expert_in_grad, expert_out_grad, halt_grad,
    )


def solution(mesh):
    in_specs = (
        P(("dp", "expert"), None),
        P(("dp", "expert")),
        P(("dp", "expert")),
        P(("dp", "expert"), None),
        P(("dp", "expert"), None),
        P(),
        P(),
        P(),
        P(),
        P(),
        P(),
        P(),
        P(),
        P(),
        P(),
        P("expert", None, None),
        P("expert", None, None),
        P(),
        P(("dp", "expert"), None),
        P(("dp", "expert"), None),
        P(("dp", "expert")),
    )
    out_specs = (
        P(("dp", "expert"), None),
        P(("dp", "expert"), None),
        P(("dp", "expert")),
        P(("dp", "expert"), None),
        P(("dp", "expert")),
        P(),
        P(),
        P(),
        P(),
        P(),
        P(),
        P(),
        P(),
        P(),
        P(),
        P("expert", None, "dp"),
        P("expert", "dp", None),
        P(),
    )
    sizes = (mesh.shape["dp"], mesh.shape["expert"])
    run = functools.partial(body, sizes)
    return jax.shard_map(run, mesh=mesh, in_specs=in_specs, out_specs=out_specs, check_vma=False)
```

```python
import functools
import math

import jax
import jax.numpy as jnp
from jax import lax
from jax.experimental import pallas as pl
from jax.experimental.pallas import tpu as pltpu
from jax.sharding import PartitionSpec as P

epsilon = 1e-05
f32 = jnp.float32
bf16 = jnp.bfloat16
MESH = pl.DeviceIdType.MESH
VMEM_LIMIT = 67043328


def dot_nn(left, right):
    return jnp.dot(left, right, preferred_element_type=f32)


def dot_nt(left, right):
    return lax.dot_general(left, right, (((1,), (1,)), ((), ())), preferred_element_type=f32)


def dot_tn(left, right):
    return lax.dot_general(left, right, (((0,), (0,)), ((), ())), preferred_element_type=f32)


def iota(shape, axis):
    return lax.broadcasted_iota(jnp.int32, shape, axis)


def norm_rows(values):
    centre = jnp.mean(values, axis=-1, keepdims=True)
    shifted = values - centre
    spread = jnp.mean(shifted * shifted, axis=-1, keepdims=True)
    inverse = lax.rsqrt(spread + epsilon)
    return shifted * inverse, inverse


def norm_back(upstream, normal, inverse, scales):
    scaled = upstream * scales
    inner = (
        scaled
        - jnp.mean(scaled, axis=-1, keepdims=True)
        - normal * jnp.mean(scaled * normal, axis=-1, keepdims=True)
    )
    return inner * inverse


def pick_heads(wide, place, odd, head_size, positions):
    pair = 2 * head_size
    kept = wide[:, :pair]
    for index in range(1, positions):
        kept = jnp.where(place == index, wide[:, index * pair : (index + 1) * pair], kept)
    return jnp.where(odd, kept[:, head_size:], kept[:, :head_size])


def place_heads(out_ref, columns, places, odds, head_size, positions):
    pair = 2 * head_size
    rows = columns[0].shape[0]
    upper = iota((rows, pair), 1) >= head_size
    doubled = [
        jnp.where(upper == odd, jnp.concatenate([column, column], axis=1), 0.0)
        for column, odd in zip(columns, odds)
    ]
    for index in range(positions):
        total = jnp.zeros((rows, pair), f32)
        for value, place in zip(doubled, places):
            total = total + jnp.where(place == index, value, 0.0)
        out_ref[:, index * pair : (index + 1) * pair] = total.astype(bf16)


def lanes_of(columns, width=128):
    rows = columns[0].shape[0]
    lane = iota((rows, width), 1)
    total = jnp.zeros((rows, width), f32)
    for index, column in enumerate(columns):
        total = jnp.where(lane == index, column, total)
    return total


def soft_columns(logits):
    peak = functools.reduce(jnp.maximum, logits)
    raised = [jnp.exp(value - peak) for value in logits]
    whole = functools.reduce(lambda a, b: a + b, raised)
    return [value / whole for value in raised]


def attend_forward(
    block_rows, tokens, head_routes, expert_routes, remain, halting, remain_cotan, first_gain, first_bias,
    second_gain, second_bias, halt_weight, query_weight, key_weight, value_weight, output_weight, head_router,
    expert_router,
    attn_in_out, query_out, key_out, value_out, heads_out, spread_out, hidden_out, ffn_out, columns_out,
    slots_out, vectors, wide,
):
    rows, width = tokens.shape
    head_size = key_weight.shape[0]
    positions = query_weight.shape[1] // (2 * head_size)
    top = head_routes.shape[0]
    experts = expert_router.shape[0]
    for index, vector in enumerate((first_gain, first_bias, second_gain, second_bias, halt_weight)):
        vectors[index : index + 1, :] = vector[...].astype(f32)
    vectors[5:8, :] = jnp.zeros((3, width), f32)
    lines = [head_routes[...], expert_routes[...], halting[...]]
    lines = [value.astype(f32) for value in lines] + [remain[...], remain_cotan[...]]
    filled = sum(value.shape[0] for value in lines)
    table = jnp.concatenate(lines + [jnp.zeros((128 - filled, rows), f32)], axis=0).T
    inputs = tokens[...].astype(f32)
    normal, _ = norm_rows(inputs)
    attn_in = (normal * vectors[0:1, :] + vectors[1:2, :]).astype(bf16)
    attn_in_out[...] = attn_in
    wide[...] = dot_nn(attn_in, query_weight[...])
    keys = dot_nt(attn_in, key_weight[...]).astype(bf16)
    key_out[...] = keys
    values = dot_nt(attn_in, value_weight[...]).astype(bf16)
    value_out[...] = values
    head_logits = dot_nt(attn_in, head_router[...])
    routes = table.astype(jnp.int32)
    chosen = [routes[:, a : a + 1] for a in range(top)]
    places = [value // 2 for value in chosen]
    odds = [value % 2 == 1 for value in chosen]
    head_lane = iota(head_logits.shape, 1)
    gates = soft_columns(
        [
            jnp.sum(jnp.where(head_lane == value, head_logits, 0.0), axis=1, keepdims=True)
            for value in chosen
        ]
    )
    for a in range(top):
        picked = pick_heads(wide, places[a], odds[a], head_size, positions)
        query_out[a] = (picked.astype(bf16).astype(f32) * head_size ** (-0.5)).astype(bf16)
    totals = [[] for _ in range(top)]
    for start in range(0, rows, block_rows):
        stop = start + block_rows
        query = jnp.concatenate([query_out[a, start:stop, :] for a in range(top)], axis=0)
        scores = dot_nt(query, key_out[0:stop, :])
        row_pos = iota((top * block_rows, block_rows), 0) % block_rows
        corner = jnp.where(
            iota((top * block_rows, block_rows), 1) <= row_pos, scores[:, start:], f32(-1e30)
        )
        if start:
            scores = jnp.concatenate([scores[:, :start], corner], axis=1)
        else:
            scores = corner
        peak = jnp.max(scores, axis=1, keepdims=True)
        raised = jnp.exp(scores - peak)
        whole = jnp.sum(raised, axis=1, keepdims=True)
        output = dot_nn(raised.astype(bf16), value_out[0:stop, :]) / whole
        log_total = peak + jnp.log(whole)
        for a in range(top):
            heads_out[a, start:stop, :] = output[a * block_rows : (a + 1) * block_rows]
            totals[a].append(log_total[a * block_rows : (a + 1) * block_rows])
    totals = [jnp.concatenate(value, axis=0) for value in totals]
    columns_out[...] = lanes_of(
        gates + totals + [table[:, index : index + 1] for index in (top + 3, top + 2, top + 4, *range(top))]
    )
    weighted = [
        (gates[a] * heads_out[a]).astype(bf16).astype(f32) for a in range(top)
    ]
    place_heads(spread_out, weighted, places, odds, head_size, positions)
    hidden_one = inputs + dot_nn(spread_out[...], output_weight[...])
    hidden_out[...] = hidden_one
    normal_two, _ = norm_rows(hidden_one)
    ffn_in = (normal_two * vectors[2:3, :] + vectors[3:4, :]).astype(bf16)
    ffn_out[...] = ffn_in
    expert_logits = dot_nt(ffn_in, expert_router[...])
    expert_lane = iota(expert_logits.shape, 1)
    named = [routes[:, top + c : top + c + 1] for c in range(2)]
    expert_gates = soft_columns(
        [
            jnp.sum(jnp.where(expert_lane == value, expert_logits, 0.0), axis=1, keepdims=True)
            for value in named
        ]
    )
    lane = iota((rows, 128), 1)
    expert = jnp.where(lane < 2 * experts, (lane // 8) * 4 + lane % 4, -1)
    first, second = expert == named[0], expert == named[1]
    hot = jnp.where(first | second, 1.0, 0.0)
    earlier = (iota((rows, rows), 1) < iota((rows, rows), 0)).astype(f32).astype(bf16)
    before = dot_nn(earlier, hot.astype(bf16))
    slot = jnp.where(hot > 0.5, before, -1.0)
    gate = jnp.where(first, expert_gates[0], jnp.where(second, expert_gates[1], 0.0))
    turned = jnp.where(lane % 8 < 4, slot, gate).T
    slots_out[...] = turned[: 2 * experts].reshape(experts // 4, 8, rows)


def attention_back(
    block_rows, hooks, tokens, vectors, query_weight, key_weight, value_weight,
    output_weight, head_router, expert_router, attn_in, query, keys, values, heads_out, spread_out, hidden_one,
    ffn_in, columns, grad_rows, grad_logits_t, grad_hidden, state_cotan, halt_sum, tokens_grad, wide, narrow,
):
    take_output, take_query, take_small, pause = hooks
    rows, width = tokens.shape
    head_size = key_weight.shape[0]
    heads = head_router.shape[0]
    positions = query_weight.shape[1] // (2 * head_size)
    top = query.shape[0]
    active_lane = 2 * top + 1
    gain_one, gain_two = vectors[0:1, :], vectors[2:3, :]
    normal_two, inverse_two = norm_rows(hidden_one[...])
    logits_low = grad_logits_t[...].astype(bf16)
    grad_ffn = grad_rows[...] + dot_tn(logits_low, expert_router[...])
    router_two = dot_nn(logits_low, ffn_in[...])
    gain_two_sum = jnp.sum(grad_ffn * normal_two, axis=0, keepdims=True)
    bias_two_sum = jnp.sum(grad_ffn, axis=0, keepdims=True)
    grad_one = grad_hidden[...] + norm_back(grad_ffn, normal_two, inverse_two, gain_two)
    tokens_grad[...] = grad_one
    grad_attn = grad_one.astype(bf16)
    take_output(lambda part: dot_tn(spread_out[:, part], grad_attn))
    pause(0)
    wide[...] = dot_nt(grad_attn, output_weight[...])
    routes = columns[...].astype(jnp.int32)
    chosen = [routes[:, 2 * top + 3 + a : 2 * top + 4 + a] for a in range(top)]
    places = [value // 2 for value in chosen]
    odds = [value % 2 == 1 for value in chosen]
    gates = [columns[:, a : a + 1] for a in range(top)]
    pause(1)
    grad_gates, grad_heads = [], []
    for a in range(top):
        picked = pick_heads(wide, places[a], odds[a], head_size, positions)
        grad_gates.append(jnp.sum(picked * heads_out[a], axis=1, keepdims=True))
        grad_heads.append((gates[a] * picked).astype(bf16))
    inner = functools.reduce(lambda a, b: a + b, [g * d for g, d in zip(gates, grad_gates)])
    grad_logit = [g * (d - inner) for g, d in zip(gates, grad_gates)]
    head_lane = iota((rows, heads), 1)
    grad_hot = functools.reduce(
        lambda a, b: a + b,
        [jnp.where(head_lane == chosen[a], grad_logit[a], 0.0) for a in range(top)],
    )
    pause(2)
    grad_keys = [jnp.zeros((block_rows, head_size), f32) for _ in range(rows // block_rows)]
    grad_values = [jnp.zeros((block_rows, head_size), f32) for _ in range(rows // block_rows)]
    grad_query = [[] for _ in range(top)]
    for start in range(0, rows, block_rows):
        stop = start + block_rows
        part = slice(start, stop)
        queries = jnp.concatenate([query[a, part, :] for a in range(top)], axis=0)
        grads = jnp.concatenate([value[part] for value in grad_heads], axis=0)
        total = jnp.concatenate([columns[part, top + a : top + a + 1] for a in range(top)], axis=0)
        scores = dot_nt(queries, keys[0:stop, :])
        row_pos = iota((top * block_rows, block_rows), 0) % block_rows
        corner = jnp.where(
            iota((top * block_rows, block_rows), 1) <= row_pos, scores[:, start:], f32(-1e30)
        )
        if start:
            scores = jnp.concatenate([scores[:, :start], corner], axis=1)
        else:
            scores = corner
        prob = jnp.exp(scores - total)
        grad_prob = dot_nt(grads, values[0:stop, :])
        row_inner = jnp.sum(prob * grad_prob, axis=1, keepdims=True)
        grad_scores = (prob * (grad_prob - row_inner)).astype(bf16)
        grad_q = (dot_nn(grad_scores, keys[0:stop, :]) * head_size ** (-0.5)).astype(bf16)
        for a in range(top):
            grad_query[a].append(grad_q[a * block_rows : (a + 1) * block_rows].astype(f32))
        step_v = dot_tn(prob.astype(bf16), grads)
        step_k = dot_tn(grad_scores, queries)
        for index in range(stop // block_rows):
            piece = slice(index * block_rows, (index + 1) * block_rows)
            grad_values[index] = grad_values[index] + step_v[piece]
            grad_keys[index] = grad_keys[index] + step_k[piece]
        pause(3 + min(start // block_rows, 3))
    grad_query = [jnp.concatenate(value, axis=0) for value in grad_query]
    place_heads(narrow, grad_query, places, odds, head_size, positions)
    take_query(lambda part: dot_tn(attn_in[...], narrow[:, part]), pause)
    grad_k = jnp.concatenate(grad_keys, axis=0).astype(bf16)
    grad_v = jnp.concatenate(grad_values, axis=0).astype(bf16)
    hot_low = grad_hot.astype(bf16)
    grad_in = (
        dot_nt(narrow[...], query_weight[...])
        + dot_nn(grad_k, key_weight[...])
        + dot_nn(grad_v, value_weight[...])
        + dot_nn(hot_low, head_router[...])
    )
    pause(10)
    normal_one, inverse_one = norm_rows(tokens[...].astype(f32))
    take_small(
        [
            dot_tn(grad_k, attn_in[...]),
            dot_tn(grad_v, attn_in[...]),
            dot_tn(hot_low, attn_in[...]),
            router_two,
            jnp.sum(grad_in * normal_one, axis=0, keepdims=True),
            jnp.sum(grad_in, axis=0, keepdims=True),
            gain_two_sum,
            bias_two_sum,
            halt_sum[0:1, :],
        ]
    )
    tokens_grad[...] = (
        tokens_grad[...]
        + norm_back(grad_in, normal_one, inverse_one, gain_one)
        + (1.0 - columns[:, active_lane : active_lane + 1]) * state_cotan[...].astype(f32)
    )


def stack_small(pieces, room):
    count = sum(piece.shape[0] for piece in pieces)
    width = pieces[0].shape[1]
    return jnp.concatenate(pieces + [jnp.zeros((room - count, width), f32)], axis=0)


def attend_backward(block_rows, *refs):
    inputs, (tokens_grad, query_sum, output_sum, small_sum, wide, narrow) = refs[:22], refs[22:]

    def take_output(term):
        output_sum[...] = term(slice(None))

    def take_query(term, pause):
        query_sum[...] = term(slice(None))

    def take_small(pieces):
        small_sum[...] = stack_small(pieces, small_sum.shape[0])

    hooks = take_output, take_query, take_small, lambda point: None
    attention_back(block_rows, hooks, *inputs, tokens_grad, wide, narrow)


class SumOverAll:
    def __init__(self, number, place, send, recv, full, final, lands, lanes):
        self.number, self.place, self.send, self.recv = number, place, send, recv
        self.full, self.final, self.lands, self.lanes = full, final, lands, lanes
        self.copies = {}

    def part(self, ref, *lead):
        return ref.at[lead + (slice(None),) * (5 - len(lead)) + (self.lanes,)]

    def go(self, stage, source, target, device):
        self.copies[stage] = pltpu.make_async_remote_copy(
            src_ref=source, dst_ref=target, send_sem=self.send.at[self.number, stage],
            recv_sem=self.recv.at[self.number, stage], device_id=device, device_id_type=MESH,
        )
        self.copies[stage].start()

    def add(self, lead, landed):
        own = self.part(self.full, *lead)
        total = own[...].astype(f32)
        for value in landed:
            total = total + value[...].astype(f32)
        own[...] = total.astype(self.full.dtype)

    def step(self, stage):
        (c, x, z, y), (to_core, to_x, to_y, to_z) = self.place
        full, final = self.full, self.final
        land_core, land_x, land_z, land_y = self.lands
        if stage == 0:
            self.go(0, self.part(full, 1 - c), land_core, to_core)
        elif stage == 1:
            self.copies[0].wait_recv()
            self.add((c, 1 - x), [land_core.at[1 - x]])
            self.go(1, self.part(full, c, 1 - x), land_x, to_x)
            self.add((c, x), [land_core.at[x]])
        elif stage == 2:
            self.copies[1].wait_recv()
            for hop in (2, 1, 3):
                there = (z + hop) % 4
                self.add((c, x, there), [land_x.at[there]])
                self.go(1 + hop, self.part(full, c, x, there), land_z.at[hop - 1], to_z(hop))
            self.add((c, x, z), [land_x.at[z]])
        elif stage == 3:
            for hop in (1, 2, 3):
                self.copies[1 + hop].wait_recv()
            self.add((c, x, z, 1 - y), [land_z.at[hop, 1 - y] for hop in range(3)])
            self.go(5, self.part(full, c, x, z, 1 - y), land_y, to_y)
            self.add((c, x, z, y), [land_z.at[hop, y] for hop in range(3)])
        elif stage == 4:
            self.copies[5].wait_recv()
            total = self.part(full, c, x, z, y)[...].astype(f32) + land_y[...].astype(f32)
            own = self.part(final, c, x, z, y)
            own[...] = total.astype(final.dtype)
            self.go(6, own, own, to_y)
        elif stage == 5:
            self.copies[6].wait_recv()
            own = self.part(final, c, x, z)
            for hop in (2, 1, 3):
                self.go(6 + hop, own, own, to_z(hop))
        elif stage == 6:
            for hop in (1, 2, 3):
                self.copies[6 + hop].wait_recv()
            own = self.part(final, c, x)
            self.go(10, own, own, to_x)
        elif stage == 7:
            self.copies[10].wait_recv()
            own = self.part(final, c)
            self.go(11, own, own, to_core)
        elif stage == 8:
            self.copies[11].wait_recv()
            for copy in self.copies.values():
                copy.wait_send()


POINTS = (2.5, 3.5, 5.0, 6.0, 7.5, 9.5, 12.0, 13.0, 14.0, 15.0, 16.0, 17.5)
OUTPUT_POINT, QUERY_POINTS, SMALL_POINT = 0, (7, 8, 9), 11
DELAYS = {"core": 1.0, "x": 1.7, "z": 2.4, "y": 1.7}
RATES = {"core": 600.0, "x": 48.0, "z": 50.0, "y": 46.0}
WAYS = ("core", "x", "z", "y", "y", "z", "x", "core")


def plan_steps(piece_bytes, items, far_chunks, chunk_bytes):
    sizes = [piece_bytes * part for part in (1 / 2, 1 / 4, 1 / 4, 1 / 32, 1 / 32, 1 / 4, 1 / 4, 1 / 2)]
    free = dict.fromkeys(RATES, 0.0)
    ready, plan, done = [], [[] for _ in POINTS], 0

    def send(way, size, now):
        free[way] = max(free[way], now) + size / RATES[way] / 1000
        return free[way] + DELAYS[way]

    far_ready = [send("core", chunk_bytes, 0.5) for _ in range(far_chunks)]
    sent_far = 0

    def begin(item, now):
        ready.append((send("core", sizes[0], now), item, 1))

    now = 0.0
    for point, time in enumerate(POINTS):
        now = max(now, time)
        last = point == len(POINTS) - 1
        if point == OUTPUT_POINT:
            for item in range(3):
                begin(item, now)
        if point in QUERY_POINTS:
            begin(3 + QUERY_POINTS.index(point), now)
        if point == SMALL_POINT:
            begin(6, now)
        while True:
            ready.sort()
            if sent_far < far_chunks and far_ready[sent_far] <= now and free["y"] <= now + 6.0:
                plan[point].append((-1, sent_far))
                now += 0.2
                send("y", chunk_bytes, now)
                sent_far += 1
                continue
            if ready and (last or ready[0][0] <= now):
                if last and sent_far < far_chunks and max(free["y"] - 6.0, far_ready[sent_far]) < ready[0][0]:
                    now = max(now, free["y"] - 6.0, far_ready[sent_far])
                    continue
                time, item, stage = ready.pop(0)
                now = max(now, time) + (0.3 if stage == 1 else 0.15)
                plan[point].append((item, stage))
                if stage < 8:
                    ready.append((send(WAYS[stage], sizes[stage], now), item, stage + 1))
                continue
            if last and sent_far < far_chunks:
                now = max(now, free["y"] - 6.0, far_ready[sent_far])
                continue
            break
    return plan, now


def backward_and_sums(block_rows, *refs):
    inputs, terms = refs[:22], refs[22]
    tokens_grad, output_final, query_final, small_final, terms_final = refs[23:28]
    (wide, narrow, output_full, query_full, small_full, own_terms, near_terms, far_terms, output_core, output_x,
     output_z, output_y, query_core, query_x, query_z, query_y, small_core, small_x, small_z, small_y, send, recv,
     load_sem, term_send, term_recv, near_send, near_recv) = refs[28:]
    units, width = terms.shape[0], terms.shape[3]
    line, group = lax.axis_index("expert"), lax.axis_index("dp")
    z, x, y, c = line // 2, line % 2, group // 2, group % 2
    to_core, to_y = {"dp": y * 2 + 1 - c}, {"dp": (1 - y) * 2 + c}
    to_x = {"expert": z * 2 + 1 - x}

    def to_z(hop):
        return {"expert": (z + hop) % 4 * 2 + x}

    barrier = pltpu.get_barrier_semaphore()
    for device in (to_core, to_x, to_y, to_z(1), to_z(2), to_z(3)):
        pl.semaphore_signal(barrier, inc=1, device_id=device, device_id_type=MESH)
    far, near = (1 - y) * 2 + c, y * 2 + c
    loads = [
        [
            pltpu.make_async_copy(terms.at[u, quarter], own_terms.at[u, side], load_sem.at[u, side])
            for side, quarter in enumerate((far, near))
        ]
        for u in range(units)
    ]
    for side in range(2):
        for u in range(units):
            loads[u][side].start()
    pl.semaphore_wait(barrier, 6)

    split_rows = width // 2

    def term_copy(u, half, stage):
        rows = pl.ds(half * split_rows, split_rows)
        if stage == 0:
            source = terms.at[u, (1 - y) * 2 + 1 - c, rows]
            target, device = near_terms.at[u, 0, rows], to_core
        else:
            source, target, device = own_terms.at[u, 0, rows], far_terms.at[u, rows], to_y
        return pltpu.make_async_remote_copy(
            src_ref=source, dst_ref=target, send_sem=term_send.at[u, half, stage],
            recv_sem=term_recv.at[u, half, stage], device_id=device, device_id_type=MESH,
        )

    def near_copy(u):
        return pltpu.make_async_remote_copy(
            src_ref=terms.at[u, y * 2 + 1 - c], dst_ref=near_terms.at[u, 1], send_sem=near_send.at[u],
            recv_sem=near_recv.at[u], device_id=to_core, device_id_type=MESH,
        )

    for chunk in range(2 * units):
        term_copy(chunk // 2, chunk % 2, 0).start()

    def send_far(chunk):
        u, half = chunk // 2, chunk % 2
        if half == 0:
            loads[u][0].wait()
        term_copy(u, half, 0).wait_recv()
        rows = pl.ds(half * split_rows, split_rows)
        total = own_terms[u, 0, rows].astype(f32) + near_terms[u, 0, rows].astype(f32)
        own_terms[u, 0, rows] = total.astype(bf16)
        term_copy(u, half, 1).start()

    def finish_near(u):
        loads[u][1].wait()
        near_copy(u).wait_recv()
        for half in range(2):
            term_copy(u, half, 1).wait_recv()
        total = own_terms[u, 1].astype(f32) + near_terms[u, 1].astype(f32) + far_terms[u].astype(f32)
        terms_final[u] = total.astype(bf16)
        near_copy(u).wait_send()
        for half in range(2):
            term_copy(u, half, 0).wait_send()
            term_copy(u, half, 1).wait_send()

    place = (c, x, z, y), (to_core, to_x, to_y, to_z)
    third = query_full.shape[5] // 3
    whole = slice(None)
    items = [
        SumOverAll(
            part, place, send, recv, output_full.at[part], output_final.at[part],
            (output_core.at[part], output_x.at[part], output_z.at[part], output_y.at[part]), whole,
        )
        for part in range(3)
    ] + [
        SumOverAll(
            3 + q, place, send, recv, query_full, query_final,
            (query_core.at[q], query_x.at[q], query_z.at[q], query_y.at[q]), pl.ds(q * third, third),
        )
        for q in range(3)
    ]
    items.append(
        SumOverAll(6, place, send, recv, small_full, small_final, (small_core, small_x, small_z, small_y), whole)
    )
    block_bytes = math.prod(small_full.shape) * 4
    plan, _ = plan_steps(block_bytes, len(items), 2 * units, split_rows * width * 2)

    def take_output(term):
        size = math.prod(output_full.shape[1:-1])
        for part in range(3):
            value = term(slice(part * size, (part + 1) * size))
            output_full[part] = value.astype(bf16).reshape(output_full.shape[1:])
            items[part].step(0)

    def take_query(term, pause):
        for q in range(3):
            part = pl.ds(q * third, third)
            value = term(part).astype(bf16).reshape(query_full.shape[:5] + (third,))
            query_full[:, :, :, :, :, part] = value
            items[3 + q].step(0)
            pause(QUERY_POINTS[q])

    def take_small(pieces):
        rows = math.prod(small_full.shape[:-1])
        small_full[...] = stack_small(pieces, rows).reshape(small_full.shape)
        items[6].step(0)

    def pause(point):
        for item, stage in plan[point]:
            if item < 0:
                send_far(stage)
            else:
                items[item].step(stage)

    attention_back(block_rows, (take_output, take_query, take_small, pause), *inputs, tokens_grad, wide, narrow)
    for u in range(units):
        near_copy(u).start()
    pause(SMALL_POINT)
    for u in range(units):
        finish_near(u)


def expert_exchange(
    capacity, chunks, lane,
    ffn_in, slots, tokens, hidden_one, state_cotan, accum_cotan, columns, vectors, first_hbm, second_hbm,
    new_state, accum_part, lines_out, grad_hidden, grad_rows, grad_logits_t, halt_sum, terms,
    first, second, column, gathered, grads_in, cross, act, slope, produced, crossed, grad_out, grad_crossed,
    partial, landed, staged, keys, shares, share_out,
    weight_sem, key_send, key_recv, gather_send, gather_recv, cross_send, cross_recv, back_send, back_recv,
    reduce_send, reduce_recv, share_send, share_recv, stage_sem,
):
    rows, width = ffn_in.shape
    local, _, hidden_size = first.shape
    tile = width
    tiles = hidden_size // tile
    piece = rows // chunks
    me = lax.axis_index("expert")
    z, x = me // 2, me % 2
    other = 1 - x
    low = z < 2
    middle = (z == 1) | (z == 2)
    edge = jnp.logical_not(middle)

    def real(mirrored):
        return jnp.where(low, mirrored, 3 - mirrored)

    def along(depth):
        return {"expert": depth * 2 + x}

    across = {"expert": z * 2 + other}

    def order(j):
        return real(jnp.where(middle, jnp.where(j < 2, 1 - j, j), j))

    barrier = pltpu.get_barrier_semaphore()
    for step in range(1, 4):
        pl.semaphore_signal(barrier, inc=1, device_id=along((z + step) % 4), device_id_type=MESH)
    pl.semaphore_signal(barrier, inc=1, device_id=across, device_id_type=MESH)
    loads = [
        pltpu.make_async_copy(first_hbm, first, weight_sem.at[0]),
        pltpu.make_async_copy(second_hbm, second, weight_sem.at[1]),
    ]
    for load in loads:
        load.start()
    column[0, z] = ffn_in[...]
    keys[z] = slots[z]
    pl.semaphore_wait(barrier, 4)

    def key_copy(step):
        there = (z + step) % 4
        return pltpu.make_async_remote_copy(
            src_ref=slots.at[there], dst_ref=keys.at[z], send_sem=key_send.at[step], recv_sem=key_recv.at[z],
            device_id=along(there), device_id_type=MESH,
        )

    def key_arrival(shard):
        return pltpu.make_async_remote_copy(
            src_ref=slots.at[0], dst_ref=keys.at[shard], send_sem=key_send.at[0], recv_sem=key_recv.at[shard],
            device_id=across, device_id_type=MESH,
        )

    def gather_copy(phase, source, shard, depth, index):
        return pltpu.make_async_remote_copy(
            src_ref=source, dst_ref=column.at[phase, shard], send_sem=gather_send.at[phase, index],
            recv_sem=gather_recv.at[phase, shard], device_id=along(depth), device_id_type=MESH,
        )

    def send_own(phase, source):
        @pl.when(edge)
        def _():
            gather_copy(phase, source, z, real(1), 0).start()

        @pl.when(middle)
        def _():
            gather_copy(phase, source, z, real(0), 0).start()
            gather_copy(phase, source, z, real(2), 1).start()

    def forward(phase, mirrored, target, index):
        shard = real(mirrored)
        return gather_copy(phase, column.at[phase, shard], shard, real(target), index)

    def finish_gather(phase, source):
        gather_copy(phase, source, z, real(1), 0).wait_send()

        @pl.when(middle)
        def _():
            gather_copy(phase, source, z, real(2), 1).wait_send()
            forward(phase, 0, 2, 2).wait_send()
            forward(phase, 2, 0, 3).wait_send()
            forward(phase, 3, 0, 4).wait_send()

    def await_shard(phase, mirrored):
        shard = real(mirrored)
        if phase == 0:
            key_arrival(shard).wait_recv()
        gather_copy(phase, column.at[phase, shard], shard, z, 0).wait_recv()

    def await_shards(phase, j):
        @pl.when(edge & (j > 0))
        def _():
            await_shard(phase, j)

        @pl.when(middle & (j == 1))
        def _():
            await_shard(phase, 0)
            forward(phase, 0, 2, 2).start()
            await_shard(phase, 2)
            forward(phase, 2, 0, 3).start()

        @pl.when(middle & (j == 2))
        def _():
            await_shard(phase, 3)
            forward(phase, 3, 0, 4).start()

    def experts_of(shard):
        table = keys[shard]
        found = []
        for own in (True, False):
            for r in range(local):
                here, there = (r, local + r) if own else (local + r, r)
                line = jnp.where(x == 0, table[here : here + 1], table[there : there + 1])
                gate = jnp.where(x == 0, table[4 + here : 5 + here], table[4 + there : 5 + there])
                mask = iota((capacity, rows), 0).astype(f32) == line
                found.append((mask, jnp.sum(jnp.where(mask, gate, 0.0), axis=1, keepdims=True)))
        return found

    def hot_rows(found):
        return jnp.concatenate([jnp.where(mask, 1.0, 0.0).astype(bf16) for mask, _ in found], axis=0)

    def cross_copy(phase, shard, r):
        target = gathered if phase == 0 else grads_in
        return pltpu.make_async_remote_copy(
            src_ref=cross.at[shard, r], dst_ref=target.at[4 + shard, r], send_sem=cross_send.at[phase, shard, r],
            recv_sem=cross_recv.at[phase, shard, r], device_id=across, device_id_type=MESH,
        )

    def back_copy(phase, shard, r):
        source, target = (produced, crossed) if phase == 0 else (grad_out, grad_crossed)
        return pltpu.make_async_remote_copy(
            src_ref=source.at[4 + shard, r], dst_ref=target.at[shard, r], send_sem=back_send.at[phase, shard, r],
            recv_sem=back_recv.at[phase, shard, r], device_id=across, device_id_type=MESH,
        )

    def share_copy(shard):
        return pltpu.make_async_remote_copy(
            src_ref=share_out.at[shard], dst_ref=shares.at[z], send_sem=share_send.at[shard],
            recv_sem=share_recv.at[z], device_id=along(shard), device_id_type=MESH,
        )

    def dispatch(phase, shard):
        found = experts_of(shard)
        taken = dot_nn(hot_rows(found), column[phase, shard])
        lines = []
        for index, (mask, gate) in enumerate(found):
            part = taken[index * capacity : (index + 1) * capacity]
            if phase == 1:
                part = gate * part
            r = index % local
            if index < local:
                (gathered if phase == 0 else grads_in)[shard, r] = part.astype(bf16)
            else:
                cross[shard, r] = part.astype(bf16)
                cross_copy(phase, shard, r).start()
            if phase == 1:
                value = (produced if index < local else crossed)[shard, r].astype(f32)
                inner = jnp.sum(part * value, axis=1, keepdims=True)
                lines.append(jnp.sum(jnp.where(mask, inner, 0.0), axis=0, keepdims=True))
        if phase == 1:
            own, far = lines[:local], lines[local:]
            stack = [jnp.where(x == 0, a, b) for a, b in zip(own + far, far + own)]
            share_out[shard] = jnp.concatenate(stack + [jnp.zeros((4, rows), f32)], axis=0)

            @pl.when(shard == z)
            def _():
                shares[z] = share_out[z]

            @pl.when(shard != z)
            def _():
                share_copy(shard).start()

    def expert_forward(shard):
        def one(r, carry):
            cross_copy(0, shard, r).wait_recv()
            taken = jnp.concatenate([gathered[shard, r], gathered[4 + shard, r]], axis=0)
            total = jnp.zeros((2 * capacity, width), f32)
            for n in range(tiles):
                part = slice(n * tile, (n + 1) * tile)
                pre = dot_nn(taken, first[r, :, part])
                cumulative = 0.5 * (1.0 + lax.erf(pre * (1.0 / math.sqrt(2.0))))
                density = jnp.exp(-0.5 * pre * pre) * (1.0 / math.sqrt(2.0 * math.pi))
                inner = (pre * cumulative).astype(bf16)
                steep = (cumulative + pre * density).astype(bf16)
                act[shard, r, :, part] = inner[:capacity]
                act[4 + shard, r, :, part] = inner[capacity:]
                slope[shard, r, :, part] = steep[:capacity]
                slope[4 + shard, r, :, part] = steep[capacity:]
                total = total + dot_nn(inner, second[r, part, :])
            produced[shard, r] = total[:capacity].astype(bf16)
            produced[4 + shard, r] = total[capacity:].astype(bf16)
            back_copy(0, shard, r).start()
            return carry

        lax.fori_loop(0, local, one, 0)

    def expert_backward(shard):
        def one(r, carry):
            cross_copy(1, shard, r).wait_recv()
            taken = jnp.concatenate([grads_in[shard, r], grads_in[4 + shard, r]], axis=0)
            total = jnp.zeros((2 * capacity, width), f32)
            for n in range(tiles):
                part = slice(n * tile, (n + 1) * tile)
                grad = dot_nt(taken, second[r, part, :])
                steep = jnp.concatenate([slope[shard, r, :, part], slope[4 + shard, r, :, part]], axis=0)
                grad_pre = (grad * steep.astype(f32)).astype(bf16)
                slope[shard, r, :, part] = grad_pre[:capacity]
                slope[4 + shard, r, :, part] = grad_pre[capacity:]
                total = total + dot_nt(grad_pre, first[r, :, part])
            grad_out[shard, r] = total[:capacity].astype(bf16)
            grad_out[4 + shard, r] = total[capacity:].astype(bf16)
            back_copy(1, shard, r).start()
            return carry

        lax.fori_loop(0, local, one, 0)

    def reduce_copy(phase, shard, index, chunk, depth):
        part = pl.ds(pl.multiple_of(chunk * piece, piece), piece)
        return pltpu.make_async_remote_copy(
            src_ref=partial.at[shard, part], dst_ref=landed.at[phase, index, part],
            send_sem=reduce_send.at[phase, index, chunk], recv_sem=reduce_recv.at[phase, index, chunk],
            device_id=along(depth), device_id_type=MESH,
        )

    def combine(phase, j):
        shard = order(j)
        for r in range(local):
            back_copy(phase, shard, r).wait_recv()
        found = experts_of(shard)
        if phase == 0:
            pieces = [
                gate * (produced if index < local else crossed)[shard, index % local].astype(f32)
                for index, (_, gate) in enumerate(found)
            ]
            pieces = [value.astype(bf16) for value in pieces]
        else:
            pieces = [
                (grad_out if index < local else grad_crossed)[shard, index % local]
                for index in range(2 * local)
            ]
        partial[shard] = dot_tn(hot_rows(found), jnp.concatenate(pieces, axis=0)).astype(bf16)

        @pl.when(edge & (j > 0))
        def _():
            for chunk in range(chunks):
                reduce_copy(phase, shard, j - 1, chunk, real(1)).start()

    def pass_on(phase, chunk, source, mirrored, index, depth):
        shard = real(mirrored)
        reduce_copy(phase, shard, source, chunk, z).wait_recv()
        part = pl.ds(pl.multiple_of(chunk * piece, piece), piece)
        partial[shard, part] = (
            partial[shard, part].astype(f32) + landed[phase, source, part].astype(f32)
        ).astype(bf16)
        reduce_copy(phase, shard, index, chunk, depth).start()

    def reduce_rows(phase, filler):
        def step(i, carry):
            @pl.when(middle & (i < chunks))
            def _():
                pass_on(phase, i, 1, 2, 3, real(2))

            @pl.when(middle & (i >= chunks))
            def _():
                pass_on(phase, i - chunks, 2, 3, 4, real(2))
                pass_on(phase, i - chunks, 4, 0, 0, real(0))

            filler(i)
            return carry

        lax.fori_loop(0, 2 * chunks, step, 0)

    def reduced(phase):
        for chunk in range(chunks):
            reduce_copy(phase, z, 0, chunk, z).wait_recv()
        total = partial[z].astype(f32) + landed[phase, 0].astype(f32)

        @pl.when(middle)
        def _():
            for chunk in range(chunks):
                reduce_copy(phase, z, 3, chunk, z).wait_recv()

        return total + jnp.where(middle, landed[phase, 3].astype(f32), 0.0)

    def finish_reduce(phase):
        @pl.when(edge)
        def _():
            for index in range(3):
                for chunk in range(chunks):
                    reduce_copy(phase, real(index + 1), index, chunk, real(1)).wait_send()

        @pl.when(middle)
        def _():
            for chunk in range(chunks):
                reduce_copy(phase, real(2), 3, chunk, real(2)).wait_send()
                reduce_copy(phase, real(3), 4, chunk, real(2)).wait_send()
                reduce_copy(phase, real(0), 0, chunk, real(0)).wait_send()

    def finish_cross(phase):
        for shard in range(4):
            for r in range(local):
                cross_copy(phase, shard, r).wait_send()
                back_copy(phase, shard, r).wait_send()

    def run(phase, experts):
        def step(j, carry):
            @pl.when(j >= 2)
            def _():
                combine(phase, j - 2)

            @pl.when((j >= 1) & (j <= 4))
            def _():
                experts(order(j - 1))

            @pl.when(j <= 3)
            def _():
                await_shards(phase, j)
                dispatch(phase, order(j))

            return carry

        lax.fori_loop(0, 6, step, 0)

    for step in range(1, 4):
        key_copy(step).start()
    send_own(0, ffn_in)
    for load in loads:
        load.wait()
    run(0, expert_forward)
    reduce_rows(0, lambda i: None)
    hidden = hidden_one[...] + reduced(0)
    remain, active, remain_cotan = [columns[:, lane + index : lane + index + 1] for index in range(3)]
    halt_vector = vectors[4:5, :]
    halt_prob = jax.nn.sigmoid(jnp.sum(hidden * halt_vector, axis=1, keepdims=True))
    halt_share = active * remain * halt_prob
    grad_accum = accum_cotan[...].astype(f32)
    grad_share = jnp.sum(grad_accum * hidden, axis=1, keepdims=True)
    grad_logit = active * remain * (grad_share - remain_cotan) * halt_prob * (1.0 - halt_prob)
    grad_here = active * state_cotan[...].astype(f32) + halt_share * grad_accum + grad_logit * halt_vector
    grad_hidden[...] = grad_here
    column[1, z] = grad_here.astype(bf16)
    send_own(1, column.at[1, z])
    new_state[...] = jnp.where(active > 0.5, hidden, tokens[...].astype(f32)).astype(bf16)
    accum_part[...] = halt_share * hidden
    pair = lanes_of(
        [
            remain * (1.0 - active * halt_prob),
            active * halt_prob * grad_share + (1.0 - active * halt_prob) * remain_cotan,
        ]
    )
    lines_out[...] = pair.T[:8]
    halt_sum[...] = jnp.concatenate(
        [jnp.sum(grad_logit * hidden, axis=0, keepdims=True), jnp.zeros((7, width), f32)], axis=0
    )
    for step in range(1, 4):
        key_copy(step).wait_send()
    finish_gather(0, ffn_in)
    finish_cross(0)
    finish_reduce(0)
    run(1, expert_backward)

    def stage(unit, n, slot):
        return pltpu.make_async_copy(staged.at[slot], terms.at[unit, n], stage_sem.at[slot])

    def weight_terms(i):
        r, n = i // tiles, i % tiles
        part = pl.ds(pl.multiple_of(n * tile, tile), tile)
        total = local * 4 * capacity

        @pl.when(i > 0)
        def _():
            stage(0, 0, 0).wait()
            stage(0, 0, 1).wait()

        left = gathered[:, r].reshape(total, width)
        right = slope[:, r, :, part].reshape(total, tile)
        staged[0] = dot_tn(left, right).astype(bf16)
        stage(r, n, 0).start()
        left = act[:, r, :, part].reshape(total, tile)
        right = grads_in[:, r].reshape(total, width)
        staged[1] = dot_tn(left, right).astype(bf16)
        stage(local + r, n, 1).start()

    reduce_rows(1, weight_terms)
    stage(0, 0, 0).wait()
    stage(0, 0, 1).wait()
    for step in range(1, 4):
        shard = (z + step) % 4
        pltpu.make_async_remote_copy(
            src_ref=share_out.at[0], dst_ref=shares.at[shard], send_sem=share_send.at[0],
            recv_sem=share_recv.at[shard], device_id=across, device_id_type=MESH,
        ).wait_recv()
        share_copy(shard).wait_send()
    share = jnp.concatenate([shares[s, 0:4] for s in range(4)], axis=0)
    gate = jnp.concatenate([slots[s, 4:8] for s in range(4)], axis=0)
    grad_logits_t[...] = share - gate * jnp.sum(share, axis=0, keepdims=True)
    grad_rows[...] = reduced(1)
    finish_gather(1, column.at[1, z])
    finish_cross(1)
    finish_reduce(1)


def slot_targets(routes, experts, room_rows):
    flattened = routes.reshape(-1)
    hot_rows = (flattened[:, None] == jnp.arange(experts, dtype=jnp.int32)[None, :]).astype(jnp.int32)
    before = jnp.cumsum(hot_rows, axis=0) - hot_rows
    return flattened * room_rows + jnp.sum(hot_rows * before, axis=1)


def experts_by_all_to_all(
    capacity, tokens, remain, halting, expert_routes, halt_weight, expert_router, expert_in, expert_out,
    state_cotan, accum_cotan, remain_cotan, hidden_one, ffn_in,
):
    rows, width = tokens.shape
    experts = expert_router.shape[1]
    top = expert_routes.shape[1]
    highest = lax.Precision.HIGHEST
    inputs = tokens.astype(f32)
    active = halting.astype(f32)
    expert_logits = jnp.dot(ffn_in, expert_router, preferred_element_type=f32)
    expert_gate = jax.nn.softmax(jnp.take_along_axis(expert_logits, expert_routes, axis=1), axis=1)
    targets = slot_targets(expert_routes, experts, capacity)

    def spread(values):
        placed = jnp.zeros((experts * capacity, width), bf16).at[targets].set(values)
        return lax.all_to_all(
            placed.reshape(experts, capacity, width), "expert", split_axis=0, concat_axis=1, tiled=True
        )

    def collect(values):
        back = lax.all_to_all(values, "expert", split_axis=1, concat_axis=0, tiled=True)
        back = back.reshape(experts * capacity, width)
        return back[targets].astype(f32).reshape(rows, top, width)

    arrived = spread(jnp.repeat(ffn_in, top, axis=0))
    pre_act = jnp.einsum("erd,edf->erf", arrived, expert_in, preferred_element_type=f32)
    inner_act = jax.nn.gelu(pre_act, approximate=False).astype(bf16)
    produced = jnp.einsum("erf,efd->erd", inner_act, expert_out, preferred_element_type=f32).astype(bf16)
    picked = collect(produced)
    hidden = hidden_one + jnp.sum(expert_gate[:, :, None] * picked, axis=1)
    halt_vector = halt_weight.astype(f32)
    halt_prob = jax.nn.sigmoid(jnp.dot(hidden, halt_vector, precision=highest))
    halt_share = active * remain * halt_prob
    new_state = jnp.where(active[:, None] > 0.5, hidden, inputs).astype(bf16)
    accum_part = halt_share[:, None] * hidden
    remain_left = remain * (1.0 - active * halt_prob)
    grad_accum = accum_cotan.astype(f32)
    grad_share = jnp.sum(grad_accum * hidden, axis=1)
    grad_logit = active * remain * (grad_share - remain_cotan) * halt_prob * (1.0 - halt_prob)
    remain_grad = active * halt_prob * grad_share + (1.0 - active * halt_prob) * remain_cotan
    grad_hidden = (
        active[:, None] * state_cotan.astype(f32)
        + halt_share[:, None] * grad_accum
        + grad_logit[:, None] * halt_vector[None, :]
    )
    halt_sum = jnp.dot(grad_logit, hidden, precision=highest)
    grad_gate = jnp.sum(grad_hidden[:, None, :] * picked, axis=2)
    grad_chosen = expert_gate * (grad_gate - jnp.sum(expert_gate * grad_gate, axis=1, keepdims=True))
    expert_hot = (expert_routes[:, :, None] == jnp.arange(experts, dtype=jnp.int32)[None, None, :]).astype(f32)
    grad_logits = jnp.einsum("tk,tke->te", grad_chosen, expert_hot, precision=highest)
    grad_prod = (expert_gate[:, :, None] * grad_hidden[:, None, :]).astype(bf16)
    grad_arrived = spread(grad_prod.reshape(rows * top, width))
    grad_inner = jnp.einsum("erd,efd->erf", grad_arrived, expert_out, preferred_element_type=f32)
    cumulative = 0.5 * (1.0 + lax.erf(pre_act * (1.0 / math.sqrt(2.0))))
    density = jnp.exp(-0.5 * pre_act * pre_act) * (1.0 / math.sqrt(2.0 * math.pi))
    grad_pre = (grad_inner * (cumulative + pre_act * density)).astype(bf16)
    grad_rows = jnp.einsum("erf,edf->erd", grad_pre, expert_in, preferred_element_type=f32).astype(bf16)
    in_terms = jnp.einsum("erd,erf->edf", arrived, grad_pre, preferred_element_type=f32)
    out_terms = jnp.einsum("erf,erd->efd", inner_act, grad_arrived, preferred_element_type=f32)
    return (
        new_state, accum_part, jnp.stack([remain_left, remain_grad]), grad_hidden,
        jnp.sum(collect(grad_rows), axis=1),
        grad_logits.T, jnp.broadcast_to(halt_sum, (8, width)), (in_terms.astype(bf16), out_terms.astype(bf16)),
    )


def vmem(count):
    return [pl.BlockSpec(memory_space=pltpu.VMEM)] * count


def hbm(count):
    return [pl.BlockSpec(memory_space=pl.ANY)] * count


def experts_on_lines(
    capacity, chunks, lane, tokens, columns, vectors, expert_in, expert_out, state_cotan, accum_cotan, hidden_one, ffn_in,
    slots,
):
    rows, width = tokens.shape
    local, _, hidden_size = expert_in.shape
    shape, buffer, flags = jax.ShapeDtypeStruct, pltpu.VMEM, pltpu.SemaphoreType.DMA
    results = pl.pallas_call(
        functools.partial(expert_exchange, capacity, chunks, lane),
        out_shape=[
            shape((rows, width), bf16),
            shape((rows, width), f32),
            shape((8, rows), f32),
            shape((rows, width), f32),
            shape((rows, width), f32),
            shape((8 * local, rows), f32),
            shape((8, width), f32),
            shape((2 * local, hidden_size // width, width, width), bf16),
        ],
        in_specs=vmem(8) + hbm(2),
        out_specs=vmem(7) + hbm(1),
        scratch_shapes=[
            buffer((local, width, hidden_size), bf16),
            buffer((local, hidden_size, width), bf16),
            buffer((2, 4, rows, width), bf16),
            buffer((8, local, capacity, width), bf16),
            buffer((8, local, capacity, width), bf16),
            buffer((4, local, capacity, width), bf16),
            buffer((8, local, capacity, hidden_size), bf16),
            buffer((8, local, capacity, hidden_size), bf16),
            buffer((8, local, capacity, width), bf16),
            buffer((4, local, capacity, width), bf16),
            buffer((8, local, capacity, width), bf16),
            buffer((4, local, capacity, width), bf16),
            buffer((4, rows, width), bf16),
            buffer((2, 5, rows, width), bf16),
            buffer((2, width, width), bf16),
            buffer((4, 8, rows), f32),
            buffer((4, 8, rows), f32),
            buffer((4, 8, rows), f32),
            flags((2,)),
            flags((4,)),
            flags((4,)),
            flags((2, 5)),
            flags((2, 4)),
            flags((2, 4, local)),
            flags((2, 4, local)),
            flags((2, 4, local)),
            flags((2, 4, local)),
            flags((2, 5, chunks)),
            flags((2, 5, chunks)),
            flags((4,)),
            flags((4,)),
            flags((2,)),
        ],
        compiler_params=pltpu.CompilerParams(
            vmem_limit_bytes=VMEM_LIMIT, collective_id=1, has_side_effects=True
        ),
        name="expert_exchange",
    )(ffn_in, slots, tokens, hidden_one, state_cotan, accum_cotan, columns, vectors, expert_in, expert_out)
    new_state, accum_part, pair, grad_hidden, grad_rows, grad_logits_t, halt_sum, terms = results
    return new_state, accum_part, pair, grad_hidden, grad_rows, grad_logits_t, halt_sum, terms


def sums_on_links(operands, terms, small_rows, wides):
    rows, width = operands[0].shape
    wide_size = wides[0].shape[1]
    units = terms.shape[0]
    shape, buffer, flags = jax.ShapeDtypeStruct, pltpu.VMEM, pltpu.SemaphoreType.DMA
    split = (2, 2, 4, 2)
    block, thin, small = wide_size // 96, width // 32, small_rows // 32
    third = wide_size // 3

    def landing(size, lanes, kind, lead=()):
        return [
            buffer(lead + dims + (size, lanes), kind) for dims in ((2, 4, 2), (4, 2), (3, 2), ())
        ]

    return pl.pallas_call(
        functools.partial(backward_and_sums, 128),
        out_shape=[
            shape((rows, width), f32),
            shape((3,) + split + (block, width), bf16),
            shape(split + (thin, wide_size), bf16),
            shape(split + (small, width), f32),
            shape((units, width, width), bf16),
        ],
        in_specs=vmem(22) + hbm(1),
        out_specs=vmem(5),
        scratch_shapes=[
            *wides,
            buffer((3,) + split + (block, width), bf16),
            buffer(split + (thin, wide_size), bf16),
            buffer(split + (small, width), f32),
            buffer((units, 2, width, width), bf16),
            buffer((units, 2, width, width), bf16),
            buffer((units, width, width), bf16),
            *landing(block, width, bf16, (3,)),
            *landing(thin, third, bf16, (3,)),
            *landing(small, width, f32),
            flags((7, 12)),
            flags((7, 12)),
            flags((units, 2)),
            flags((units, 2, 2)),
            flags((units, 2, 2)),
            flags((units,)),
            flags((units,)),
        ],
        compiler_params=pltpu.CompilerParams(
            vmem_limit_bytes=VMEM_LIMIT, collective_id=2, has_side_effects=True
        ),
        name="backward_and_sums",
    )(*operands, terms)


def write_results(
    edges, output_low, query_low, terms_low, small, lines, new_state_in, accum_in, tokens_in,
    output_grad, query_grad, in_grad, out_grad, new_state, accum_part, tokens_grad, *rest,
):
    local = in_grad.shape[0]
    output_grad[...] = output_low[...].astype(f32)
    query_grad[...] = query_low[...].astype(f32)
    in_grad[...] = terms_low[0:local].astype(f32)
    out_grad[...] = terms_low[local:].astype(f32)
    new_state[...] = new_state_in[...]
    accum_part[...] = accum_in[...]
    tokens_grad[...] = tokens_in[...]
    for ref, start, stop in zip(rest, edges[:-1], edges[1:]):
        ref[...] = small[start:stop, :]
    rest[-2][...] = lines[0:1, :]
    rest[-1][...] = lines[1:2, :]


def results(edges, output_low, query_low, terms_low, small, lines, new_state, accum_part, tokens_grad):
    shape, steps = jax.ShapeDtypeStruct, 4
    wide_size, width = output_low.shape
    rows = new_state.shape[0]
    units = terms_low.shape[0]

    def by_rows(count, lanes):
        return pl.BlockSpec((count // steps, lanes), lambda i: (i, 0))

    def by_units(count):
        return pl.BlockSpec((count, width // steps, width), lambda i: (0, i, 0))

    def whole(count):
        return pl.BlockSpec((count, width), lambda i: (0, 0))

    parts = [stop - start for start, stop in zip(edges[:-1], edges[1:])] + [1, 1]
    return pl.pallas_call(
        functools.partial(write_results, edges),
        grid=(steps,),
        out_shape=[
            shape((wide_size, width), f32),
            shape((width, wide_size), f32),
            shape((units // 2, width, width), f32),
            shape((units // 2, width, width), f32),
            shape((rows, width), bf16),
            shape((rows, width), f32),
            shape((rows, width), f32),
            *[shape((count, width), f32) for count in parts],
        ],
        in_specs=[
            by_rows(wide_size, width), by_rows(width, wide_size), by_units(units), whole(small.shape[0]),
            whole(lines.shape[0]), by_rows(rows, width), by_rows(rows, width), by_rows(rows, width),
        ],
        out_specs=[
            by_rows(wide_size, width), by_rows(width, wide_size), by_units(units // 2), by_units(units // 2),
            by_rows(rows, width), by_rows(rows, width), by_rows(rows, width), *[whole(count) for count in parts],
        ],
        compiler_params=pltpu.CompilerParams(vmem_limit_bytes=VMEM_LIMIT),
        name="results",
    )(output_low, query_low, terms_low, small, lines, new_state, accum_part, tokens_grad)


def body(
    mesh_sizes, tokens, remain, halting, head_routes, expert_routes, first_gain, first_bias, query_weight,
    key_weight, value_weight, output_weight, head_router, second_gain, second_bias, expert_router, expert_in,
    expert_out, halt_weight, state_cotan, accum_cotan, remain_cotan,
):
    rows, width = tokens.shape
    head_size = key_weight.shape[1]
    top = head_routes.shape[1]
    wide_size = query_weight.shape[1]
    experts = expert_router.shape[1]
    heads = head_router.shape[1]
    capacity = 4 * rows // experts
    shape = jax.ShapeDtypeStruct
    attn_in, query, keys, values, heads_out, spread_out, hidden_one, ffn_in, columns, slots, vectors = pl.pallas_call(
        functools.partial(attend_forward, 128),
        out_shape=[
            shape((rows, width), bf16),
            shape((top, rows, head_size), bf16),
            shape((rows, head_size), bf16),
            shape((rows, head_size), bf16),
            shape((top, rows, head_size), f32),
            shape((rows, wide_size), bf16),
            shape((rows, width), f32),
            shape((rows, width), bf16),
            shape((rows, 128), f32),
            shape((experts // 4, 8, rows), f32),
            shape((8, width), f32),
        ],
        in_specs=vmem(17),
        out_specs=vmem(11),
        scratch_shapes=[pltpu.VMEM((rows, wide_size), f32)],
        compiler_params=pltpu.CompilerParams(vmem_limit_bytes=VMEM_LIMIT),
        name="attend_forward",
    )(
        tokens, head_routes.T, expert_routes.T, remain[None], halting[None], remain_cotan[None], first_gain[None],
        first_bias[None], second_gain[None], second_bias[None], halt_weight[None], query_weight, key_weight.T,
        value_weight.T, output_weight, head_router.T, expert_router.T,
    )
    if mesh_sizes == (4, 8):
        stage = experts_on_lines(
            capacity, 4, 2 * top, tokens, columns, vectors, expert_in, expert_out, state_cotan, accum_cotan, hidden_one,
            ffn_in, slots,
        )
    else:
        stage = experts_by_all_to_all(
            capacity, tokens, remain, halting, expert_routes, halt_weight, expert_router, expert_in, expert_out,
            state_cotan, accum_cotan, remain_cotan, hidden_one, ffn_in,
        )
    new_state, accum_part, lines, grad_hidden, grad_rows, grad_logits_t, halt_sum, terms = stage
    operands = (
        tokens, vectors, query_weight, key_weight.T, value_weight.T, output_weight,
        head_router.T, expert_router.T, attn_in, query, keys, values, heads_out, spread_out, hidden_one, ffn_in,
        columns, grad_rows, grad_logits_t, grad_hidden, state_cotan, halt_sum,
    )
    edges = [0, head_size, 2 * head_size, 2 * head_size + heads, 2 * head_size + heads + experts]
    small_rows = 256
    wides = [pltpu.VMEM((rows, wide_size), f32), pltpu.VMEM((rows, wide_size), bf16)]
    if mesh_sizes == (4, 8):
        tokens_grad, output_grad, query_grad, small, expert_grads = sums_on_links(
            operands, terms, small_rows, wides
        )
        (output_grad, query_grad, expert_in_grad, expert_out_grad, new_state, accum_part, tokens_grad, *rest) = results(
            [*edges, *range(edges[-1] + 1, edges[-1] + 6)], output_grad.reshape(wide_size, width),
            query_grad.reshape(width, wide_size), expert_grads, small.reshape(small_rows, width), lines,
            new_state, accum_part, tokens_grad,
        )
        key_grad, value_grad, head_router_grad, expert_router_grad = [value.T for value in rest[:4]]
        first_gain_grad, first_bias_grad, second_gain_grad, second_bias_grad, halt_grad, remain_left, remain_grad = [
            value.reshape(width) for value in rest[4:]
        ]
    else:
        in_terms, out_terms = terms
        expert_in_grad = lax.psum_scatter(in_terms, "dp", scatter_dimension=2, tiled=True).astype(f32)
        expert_out_grad = lax.psum_scatter(out_terms, "dp", scatter_dimension=1, tiled=True).astype(f32)
        small_rows = -(-(2 * head_size + heads + experts + 5) // 8) * 8
        tokens_grad, query_sum, output_sum, small_sum = pl.pallas_call(
            functools.partial(attend_backward, 128),
            out_shape=[
                shape((rows, width), f32),
                shape((width, wide_size), f32),
                shape((wide_size, width), f32),
                shape((small_rows, width), f32),
            ],
            in_specs=vmem(22),
            out_specs=vmem(4),
            scratch_shapes=wides,
            compiler_params=pltpu.CompilerParams(vmem_limit_bytes=VMEM_LIMIT),
            name="attend_backward",
        )(*operands)
        query_grad, output_grad, small = lax.psum((query_sum, output_sum, small_sum), ("dp", "expert"))
        key_grad, value_grad, head_router_grad, expert_router_grad = [
            small[start:stop].T for start, stop in zip(edges[:-1], edges[1:])
        ]
        first_gain_grad, first_bias_grad, second_gain_grad, second_bias_grad, halt_grad = [
            small[edges[-1] + index] for index in range(5)
        ]
        remain_left, remain_grad = lines[0], lines[1]
    return (
        new_state, accum_part, remain_left, tokens_grad, remain_grad, first_gain_grad, first_bias_grad, query_grad,
        key_grad, value_grad, output_grad, head_router_grad, second_gain_grad, second_bias_grad,
        expert_router_grad, expert_in_grad, expert_out_grad, halt_grad,
    )


def solution(mesh):
    in_specs = (
        P(("dp", "expert"), None),
        P(("dp", "expert")),
        P(("dp", "expert")),
        P(("dp", "expert"), None),
        P(("dp", "expert"), None),
        P(),
        P(),
        P(),
        P(),
        P(),
        P(),
        P(),
        P(),
        P(),
        P(),
        P("expert", None, None),
        P("expert", None, None),
        P(),
        P(("dp", "expert"), None),
        P(("dp", "expert"), None),
        P(("dp", "expert")),
    )
    out_specs = (
        P(("dp", "expert"), None),
        P(("dp", "expert"), None),
        P(("dp", "expert")),
        P(("dp", "expert"), None),
        P(("dp", "expert")),
        P(),
        P(),
        P(),
        P(),
        P(),
        P(),
        P(),
        P(),
        P(),
        P(),
        P("expert", None, "dp"),
        P("expert", "dp", None),
        P(),
    )
    sizes = (mesh.shape["dp"], mesh.shape["expert"])
    run = functools.partial(body, sizes)
    return jax.shard_map(run, mesh=mesh, in_specs=in_specs, out_specs=out_specs, check_vma=False)
```

```python
import functools
import math

import jax
import jax.numpy as jnp
from jax import lax
from jax.experimental import pallas as pl
from jax.experimental.pallas import tpu as pltpu
from jax.sharding import PartitionSpec as P

epsilon = 1e-05
f32 = jnp.float32
bf16 = jnp.bfloat16
MESH = pl.DeviceIdType.MESH
VMEM_LIMIT = 67043328


def dot_nn(left, right):
    return jnp.dot(left, right, preferred_element_type=f32)


def dot_nt(left, right):
    return lax.dot_general(left, right, (((1,), (1,)), ((), ())), preferred_element_type=f32)


def dot_tn(left, right):
    return lax.dot_general(left, right, (((0,), (0,)), ((), ())), preferred_element_type=f32)


def iota(shape, axis):
    return lax.broadcasted_iota(jnp.int32, shape, axis)


def norm_rows(values):
    centre = jnp.mean(values, axis=-1, keepdims=True)
    shifted = values - centre
    spread = jnp.mean(shifted * shifted, axis=-1, keepdims=True)
    inverse = lax.rsqrt(spread + epsilon)
    return shifted * inverse, inverse


def norm_back(upstream, normal, inverse, scales):
    scaled = upstream * scales
    inner = (
        scaled
        - jnp.mean(scaled, axis=-1, keepdims=True)
        - normal * jnp.mean(scaled * normal, axis=-1, keepdims=True)
    )
    return inner * inverse


def pick_heads(wide, place, odd, head_size, positions):
    pair = 2 * head_size
    kept = wide[:, :pair]
    for index in range(1, positions):
        kept = jnp.where(place == index, wide[:, index * pair : (index + 1) * pair], kept)
    return jnp.where(odd, kept[:, head_size:], kept[:, :head_size])


def place_heads(out_ref, columns, places, odds, head_size, positions):
    pair = 2 * head_size
    rows = columns[0].shape[0]
    upper = iota((rows, pair), 1) >= head_size
    doubled = [
        jnp.where(upper == odd, jnp.concatenate([column, column], axis=1), 0.0)
        for column, odd in zip(columns, odds)
    ]
    for index in range(positions):
        total = jnp.zeros((rows, pair), f32)
        for value, place in zip(doubled, places):
            total = total + jnp.where(place == index, value, 0.0)
        out_ref[:, index * pair : (index + 1) * pair] = total.astype(bf16)


def lanes_of(columns, width=128):
    rows = columns[0].shape[0]
    lane = iota((rows, width), 1)
    total = jnp.zeros((rows, width), f32)
    for index, column in enumerate(columns):
        total = jnp.where(lane == index, column, total)
    return total


def soft_columns(logits):
    peak = functools.reduce(jnp.maximum, logits)
    raised = [jnp.exp(value - peak) for value in logits]
    whole = functools.reduce(lambda a, b: a + b, raised)
    return [value / whole for value in raised]


def attend_forward(
    block_rows, tokens, head_routes, expert_routes, remain, halting, remain_cotan, first_gain, first_bias,
    second_gain, second_bias, halt_weight, query_weight, key_weight, value_weight, output_weight, head_router,
    expert_router,
    attn_in_out, query_out, key_out, value_out, heads_out, spread_out, hidden_out, ffn_out, columns_out,
    slots_out, vectors, wide,
):
    rows, width = tokens.shape
    head_size = key_weight.shape[0]
    positions = query_weight.shape[1] // (2 * head_size)
    top = head_routes.shape[0]
    experts = expert_router.shape[0]
    for index, vector in enumerate((first_gain, first_bias, second_gain, second_bias, halt_weight)):
        vectors[index : index + 1, :] = vector[...].astype(f32).reshape(1, width)
    vectors[5:8, :] = jnp.zeros((3, width), f32)
    lines = [head_routes[...], expert_routes[...], halting[...]]
    lines = [value.astype(f32) for value in lines] + [remain[...], remain_cotan[...]]
    filled = sum(value.shape[0] for value in lines)
    table = jnp.concatenate(lines + [jnp.zeros((128 - filled, rows), f32)], axis=0).T
    inputs = tokens[...].astype(f32)
    normal, _ = norm_rows(inputs)
    attn_in = (normal * vectors[0:1, :] + vectors[1:2, :]).astype(bf16)
    attn_in_out[...] = attn_in
    wide[...] = dot_nn(attn_in, query_weight[...])
    keys = dot_nt(attn_in, key_weight[...]).astype(bf16)
    key_out[...] = keys
    values = dot_nt(attn_in, value_weight[...]).astype(bf16)
    value_out[...] = values
    head_logits = dot_nt(attn_in, head_router[...])
    routes = table.astype(jnp.int32)
    chosen = [routes[:, a : a + 1] for a in range(top)]
    places = [value // 2 for value in chosen]
    odds = [value % 2 == 1 for value in chosen]
    head_lane = iota(head_logits.shape, 1)
    gates = soft_columns(
        [
            jnp.sum(jnp.where(head_lane == value, head_logits, 0.0), axis=1, keepdims=True)
            for value in chosen
        ]
    )
    for a in range(top):
        picked = pick_heads(wide, places[a], odds[a], head_size, positions)
        query_out[a] = (picked.astype(bf16).astype(f32) * head_size ** (-0.5)).astype(bf16)
    totals = [[] for _ in range(top)]
    for start in range(0, rows, block_rows):
        stop = start + block_rows
        query = jnp.concatenate([query_out[a, start:stop, :] for a in range(top)], axis=0)
        scores = dot_nt(query, key_out[0:stop, :])
        row_pos = iota((top * block_rows, block_rows), 0) % block_rows
        corner = jnp.where(
            iota((top * block_rows, block_rows), 1) <= row_pos, scores[:, start:], f32(-1e30)
        )
        if start:
            scores = jnp.concatenate([scores[:, :start], corner], axis=1)
        else:
            scores = corner
        peak = jnp.max(scores, axis=1, keepdims=True)
        raised = jnp.exp(scores - peak)
        whole = jnp.sum(raised, axis=1, keepdims=True)
        output = dot_nn(raised.astype(bf16), value_out[0:stop, :]) / whole
        log_total = peak + jnp.log(whole)
        for a in range(top):
            heads_out[a, start:stop, :] = output[a * block_rows : (a + 1) * block_rows]
            totals[a].append(log_total[a * block_rows : (a + 1) * block_rows])
    totals = [jnp.concatenate(value, axis=0) for value in totals]
    columns_out[...] = lanes_of(
        gates + totals + [table[:, index : index + 1] for index in (top + 3, top + 2, top + 4, *range(top))]
    )
    weighted = [
        (gates[a] * heads_out[a]).astype(bf16).astype(f32) for a in range(top)
    ]
    place_heads(spread_out, weighted, places, odds, head_size, positions)
    hidden_one = inputs + dot_nn(spread_out[...], output_weight[...])
    hidden_out[...] = hidden_one
    normal_two, _ = norm_rows(hidden_one)
    ffn_in = (normal_two * vectors[2:3, :] + vectors[3:4, :]).astype(bf16)
    ffn_out[...] = ffn_in
    expert_logits = dot_nt(ffn_in, expert_router[...])
    expert_lane = iota(expert_logits.shape, 1)
    named = [routes[:, top + c : top + c + 1] for c in range(2)]
    expert_gates = soft_columns(
        [
            jnp.sum(jnp.where(expert_lane == value, expert_logits, 0.0), axis=1, keepdims=True)
            for value in named
        ]
    )
    lane = iota((rows, 128), 1)
    expert = jnp.where(lane < 2 * experts, (lane // 8) * 4 + lane % 4, -1)
    first, second = expert == named[0], expert == named[1]
    hot = jnp.where(first | second, 1.0, 0.0)
    earlier = (iota((rows, rows), 1) < iota((rows, rows), 0)).astype(f32).astype(bf16)
    before = dot_nn(earlier, hot.astype(bf16))
    slot = jnp.where(hot > 0.5, before, -1.0)
    gate = jnp.where(first, expert_gates[0], jnp.where(second, expert_gates[1], 0.0))
    turned = jnp.where(lane % 8 < 4, slot, gate).T
    slots_out[...] = turned[: 2 * experts].reshape(experts // 4, 8, rows)


def attention_back(
    block_rows, hooks, tokens, vectors, query_weight, key_weight, value_weight,
    output_weight, head_router, expert_router, attn_in, query, keys, values, heads_out, spread_out, hidden_one,
    ffn_in, columns, grad_rows, grad_logits_t, grad_hidden, state_cotan, halt_sum, tokens_grad, wide, narrow,
):
    take_output, take_query, take_small, pause = hooks
    rows, width = tokens.shape
    head_size = key_weight.shape[0]
    heads = head_router.shape[0]
    positions = query_weight.shape[1] // (2 * head_size)
    top = query.shape[0]
    active_lane = 2 * top + 1
    gain_one, gain_two = vectors[0:1, :], vectors[2:3, :]
    normal_two, inverse_two = norm_rows(hidden_one[...])
    logits_low = grad_logits_t[...].astype(bf16)
    grad_ffn = grad_rows[...] + dot_tn(logits_low, expert_router[...])
    router_two = dot_nn(logits_low, ffn_in[...])
    gain_two_sum = jnp.sum(grad_ffn * normal_two, axis=0, keepdims=True)
    bias_two_sum = jnp.sum(grad_ffn, axis=0, keepdims=True)
    grad_one = grad_hidden[...] + norm_back(grad_ffn, normal_two, inverse_two, gain_two)
    tokens_grad[...] = grad_one
    grad_attn = grad_one.astype(bf16)
    take_output(lambda part: dot_tn(spread_out[:, part], grad_attn))
    pause(0)
    wide[...] = dot_nt(grad_attn, output_weight[...])
    routes = columns[...].astype(jnp.int32)
    chosen = [routes[:, 2 * top + 3 + a : 2 * top + 4 + a] for a in range(top)]
    places = [value // 2 for value in chosen]
    odds = [value % 2 == 1 for value in chosen]
    gates = [columns[:, a : a + 1] for a in range(top)]
    pause(1)
    grad_gates, grad_heads = [], []
    for a in range(top):
        picked = pick_heads(wide, places[a], odds[a], head_size, positions)
        grad_gates.append(jnp.sum(picked * heads_out[a], axis=1, keepdims=True))
        grad_heads.append((gates[a] * picked).astype(bf16))
    inner = functools.reduce(lambda a, b: a + b, [g * d for g, d in zip(gates, grad_gates)])
    grad_logit = [g * (d - inner) for g, d in zip(gates, grad_gates)]
    head_lane = iota((rows, heads), 1)
    grad_hot = functools.reduce(
        lambda a, b: a + b,
        [jnp.where(head_lane == chosen[a], grad_logit[a], 0.0) for a in range(top)],
    )
    pause(2)
    grad_keys = [jnp.zeros((block_rows, head_size), f32) for _ in range(rows // block_rows)]
    grad_values = [jnp.zeros((block_rows, head_size), f32) for _ in range(rows // block_rows)]
    grad_query = [[] for _ in range(top)]
    for start in range(0, rows, block_rows):
        stop = start + block_rows
        part = slice(start, stop)
        queries = jnp.concatenate([query[a, part, :] for a in range(top)], axis=0)
        grads = jnp.concatenate([value[part] for value in grad_heads], axis=0)
        total = jnp.concatenate([columns[part, top + a : top + a + 1] for a in range(top)], axis=0)
        scores = dot_nt(queries, keys[0:stop, :])
        row_pos = iota((top * block_rows, block_rows), 0) % block_rows
        corner = jnp.where(
            iota((top * block_rows, block_rows), 1) <= row_pos, scores[:, start:], f32(-1e30)
        )
        if start:
            scores = jnp.concatenate([scores[:, :start], corner], axis=1)
        else:
            scores = corner
        prob = jnp.exp(scores - total)
        grad_prob = dot_nt(grads, values[0:stop, :])
        row_inner = jnp.sum(prob * grad_prob, axis=1, keepdims=True)
        grad_scores = (prob * (grad_prob - row_inner)).astype(bf16)
        grad_q = (dot_nn(grad_scores, keys[0:stop, :]) * head_size ** (-0.5)).astype(bf16)
        for a in range(top):
            grad_query[a].append(grad_q[a * block_rows : (a + 1) * block_rows].astype(f32))
        step_v = dot_tn(prob.astype(bf16), grads)
        step_k = dot_tn(grad_scores, queries)
        for index in range(stop // block_rows):
            piece = slice(index * block_rows, (index + 1) * block_rows)
            grad_values[index] = grad_values[index] + step_v[piece]
            grad_keys[index] = grad_keys[index] + step_k[piece]
        pause(3 + min(start // block_rows, 3))
    grad_query = [jnp.concatenate(value, axis=0) for value in grad_query]
    place_heads(narrow, grad_query, places, odds, head_size, positions)
    take_query(lambda part: dot_tn(attn_in[...], narrow[:, part]), pause)
    grad_k = jnp.concatenate(grad_keys, axis=0).astype(bf16)
    grad_v = jnp.concatenate(grad_values, axis=0).astype(bf16)
    hot_low = grad_hot.astype(bf16)
    grad_in = (
        dot_nt(narrow[...], query_weight[...])
        + dot_nn(grad_k, key_weight[...])
        + dot_nn(grad_v, value_weight[...])
        + dot_nn(hot_low, head_router[...])
    )
    pause(10)
    normal_one, inverse_one = norm_rows(tokens[...].astype(f32))
    take_small(
        [
            dot_tn(grad_k, attn_in[...]),
            dot_tn(grad_v, attn_in[...]),
            dot_tn(hot_low, attn_in[...]),
            router_two,
            jnp.sum(grad_in * normal_one, axis=0, keepdims=True),
            jnp.sum(grad_in, axis=0, keepdims=True),
            gain_two_sum,
            bias_two_sum,
            halt_sum[0:1, :],
        ]
    )
    tokens_grad[...] = (
        tokens_grad[...]
        + norm_back(grad_in, normal_one, inverse_one, gain_one)
        + (1.0 - columns[:, active_lane : active_lane + 1]) * state_cotan[...].astype(f32)
    )


def stack_small(pieces, room):
    count = sum(piece.shape[0] for piece in pieces)
    width = pieces[0].shape[1]
    return jnp.concatenate(pieces + [jnp.zeros((room - count, width), f32)], axis=0)


def attend_backward(block_rows, *refs):
    inputs, (tokens_grad, query_sum, output_sum, small_sum, wide, narrow) = refs[:22], refs[22:]

    def take_output(term):
        output_sum[...] = term(slice(None))

    def take_query(term, pause):
        query_sum[...] = term(slice(None))

    def take_small(pieces):
        small_sum[...] = stack_small(pieces, small_sum.shape[0])

    hooks = take_output, take_query, take_small, lambda point: None
    attention_back(block_rows, hooks, *inputs, tokens_grad, wide, narrow)


class SumOverAll:
    def __init__(self, number, peers, send, recv, full, final, lands):
        self.number, self.peers, self.send, self.recv = number, peers, send, recv
        self.full, self.final, self.lands = full, final, lands
        self.copies = [[] for _ in range(8)]

    def go(self, stage, source, target, device):
        index = sum(len(copies) for copies in self.copies)
        copy = pltpu.make_async_remote_copy(
            src_ref=source, dst_ref=target, send_sem=self.send.at[self.number, index],
            recv_sem=self.recv.at[self.number, index], device_id=device, device_id_type=MESH,
        )
        copy.start()
        self.copies[stage].append(copy)

    def total(self, lead, landed):
        total = self.full[lead].astype(f32)
        for value in landed:
            total = total + value[...].astype(f32)
        return total

    def step(self, stage):
        full, final = self.full, self.final
        own = tuple(place for place, _ in self.peers)
        if stage:
            for copy in self.copies[stage - 1]:
                copy.wait_recv()
        if stage < 4:
            lead, (place, others) = own[:stage], self.peers[stage]
            arrived = self.lands[stage - 1] if stage else None

            def add(index):
                if stage:
                    landed = [arrived.at[hop, index] for hop in range(arrived.shape[0])]
                    full[lead + (index,)] = self.total(lead + (index,), landed).astype(full.dtype)

            for hop, (index, device) in enumerate(others):
                add(index)
                self.go(stage, full.at[lead + (index,)], self.lands[stage].at[hop], device)
            add(place)
        elif stage < 8:
            if stage == 4:
                arrived = self.lands[3]
                final[own] = self.total(own, [arrived.at[hop] for hop in range(arrived.shape[0])]).astype(final.dtype)
            lead = own[: 8 - stage]
            for _, device in self.peers[7 - stage][1]:
                self.go(stage, final.at[lead], final.at[lead], device)
        else:
            for copies in self.copies:
                for copy in copies:
                    copy.wait_send()


POINTS = (2.5, 3.5, 5.0, 6.0, 7.5, 9.5, 12.0, 13.0, 14.0, 15.0, 16.0, 17.5)
OUTPUT_POINT, QUERY_POINTS, SMALL_POINT = 0, (7, 8, 9), 11
DELAYS = {"core": 1.0, "x": 1.7, "z": 2.4, "y": 1.7}
RATES = {"core": 600.0, "x": 48.0, "z": 50.0, "y": 46.0}
ORDERS = ("xzy", "xzy", "zxy", "xyz", "xzy", "zxy", "yxz")


def ways_of(order, piece_bytes):
    left, ways = piece_bytes / 2, [("core", piece_bytes / 2)]
    for axis in order:
        ways.append((axis, left if axis == "z" else left / 2))
        left = left / 4 if axis == "z" else left / 2
    return ways + ways[::-1]


def plan_steps(piece_bytes, orders, far_chunks, chunk_bytes):
    ways = [ways_of(order, piece_bytes) for order in orders]
    free = dict.fromkeys(RATES, 0.0)
    ready, plan, done = [], [[] for _ in POINTS], 0

    def send(way, size, now):
        free[way] = max(free[way], now) + size / RATES[way] / 1000
        return free[way] + DELAYS[way]

    far_ready = [send("core", chunk_bytes, 0.5) for _ in range(far_chunks)]
    sent_far = 0

    def begin(item, now):
        ready.append((send(*ways[item][0], now), item, 1))

    now = 0.0
    for point, time in enumerate(POINTS):
        now = max(now, time)
        last = point == len(POINTS) - 1
        if point == OUTPUT_POINT:
            for item in range(3):
                begin(item, now)
        if point in QUERY_POINTS:
            begin(3 + QUERY_POINTS.index(point), now)
        if point == SMALL_POINT:
            begin(6, now)
        while True:
            ready.sort()
            if sent_far < far_chunks and far_ready[sent_far] <= now and free["y"] <= now + 1.0:
                plan[point].append((-1, sent_far))
                now += 0.2
                send("y", chunk_bytes, now)
                sent_far += 1
                continue
            if ready and (last or ready[0][0] <= now):
                if last and sent_far < far_chunks and max(free["y"] - 1.0, far_ready[sent_far]) < ready[0][0]:
                    now = max(now, free["y"] - 1.0, far_ready[sent_far])
                    continue
                time, item, stage = ready.pop(0)
                now = max(now, time) + (0.3 if stage == 1 else 0.15)
                plan[point].append((item, stage))
                if stage < 8:
                    ready.append((send(*ways[item][stage], now), item, stage + 1))
                continue
            if last and sent_far < far_chunks:
                now = max(now, free["y"] - 1.0, far_ready[sent_far])
                continue
            break
    return plan, now


def backward_and_sums(block_rows, *refs):
    inputs, terms = refs[:22], refs[22]
    count = len(ORDERS)
    tokens_grad, terms_final, finals = refs[23], refs[24], refs[25 : 25 + count]
    wide, narrow, own_terms, near_terms, far_terms = refs[25 + count : 30 + count]
    fulls, lands = refs[30 + count : 30 + 2 * count], refs[30 + 2 * count : 30 + 6 * count]
    send, recv, load_sem, term_send, term_recv, near_send, near_recv = refs[30 + 6 * count :]
    units, width = terms.shape[0], terms.shape[3]
    line, group = lax.axis_index("expert"), lax.axis_index("dp")
    z, x, y, c = line // 2, line % 2, group // 2, group % 2
    to_core, to_y = {"dp": y * 2 + 1 - c}, {"dp": (1 - y) * 2 + c}
    to_x = {"expert": z * 2 + 1 - x}

    def to_z(hop):
        return {"expert": (z + hop) % 4 * 2 + x}

    barrier = pltpu.get_barrier_semaphore()
    for device in (to_core, to_x, to_y, to_z(1), to_z(2), to_z(3)):
        pl.semaphore_signal(barrier, inc=1, device_id=device, device_id_type=MESH)
    far, near = (1 - y) * 2 + c, y * 2 + c
    loads = [
        [
            pltpu.make_async_copy(terms.at[u, quarter], own_terms.at[u, side], load_sem.at[u, side])
            for side, quarter in enumerate((far, near))
        ]
        for u in range(units)
    ]
    for side in range(2):
        for u in range(units):
            loads[u][side].start()
    pl.semaphore_wait(barrier, 6)

    split_rows = width // 2

    def term_copy(u, half, stage):
        rows = pl.ds(half * split_rows, split_rows)
        if stage == 0:
            source = terms.at[u, (1 - y) * 2 + 1 - c, rows]
            target, device = near_terms.at[u, 0, rows], to_core
        else:
            source, target, device = own_terms.at[u, 0, rows], far_terms.at[u, rows], to_y
        return pltpu.make_async_remote_copy(
            src_ref=source, dst_ref=target, send_sem=term_send.at[u, half, stage],
            recv_sem=term_recv.at[u, half, stage], device_id=device, device_id_type=MESH,
        )

    def near_copy(u):
        return pltpu.make_async_remote_copy(
            src_ref=terms.at[u, y * 2 + 1 - c], dst_ref=near_terms.at[u, 1], send_sem=near_send.at[u],
            recv_sem=near_recv.at[u], device_id=to_core, device_id_type=MESH,
        )

    for chunk in range(2 * units):
        term_copy(chunk // 2, chunk % 2, 0).start()

    def send_far(chunk):
        u, half = chunk // 2, chunk % 2
        if half == 0:
            loads[u][0].wait()
        term_copy(u, half, 0).wait_recv()
        rows = pl.ds(half * split_rows, split_rows)
        total = own_terms[u, 0, rows].astype(f32) + near_terms[u, 0, rows].astype(f32)
        own_terms[u, 0, rows] = total.astype(bf16)
        term_copy(u, half, 1).start()

    def finish_near(u):
        loads[u][1].wait()
        near_copy(u).wait_recv()
        for half in range(2):
            term_copy(u, half, 1).wait_recv()
        total = own_terms[u, 1].astype(f32) + near_terms[u, 1].astype(f32) + far_terms[u].astype(f32)
        terms_final[u] = total.astype(bf16)
        near_copy(u).wait_send()
        for half in range(2):
            term_copy(u, half, 0).wait_send()
            term_copy(u, half, 1).wait_send()

    axes = {
        "x": (x, [(1 - x, to_x)]),
        "y": (y, [(1 - y, to_y)]),
        "z": (z, [((z + hop) % 4, to_z(hop)) for hop in (2, 1, 3)]),
    }
    items = [
        SumOverAll(
            index, [(c, [(1 - c, to_core)])] + [axes[axis] for axis in order], send, recv, fulls[index],
            finals[index], lands[4 * index : 4 * index + 4],
        )
        for index, order in enumerate(ORDERS)
    ]
    small_full = fulls[-1]
    third = math.prod(fulls[0].shape[:-1])
    block_bytes = math.prod(small_full.shape) * 4
    plan, _ = plan_steps(block_bytes, ORDERS, 2 * units, split_rows * width * 2)

    def take(index, term):
        part = index % 3
        value = term(slice(part * third, (part + 1) * third))
        fulls[index][...] = value.astype(bf16).reshape(fulls[index].shape)
        items[index].step(0)

    def take_output(term):
        for part in range(3):
            take(part, term)

    def take_query(term, pause):
        for part in range(3):
            take(3 + part, term)
            pause(QUERY_POINTS[part])

    def take_small(pieces):
        rows = math.prod(small_full.shape[:-1])
        small_full[...] = stack_small(pieces, rows).reshape(small_full.shape)
        items[6].step(0)

    def pause(point):
        for item, stage in plan[point]:
            if item < 0:
                send_far(stage)
            else:
                items[item].step(stage)

    attention_back(block_rows, (take_output, take_query, take_small, pause), *inputs, tokens_grad, wide, narrow)
    for u in range(units):
        near_copy(u).start()
    pause(SMALL_POINT)
    for u in range(units):
        finish_near(u)


def expert_exchange(
    capacity, chunks, lane,
    ffn_in, slots, tokens, hidden_one, state_cotan, accum_cotan, columns, vectors, first_hbm, second_hbm,
    new_state, accum_part, lines_out, grad_hidden, grad_rows, grad_logits_t, halt_sum, terms,
    first, second, column, gathered, grads_in, cross, act, slope, produced, crossed, grad_out, grad_crossed,
    partial, landed, staged, keys, shares, share_out,
    weight_sem, key_send, key_recv, gather_send, gather_recv, cross_send, cross_recv, back_send, back_recv,
    reduce_send, reduce_recv, share_send, share_recv, stage_sem,
):
    rows, width = ffn_in.shape
    local, _, hidden_size = first.shape
    tile = width
    tiles = hidden_size // tile
    piece = rows // chunks
    me = lax.axis_index("expert")
    z, x = me // 2, me % 2
    other = 1 - x
    low = z < 2
    middle = (z == 1) | (z == 2)
    edge = jnp.logical_not(middle)

    def real(mirrored):
        return jnp.where(low, mirrored, 3 - mirrored)

    def along(depth):
        return {"expert": depth * 2 + x}

    across = {"expert": z * 2 + other}

    def order(j):
        return real(jnp.where(middle, jnp.where(j < 2, 1 - j, j), j))

    barrier = pltpu.get_barrier_semaphore()
    for step in range(1, 4):
        pl.semaphore_signal(barrier, inc=1, device_id=along((z + step) % 4), device_id_type=MESH)
    pl.semaphore_signal(barrier, inc=1, device_id=across, device_id_type=MESH)
    loads = [
        pltpu.make_async_copy(first_hbm, first, weight_sem.at[0]),
        pltpu.make_async_copy(second_hbm, second, weight_sem.at[1]),
    ]
    for load in loads:
        load.start()
    column[0, z] = ffn_in[...]
    keys[z] = slots[z]
    pl.semaphore_wait(barrier, 4)

    def key_copy(step):
        there = (z + step) % 4
        return pltpu.make_async_remote_copy(
            src_ref=slots.at[there], dst_ref=keys.at[z], send_sem=key_send.at[step], recv_sem=key_recv.at[z],
            device_id=along(there), device_id_type=MESH,
        )

    def key_arrival(shard):
        return pltpu.make_async_remote_copy(
            src_ref=slots.at[0], dst_ref=keys.at[shard], send_sem=key_send.at[0], recv_sem=key_recv.at[shard],
            device_id=across, device_id_type=MESH,
        )

    def gather_copy(phase, source, shard, depth, index):
        return pltpu.make_async_remote_copy(
            src_ref=source, dst_ref=column.at[phase, shard], send_sem=gather_send.at[phase, index],
            recv_sem=gather_recv.at[phase, shard], device_id=along(depth), device_id_type=MESH,
        )

    def send_own(phase, source):
        @pl.when(edge)
        def _():
            gather_copy(phase, source, z, real(1), 0).start()

        @pl.when(middle)
        def _():
            gather_copy(phase, source, z, real(0), 0).start()
            gather_copy(phase, source, z, real(2), 1).start()

    def forward(phase, mirrored, target, index):
        shard = real(mirrored)
        return gather_copy(phase, column.at[phase, shard], shard, real(target), index)

    def finish_gather(phase, source):
        gather_copy(phase, source, z, real(1), 0).wait_send()

        @pl.when(middle)
        def _():
            gather_copy(phase, source, z, real(2), 1).wait_send()
            forward(phase, 0, 2, 2).wait_send()
            forward(phase, 2, 0, 3).wait_send()
            forward(phase, 3, 0, 4).wait_send()

    def await_shard(phase, mirrored):
        shard = real(mirrored)
        if phase == 0:
            key_arrival(shard).wait_recv()
        gather_copy(phase, column.at[phase, shard], shard, z, 0).wait_recv()

    def await_shards(phase, j):
        @pl.when(edge & (j > 0))
        def _():
            await_shard(phase, j)

        @pl.when(middle & (j == 1))
        def _():
            await_shard(phase, 0)
            forward(phase, 0, 2, 2).start()
            await_shard(phase, 2)
            forward(phase, 2, 0, 3).start()

        @pl.when(middle & (j == 2))
        def _():
            await_shard(phase, 3)
            forward(phase, 3, 0, 4).start()

    def experts_of(shard):
        table = keys[shard]
        found = []
        for own in (True, False):
            for r in range(local):
                here, there = (r, local + r) if own else (local + r, r)
                line = jnp.where(x == 0, table[here : here + 1], table[there : there + 1])
                gate = jnp.where(x == 0, table[4 + here : 5 + here], table[4 + there : 5 + there])
                mask = iota((capacity, rows), 0).astype(f32) == line
                found.append((mask, jnp.sum(jnp.where(mask, gate, 0.0), axis=1, keepdims=True)))
        return found

    def hot_rows(found):
        return jnp.concatenate([jnp.where(mask, 1.0, 0.0).astype(bf16) for mask, _ in found], axis=0)

    def cross_copy(phase, shard, r):
        target = gathered if phase == 0 else grads_in
        return pltpu.make_async_remote_copy(
            src_ref=cross.at[shard, r], dst_ref=target.at[4 + shard, r], send_sem=cross_send.at[phase, shard, r],
            recv_sem=cross_recv.at[phase, shard, r], device_id=across, device_id_type=MESH,
        )

    def back_copy(phase, shard, r):
        source, target = (produced, crossed) if phase == 0 else (grad_out, grad_crossed)
        return pltpu.make_async_remote_copy(
            src_ref=source.at[4 + shard, r], dst_ref=target.at[shard, r], send_sem=back_send.at[phase, shard, r],
            recv_sem=back_recv.at[phase, shard, r], device_id=across, device_id_type=MESH,
        )

    def share_copy(shard):
        return pltpu.make_async_remote_copy(
            src_ref=share_out.at[shard], dst_ref=shares.at[z], send_sem=share_send.at[shard],
            recv_sem=share_recv.at[z], device_id=along(shard), device_id_type=MESH,
        )

    def dispatch(phase, shard):
        found = experts_of(shard)
        taken = dot_nn(hot_rows(found), column[phase, shard])
        lines = []
        for index, (mask, gate) in enumerate(found):
            part = taken[index * capacity : (index + 1) * capacity]
            if phase == 1:
                part = gate * part
            r = index % local
            if index < local:
                (gathered if phase == 0 else grads_in)[shard, r] = part.astype(bf16)
            else:
                cross[shard, r] = part.astype(bf16)
                cross_copy(phase, shard, r).start()
            if phase == 1:
                value = (produced if index < local else crossed)[shard, r].astype(f32)
                inner = jnp.sum(part * value, axis=1, keepdims=True)
                lines.append(jnp.sum(jnp.where(mask, inner, 0.0), axis=0, keepdims=True))
        if phase == 1:
            own, far = lines[:local], lines[local:]
            stack = [jnp.where(x == 0, a, b) for a, b in zip(own + far, far + own)]
            share_out[shard] = jnp.concatenate(stack + [jnp.zeros((4, rows), f32)], axis=0)

            @pl.when(shard == z)
            def _():
                shares[z] = share_out[z]

            @pl.when(shard != z)
            def _():
                share_copy(shard).start()

    def expert_forward(shard):
        def one(r, carry):
            cross_copy(0, shard, r).wait_recv()
            taken = jnp.concatenate([gathered[shard, r], gathered[4 + shard, r]], axis=0)
            total = jnp.zeros((2 * capacity, width), f32)
            for n in range(tiles):
                part = slice(n * tile, (n + 1) * tile)
                pre = dot_nn(taken, first[r, :, part])
                cumulative = 0.5 * (1.0 + lax.erf(pre * (1.0 / math.sqrt(2.0))))
                density = jnp.exp(-0.5 * pre * pre) * (1.0 / math.sqrt(2.0 * math.pi))
                inner = (pre * cumulative).astype(bf16)
                steep = (cumulative + pre * density).astype(bf16)
                act[shard, r, :, part] = inner[:capacity]
                act[4 + shard, r, :, part] = inner[capacity:]
                slope[shard, r, :, part] = steep[:capacity]
                slope[4 + shard, r, :, part] = steep[capacity:]
                total = total + dot_nn(inner, second[r, part, :])
            produced[shard, r] = total[:capacity].astype(bf16)
            produced[4 + shard, r] = total[capacity:].astype(bf16)
            back_copy(0, shard, r).start()
            return carry

        lax.fori_loop(0, local, one, 0)

    def expert_backward(shard):
        def one(r, carry):
            cross_copy(1, shard, r).wait_recv()
            taken = jnp.concatenate([grads_in[shard, r], grads_in[4 + shard, r]], axis=0)
            total = jnp.zeros((2 * capacity, width), f32)
            for n in range(tiles):
                part = slice(n * tile, (n + 1) * tile)
                grad = dot_nt(taken, second[r, part, :])
                steep = jnp.concatenate([slope[shard, r, :, part], slope[4 + shard, r, :, part]], axis=0)
                grad_pre = (grad * steep.astype(f32)).astype(bf16)
                slope[shard, r, :, part] = grad_pre[:capacity]
                slope[4 + shard, r, :, part] = grad_pre[capacity:]
                total = total + dot_nt(grad_pre, first[r, :, part])
            grad_out[shard, r] = total[:capacity].astype(bf16)
            grad_out[4 + shard, r] = total[capacity:].astype(bf16)
            back_copy(1, shard, r).start()
            return carry

        lax.fori_loop(0, local, one, 0)

    def reduce_copy(phase, shard, index, chunk, depth):
        part = pl.ds(pl.multiple_of(chunk * piece, piece), piece)
        return pltpu.make_async_remote_copy(
            src_ref=partial.at[shard, part], dst_ref=landed.at[phase, index, part],
            send_sem=reduce_send.at[phase, index, chunk], recv_sem=reduce_recv.at[phase, index, chunk],
            device_id=along(depth), device_id_type=MESH,
        )

    def combine(phase, j):
        shard = order(j)
        for r in range(local):
            back_copy(phase, shard, r).wait_recv()
        found = experts_of(shard)
        if phase == 0:
            pieces = [
                gate * (produced if index < local else crossed)[shard, index % local].astype(f32)
                for index, (_, gate) in enumerate(found)
            ]
            pieces = [value.astype(bf16) for value in pieces]
        else:
            pieces = [
                (grad_out if index < local else grad_crossed)[shard, index % local]
                for index in range(2 * local)
            ]
        partial[shard] = dot_tn(hot_rows(found), jnp.concatenate(pieces, axis=0)).astype(bf16)

        @pl.when(edge & (j > 0))
        def _():
            for chunk in range(chunks):
                reduce_copy(phase, shard, j - 1, chunk, real(1)).start()

    def pass_on(phase, chunk, source, mirrored, index, depth):
        shard = real(mirrored)
        reduce_copy(phase, shard, source, chunk, z).wait_recv()
        part = pl.ds(pl.multiple_of(chunk * piece, piece), piece)
        partial[shard, part] = (
            partial[shard, part].astype(f32) + landed[phase, source, part].astype(f32)
        ).astype(bf16)
        reduce_copy(phase, shard, index, chunk, depth).start()

    def reduce_rows(phase, filler):
        def step(i, carry):
            @pl.when(middle & (i < chunks))
            def _():
                pass_on(phase, i, 1, 2, 3, real(2))

            @pl.when(middle & (i >= chunks))
            def _():
                pass_on(phase, i - chunks, 2, 3, 4, real(2))
                pass_on(phase, i - chunks, 4, 0, 0, real(0))

            filler(i)
            return carry

        lax.fori_loop(0, 2 * chunks, step, 0)

    def reduced(phase):
        for chunk in range(chunks):
            reduce_copy(phase, z, 0, chunk, z).wait_recv()
        total = partial[z].astype(f32) + landed[phase, 0].astype(f32)

        @pl.when(middle)
        def _():
            for chunk in range(chunks):
                reduce_copy(phase, z, 3, chunk, z).wait_recv()

        return total + jnp.where(middle, landed[phase, 3].astype(f32), 0.0)

    def finish_reduce(phase):
        @pl.when(edge)
        def _():
            for index in range(3):
                for chunk in range(chunks):
                    reduce_copy(phase, real(index + 1), index, chunk, real(1)).wait_send()

        @pl.when(middle)
        def _():
            for chunk in range(chunks):
                reduce_copy(phase, real(2), 3, chunk, real(2)).wait_send()
                reduce_copy(phase, real(3), 4, chunk, real(2)).wait_send()
                reduce_copy(phase, real(0), 0, chunk, real(0)).wait_send()

    def finish_cross(phase):
        for shard in range(4):
            for r in range(local):
                cross_copy(phase, shard, r).wait_send()
                back_copy(phase, shard, r).wait_send()

    def run(phase, experts):
        def step(j, carry):
            @pl.when(j >= 2)
            def _():
                combine(phase, j - 2)

            @pl.when((j >= 1) & (j <= 4))
            def _():
                experts(order(j - 1))

            @pl.when(j <= 3)
            def _():
                await_shards(phase, j)
                dispatch(phase, order(j))

            return carry

        lax.fori_loop(0, 6, step, 0)

    for step in range(1, 4):
        key_copy(step).start()
    send_own(0, ffn_in)
    for load in loads:
        load.wait()
    run(0, expert_forward)
    reduce_rows(0, lambda i: None)
    hidden = hidden_one[...] + reduced(0)
    remain, active, remain_cotan = [columns[:, lane + index : lane + index + 1] for index in range(3)]
    halt_vector = vectors[4:5, :]
    halt_prob = jax.nn.sigmoid(jnp.sum(hidden * halt_vector, axis=1, keepdims=True))
    halt_share = active * remain * halt_prob
    grad_accum = accum_cotan[...].astype(f32)
    grad_share = jnp.sum(grad_accum * hidden, axis=1, keepdims=True)
    grad_logit = active * remain * (grad_share - remain_cotan) * halt_prob * (1.0 - halt_prob)
    grad_here = active * state_cotan[...].astype(f32) + halt_share * grad_accum + grad_logit * halt_vector
    grad_hidden[...] = grad_here
    column[1, z] = grad_here.astype(bf16)
    send_own(1, column.at[1, z])
    new_state[...] = jnp.where(active > 0.5, hidden, tokens[...].astype(f32)).astype(bf16)
    accum_part[...] = halt_share * hidden
    pair = lanes_of(
        [
            remain * (1.0 - active * halt_prob),
            active * halt_prob * grad_share + (1.0 - active * halt_prob) * remain_cotan,
        ]
    )
    lines_out[...] = pair.T[:8]
    halt_sum[...] = jnp.concatenate(
        [jnp.sum(grad_logit * hidden, axis=0, keepdims=True), jnp.zeros((7, width), f32)], axis=0
    )
    for step in range(1, 4):
        key_copy(step).wait_send()
    finish_gather(0, ffn_in)
    finish_cross(0)
    finish_reduce(0)
    run(1, expert_backward)

    def stage(unit, n, slot):
        return pltpu.make_async_copy(staged.at[slot], terms.at[unit, n], stage_sem.at[slot])

    def weight_terms(i):
        r, n = i // tiles, i % tiles
        part = pl.ds(pl.multiple_of(n * tile, tile), tile)
        total = local * 4 * capacity

        @pl.when(i > 0)
        def _():
            stage(0, 0, 0).wait()
            stage(0, 0, 1).wait()

        left = gathered[:, r].reshape(total, width)
        right = slope[:, r, :, part].reshape(total, tile)
        staged[0] = dot_tn(left, right).astype(bf16)
        stage(r, n, 0).start()
        left = act[:, r, :, part].reshape(total, tile)
        right = grads_in[:, r].reshape(total, width)
        staged[1] = dot_tn(left, right).astype(bf16)
        stage(local + r, n, 1).start()

    reduce_rows(1, weight_terms)
    stage(0, 0, 0).wait()
    stage(0, 0, 1).wait()
    for step in range(1, 4):
        shard = (z + step) % 4
        pltpu.make_async_remote_copy(
            src_ref=share_out.at[0], dst_ref=shares.at[shard], send_sem=share_send.at[0],
            recv_sem=share_recv.at[shard], device_id=across, device_id_type=MESH,
        ).wait_recv()
        share_copy(shard).wait_send()
    share = jnp.concatenate([shares[s, 0:4] for s in range(4)], axis=0)
    gate = jnp.concatenate([slots[s, 4:8] for s in range(4)], axis=0)
    grad_logits_t[...] = share - gate * jnp.sum(share, axis=0, keepdims=True)
    grad_rows[...] = reduced(1)
    finish_gather(1, column.at[1, z])
    finish_cross(1)
    finish_reduce(1)


def slot_targets(routes, experts, room_rows):
    flattened = routes.reshape(-1)
    hot_rows = (flattened[:, None] == jnp.arange(experts, dtype=jnp.int32)[None, :]).astype(jnp.int32)
    before = jnp.cumsum(hot_rows, axis=0) - hot_rows
    return flattened * room_rows + jnp.sum(hot_rows * before, axis=1)


def experts_by_all_to_all(
    capacity, tokens, remain, halting, expert_routes, halt_weight, expert_router, expert_in, expert_out,
    state_cotan, accum_cotan, remain_cotan, hidden_one, ffn_in,
):
    rows, width = tokens.shape
    experts = expert_router.shape[1]
    top = expert_routes.shape[1]
    highest = lax.Precision.HIGHEST
    inputs = tokens.astype(f32)
    active = halting.astype(f32)
    expert_logits = jnp.dot(ffn_in, expert_router, preferred_element_type=f32)
    expert_gate = jax.nn.softmax(jnp.take_along_axis(expert_logits, expert_routes, axis=1), axis=1)
    targets = slot_targets(expert_routes, experts, capacity)

    def spread(values):
        placed = jnp.zeros((experts * capacity, width), bf16).at[targets].set(values)
        return lax.all_to_all(
            placed.reshape(experts, capacity, width), "expert", split_axis=0, concat_axis=1, tiled=True
        )

    def collect(values):
        back = lax.all_to_all(values, "expert", split_axis=1, concat_axis=0, tiled=True)
        back = back.reshape(experts * capacity, width)
        return back[targets].astype(f32).reshape(rows, top, width)

    arrived = spread(jnp.repeat(ffn_in, top, axis=0))
    pre_act = jnp.einsum("erd,edf->erf", arrived, expert_in, preferred_element_type=f32)
    inner_act = jax.nn.gelu(pre_act, approximate=False).astype(bf16)
    produced = jnp.einsum("erf,efd->erd", inner_act, expert_out, preferred_element_type=f32).astype(bf16)
    picked = collect(produced)
    hidden = hidden_one + jnp.sum(expert_gate[:, :, None] * picked, axis=1)
    halt_vector = halt_weight.astype(f32)
    halt_prob = jax.nn.sigmoid(jnp.dot(hidden, halt_vector, precision=highest))
    halt_share = active * remain * halt_prob
    new_state = jnp.where(active[:, None] > 0.5, hidden, inputs).astype(bf16)
    accum_part = halt_share[:, None] * hidden
    remain_left = remain * (1.0 - active * halt_prob)
    grad_accum = accum_cotan.astype(f32)
    grad_share = jnp.sum(grad_accum * hidden, axis=1)
    grad_logit = active * remain * (grad_share - remain_cotan) * halt_prob * (1.0 - halt_prob)
    remain_grad = active * halt_prob * grad_share + (1.0 - active * halt_prob) * remain_cotan
    grad_hidden = (
        active[:, None] * state_cotan.astype(f32)
        + halt_share[:, None] * grad_accum
        + grad_logit[:, None] * halt_vector[None, :]
    )
    halt_sum = jnp.dot(grad_logit, hidden, precision=highest)
    grad_gate = jnp.sum(grad_hidden[:, None, :] * picked, axis=2)
    grad_chosen = expert_gate * (grad_gate - jnp.sum(expert_gate * grad_gate, axis=1, keepdims=True))
    expert_hot = (expert_routes[:, :, None] == jnp.arange(experts, dtype=jnp.int32)[None, None, :]).astype(f32)
    grad_logits = jnp.einsum("tk,tke->te", grad_chosen, expert_hot, precision=highest)
    grad_prod = (expert_gate[:, :, None] * grad_hidden[:, None, :]).astype(bf16)
    grad_arrived = spread(grad_prod.reshape(rows * top, width))
    grad_inner = jnp.einsum("erd,efd->erf", grad_arrived, expert_out, preferred_element_type=f32)
    cumulative = 0.5 * (1.0 + lax.erf(pre_act * (1.0 / math.sqrt(2.0))))
    density = jnp.exp(-0.5 * pre_act * pre_act) * (1.0 / math.sqrt(2.0 * math.pi))
    grad_pre = (grad_inner * (cumulative + pre_act * density)).astype(bf16)
    grad_rows = jnp.einsum("erf,edf->erd", grad_pre, expert_in, preferred_element_type=f32).astype(bf16)
    in_terms = jnp.einsum("erd,erf->edf", arrived, grad_pre, preferred_element_type=f32)
    out_terms = jnp.einsum("erf,erd->efd", inner_act, grad_arrived, preferred_element_type=f32)
    return (
        new_state, accum_part, jnp.stack([remain_left, remain_grad]), grad_hidden,
        jnp.sum(collect(grad_rows), axis=1),
        grad_logits.T, jnp.broadcast_to(halt_sum, (8, width)), (in_terms.astype(bf16), out_terms.astype(bf16)),
    )


def vmem(count):
    return [pl.BlockSpec(memory_space=pltpu.VMEM)] * count


def hbm(count):
    return [pl.BlockSpec(memory_space=pl.ANY)] * count


def experts_on_lines(
    capacity, chunks, lane, tokens, columns, vectors, expert_in, expert_out, state_cotan, accum_cotan, hidden_one, ffn_in,
    slots,
):
    rows, width = tokens.shape
    local, _, hidden_size = expert_in.shape
    shape, buffer, flags = jax.ShapeDtypeStruct, pltpu.VMEM, pltpu.SemaphoreType.DMA
    results = pl.pallas_call(
        functools.partial(expert_exchange, capacity, chunks, lane),
        out_shape=[
            shape((rows, width), bf16),
            shape((rows, width), f32),
            shape((8, rows), f32),
            shape((rows, width), f32),
            shape((rows, width), f32),
            shape((8 * local, rows), f32),
            shape((8, width), f32),
            shape((2 * local, hidden_size // width, width, width), bf16),
        ],
        in_specs=vmem(8) + hbm(2),
        out_specs=vmem(7) + hbm(1),
        scratch_shapes=[
            buffer((local, width, hidden_size), bf16),
            buffer((local, hidden_size, width), bf16),
            buffer((2, 4, rows, width), bf16),
            buffer((8, local, capacity, width), bf16),
            buffer((8, local, capacity, width), bf16),
            buffer((4, local, capacity, width), bf16),
            buffer((8, local, capacity, hidden_size), bf16),
            buffer((8, local, capacity, hidden_size), bf16),
            buffer((8, local, capacity, width), bf16),
            buffer((4, local, capacity, width), bf16),
            buffer((8, local, capacity, width), bf16),
            buffer((4, local, capacity, width), bf16),
            buffer((4, rows, width), bf16),
            buffer((2, 5, rows, width), bf16),
            buffer((2, width, width), bf16),
            buffer((4, 8, rows), f32),
            buffer((4, 8, rows), f32),
            buffer((4, 8, rows), f32),
            flags((2,)),
            flags((4,)),
            flags((4,)),
            flags((2, 5)),
            flags((2, 4)),
            flags((2, 4, local)),
            flags((2, 4, local)),
            flags((2, 4, local)),
            flags((2, 4, local)),
            flags((2, 5, chunks)),
            flags((2, 5, chunks)),
            flags((4,)),
            flags((4,)),
            flags((2,)),
        ],
        compiler_params=pltpu.CompilerParams(
            vmem_limit_bytes=VMEM_LIMIT, collective_id=1, has_side_effects=True
        ),
        name="expert_exchange",
    )(ffn_in, slots, tokens, hidden_one, state_cotan, accum_cotan, columns, vectors, expert_in, expert_out)
    new_state, accum_part, pair, grad_hidden, grad_rows, grad_logits_t, halt_sum, terms = results
    return new_state, accum_part, pair, grad_hidden, grad_rows, grad_logits_t, halt_sum, terms


def sums_on_links(operands, terms, small_rows, wides):
    rows, width = operands[0].shape
    wide_size = wides[0].shape[1]
    units = terms.shape[0]
    shape, buffer, flags = jax.ShapeDtypeStruct, pltpu.VMEM, pltpu.SemaphoreType.DMA
    parts = [wide_size // 3] * (len(ORDERS) - 1) + [small_rows]
    kinds = [bf16] * (len(ORDERS) - 1) + [f32]
    hops = {"x": 1, "y": 1, "z": 3}
    splits, landings = [], []
    for order, part, kind in zip(ORDERS, parts, kinds):
        split = (2,) + tuple(hops[axis] + 1 for axis in order) + (part // 32, width)
        splits.append((split, kind))
        for stage, size in enumerate((1, *[hops[axis] for axis in order])):
            landings.append(buffer((size,) + split[stage + 1 :], kind))
    tokens_grad, terms_final, *finals = pl.pallas_call(
        functools.partial(backward_and_sums, 128),
        out_shape=[
            shape((rows, width), f32),
            shape((units, width, width), bf16),
            *[shape(*split) for split in splits],
        ],
        in_specs=vmem(22) + hbm(1),
        out_specs=vmem(2 + len(splits)),
        scratch_shapes=[
            *wides,
            buffer((units, 2, width, width), bf16),
            buffer((units, 2, width, width), bf16),
            buffer((units, width, width), bf16),
            *[buffer(*split) for split in splits],
            *landings,
            flags((len(ORDERS), 12)),
            flags((len(ORDERS), 12)),
            flags((units, 2)),
            flags((units, 2, 2)),
            flags((units, 2, 2)),
            flags((units,)),
            flags((units,)),
        ],
        compiler_params=pltpu.CompilerParams(
            vmem_limit_bytes=VMEM_LIMIT, collective_id=2, has_side_effects=True
        ),
        name="backward_and_sums",
    )(*operands, terms)
    return tokens_grad, terms_final, [value.reshape(part, width) for value, part in zip(finals, parts)]


def write_results(edges, *refs):
    thirds, (terms_low, small, lines, new_state_in, accum_in, tokens_in) = refs[:6], refs[6:12]
    output_grad, query_grad, in_grad, out_grad, new_state, accum_part, tokens_grad, *rest = refs[12:]
    local = in_grad.shape[0]
    width = small.shape[1]
    for index in range(3):
        output_grad[index] = thirds[index][...].astype(f32)
        query_grad[:, index * width : (index + 1) * width] = thirds[3 + index][...].astype(f32)
    in_grad[...] = terms_low[0:local].astype(f32)
    out_grad[...] = terms_low[local:].astype(f32)
    new_state[...] = new_state_in[...]
    accum_part[...] = accum_in[...]
    tokens_grad[...] = tokens_in[...]
    for ref, start, stop in zip(rest, edges[:-1], edges[1:]):
        ref[...] = small[start:stop, :]
    rest[-2][...] = lines[0:1, :]
    rest[-1][...] = lines[1:2, :]


def results(edges, thirds, terms_low, small, lines, new_state, accum_part, tokens_grad):
    shape, steps = jax.ShapeDtypeStruct, 4
    rows, width = new_state.shape
    units = terms_low.shape[0]

    def by_rows(lanes):
        return pl.BlockSpec((width // steps, lanes), lambda i: (i, 0))

    def by_units(count):
        return pl.BlockSpec((count, width // steps, width), lambda i: (0, i, 0))

    def whole(count):
        return pl.BlockSpec((count, width), lambda i: (0, 0))

    def by_tokens():
        return pl.BlockSpec((rows // steps, width), lambda i: (i, 0))

    parts = [stop - start for start, stop in zip(edges[:-1], edges[1:])] + [1, 1]
    return pl.pallas_call(
        functools.partial(write_results, edges),
        grid=(steps,),
        out_shape=[
            shape((3, width, width), f32),
            shape((width, 3 * width), f32),
            shape((units // 2, width, width), f32),
            shape((units // 2, width, width), f32),
            shape((rows, width), bf16),
            shape((rows, width), f32),
            shape((rows, width), f32),
            *[shape((count, width), f32) for count in parts],
        ],
        in_specs=[
            *[by_rows(width) for _ in range(6)], by_units(units), whole(small.shape[0]), whole(lines.shape[0]),
            by_tokens(), by_tokens(), by_tokens(),
        ],
        out_specs=[
            by_units(3), by_rows(3 * width), by_units(units // 2), by_units(units // 2), by_tokens(), by_tokens(),
            by_tokens(), *[whole(count) for count in parts],
        ],
        compiler_params=pltpu.CompilerParams(vmem_limit_bytes=VMEM_LIMIT),
        name="results",
    )(*thirds, terms_low, small, lines, new_state, accum_part, tokens_grad)


def body(
    mesh_sizes, tokens, remain, halting, head_routes, expert_routes, first_gain, first_bias, query_weight,
    key_weight, value_weight, output_weight, head_router, second_gain, second_bias, expert_router, expert_in,
    expert_out, halt_weight, state_cotan, accum_cotan, remain_cotan,
):
    rows, width = tokens.shape
    head_size = key_weight.shape[1]
    top = head_routes.shape[1]
    wide_size = query_weight.shape[1]
    experts = expert_router.shape[1]
    heads = head_router.shape[1]
    capacity = 4 * rows // experts
    shape = jax.ShapeDtypeStruct
    attn_in, query, keys, values, heads_out, spread_out, hidden_one, ffn_in, columns, slots, vectors = pl.pallas_call(
        functools.partial(attend_forward, 128),
        out_shape=[
            shape((rows, width), bf16),
            shape((top, rows, head_size), bf16),
            shape((rows, head_size), bf16),
            shape((rows, head_size), bf16),
            shape((top, rows, head_size), f32),
            shape((rows, wide_size), bf16),
            shape((rows, width), f32),
            shape((rows, width), bf16),
            shape((rows, 128), f32),
            shape((experts // 4, 8, rows), f32),
            shape((8, width), f32),
        ],
        in_specs=vmem(17),
        out_specs=vmem(11),
        scratch_shapes=[pltpu.VMEM((rows, wide_size), f32)],
        compiler_params=pltpu.CompilerParams(vmem_limit_bytes=VMEM_LIMIT),
        name="attend_forward",
    )(
        tokens, head_routes.T, expert_routes.T, remain[None], halting[None], remain_cotan[None], first_gain,
        first_bias, second_gain, second_bias, halt_weight, query_weight, key_weight.T,
        value_weight.T, output_weight, head_router.T, expert_router.T,
    )
    if mesh_sizes == (4, 8):
        stage = experts_on_lines(
            capacity, 4, 2 * top, tokens, columns, vectors, expert_in, expert_out, state_cotan, accum_cotan, hidden_one,
            ffn_in, slots,
        )
    else:
        stage = experts_by_all_to_all(
            capacity, tokens, remain, halting, expert_routes, halt_weight, expert_router, expert_in, expert_out,
            state_cotan, accum_cotan, remain_cotan, hidden_one, ffn_in,
        )
    new_state, accum_part, lines, grad_hidden, grad_rows, grad_logits_t, halt_sum, terms = stage
    operands = (
        tokens, vectors, query_weight, key_weight.T, value_weight.T, output_weight,
        head_router.T, expert_router.T, attn_in, query, keys, values, heads_out, spread_out, hidden_one, ffn_in,
        columns, grad_rows, grad_logits_t, grad_hidden, state_cotan, halt_sum,
    )
    edges = [0, head_size, 2 * head_size, 2 * head_size + heads, 2 * head_size + heads + experts]
    small_rows = 256
    wides = [pltpu.VMEM((rows, wide_size), f32), pltpu.VMEM((rows, wide_size), bf16)]
    if mesh_sizes == (4, 8):
        tokens_grad, expert_grads, (*thirds, small) = sums_on_links(operands, terms, small_rows, wides)
        (output_grad, query_grad, expert_in_grad, expert_out_grad, new_state, accum_part, tokens_grad, *rest) = results(
            [*edges, *range(edges[-1] + 1, edges[-1] + 6)], thirds, expert_grads, small, lines, new_state,
            accum_part, tokens_grad,
        )
        output_grad = output_grad.reshape(wide_size, width)
        key_grad, value_grad, head_router_grad, expert_router_grad = [value.T for value in rest[:4]]
        first_gain_grad, first_bias_grad, second_gain_grad, second_bias_grad, halt_grad, remain_left, remain_grad = [
            value.reshape(width) for value in rest[4:]
        ]
    else:
        in_terms, out_terms = terms
        expert_in_grad = lax.psum_scatter(in_terms, "dp", scatter_dimension=2, tiled=True).astype(f32)
        expert_out_grad = lax.psum_scatter(out_terms, "dp", scatter_dimension=1, tiled=True).astype(f32)
        small_rows = -(-(2 * head_size + heads + experts + 5) // 8) * 8
        tokens_grad, query_sum, output_sum, small_sum = pl.pallas_call(
            functools.partial(attend_backward, 128),
            out_shape=[
                shape((rows, width), f32),
                shape((width, wide_size), f32),
                shape((wide_size, width), f32),
                shape((small_rows, width), f32),
            ],
            in_specs=vmem(22),
            out_specs=vmem(4),
            scratch_shapes=wides,
            compiler_params=pltpu.CompilerParams(vmem_limit_bytes=VMEM_LIMIT),
            name="attend_backward",
        )(*operands)
        query_grad, output_grad, small = lax.psum((query_sum, output_sum, small_sum), ("dp", "expert"))
        key_grad, value_grad, head_router_grad, expert_router_grad = [
            small[start:stop].T for start, stop in zip(edges[:-1], edges[1:])
        ]
        first_gain_grad, first_bias_grad, second_gain_grad, second_bias_grad, halt_grad = [
            small[edges[-1] + index] for index in range(5)
        ]
        remain_left, remain_grad = lines[0], lines[1]
    return (
        new_state, accum_part, remain_left, tokens_grad, remain_grad, first_gain_grad, first_bias_grad, query_grad,
        key_grad, value_grad, output_grad, head_router_grad, second_gain_grad, second_bias_grad,
        expert_router_grad, expert_in_grad, expert_out_grad, halt_grad,
    )


def solution(mesh):
    in_specs = (
        P(("dp", "expert"), None),
        P(("dp", "expert")),
        P(("dp", "expert")),
        P(("dp", "expert"), None),
        P(("dp", "expert"), None),
        P(),
        P(),
        P(),
        P(),
        P(),
        P(),
        P(),
        P(),
        P(),
        P(),
        P("expert", None, None),
        P("expert", None, None),
        P(),
        P(("dp", "expert"), None),
        P(("dp", "expert"), None),
        P(("dp", "expert")),
    )
    out_specs = (
        P(("dp", "expert"), None),
        P(("dp", "expert"), None),
        P(("dp", "expert")),
        P(("dp", "expert"), None),
        P(("dp", "expert")),
        P(),
        P(),
        P(),
        P(),
        P(),
        P(),
        P(),
        P(),
        P(),
        P(),
        P("expert", None, "dp"),
        P("expert", "dp", None),
        P(),
    )
    sizes = (mesh.shape["dp"], mesh.shape["expert"])
    run = functools.partial(body, sizes)
    return jax.shard_map(run, mesh=mesh, in_specs=in_specs, out_specs=out_specs, check_vma=False)
```

```python
import functools
import math

import jax
import jax.numpy as jnp
from jax import lax
from jax.experimental import pallas as pl
from jax.experimental.pallas import tpu as pltpu
from jax.sharding import PartitionSpec as P

epsilon = 1e-05
f32 = jnp.float32
bf16 = jnp.bfloat16
MESH = pl.DeviceIdType.MESH
VMEM_LIMIT = 67043328


def dot_nn(left, right):
    return jnp.dot(left, right, preferred_element_type=f32)


def dot_nt(left, right):
    return lax.dot_general(left, right, (((1,), (1,)), ((), ())), preferred_element_type=f32)


def dot_tn(left, right):
    return lax.dot_general(left, right, (((0,), (0,)), ((), ())), preferred_element_type=f32)


def iota(shape, axis):
    return lax.broadcasted_iota(jnp.int32, shape, axis)


def by_thirds(width, count, work):
    def one(index, carry):
        work(pl.ds(pl.multiple_of(index * width, width), width))
        return carry

    lax.fori_loop(0, count, one, 0)


def norm_rows(values):
    centre = jnp.mean(values, axis=-1, keepdims=True)
    shifted = values - centre
    spread = jnp.mean(shifted * shifted, axis=-1, keepdims=True)
    inverse = lax.rsqrt(spread + epsilon)
    return shifted * inverse, inverse


def norm_back(upstream, normal, inverse, scales):
    scaled = upstream * scales
    inner = (
        scaled
        - jnp.mean(scaled, axis=-1, keepdims=True)
        - normal * jnp.mean(scaled * normal, axis=-1, keepdims=True)
    )
    return inner * inverse


def pick_heads(wide, place, odd, head_size, positions):
    pair = 2 * head_size
    kept = wide[:, :pair]
    for index in range(1, positions):
        kept = jnp.where(place == index, wide[:, index * pair : (index + 1) * pair], kept)
    return jnp.where(odd, kept[:, head_size:], kept[:, :head_size])


def place_heads(out_ref, columns, places, odds, head_size, positions):
    pair = 2 * head_size
    rows = columns[0].shape[0]
    upper = iota((rows, pair), 1) >= head_size
    doubled = [
        jnp.where(upper == odd, jnp.concatenate([column, column], axis=1), 0.0)
        for column, odd in zip(columns, odds)
    ]
    for index in range(positions):
        total = jnp.zeros((rows, pair), f32)
        for value, place in zip(doubled, places):
            total = total + jnp.where(place == index, value, 0.0)
        out_ref[:, index * pair : (index + 1) * pair] = total.astype(bf16)


def lanes_of(columns, width=128):
    rows = columns[0].shape[0]
    lane = iota((rows, width), 1)
    total = jnp.zeros((rows, width), f32)
    for index, column in enumerate(columns):
        total = jnp.where(lane == index, column, total)
    return total


def soft_columns(logits):
    peak = functools.reduce(jnp.maximum, logits)
    raised = [jnp.exp(value - peak) for value in logits]
    whole = functools.reduce(lambda a, b: a + b, raised)
    return [value / whole for value in raised]


def attend_forward(
    block_rows, tokens, head_routes, expert_routes, remain, halting, remain_cotan, first_gain, first_bias,
    second_gain, second_bias, halt_weight, query_weight, key_weight, value_weight, output_weight, head_router,
    expert_router,
    attn_in_out, query_out, key_out, value_out, heads_out, spread_out, hidden_out, ffn_out, columns_out,
    slots_out, vectors, wide,
):
    rows, width = tokens.shape
    head_size = key_weight.shape[0]
    positions = query_weight.shape[1] // (2 * head_size)
    top = head_routes.shape[0]
    experts = expert_router.shape[0]
    for index, vector in enumerate((first_gain, first_bias, second_gain, second_bias, halt_weight)):
        vectors[index : index + 1, :] = vector[...].astype(f32).reshape(1, width)
    vectors[5:8, :] = jnp.zeros((3, width), f32)
    lines = [head_routes[...], expert_routes[...], halting[...]]
    lines = [value.astype(f32) for value in lines] + [remain[...], remain_cotan[...]]
    filled = sum(value.shape[0] for value in lines)
    table = jnp.concatenate(lines + [jnp.zeros((128 - filled, rows), f32)], axis=0).T
    inputs = tokens[...].astype(f32)
    normal, _ = norm_rows(inputs)
    attn_in = (normal * vectors[0:1, :] + vectors[1:2, :]).astype(bf16)
    attn_in_out[...] = attn_in
    wide[...] = dot_nn(attn_in, query_weight[...])
    keys = dot_nt(attn_in, key_weight[...]).astype(bf16)
    key_out[...] = keys
    values = dot_nt(attn_in, value_weight[...]).astype(bf16)
    value_out[...] = values
    head_logits = dot_nt(attn_in, head_router[...])
    routes = table.astype(jnp.int32)
    chosen = [routes[:, a : a + 1] for a in range(top)]
    places = [value // 2 for value in chosen]
    odds = [value % 2 == 1 for value in chosen]
    head_lane = iota(head_logits.shape, 1)
    gates = soft_columns(
        [
            jnp.sum(jnp.where(head_lane == value, head_logits, 0.0), axis=1, keepdims=True)
            for value in chosen
        ]
    )
    for a in range(top):
        picked = pick_heads(wide, places[a], odds[a], head_size, positions)
        query_out[a] = (picked.astype(bf16).astype(f32) * head_size ** (-0.5)).astype(bf16)
    totals = [[] for _ in range(top)]
    for start in range(0, rows, block_rows):
        stop = start + block_rows
        query = jnp.concatenate([query_out[a, start:stop, :] for a in range(top)], axis=0)
        scores = dot_nt(query, key_out[0:stop, :])
        row_pos = iota((top * block_rows, block_rows), 0) % block_rows
        corner = jnp.where(
            iota((top * block_rows, block_rows), 1) <= row_pos, scores[:, start:], f32(-1e30)
        )
        if start:
            scores = jnp.concatenate([scores[:, :start], corner], axis=1)
        else:
            scores = corner
        peak = jnp.max(scores, axis=1, keepdims=True)
        raised = jnp.exp(scores - peak)
        whole = jnp.sum(raised, axis=1, keepdims=True)
        output = dot_nn(raised.astype(bf16), value_out[0:stop, :]) / whole
        log_total = peak + jnp.log(whole)
        for a in range(top):
            heads_out[a, start:stop, :] = output[a * block_rows : (a + 1) * block_rows]
            totals[a].append(log_total[a * block_rows : (a + 1) * block_rows])
    totals = [jnp.concatenate(value, axis=0) for value in totals]
    columns_out[...] = lanes_of(
        gates + totals + [table[:, index : index + 1] for index in (top + 3, top + 2, top + 4, *range(top))]
    )
    weighted = [
        (gates[a] * heads_out[a]).astype(bf16).astype(f32) for a in range(top)
    ]
    place_heads(spread_out, weighted, places, odds, head_size, positions)
    hidden_one = inputs + dot_nn(spread_out[...], output_weight[...])
    hidden_out[...] = hidden_one
    normal_two, _ = norm_rows(hidden_one)
    ffn_in = (normal_two * vectors[2:3, :] + vectors[3:4, :]).astype(bf16)
    ffn_out[...] = ffn_in
    expert_logits = dot_nt(ffn_in, expert_router[...])
    expert_lane = iota(expert_logits.shape, 1)
    named = [routes[:, top + c : top + c + 1] for c in range(2)]
    expert_gates = soft_columns(
        [
            jnp.sum(jnp.where(expert_lane == value, expert_logits, 0.0), axis=1, keepdims=True)
            for value in named
        ]
    )
    lane = iota((rows, 128), 1)
    expert = jnp.where(lane < 2 * experts, (lane // 8) * 4 + lane % 4, -1)
    first, second = expert == named[0], expert == named[1]
    hot = jnp.where(first | second, 1.0, 0.0)
    earlier = (iota((rows, rows), 1) < iota((rows, rows), 0)).astype(f32).astype(bf16)
    before = dot_nn(earlier, hot.astype(bf16))
    slot = jnp.where(hot > 0.5, before, -1.0)
    gate = jnp.where(first, expert_gates[0], jnp.where(second, expert_gates[1], 0.0))
    turned = jnp.where(lane % 8 < 4, slot, gate).T
    slots_out[...] = turned[: 2 * experts].reshape(experts // 4, 8, rows)


def attention_back(
    block_rows, hooks, tokens, vectors, query_weight, key_weight, value_weight,
    output_weight, head_router, expert_router, attn_in, query, keys, values, heads_out, spread_out, hidden_one,
    ffn_in, columns, grad_rows, grad_logits_t, grad_hidden, state_cotan, halt_sum, tokens_grad, wide, narrow,
):
    take_output, take_query, take_small, pause = hooks
    rows, width = tokens.shape
    head_size = key_weight.shape[0]
    heads = head_router.shape[0]
    positions = query_weight.shape[1] // (2 * head_size)
    top = query.shape[0]
    active_lane = 2 * top + 1
    gain_one, gain_two = vectors[0:1, :], vectors[2:3, :]
    normal_two, inverse_two = norm_rows(hidden_one[...])
    logits_low = grad_logits_t[...].astype(bf16)
    grad_ffn = grad_rows[...] + dot_tn(logits_low, expert_router[...])
    router_two = dot_nn(logits_low, ffn_in[...])
    gain_two_sum = jnp.sum(grad_ffn * normal_two, axis=0, keepdims=True)
    bias_two_sum = jnp.sum(grad_ffn, axis=0, keepdims=True)
    grad_one = grad_hidden[...] + norm_back(grad_ffn, normal_two, inverse_two, gain_two)
    tokens_grad[...] = grad_one
    grad_attn = grad_one.astype(bf16)
    take_output(lambda part: dot_tn(spread_out[:, part], grad_attn))
    pause(0)
    wide[...] = dot_nt(grad_attn, output_weight[...])
    routes = columns[...].astype(jnp.int32)
    chosen = [routes[:, 2 * top + 3 + a : 2 * top + 4 + a] for a in range(top)]
    places = [value // 2 for value in chosen]
    odds = [value % 2 == 1 for value in chosen]
    gates = [columns[:, a : a + 1] for a in range(top)]
    pause(1)
    grad_gates, grad_heads = [], []
    for a in range(top):
        picked = pick_heads(wide, places[a], odds[a], head_size, positions)
        grad_gates.append(jnp.sum(picked * heads_out[a], axis=1, keepdims=True))
        grad_heads.append((gates[a] * picked).astype(bf16))
    inner = functools.reduce(lambda a, b: a + b, [g * d for g, d in zip(gates, grad_gates)])
    grad_logit = [g * (d - inner) for g, d in zip(gates, grad_gates)]
    head_lane = iota((rows, heads), 1)
    grad_hot = functools.reduce(
        lambda a, b: a + b,
        [jnp.where(head_lane == chosen[a], grad_logit[a], 0.0) for a in range(top)],
    )
    pause(2)
    grad_keys = [jnp.zeros((block_rows, head_size), f32) for _ in range(rows // block_rows)]
    grad_values = [jnp.zeros((block_rows, head_size), f32) for _ in range(rows // block_rows)]
    grad_query = [[] for _ in range(top)]
    for start in range(0, rows, block_rows):
        stop = start + block_rows
        part = slice(start, stop)
        queries = jnp.concatenate([query[a, part, :] for a in range(top)], axis=0)
        grads = jnp.concatenate([value[part] for value in grad_heads], axis=0)
        total = jnp.concatenate([columns[part, top + a : top + a + 1] for a in range(top)], axis=0)
        scores = dot_nt(queries, keys[0:stop, :])
        row_pos = iota((top * block_rows, block_rows), 0) % block_rows
        corner = jnp.where(
            iota((top * block_rows, block_rows), 1) <= row_pos, scores[:, start:], f32(-1e30)
        )
        if start:
            scores = jnp.concatenate([scores[:, :start], corner], axis=1)
        else:
            scores = corner
        prob = jnp.exp(scores - total)
        grad_prob = dot_nt(grads, values[0:stop, :])
        row_inner = jnp.sum(prob * grad_prob, axis=1, keepdims=True)
        grad_scores = (prob * (grad_prob - row_inner)).astype(bf16)
        grad_q = (dot_nn(grad_scores, keys[0:stop, :]) * head_size ** (-0.5)).astype(bf16)
        for a in range(top):
            grad_query[a].append(grad_q[a * block_rows : (a + 1) * block_rows].astype(f32))
        step_v = dot_tn(prob.astype(bf16), grads)
        step_k = dot_tn(grad_scores, queries)
        for index in range(stop // block_rows):
            piece = slice(index * block_rows, (index + 1) * block_rows)
            grad_values[index] = grad_values[index] + step_v[piece]
            grad_keys[index] = grad_keys[index] + step_k[piece]
        pause(3 + min(start // block_rows, 3))
    grad_query = [jnp.concatenate(value, axis=0) for value in grad_query]
    place_heads(narrow, grad_query, places, odds, head_size, positions)
    take_query(lambda part: dot_tn(attn_in[...], narrow[:, part]), pause)
    grad_k = jnp.concatenate(grad_keys, axis=0).astype(bf16)
    grad_v = jnp.concatenate(grad_values, axis=0).astype(bf16)
    hot_low = grad_hot.astype(bf16)
    grad_in = (
        dot_nt(narrow[...], query_weight[...])
        + dot_nn(grad_k, key_weight[...])
        + dot_nn(grad_v, value_weight[...])
        + dot_nn(hot_low, head_router[...])
    )
    pause(10)
    normal_one, inverse_one = norm_rows(tokens[...].astype(f32))
    take_small(
        [
            dot_tn(grad_k, attn_in[...]),
            dot_tn(grad_v, attn_in[...]),
            dot_tn(hot_low, attn_in[...]),
            router_two,
            jnp.sum(grad_in * normal_one, axis=0, keepdims=True),
            jnp.sum(grad_in, axis=0, keepdims=True),
            gain_two_sum,
            bias_two_sum,
            halt_sum[0:1, :],
        ]
    )
    tokens_grad[...] = (
        tokens_grad[...]
        + norm_back(grad_in, normal_one, inverse_one, gain_one)
        + (1.0 - columns[:, active_lane : active_lane + 1]) * state_cotan[...].astype(f32)
    )


def stack_small(pieces, room):
    count = sum(piece.shape[0] for piece in pieces)
    width = pieces[0].shape[1]
    return jnp.concatenate(pieces + [jnp.zeros((room - count, width), f32)], axis=0)


def attend_backward(block_rows, *refs):
    inputs, (tokens_grad, query_sum, output_sum, small_sum, wide, narrow) = refs[:22], refs[22:]

    def take_output(term):
        output_sum[...] = term(slice(None))

    def take_query(term, pause):
        query_sum[...] = term(slice(None))

    def take_small(pieces):
        small_sum[...] = stack_small(pieces, small_sum.shape[0])

    hooks = take_output, take_query, take_small, lambda point: None
    attention_back(block_rows, hooks, *inputs, tokens_grad, wide, narrow)


class SumOverAll:
    def __init__(self, number, peers, send, recv, full, final, lands):
        self.number, self.peers, self.send, self.recv = number, peers, send, recv
        self.full, self.final, self.lands = full, final, lands
        self.copies = [[] for _ in range(8)]

    def go(self, stage, source, target, device):
        index = sum(len(copies) for copies in self.copies)
        copy = pltpu.make_async_remote_copy(
            src_ref=source, dst_ref=target, send_sem=self.send.at[self.number, index],
            recv_sem=self.recv.at[self.number, index], device_id=device, device_id_type=MESH,
        )
        copy.start()
        self.copies[stage].append(copy)

    def total(self, lead, landed):
        total = self.full[lead].astype(f32)
        for value in landed:
            total = total + value[...].astype(f32)
        return total

    def step(self, stage):
        full, final = self.full, self.final
        own = tuple(place for place, _ in self.peers)
        if stage:
            for copy in self.copies[stage - 1]:
                copy.wait_recv()
        if stage < 4:
            lead, (place, others) = own[:stage], self.peers[stage]
            arrived = self.lands[stage - 1] if stage else None

            def add(index):
                if stage:
                    landed = [arrived.at[hop, index] for hop in range(arrived.shape[0])]
                    full[lead + (index,)] = self.total(lead + (index,), landed).astype(full.dtype)

            for hop, (index, device) in enumerate(others):
                add(index)
                self.go(stage, full.at[lead + (index,)], self.lands[stage].at[hop], device)
            add(place)
        elif stage < 8:
            if stage == 4:
                arrived = self.lands[3]
                final[own] = self.total(own, [arrived.at[hop] for hop in range(arrived.shape[0])]).astype(final.dtype)
            lead = own[: 8 - stage]
            for _, device in self.peers[7 - stage][1]:
                self.go(stage, final.at[lead], final.at[lead], device)
        else:
            for copies in self.copies:
                for copy in copies:
                    copy.wait_send()


POINTS = (2.5, 3.5, 5.0, 6.0, 7.5, 9.5, 12.0, 13.0, 14.0, 15.0, 16.0, 17.5)
OUTPUT_POINT, QUERY_POINTS, SMALL_POINT = 0, (7, 8, 9), 11
DELAYS = {"core": 1.0, "x": 1.7, "z": 2.4, "y": 1.7}
RATES = {"core": 600.0, "x": 48.0, "z": 50.0, "y": 46.0}
ORDERS = ("xzy", "yxz", "yxz", "zxy", "yxz", "yxz", "xyz")


def ways_of(order, piece_bytes):
    left, ways = piece_bytes / 2, [("core", piece_bytes / 2)]
    for axis in order:
        ways.append((axis, left if axis == "z" else left / 2))
        left = left / 4 if axis == "z" else left / 2
    return ways + ways[::-1]


def plan_steps(piece_bytes, orders, far_chunks, chunk_bytes):
    ways = [ways_of(order, piece_bytes) for order in orders]
    free = dict.fromkeys(RATES, 0.0)
    ready, plan, done = [], [[] for _ in POINTS], 0

    def send(way, size, now):
        free[way] = max(free[way], now) + size / RATES[way] / 1000
        return free[way] + DELAYS[way]

    far_ready = [send("core", chunk_bytes, 0.5) for _ in range(far_chunks)]
    sent_far = 0

    def begin(item, now):
        ready.append((send(*ways[item][0], now), item, 1))

    now = 0.0
    for point, time in enumerate(POINTS):
        now = max(now, time)
        last = point == len(POINTS) - 1
        if point == OUTPUT_POINT:
            for item in range(3):
                begin(item, now)
        if point in QUERY_POINTS:
            begin(3 + QUERY_POINTS.index(point), now)
        if point == SMALL_POINT:
            begin(6, now)
        while True:
            ready.sort()
            if sent_far < far_chunks and far_ready[sent_far] <= now and free["y"] <= now + 1.0:
                plan[point].append((-1, sent_far))
                now += 0.2
                send("y", chunk_bytes, now)
                sent_far += 1
                continue
            if ready and (last or ready[0][0] <= now):
                if last and sent_far < far_chunks and max(free["y"] - 1.0, far_ready[sent_far]) < ready[0][0]:
                    now = max(now, free["y"] - 1.0, far_ready[sent_far])
                    continue
                time, item, stage = ready.pop(0)
                now = max(now, time) + (0.3 if stage == 1 else 0.15)
                plan[point].append((item, stage))
                if stage < 8:
                    ready.append((send(*ways[item][stage], now), item, stage + 1))
                continue
            if last and sent_far < far_chunks:
                now = max(now, free["y"] - 1.0, far_ready[sent_far])
                continue
            break
    return plan, now


def backward_and_sums(block_rows, *refs):
    inputs, terms = refs[:22], refs[22]
    count = len(ORDERS)
    tokens_grad, terms_final, finals = refs[23], refs[24], refs[25 : 25 + count]
    wide, narrow, own_terms, near_terms, far_terms = refs[25 + count : 30 + count]
    fulls, lands = refs[30 + count : 30 + 2 * count], refs[30 + 2 * count : 30 + 6 * count]
    send, recv, load_sem, term_send, term_recv, near_send, near_recv = refs[30 + 6 * count :]
    units, width = terms.shape[0], terms.shape[3]
    line, group = lax.axis_index("expert"), lax.axis_index("dp")
    z, x, y, c = line // 2, line % 2, group // 2, group % 2
    to_core, to_y = {"dp": y * 2 + 1 - c}, {"dp": (1 - y) * 2 + c}
    to_x = {"expert": z * 2 + 1 - x}

    def to_z(hop):
        return {"expert": (z + hop) % 4 * 2 + x}

    barrier = pltpu.get_barrier_semaphore()
    for device in (to_core, to_x, to_y, to_z(1), to_z(2), to_z(3)):
        pl.semaphore_signal(barrier, inc=1, device_id=device, device_id_type=MESH)
    far, near = (1 - y) * 2 + c, y * 2 + c
    loads = [
        [
            pltpu.make_async_copy(terms.at[u, quarter], own_terms.at[u, side], load_sem.at[u, side])
            for side, quarter in enumerate((far, near))
        ]
        for u in range(units)
    ]
    for side in range(2):
        for u in range(units):
            loads[u][side].start()
    pl.semaphore_wait(barrier, 6)

    split_rows = width // 2

    def term_copy(u, half, stage):
        rows = pl.ds(half * split_rows, split_rows)
        if stage == 0:
            source = terms.at[u, (1 - y) * 2 + 1 - c, rows]
            target, device = near_terms.at[u, 0, rows], to_core
        else:
            source, target, device = own_terms.at[u, 0, rows], far_terms.at[u, rows], to_y
        return pltpu.make_async_remote_copy(
            src_ref=source, dst_ref=target, send_sem=term_send.at[u, half, stage],
            recv_sem=term_recv.at[u, half, stage], device_id=device, device_id_type=MESH,
        )

    def near_copy(u):
        return pltpu.make_async_remote_copy(
            src_ref=terms.at[u, y * 2 + 1 - c], dst_ref=near_terms.at[u, 1], send_sem=near_send.at[u],
            recv_sem=near_recv.at[u], device_id=to_core, device_id_type=MESH,
        )

    for chunk in range(2 * units):
        term_copy(chunk // 2, chunk % 2, 0).start()

    def send_far(chunk):
        u, half = chunk // 2, chunk % 2
        if half == 0:
            loads[u][0].wait()
        term_copy(u, half, 0).wait_recv()
        rows = pl.ds(half * split_rows, split_rows)
        total = own_terms[u, 0, rows].astype(f32) + near_terms[u, 0, rows].astype(f32)
        own_terms[u, 0, rows] = total.astype(bf16)
        term_copy(u, half, 1).start()

    def finish_near(u):
        loads[u][1].wait()
        near_copy(u).wait_recv()
        for half in range(2):
            term_copy(u, half, 1).wait_recv()
        total = own_terms[u, 1].astype(f32) + near_terms[u, 1].astype(f32) + far_terms[u].astype(f32)
        terms_final[u] = total.astype(bf16)
        near_copy(u).wait_send()
        for half in range(2):
            term_copy(u, half, 0).wait_send()
            term_copy(u, half, 1).wait_send()

    axes = {
        "x": (x, [(1 - x, to_x)]),
        "y": (y, [(1 - y, to_y)]),
        "z": (z, [((z + hop) % 4, to_z(hop)) for hop in (2, 1, 3)]),
    }
    items = [
        SumOverAll(
            index, [(c, [(1 - c, to_core)])] + [axes[axis] for axis in order], send, recv, fulls[index],
            finals[index], lands[4 * index : 4 * index + 4],
        )
        for index, order in enumerate(ORDERS)
    ]
    small_full = fulls[-1]
    third = math.prod(fulls[0].shape[:-1])
    block_bytes = math.prod(small_full.shape) * 4
    plan, _ = plan_steps(block_bytes, ORDERS, 2 * units, split_rows * width * 2)

    def take(index, term):
        part = index % 3
        value = term(slice(part * third, (part + 1) * third))
        fulls[index][...] = value.astype(bf16).reshape(fulls[index].shape)
        items[index].step(0)

    def take_output(term):
        for part in range(3):
            take(part, term)

    def take_query(term, pause):
        for part in range(3):
            take(3 + part, term)
            pause(QUERY_POINTS[part])

    def take_small(pieces):
        rows = math.prod(small_full.shape[:-1])
        small_full[...] = stack_small(pieces, rows).reshape(small_full.shape)
        items[6].step(0)

    def pause(point):
        for item, stage in plan[point]:
            if item < 0:
                send_far(stage)
            else:
                items[item].step(stage)

    attention_back(block_rows, (take_output, take_query, take_small, pause), *inputs, tokens_grad, wide, narrow)
    for u in range(units):
        near_copy(u).start()
    pause(SMALL_POINT)
    for u in range(units):
        finish_near(u)


def expert_exchange(
    capacity, chunks, lane,
    ffn_in, slots, tokens, hidden_one, state_cotan, accum_cotan, columns, vectors, first_hbm, second_hbm,
    new_state, accum_part, lines_out, grad_hidden, grad_rows, grad_logits_t, halt_sum, terms, out_final,
    first, second, column, gathered, grads_in, cross, act, slope, produced, crossed, grad_out, grad_crossed,
    partial, landed, keys, shares, share_out, out_core, out_y,
    weight_sem, key_send, key_recv, gather_send, gather_recv, cross_send, cross_recv, back_send, back_recv,
    reduce_send, reduce_recv, share_send, share_recv, stage_sem, own_send, own_recv, out_send, out_recv,
):
    rows, width = ffn_in.shape
    local, _, hidden_size = first.shape
    tile = width
    tiles = hidden_size // tile
    piece = rows // chunks
    me = lax.axis_index("expert")
    z, x = me // 2, me % 2
    other = 1 - x
    low = z < 2
    middle = (z == 1) | (z == 2)
    edge = jnp.logical_not(middle)

    def real(mirrored):
        return jnp.where(low, mirrored, 3 - mirrored)

    def along(depth):
        return {"expert": depth * 2 + x}

    across = {"expert": z * 2 + other}
    group = lax.axis_index("dp")
    y, c = group // 2, group % 2
    to_core, to_y = {"dp": y * 2 + 1 - c}, {"dp": (1 - y) * 2 + c}

    def order(j):
        return real(jnp.where(middle, jnp.where(j < 2, 1 - j, j), j))

    barrier = pltpu.get_barrier_semaphore()
    for step in range(1, 4):
        pl.semaphore_signal(barrier, inc=1, device_id=along((z + step) % 4), device_id_type=MESH)
    for device in (across, to_core, to_y):
        pl.semaphore_signal(barrier, inc=1, device_id=device, device_id_type=MESH)
    loads = [
        pltpu.make_async_copy(first_hbm, first, weight_sem.at[0]),
        pltpu.make_async_copy(second_hbm, second, weight_sem.at[1]),
    ]
    for load in loads:
        load.start()
    column[0, z] = ffn_in[...]
    keys[z] = slots[z]
    pl.semaphore_wait(barrier, 6)

    def key_copy(step):
        there = (z + step) % 4
        return pltpu.make_async_remote_copy(
            src_ref=slots.at[there], dst_ref=keys.at[z], send_sem=key_send.at[step], recv_sem=key_recv.at[z],
            device_id=along(there), device_id_type=MESH,
        )

    def key_arrival(shard):
        return pltpu.make_async_remote_copy(
            src_ref=slots.at[0], dst_ref=keys.at[shard], send_sem=key_send.at[0], recv_sem=key_recv.at[shard],
            device_id=across, device_id_type=MESH,
        )

    def gather_copy(phase, source, shard, depth, index):
        return pltpu.make_async_remote_copy(
            src_ref=source, dst_ref=column.at[phase, shard], send_sem=gather_send.at[phase, index],
            recv_sem=gather_recv.at[phase, shard], device_id=along(depth), device_id_type=MESH,
        )

    def send_own():
        @pl.when(edge)
        def _():
            gather_copy(0, ffn_in, z, real(1), 0).start()

        @pl.when(middle)
        def _():
            gather_copy(0, ffn_in, z, real(0), 0).start()
            gather_copy(0, ffn_in, z, real(2), 1).start()

    def chunk_copy(shard, chunk, depth, index):
        part = pl.ds(pl.multiple_of(chunk * piece, piece), piece)
        return pltpu.make_async_remote_copy(
            src_ref=column.at[1, shard, part], dst_ref=column.at[1, shard, part],
            send_sem=own_send.at[index, chunk], recv_sem=own_recv.at[shard, chunk], device_id=along(depth),
            device_id_type=MESH,
        )

    def send_chunk(chunk):
        @pl.when(edge)
        def _():
            chunk_copy(z, chunk, real(1), 0).start()

        @pl.when(middle)
        def _():
            chunk_copy(z, chunk, real(0), 0).start()
            chunk_copy(z, chunk, real(2), 1).start()

    def forward(phase, mirrored, target, index):
        shard = real(mirrored)
        return gather_copy(phase, column.at[phase, shard], shard, real(target), index)

    def finish_gather(phase):
        if phase == 0:
            gather_copy(0, ffn_in, z, real(1), 0).wait_send()
        else:
            for chunk in range(chunks):
                chunk_copy(z, chunk, real(1), 0).wait_send()

        @pl.when(middle)
        def _():
            if phase == 0:
                gather_copy(0, ffn_in, z, real(2), 1).wait_send()
            else:
                for chunk in range(chunks):
                    chunk_copy(z, chunk, real(2), 1).wait_send()
            forward(phase, 0, 2, 2).wait_send()
            forward(phase, 2, 0, 3).wait_send()
            forward(phase, 3, 0, 4).wait_send()

    def await_shard(phase, mirrored, next_to):
        shard = real(mirrored)
        if phase == 0:
            key_arrival(shard).wait_recv()
        if phase == 1 and next_to:
            for chunk in range(chunks):
                chunk_copy(shard, chunk, z, 0).wait_recv()
        else:
            gather_copy(phase, column.at[phase, shard], shard, z, 0).wait_recv()

    def await_shards(phase, j):
        @pl.when(edge & (j == 1))
        def _():
            await_shard(phase, 1, True)

        @pl.when(edge & (j > 1))
        def _():
            await_shard(phase, j, False)

        @pl.when(middle & (j == 1))
        def _():
            await_shard(phase, 0, True)
            forward(phase, 0, 2, 2).start()
            await_shard(phase, 2, True)
            forward(phase, 2, 0, 3).start()

        @pl.when(middle & (j == 2))
        def _():
            await_shard(phase, 3, False)
            forward(phase, 3, 0, 4).start()

    def experts_of(shard):
        table = keys[shard]
        found = []
        for own in (True, False):
            for r in range(local):
                here, there = (r, local + r) if own else (local + r, r)
                line = jnp.where(x == 0, table[here : here + 1], table[there : there + 1])
                gate = jnp.where(x == 0, table[4 + here : 5 + here], table[4 + there : 5 + there])
                mask = iota((capacity, rows), 0).astype(f32) == line
                found.append((mask, jnp.sum(jnp.where(mask, gate, 0.0), axis=1, keepdims=True)))
        return found

    def hot_rows(found):
        return jnp.concatenate([jnp.where(mask, 1.0, 0.0).astype(bf16) for mask, _ in found], axis=0)

    def cross_copy(phase, shard, r):
        target = gathered if phase == 0 else grads_in
        return pltpu.make_async_remote_copy(
            src_ref=cross.at[shard, r], dst_ref=target.at[4 + shard, r], send_sem=cross_send.at[phase, shard, r],
            recv_sem=cross_recv.at[phase, shard, r], device_id=across, device_id_type=MESH,
        )

    def back_copy(phase, shard, r):
        source, target = (produced, crossed) if phase == 0 else (grad_out, grad_crossed)
        return pltpu.make_async_remote_copy(
            src_ref=source.at[4 + shard, r], dst_ref=target.at[shard, r], send_sem=back_send.at[phase, shard, r],
            recv_sem=back_recv.at[phase, shard, r], device_id=across, device_id_type=MESH,
        )

    def share_copy(shard):
        return pltpu.make_async_remote_copy(
            src_ref=share_out.at[shard], dst_ref=shares.at[z], send_sem=share_send.at[shard],
            recv_sem=share_recv.at[z], device_id=along(shard), device_id_type=MESH,
        )

    def dispatch(phase, shard):
        found = experts_of(shard)
        taken = dot_nn(hot_rows(found), column[phase, shard])
        lines = []
        for index, (mask, gate) in enumerate(found):
            part = taken[index * capacity : (index + 1) * capacity]
            if phase == 1:
                part = gate * part
            r = index % local
            if index < local:
                (gathered if phase == 0 else grads_in)[shard, r] = part.astype(bf16)
            else:
                cross[shard, r] = part.astype(bf16)
                cross_copy(phase, shard, r).start()
            if phase == 1:
                value = (produced if index < local else crossed)[shard, r].astype(f32)
                inner = jnp.sum(part * value, axis=1, keepdims=True)
                lines.append(jnp.sum(jnp.where(mask, inner, 0.0), axis=0, keepdims=True))
        if phase == 1:
            own, far = lines[:local], lines[local:]
            stack = [jnp.where(x == 0, a, b) for a, b in zip(own + far, far + own)]
            share_out[shard] = jnp.concatenate(stack + [jnp.zeros((4, rows), f32)], axis=0)

            @pl.when(shard == z)
            def _():
                shares[z] = share_out[z]

            @pl.when(shard != z)
            def _():
                share_copy(shard).start()

    def expert_forward(shard):
        def one(r, carry):
            cross_copy(0, shard, r).wait_recv()
            taken = jnp.concatenate([gathered[shard, r], gathered[4 + shard, r]], axis=0)
            total = jnp.zeros((2 * capacity, width), f32)
            for n in range(tiles):
                part = slice(n * tile, (n + 1) * tile)
                pre = dot_nn(taken, first[r, :, part])
                cumulative = 0.5 * (1.0 + lax.erf(pre * (1.0 / math.sqrt(2.0))))
                density = jnp.exp(-0.5 * pre * pre) * (1.0 / math.sqrt(2.0 * math.pi))
                inner = (pre * cumulative).astype(bf16)
                steep = (cumulative + pre * density).astype(bf16)
                act[shard, r, :, part] = inner[:capacity]
                act[4 + shard, r, :, part] = inner[capacity:]
                slope[shard, r, :, part] = steep[:capacity]
                slope[4 + shard, r, :, part] = steep[capacity:]
                total = total + dot_nn(inner, second[r, part, :])
            produced[shard, r] = total[:capacity].astype(bf16)
            produced[4 + shard, r] = total[capacity:].astype(bf16)
            back_copy(0, shard, r).start()
            return carry

        lax.fori_loop(0, local, one, 0)

    def expert_backward(shard):
        def one(r, carry):
            cross_copy(1, shard, r).wait_recv()
            taken = jnp.concatenate([grads_in[shard, r], grads_in[4 + shard, r]], axis=0)
            total = jnp.zeros((2 * capacity, width), f32)
            for n in range(tiles):
                part = slice(n * tile, (n + 1) * tile)
                grad = dot_nt(taken, second[r, part, :])
                steep = jnp.concatenate([slope[shard, r, :, part], slope[4 + shard, r, :, part]], axis=0)
                grad_pre = (grad * steep.astype(f32)).astype(bf16)
                slope[shard, r, :, part] = grad_pre[:capacity]
                slope[4 + shard, r, :, part] = grad_pre[capacity:]
                total = total + dot_nt(grad_pre, first[r, :, part])
            grad_out[shard, r] = total[:capacity].astype(bf16)
            grad_out[4 + shard, r] = total[capacity:].astype(bf16)
            back_copy(1, shard, r).start()
            return carry

        lax.fori_loop(0, local, one, 0)

    def reduce_copy(phase, shard, index, chunk, depth):
        part = pl.ds(pl.multiple_of(chunk * piece, piece), piece)
        return pltpu.make_async_remote_copy(
            src_ref=partial.at[shard, part], dst_ref=landed.at[phase, index, part],
            send_sem=reduce_send.at[phase, index, chunk], recv_sem=reduce_recv.at[phase, index, chunk],
            device_id=along(depth), device_id_type=MESH,
        )

    def combine(phase, j):
        shard = order(j)
        for r in range(local):
            back_copy(phase, shard, r).wait_recv()
        found = experts_of(shard)
        if phase == 0:
            pieces = [
                gate * (produced if index < local else crossed)[shard, index % local].astype(f32)
                for index, (_, gate) in enumerate(found)
            ]
            pieces = [value.astype(bf16) for value in pieces]
        else:
            pieces = [
                (grad_out if index < local else grad_crossed)[shard, index % local]
                for index in range(2 * local)
            ]
        partial[shard] = dot_tn(hot_rows(found), jnp.concatenate(pieces, axis=0)).astype(bf16)

        @pl.when(edge & (j > 0))
        def _():
            for chunk in range(chunks):
                reduce_copy(phase, shard, j - 1, chunk, real(1)).start()

    def pass_on(phase, chunk, source, mirrored, index, depth):
        shard = real(mirrored)
        reduce_copy(phase, shard, source, chunk, z).wait_recv()
        part = pl.ds(pl.multiple_of(chunk * piece, piece), piece)
        partial[shard, part] = (
            partial[shard, part].astype(f32) + landed[phase, source, part].astype(f32)
        ).astype(bf16)
        reduce_copy(phase, shard, index, chunk, depth).start()

    def reduce_rows(phase, filler):
        def step(i, carry):
            @pl.when(middle & (i < chunks))
            def _():
                pass_on(phase, i, 1, 2, 3, real(2))

            @pl.when(middle & (i >= chunks))
            def _():
                pass_on(phase, i - chunks, 2, 3, 4, real(2))
                pass_on(phase, i - chunks, 4, 0, 0, real(0))

            filler(i)
            return carry

        lax.fori_loop(0, 2 * chunks, step, 0)

    def reduced_chunk(phase, chunk):
        reduce_copy(phase, z, 0, chunk, z).wait_recv()

        @pl.when(middle)
        def _():
            reduce_copy(phase, z, 3, chunk, z).wait_recv()

        part = pl.ds(pl.multiple_of(chunk * piece, piece), piece)
        total = partial[z, part].astype(f32) + landed[phase, 0, part].astype(f32)
        return total + jnp.where(middle, landed[phase, 3, part].astype(f32), 0.0)

    def reduced(phase):
        return jnp.concatenate([reduced_chunk(phase, chunk) for chunk in range(chunks)], axis=0)

    def finish_reduce(phase):
        @pl.when(edge)
        def _():
            for index in range(3):
                for chunk in range(chunks):
                    reduce_copy(phase, real(index + 1), index, chunk, real(1)).wait_send()

        @pl.when(middle)
        def _():
            for chunk in range(chunks):
                reduce_copy(phase, real(2), 3, chunk, real(2)).wait_send()
                reduce_copy(phase, real(3), 4, chunk, real(2)).wait_send()
                reduce_copy(phase, real(0), 0, chunk, real(0)).wait_send()

    def finish_cross(phase):
        for shard in range(4):
            for r in range(local):
                cross_copy(phase, shard, r).wait_send()
                back_copy(phase, shard, r).wait_send()

    out_terms = [column.at[0], landed.at[0]]

    def out_copy(r, stage):
        source, target, device = (
            (out_terms[r].at[0], out_core.at[r, 0], to_core),
            (out_terms[r].at[2], out_core.at[r, 1], to_core),
            (out_terms[r].at[1], out_y.at[r], to_y),
        )[stage]
        return pltpu.make_async_remote_copy(
            src_ref=source, dst_ref=target, send_sem=out_send.at[r, stage], recv_sem=out_recv.at[r, stage],
            device_id=device, device_id_type=MESH,
        )

    def make_out_terms():
        total = local * 4 * capacity
        for r in range(local):

            def one(k, carry):
                quarter = jnp.where(k < 2, 1 - y, y) * 2 + jnp.where(k % 2 == 0, 1 - c, c)
                part = pl.ds(pl.multiple_of(quarter * tile, tile), tile)
                left = act[:, r, :, part].reshape(total, tile)
                right = grads_in[:, r].reshape(total, width)
                out_terms[r][k] = dot_tn(left, right).astype(bf16)
                return carry

            lax.fori_loop(0, 4, one, 0)
            out_copy(r, 0).start()
            out_copy(r, 1).start()

    def send_out_terms():
        for r in range(local):
            out_copy(r, 0).wait_recv()
            out_terms[r][1] = (out_terms[r][1].astype(f32) + out_core[r, 0].astype(f32)).astype(bf16)
            out_copy(r, 2).start()

    def finish_out_terms():
        for r in range(local):
            out_copy(r, 1).wait_recv()
            out_copy(r, 2).wait_recv()
            total = out_terms[r][3].astype(f32) + out_core[r, 1].astype(f32) + out_y[r].astype(f32)
            out_final[r] = total.astype(bf16)
            for stage in range(3):
                out_copy(r, stage).wait_send()

    def run(phase, experts):
        def step(j, carry):
            if phase == 1:

                @pl.when(j == 5)
                def _():
                    make_out_terms()

            @pl.when(j >= 2)
            def _():
                combine(phase, j - 2)

            @pl.when((j >= 1) & (j <= 4))
            def _():
                experts(order(j - 1))

            @pl.when(j <= 3)
            def _():
                await_shards(phase, j)
                dispatch(phase, order(j))

            return carry

        lax.fori_loop(0, 6, step, 0)

    for step in range(1, 4):
        key_copy(step).start()
    send_own()
    for load in loads:
        load.wait()
    run(0, expert_forward)
    reduce_rows(0, lambda i: None)
    halt_vector = vectors[4:5, :]
    halt_sum[...] = jnp.zeros((8, width), f32)

    def halt(chunk, carry):
        part = pl.ds(pl.multiple_of(chunk * piece, piece), piece)
        hidden = hidden_one[part, :] + reduced_chunk(0, chunk)
        remain, active, remain_cotan = [columns[part, lane + index : lane + index + 1] for index in range(3)]
        halt_prob = jax.nn.sigmoid(jnp.sum(hidden * halt_vector, axis=1, keepdims=True))
        halt_share = active * remain * halt_prob
        grad_accum = accum_cotan[part, :].astype(f32)
        grad_share = jnp.sum(grad_accum * hidden, axis=1, keepdims=True)
        grad_logit = active * remain * (grad_share - remain_cotan) * halt_prob * (1.0 - halt_prob)
        grad_here = active * state_cotan[part, :].astype(f32) + halt_share * grad_accum + grad_logit * halt_vector
        column[1, z, part, :] = grad_here.astype(bf16)
        send_chunk(chunk)
        grad_hidden[part, :] = grad_here
        new_state[part, :] = jnp.where(active > 0.5, hidden, tokens[part, :].astype(f32)).astype(bf16)
        accum_part[part, :] = halt_share * hidden
        pair = lanes_of(
            [
                remain * (1.0 - active * halt_prob),
                active * halt_prob * grad_share + (1.0 - active * halt_prob) * remain_cotan,
            ]
        )
        lines_out[:, part] = pair.T[:8]
        halt_sum[0:1, :] = halt_sum[0:1, :] + jnp.sum(grad_logit * hidden, axis=0, keepdims=True)
        return carry

    lax.fori_loop(0, chunks, halt, 0)
    for step in range(1, 4):
        key_copy(step).wait_send()
    finish_gather(0)
    finish_cross(0)
    finish_reduce(0)
    run(1, expert_backward)

    def stage(r, n):
        return pltpu.make_async_copy(landed.at[0, 4], terms.at[r, n], stage_sem)

    def weight_terms(i):
        r, n = i // tiles, i % tiles
        part = pl.ds(pl.multiple_of(n * tile, tile), tile)
        total = local * 4 * capacity

        @pl.when(i > 0)
        def _():
            stage(0, 0).wait()

        left = gathered[:, r].reshape(total, width)
        right = slope[:, r, :, part].reshape(total, tile)
        landed[0, 4] = dot_tn(left, right).astype(bf16)
        stage(r, n).start()

    send_out_terms()
    reduce_rows(1, weight_terms)
    stage(0, 0).wait()
    for step in range(1, 4):
        shard = (z + step) % 4
        pltpu.make_async_remote_copy(
            src_ref=share_out.at[0], dst_ref=shares.at[shard], send_sem=share_send.at[0],
            recv_sem=share_recv.at[shard], device_id=across, device_id_type=MESH,
        ).wait_recv()
        share_copy(shard).wait_send()
    share = jnp.concatenate([shares[s, 0:4] for s in range(4)], axis=0)
    gate = jnp.concatenate([slots[s, 4:8] for s in range(4)], axis=0)
    grad_logits_t[...] = share - gate * jnp.sum(share, axis=0, keepdims=True)
    finish_out_terms()
    grad_rows[...] = reduced(1)
    finish_gather(1)
    finish_cross(1)
    finish_reduce(1)


def slot_targets(routes, experts, room_rows):
    flattened = routes.reshape(-1)
    hot_rows = (flattened[:, None] == jnp.arange(experts, dtype=jnp.int32)[None, :]).astype(jnp.int32)
    before = jnp.cumsum(hot_rows, axis=0) - hot_rows
    return flattened * room_rows + jnp.sum(hot_rows * before, axis=1)


def experts_by_all_to_all(
    capacity, tokens, remain, halting, expert_routes, halt_weight, expert_router, expert_in, expert_out,
    state_cotan, accum_cotan, remain_cotan, hidden_one, ffn_in,
):
    rows, width = tokens.shape
    experts = expert_router.shape[1]
    top = expert_routes.shape[1]
    highest = lax.Precision.HIGHEST
    inputs = tokens.astype(f32)
    active = halting.astype(f32)
    expert_logits = jnp.dot(ffn_in, expert_router, preferred_element_type=f32)
    expert_gate = jax.nn.softmax(jnp.take_along_axis(expert_logits, expert_routes, axis=1), axis=1)
    targets = slot_targets(expert_routes, experts, capacity)

    def spread(values):
        placed = jnp.zeros((experts * capacity, width), bf16).at[targets].set(values)
        return lax.all_to_all(
            placed.reshape(experts, capacity, width), "expert", split_axis=0, concat_axis=1, tiled=True
        )

    def collect(values):
        back = lax.all_to_all(values, "expert", split_axis=1, concat_axis=0, tiled=True)
        back = back.reshape(experts * capacity, width)
        return back[targets].astype(f32).reshape(rows, top, width)

    arrived = spread(jnp.repeat(ffn_in, top, axis=0))
    pre_act = jnp.einsum("erd,edf->erf", arrived, expert_in, preferred_element_type=f32)
    inner_act = jax.nn.gelu(pre_act, approximate=False).astype(bf16)
    produced = jnp.einsum("erf,efd->erd", inner_act, expert_out, preferred_element_type=f32).astype(bf16)
    picked = collect(produced)
    hidden = hidden_one + jnp.sum(expert_gate[:, :, None] * picked, axis=1)
    halt_vector = halt_weight.astype(f32)
    halt_prob = jax.nn.sigmoid(jnp.dot(hidden, halt_vector, precision=highest))
    halt_share = active * remain * halt_prob
    new_state = jnp.where(active[:, None] > 0.5, hidden, inputs).astype(bf16)
    accum_part = halt_share[:, None] * hidden
    remain_left = remain * (1.0 - active * halt_prob)
    grad_accum = accum_cotan.astype(f32)
    grad_share = jnp.sum(grad_accum * hidden, axis=1)
    grad_logit = active * remain * (grad_share - remain_cotan) * halt_prob * (1.0 - halt_prob)
    remain_grad = active * halt_prob * grad_share + (1.0 - active * halt_prob) * remain_cotan
    grad_hidden = (
        active[:, None] * state_cotan.astype(f32)
        + halt_share[:, None] * grad_accum
        + grad_logit[:, None] * halt_vector[None, :]
    )
    halt_sum = jnp.dot(grad_logit, hidden, precision=highest)
    grad_gate = jnp.sum(grad_hidden[:, None, :] * picked, axis=2)
    grad_chosen = expert_gate * (grad_gate - jnp.sum(expert_gate * grad_gate, axis=1, keepdims=True))
    expert_hot = (expert_routes[:, :, None] == jnp.arange(experts, dtype=jnp.int32)[None, None, :]).astype(f32)
    grad_logits = jnp.einsum("tk,tke->te", grad_chosen, expert_hot, precision=highest)
    grad_prod = (expert_gate[:, :, None] * grad_hidden[:, None, :]).astype(bf16)
    grad_arrived = spread(grad_prod.reshape(rows * top, width))
    grad_inner = jnp.einsum("erd,efd->erf", grad_arrived, expert_out, preferred_element_type=f32)
    cumulative = 0.5 * (1.0 + lax.erf(pre_act * (1.0 / math.sqrt(2.0))))
    density = jnp.exp(-0.5 * pre_act * pre_act) * (1.0 / math.sqrt(2.0 * math.pi))
    grad_pre = (grad_inner * (cumulative + pre_act * density)).astype(bf16)
    grad_rows = jnp.einsum("erf,edf->erd", grad_pre, expert_in, preferred_element_type=f32).astype(bf16)
    in_terms = jnp.einsum("erd,erf->edf", arrived, grad_pre, preferred_element_type=f32)
    out_terms = jnp.einsum("erf,erd->efd", inner_act, grad_arrived, preferred_element_type=f32)
    return (
        new_state, accum_part, jnp.stack([remain_left, remain_grad]), grad_hidden,
        jnp.sum(collect(grad_rows), axis=1),
        grad_logits.T, jnp.broadcast_to(halt_sum, (8, width)), (in_terms.astype(bf16), out_terms.astype(bf16)),
    )


def vmem(count):
    return [pl.BlockSpec(memory_space=pltpu.VMEM)] * count


def hbm(count):
    return [pl.BlockSpec(memory_space=pl.ANY)] * count


def experts_on_lines(
    capacity, chunks, lane, tokens, columns, vectors, expert_in, expert_out, state_cotan, accum_cotan, hidden_one, ffn_in,
    slots,
):
    rows, width = tokens.shape
    local, _, hidden_size = expert_in.shape
    shape, buffer, flags = jax.ShapeDtypeStruct, pltpu.VMEM, pltpu.SemaphoreType.DMA
    results = pl.pallas_call(
        functools.partial(expert_exchange, capacity, chunks, lane),
        out_shape=[
            shape((rows, width), bf16),
            shape((rows, width), f32),
            shape((8, rows), f32),
            shape((rows, width), f32),
            shape((rows, width), f32),
            shape((8 * local, rows), f32),
            shape((8, width), f32),
            shape((local, hidden_size // width, width, width), bf16),
            shape((local, width, width), bf16),
        ],
        in_specs=vmem(8) + hbm(2),
        out_specs=vmem(7) + hbm(1) + vmem(1),
        scratch_shapes=[
            buffer((local, width, hidden_size), bf16),
            buffer((local, hidden_size, width), bf16),
            buffer((2, 4, rows, width), bf16),
            buffer((8, local, capacity, width), bf16),
            buffer((8, local, capacity, width), bf16),
            buffer((4, local, capacity, width), bf16),
            buffer((8, local, capacity, hidden_size), bf16),
            buffer((8, local, capacity, hidden_size), bf16),
            buffer((8, local, capacity, width), bf16),
            buffer((4, local, capacity, width), bf16),
            buffer((8, local, capacity, width), bf16),
            buffer((4, local, capacity, width), bf16),
            buffer((4, rows, width), bf16),
            buffer((2, 5, rows, width), bf16),
            buffer((4, 8, rows), f32),
            buffer((4, 8, rows), f32),
            buffer((4, 8, rows), f32),
            buffer((local, 2, width, width), bf16),
            buffer((local, width, width), bf16),
            flags((2,)),
            flags((4,)),
            flags((4,)),
            flags((2, 5)),
            flags((2, 4)),
            flags((2, 4, local)),
            flags((2, 4, local)),
            flags((2, 4, local)),
            flags((2, 4, local)),
            flags((2, 5, chunks)),
            flags((2, 5, chunks)),
            flags((4,)),
            flags((4,)),
            flags(()),
            flags((2, chunks)),
            flags((4, chunks)),
            flags((local, 3)),
            flags((local, 3)),
        ],
        compiler_params=pltpu.CompilerParams(
            vmem_limit_bytes=VMEM_LIMIT, collective_id=1, has_side_effects=True
        ),
        name="expert_exchange",
    )(ffn_in, slots, tokens, hidden_one, state_cotan, accum_cotan, columns, vectors, expert_in, expert_out)
    *most, terms, out_final = results
    return *most, (terms, out_final)


def sums_on_links(operands, terms, small_rows, wides):
    rows, width = operands[0].shape
    wide_size = wides[0].shape[1]
    units = terms.shape[0]
    shape, buffer, flags = jax.ShapeDtypeStruct, pltpu.VMEM, pltpu.SemaphoreType.DMA
    parts = [wide_size // 3] * (len(ORDERS) - 1) + [small_rows]
    kinds = [bf16] * (len(ORDERS) - 1) + [f32]
    hops = {"x": 1, "y": 1, "z": 3}
    splits, landings = [], []
    for order, part, kind in zip(ORDERS, parts, kinds):
        split = (2,) + tuple(hops[axis] + 1 for axis in order) + (part // 32, width)
        splits.append((split, kind))
        for stage, size in enumerate((1, *[hops[axis] for axis in order])):
            landings.append(buffer((size,) + split[stage + 1 :], kind))
    tokens_grad, terms_final, *finals = pl.pallas_call(
        functools.partial(backward_and_sums, 128),
        out_shape=[
            shape((rows, width), f32),
            shape((units, width, width), bf16),
            *[shape(*split) for split in splits],
        ],
        in_specs=vmem(22) + hbm(1),
        out_specs=vmem(2 + len(splits)),
        scratch_shapes=[
            *wides,
            buffer((units, 2, width, width), bf16),
            buffer((units, 2, width, width), bf16),
            buffer((units, width, width), bf16),
            *[buffer(*split) for split in splits],
            *landings,
            flags((len(ORDERS), 12)),
            flags((len(ORDERS), 12)),
            flags((units, 2)),
            flags((units, 2, 2)),
            flags((units, 2, 2)),
            flags((units,)),
            flags((units,)),
        ],
        compiler_params=pltpu.CompilerParams(
            vmem_limit_bytes=VMEM_LIMIT, collective_id=2, has_side_effects=True
        ),
        name="backward_and_sums",
    )(*operands, terms)
    return tokens_grad, terms_final, [value.reshape(part, width) for value, part in zip(finals, parts)]


def write_results(edges, *refs):
    thirds, (in_low, out_low, small, lines, new_state_in, accum_in, tokens_in) = refs[:6], refs[6:13]
    output_grad, query_grad, in_grad, out_grad, new_state, accum_part, tokens_grad, *rest = refs[13:]
    width = small.shape[1]
    for index in range(3):
        output_grad[index] = thirds[index][...].astype(f32)
        query_grad[:, index * width : (index + 1) * width] = thirds[3 + index][...].astype(f32)
    in_grad[...] = in_low[...].astype(f32)
    out_grad[...] = out_low[...].astype(f32)
    new_state[...] = new_state_in[...]
    accum_part[...] = accum_in[...]
    tokens_grad[...] = tokens_in[...]
    for ref, start, stop in zip(rest, edges[:-1], edges[1:]):
        ref[...] = small[start:stop, :]
    rest[-2][...] = lines[0:1, :]
    rest[-1][...] = lines[1:2, :]


def results(edges, thirds, in_low, out_low, small, lines, new_state, accum_part, tokens_grad):
    shape, steps = jax.ShapeDtypeStruct, 4
    rows, width = new_state.shape
    units = in_low.shape[0]

    def by_rows(lanes):
        return pl.BlockSpec((width // steps, lanes), lambda i: (i, 0))

    def by_units(count):
        return pl.BlockSpec((count, width // steps, width), lambda i: (0, i, 0))

    def whole(count):
        return pl.BlockSpec((count, width), lambda i: (0, 0))

    def by_tokens():
        return pl.BlockSpec((rows // steps, width), lambda i: (i, 0))

    parts = [stop - start for start, stop in zip(edges[:-1], edges[1:])] + [1, 1]
    return pl.pallas_call(
        functools.partial(write_results, edges),
        grid=(steps,),
        out_shape=[
            shape((3, width, width), f32),
            shape((width, 3 * width), f32),
            shape((units, width, width), f32),
            shape((units, width, width), f32),
            shape((rows, width), bf16),
            shape((rows, width), f32),
            shape((rows, width), f32),
            *[shape((count, width), f32) for count in parts],
        ],
        in_specs=[
            *[by_rows(width) for _ in range(6)], by_units(units), by_units(units), whole(small.shape[0]), whole(lines.shape[0]),
            by_tokens(), by_tokens(), by_tokens(),
        ],
        out_specs=[
            by_units(3), by_rows(3 * width), by_units(units), by_units(units), by_tokens(), by_tokens(),
            by_tokens(), *[whole(count) for count in parts],
        ],
        compiler_params=pltpu.CompilerParams(vmem_limit_bytes=VMEM_LIMIT),
        name="results",
    )(*thirds, in_low, out_low, small, lines, new_state, accum_part, tokens_grad)


def body(
    mesh_sizes, tokens, remain, halting, head_routes, expert_routes, first_gain, first_bias, query_weight,
    key_weight, value_weight, output_weight, head_router, second_gain, second_bias, expert_router, expert_in,
    expert_out, halt_weight, state_cotan, accum_cotan, remain_cotan,
):
    rows, width = tokens.shape
    head_size = key_weight.shape[1]
    top = head_routes.shape[1]
    wide_size = query_weight.shape[1]
    experts = expert_router.shape[1]
    heads = head_router.shape[1]
    capacity = 4 * rows // experts
    shape = jax.ShapeDtypeStruct
    attn_in, query, keys, values, heads_out, spread_out, hidden_one, ffn_in, columns, slots, vectors = pl.pallas_call(
        functools.partial(attend_forward, 128),
        out_shape=[
            shape((rows, width), bf16),
            shape((top, rows, head_size), bf16),
            shape((rows, head_size), bf16),
            shape((rows, head_size), bf16),
            shape((top, rows, head_size), f32),
            shape((rows, wide_size), bf16),
            shape((rows, width), f32),
            shape((rows, width), bf16),
            shape((rows, 128), f32),
            shape((experts // 4, 8, rows), f32),
            shape((8, width), f32),
        ],
        in_specs=vmem(17),
        out_specs=vmem(11),
        scratch_shapes=[pltpu.VMEM((rows, wide_size), f32)],
        compiler_params=pltpu.CompilerParams(vmem_limit_bytes=VMEM_LIMIT),
        name="attend_forward",
    )(
        tokens, head_routes.T, expert_routes.T, remain[None], halting[None], remain_cotan[None], first_gain,
        first_bias, second_gain, second_bias, halt_weight, query_weight, key_weight.T,
        value_weight.T, output_weight, head_router.T, expert_router.T,
    )
    if mesh_sizes == (4, 8):
        stage = experts_on_lines(
            capacity, 4, 2 * top, tokens, columns, vectors, expert_in, expert_out, state_cotan, accum_cotan, hidden_one,
            ffn_in, slots,
        )
    else:
        stage = experts_by_all_to_all(
            capacity, tokens, remain, halting, expert_routes, halt_weight, expert_router, expert_in, expert_out,
            state_cotan, accum_cotan, remain_cotan, hidden_one, ffn_in,
        )
    new_state, accum_part, lines, grad_hidden, grad_rows, grad_logits_t, halt_sum, terms = stage
    operands = (
        tokens, vectors, query_weight, key_weight.T, value_weight.T, output_weight,
        head_router.T, expert_router.T, attn_in, query, keys, values, heads_out, spread_out, hidden_one, ffn_in,
        columns, grad_rows, grad_logits_t, grad_hidden, state_cotan, halt_sum,
    )
    edges = [0, head_size, 2 * head_size, 2 * head_size + heads, 2 * head_size + heads + experts]
    small_rows = 256
    wides = [pltpu.VMEM((rows, wide_size), f32), pltpu.VMEM((rows, wide_size), bf16)]
    if mesh_sizes == (4, 8):
        in_terms, out_final = terms
        tokens_grad, in_final, (*thirds, small) = sums_on_links(operands, in_terms, small_rows, wides)
        (output_grad, query_grad, expert_in_grad, expert_out_grad, new_state, accum_part, tokens_grad, *rest) = results(
            [*edges, *range(edges[-1] + 1, edges[-1] + 6)], thirds, in_final, out_final, small, lines, new_state,
            accum_part, tokens_grad,
        )
        output_grad = output_grad.reshape(wide_size, width)
        key_grad, value_grad, head_router_grad, expert_router_grad = [value.T for value in rest[:4]]
        first_gain_grad, first_bias_grad, second_gain_grad, second_bias_grad, halt_grad, remain_left, remain_grad = [
            value.reshape(width) for value in rest[4:]
        ]
    else:
        in_terms, out_terms = terms
        expert_in_grad = lax.psum_scatter(in_terms, "dp", scatter_dimension=2, tiled=True).astype(f32)
        expert_out_grad = lax.psum_scatter(out_terms, "dp", scatter_dimension=1, tiled=True).astype(f32)
        small_rows = -(-(2 * head_size + heads + experts + 5) // 8) * 8
        tokens_grad, query_sum, output_sum, small_sum = pl.pallas_call(
            functools.partial(attend_backward, 128),
            out_shape=[
                shape((rows, width), f32),
                shape((width, wide_size), f32),
                shape((wide_size, width), f32),
                shape((small_rows, width), f32),
            ],
            in_specs=vmem(22),
            out_specs=vmem(4),
            scratch_shapes=wides,
            compiler_params=pltpu.CompilerParams(vmem_limit_bytes=VMEM_LIMIT),
            name="attend_backward",
        )(*operands)
        query_grad, output_grad, small = lax.psum((query_sum, output_sum, small_sum), ("dp", "expert"))
        key_grad, value_grad, head_router_grad, expert_router_grad = [
            small[start:stop].T for start, stop in zip(edges[:-1], edges[1:])
        ]
        first_gain_grad, first_bias_grad, second_gain_grad, second_bias_grad, halt_grad = [
            small[edges[-1] + index] for index in range(5)
        ]
        remain_left, remain_grad = lines[0], lines[1]
    return (
        new_state, accum_part, remain_left, tokens_grad, remain_grad, first_gain_grad, first_bias_grad, query_grad,
        key_grad, value_grad, output_grad, head_router_grad, second_gain_grad, second_bias_grad,
        expert_router_grad, expert_in_grad, expert_out_grad, halt_grad,
    )


def solution(mesh):
    in_specs = (
        P(("dp", "expert"), None),
        P(("dp", "expert")),
        P(("dp", "expert")),
        P(("dp", "expert"), None),
        P(("dp", "expert"), None),
        P(),
        P(),
        P(),
        P(),
        P(),
        P(),
        P(),
        P(),
        P(),
        P(),
        P("expert", None, None),
        P("expert", None, None),
        P(),
        P(("dp", "expert"), None),
        P(("dp", "expert"), None),
        P(("dp", "expert")),
    )
    out_specs = (
        P(("dp", "expert"), None),
        P(("dp", "expert"), None),
        P(("dp", "expert")),
        P(("dp", "expert"), None),
        P(("dp", "expert")),
        P(),
        P(),
        P(),
        P(),
        P(),
        P(),
        P(),
        P(),
        P(),
        P(),
        P("expert", None, "dp"),
        P("expert", "dp", None),
        P(),
    )
    sizes = (mesh.shape["dp"], mesh.shape["expert"])
    run = functools.partial(body, sizes)
    return jax.shard_map(run, mesh=mesh, in_specs=in_specs, out_specs=out_specs, check_vma=False)
```

```python
import functools
import math

import jax
import jax.numpy as jnp
from jax import lax
from jax.experimental import pallas as pl
from jax.experimental.pallas import tpu as pltpu
from jax.sharding import PartitionSpec as P

epsilon = 1e-05
f32 = jnp.float32
bf16 = jnp.bfloat16
MESH = pl.DeviceIdType.MESH
VMEM_LIMIT = 67043328


def dot_nn(left, right):
    return jnp.dot(left, right, preferred_element_type=f32)


def dot_nt(left, right):
    return lax.dot_general(left, right, (((1,), (1,)), ((), ())), preferred_element_type=f32)


def dot_tn(left, right):
    return lax.dot_general(left, right, (((0,), (0,)), ((), ())), preferred_element_type=f32)


def iota(shape, axis):
    return lax.broadcasted_iota(jnp.int32, shape, axis)


def by_thirds(width, count, work):
    def one(index, carry):
        work(pl.ds(pl.multiple_of(index * width, width), width))
        return carry

    lax.fori_loop(0, count, one, 0)


def norm_rows(values):
    centre = jnp.mean(values, axis=-1, keepdims=True)
    shifted = values - centre
    spread = jnp.mean(shifted * shifted, axis=-1, keepdims=True)
    inverse = lax.rsqrt(spread + epsilon)
    return shifted * inverse, inverse


def norm_back(upstream, normal, inverse, scales):
    scaled = upstream * scales
    inner = (
        scaled
        - jnp.mean(scaled, axis=-1, keepdims=True)
        - normal * jnp.mean(scaled * normal, axis=-1, keepdims=True)
    )
    return inner * inverse


def pick_heads(wide, place, odd, head_size, positions, lines=slice(None)):
    pair = 2 * head_size
    kept = wide[lines, :pair]
    for index in range(1, positions):
        kept = jnp.where(place == index, wide[lines, index * pair : (index + 1) * pair], kept)
    return jnp.where(odd, kept[:, head_size:], kept[:, :head_size])


def place_heads(out_ref, columns, places, odds, head_size, positions, lines=slice(None)):
    pair = 2 * head_size
    rows = columns[0].shape[0]
    upper = iota((rows, pair), 1) >= head_size
    doubled = [
        jnp.where(upper == odd, jnp.concatenate([column, column], axis=1), 0.0)
        for column, odd in zip(columns, odds)
    ]
    for index in range(positions):
        total = jnp.zeros((rows, pair), f32)
        for value, place in zip(doubled, places):
            total = total + jnp.where(place == index, value, 0.0)
        out_ref[lines, index * pair : (index + 1) * pair] = total.astype(bf16)


def lanes_of(columns, width=128):
    rows = columns[0].shape[0]
    lane = iota((rows, width), 1)
    total = jnp.zeros((rows, width), f32)
    for index, column in enumerate(columns):
        total = jnp.where(lane == index, column, total)
    return total


def soft_columns(logits):
    peak = functools.reduce(jnp.maximum, logits)
    raised = [jnp.exp(value - peak) for value in logits]
    whole = functools.reduce(lambda a, b: a + b, raised)
    return [value / whole for value in raised]


def attend_forward(
    block_rows, tokens, head_routes, expert_routes, remain, halting, remain_cotan, first_gain, first_bias,
    second_gain, second_bias, halt_weight, query_weight, key_weight, value_weight, output_weight, head_router,
    expert_router,
    attn_in_out, query_out, key_out, value_out, heads_out, spread_out, hidden_out, ffn_out, columns_out,
    slots_out, vectors, wide,
):
    rows, width = tokens.shape
    head_size = key_weight.shape[0]
    positions = query_weight.shape[1] // (2 * head_size)
    top = head_routes.shape[0]
    experts = expert_router.shape[0]
    for index, vector in enumerate((first_gain, first_bias, second_gain, second_bias, halt_weight)):
        vectors[index : index + 1, :] = vector[...].astype(f32).reshape(1, width)
    vectors[5:8, :] = jnp.zeros((3, width), f32)
    lines = [head_routes[...], expert_routes[...], halting[...]]
    lines = [value.astype(f32) for value in lines] + [remain[...], remain_cotan[...]]
    filled = sum(value.shape[0] for value in lines)
    table = jnp.concatenate(lines + [jnp.zeros((128 - filled, rows), f32)], axis=0).T
    inputs = tokens[...].astype(f32)
    normal, _ = norm_rows(inputs)
    attn_in = (normal * vectors[0:1, :] + vectors[1:2, :]).astype(bf16)
    attn_in_out[...] = attn_in
    wide[...] = dot_nn(attn_in, query_weight[...])
    keys = dot_nt(attn_in, key_weight[...]).astype(bf16)
    key_out[...] = keys
    values = dot_nt(attn_in, value_weight[...]).astype(bf16)
    value_out[...] = values
    head_logits = dot_nt(attn_in, head_router[...])
    routes = table.astype(jnp.int32)
    chosen = [routes[:, a : a + 1] for a in range(top)]
    head_lane = iota(head_logits.shape, 1)
    gates = soft_columns(
        [
            jnp.sum(jnp.where(head_lane == value, head_logits, 0.0), axis=1, keepdims=True)
            for value in chosen
        ]
    )
    columns_out[...] = table

    def pick_lines(index, carry):
        lines = pl.ds(pl.multiple_of(index * block_rows, block_rows), block_rows)
        here = columns_out[lines, :].astype(jnp.int32)
        for a in range(top):
            head = here[:, a : a + 1]
            picked = pick_heads(wide, head // 2, head % 2 == 1, head_size, positions, lines)
            query_out[a, lines, :] = (picked.astype(bf16).astype(f32) * head_size ** (-0.5)).astype(bf16)
        return carry

    lax.fori_loop(0, rows // block_rows, pick_lines, 0)
    totals = [[] for _ in range(top)]
    for start in range(0, rows, block_rows):
        stop = start + block_rows
        query = jnp.concatenate([query_out[a, start:stop, :] for a in range(top)], axis=0)
        scores = dot_nt(query, key_out[0:stop, :])
        row_pos = iota((top * block_rows, block_rows), 0) % block_rows
        corner = jnp.where(
            iota((top * block_rows, block_rows), 1) <= row_pos, scores[:, start:], f32(-1e30)
        )
        if start:
            scores = jnp.concatenate([scores[:, :start], corner], axis=1)
        else:
            scores = corner
        peak = jnp.max(scores, axis=1, keepdims=True)
        raised = jnp.exp(scores - peak)
        whole = jnp.sum(raised, axis=1, keepdims=True)
        output = dot_nn(raised.astype(bf16), value_out[0:stop, :]) / whole
        log_total = peak + jnp.log(whole)
        for a in range(top):
            heads_out[a, start:stop, :] = output[a * block_rows : (a + 1) * block_rows]
            totals[a].append(log_total[a * block_rows : (a + 1) * block_rows])
    totals = [jnp.concatenate(value, axis=0) for value in totals]
    columns_out[...] = lanes_of(
        gates + totals + [table[:, index : index + 1] for index in (top + 3, top + 2, top + 4, *range(top))]
    )

    def place_lines(index, carry):
        lines = pl.ds(pl.multiple_of(index * block_rows, block_rows), block_rows)
        here = columns_out[lines, :]
        heads = [here[:, 2 * top + 3 + a : 2 * top + 4 + a].astype(jnp.int32) for a in range(top)]
        weighted = [
            (here[:, a : a + 1] * heads_out[a, lines, :]).astype(bf16).astype(f32) for a in range(top)
        ]
        place_heads(
            spread_out, weighted, [head // 2 for head in heads], [head % 2 == 1 for head in heads], head_size,
            positions, lines,
        )
        return carry

    lax.fori_loop(0, rows // block_rows, place_lines, 0)
    hidden_one = inputs + dot_nn(spread_out[...], output_weight[...])
    hidden_out[...] = hidden_one
    normal_two, _ = norm_rows(hidden_one)
    ffn_in = (normal_two * vectors[2:3, :] + vectors[3:4, :]).astype(bf16)
    ffn_out[...] = ffn_in
    expert_logits = dot_nt(ffn_in, expert_router[...])
    expert_lane = iota(expert_logits.shape, 1)
    named = [routes[:, top + c : top + c + 1] for c in range(2)]
    expert_gates = soft_columns(
        [
            jnp.sum(jnp.where(expert_lane == value, expert_logits, 0.0), axis=1, keepdims=True)
            for value in named
        ]
    )
    lane = iota((rows, 128), 1)
    expert = jnp.where(lane < 2 * experts, (lane // 8) * 4 + lane % 4, -1)
    first, second = expert == named[0], expert == named[1]
    hot = jnp.where(first | second, 1.0, 0.0)
    earlier = (iota((rows, rows), 1) < iota((rows, rows), 0)).astype(f32).astype(bf16)
    before = dot_nn(earlier, hot.astype(bf16))
    slot = jnp.where(hot > 0.5, before, -1.0)
    gate = jnp.where(first, expert_gates[0], jnp.where(second, expert_gates[1], 0.0))
    turned = jnp.where(lane % 8 < 4, slot, gate).T
    slots_out[...] = turned[: 2 * experts].reshape(experts // 4, 8, rows)


def attention_back(
    block_rows, hooks, tokens, vectors, query_weight, key_weight, value_weight,
    output_weight, head_router, expert_router, attn_in, query, keys, values, heads_out, spread_out, hidden_one,
    ffn_in, columns, grad_rows, grad_logits_t, grad_hidden, state_cotan, halt_sum, tokens_grad, wide, narrow,
):
    take_output, take_query, take_small, pause = hooks
    rows, width = tokens.shape
    head_size = key_weight.shape[0]
    heads = head_router.shape[0]
    positions = query_weight.shape[1] // (2 * head_size)
    top = query.shape[0]
    active_lane = 2 * top + 1
    gain_one, gain_two = vectors[0:1, :], vectors[2:3, :]
    normal_two, inverse_two = norm_rows(hidden_one[...])
    logits_low = grad_logits_t[...].astype(bf16)
    grad_ffn = grad_rows[...] + dot_tn(logits_low, expert_router[...])
    router_two = dot_nn(logits_low, ffn_in[...])
    gain_two_sum = jnp.sum(grad_ffn * normal_two, axis=0, keepdims=True)
    bias_two_sum = jnp.sum(grad_ffn, axis=0, keepdims=True)
    grad_one = grad_hidden[...] + norm_back(grad_ffn, normal_two, inverse_two, gain_two)
    tokens_grad[...] = grad_one
    grad_attn = grad_one.astype(bf16)
    take_output(lambda part: dot_tn(spread_out[:, part], grad_attn))
    pause(0)
    wide[...] = dot_nt(grad_attn, output_weight[...])
    routes = columns[...].astype(jnp.int32)
    chosen = [routes[:, 2 * top + 3 + a : 2 * top + 4 + a] for a in range(top)]
    places = [value // 2 for value in chosen]
    odds = [value % 2 == 1 for value in chosen]
    gates = [columns[:, a : a + 1] for a in range(top)]
    pause(1)
    grad_gates, grad_heads = [], []
    for a in range(top):
        picked = pick_heads(wide, places[a], odds[a], head_size, positions)
        grad_gates.append(jnp.sum(picked * heads_out[a], axis=1, keepdims=True))
        grad_heads.append((gates[a] * picked).astype(bf16))
    inner = functools.reduce(lambda a, b: a + b, [g * d for g, d in zip(gates, grad_gates)])
    grad_logit = [g * (d - inner) for g, d in zip(gates, grad_gates)]
    head_lane = iota((rows, heads), 1)
    grad_hot = functools.reduce(
        lambda a, b: a + b,
        [jnp.where(head_lane == chosen[a], grad_logit[a], 0.0) for a in range(top)],
    )
    pause(2)
    grad_keys = [jnp.zeros((block_rows, head_size), f32) for _ in range(rows // block_rows)]
    grad_values = [jnp.zeros((block_rows, head_size), f32) for _ in range(rows // block_rows)]
    grad_query = [[] for _ in range(top)]
    for start in range(0, rows, block_rows):
        stop = start + block_rows
        part = slice(start, stop)
        queries = jnp.concatenate([query[a, part, :] for a in range(top)], axis=0)
        grads = jnp.concatenate([value[part] for value in grad_heads], axis=0)
        total = jnp.concatenate([columns[part, top + a : top + a + 1] for a in range(top)], axis=0)
        scores = dot_nt(queries, keys[0:stop, :])
        row_pos = iota((top * block_rows, block_rows), 0) % block_rows
        corner = jnp.where(
            iota((top * block_rows, block_rows), 1) <= row_pos, scores[:, start:], f32(-1e30)
        )
        if start:
            scores = jnp.concatenate([scores[:, :start], corner], axis=1)
        else:
            scores = corner
        prob = jnp.exp(scores - total)
        grad_prob = dot_nt(grads, values[0:stop, :])
        row_inner = jnp.sum(prob * grad_prob, axis=1, keepdims=True)
        grad_scores = (prob * (grad_prob - row_inner)).astype(bf16)
        grad_q = (dot_nn(grad_scores, keys[0:stop, :]) * head_size ** (-0.5)).astype(bf16)
        for a in range(top):
            grad_query[a].append(grad_q[a * block_rows : (a + 1) * block_rows].astype(f32))
        step_v = dot_tn(prob.astype(bf16), grads)
        step_k = dot_tn(grad_scores, queries)
        for index in range(stop // block_rows):
            piece = slice(index * block_rows, (index + 1) * block_rows)
            grad_values[index] = grad_values[index] + step_v[piece]
            grad_keys[index] = grad_keys[index] + step_k[piece]
        pause(3 + min(start // block_rows, 3))
    grad_query = [jnp.concatenate(value, axis=0) for value in grad_query]
    place_heads(narrow, grad_query, places, odds, head_size, positions)
    take_query(lambda part: dot_tn(attn_in[...], narrow[:, part]), pause)
    grad_k = jnp.concatenate(grad_keys, axis=0).astype(bf16)
    grad_v = jnp.concatenate(grad_values, axis=0).astype(bf16)
    hot_low = grad_hot.astype(bf16)
    grad_in = (
        dot_nt(narrow[...], query_weight[...])
        + dot_nn(grad_k, key_weight[...])
        + dot_nn(grad_v, value_weight[...])
        + dot_nn(hot_low, head_router[...])
    )
    pause(10)
    normal_one, inverse_one = norm_rows(tokens[...].astype(f32))
    take_small(
        [
            dot_tn(grad_k, attn_in[...]),
            dot_tn(grad_v, attn_in[...]),
            dot_tn(hot_low, attn_in[...]),
            router_two,
            jnp.sum(grad_in * normal_one, axis=0, keepdims=True),
            jnp.sum(grad_in, axis=0, keepdims=True),
            gain_two_sum,
            bias_two_sum,
            halt_sum[0:1, :],
        ]
    )
    tokens_grad[...] = (
        tokens_grad[...]
        + norm_back(grad_in, normal_one, inverse_one, gain_one)
        + (1.0 - columns[:, active_lane : active_lane + 1]) * state_cotan[...].astype(f32)
    )


def stack_small(pieces, room):
    count = sum(piece.shape[0] for piece in pieces)
    width = pieces[0].shape[1]
    return jnp.concatenate(pieces + [jnp.zeros((room - count, width), f32)], axis=0)


def attend_backward(block_rows, *refs):
    inputs, (tokens_grad, query_sum, output_sum, small_sum, wide, narrow) = refs[:22], refs[22:]

    def take_output(term):
        output_sum[...] = term(slice(None))

    def take_query(term, pause):
        query_sum[...] = term(slice(None))

    def take_small(pieces):
        small_sum[...] = stack_small(pieces, small_sum.shape[0])

    hooks = take_output, take_query, take_small, lambda point: None
    attention_back(block_rows, hooks, *inputs, tokens_grad, wide, narrow)


class SumOverAll:
    def __init__(self, number, peers, send, recv, full, final, lands):
        self.number, self.peers, self.send, self.recv = number, peers, send, recv
        self.full, self.final, self.lands = full, final, lands
        self.copies = [[] for _ in range(8)]

    def go(self, stage, source, target, device):
        index = sum(len(copies) for copies in self.copies)
        copy = pltpu.make_async_remote_copy(
            src_ref=source, dst_ref=target, send_sem=self.send.at[self.number, index],
            recv_sem=self.recv.at[self.number, index], device_id=device, device_id_type=MESH,
        )
        copy.start()
        self.copies[stage].append(copy)

    def total(self, lead, landed):
        total = self.full[lead].astype(f32)
        for value in landed:
            total = total + value[...].astype(f32)
        return total

    def step(self, stage):
        full, final = self.full, self.final
        own = tuple(place for place, _ in self.peers)
        if stage:
            for copy in self.copies[stage - 1]:
                copy.wait_recv()
        if stage < 4:
            lead, (place, others) = own[:stage], self.peers[stage]
            arrived = self.lands[stage - 1] if stage else None

            def add(index):
                spot = lead + (index,)
                if 0 < stage < 3:

                    def one(row, carry):
                        landed = [arrived.at[hop, index, row] for hop in range(arrived.shape[0])]
                        full[spot + (row,)] = self.total(spot + (row,), landed).astype(full.dtype)
                        return carry

                    lax.fori_loop(0, full.shape[stage + 1], one, 0)
                elif stage == 3:
                    landed = [arrived.at[hop, index] for hop in range(arrived.shape[0])]
                    full[spot] = self.total(spot, landed).astype(full.dtype)

            for hop, (index, device) in enumerate(others):
                add(index)
                self.go(stage, full.at[lead + (index,)], self.lands[stage].at[hop], device)
            add(place)
        elif stage < 8:
            if stage == 4:
                arrived = self.lands[3]
                final[own] = self.total(own, [arrived.at[hop] for hop in range(arrived.shape[0])]).astype(final.dtype)
            lead = own[: 8 - stage]
            for _, device in self.peers[7 - stage][1]:
                self.go(stage, final.at[lead], final.at[lead], device)
        else:
            for copies in self.copies:
                for copy in copies:
                    copy.wait_send()


POINTS = (2.5, 3.5, 5.0, 6.0, 7.5, 9.5, 12.0, 13.0, 14.0, 15.0, 16.0, 17.5)
OUTPUT_POINT, QUERY_POINTS, SMALL_POINT = 0, (7, 8, 9), 11
DELAYS = {"core": 1.0, "x": 1.7, "z": 2.4, "y": 1.7}
RATES = {"core": 600.0, "x": 48.0, "z": 50.0, "y": 46.0}
ORDERS = ("xzy", "yxz", "yxz", "zxy", "yxz", "yxz", "xyz")


def ways_of(order, piece_bytes):
    left, ways = piece_bytes / 2, [("core", piece_bytes / 2)]
    for axis in order:
        ways.append((axis, left if axis == "z" else left / 2))
        left = left / 4 if axis == "z" else left / 2
    return ways + ways[::-1]


def plan_steps(piece_bytes, orders, far_chunks, chunk_bytes):
    ways = [ways_of(order, piece_bytes) for order in orders]
    free = dict.fromkeys(RATES, 0.0)
    ready, plan, done = [], [[] for _ in POINTS], 0

    def send(way, size, now):
        free[way] = max(free[way], now) + size / RATES[way] / 1000
        return free[way] + DELAYS[way]

    far_ready = [send("core", chunk_bytes, 0.5) for _ in range(far_chunks)]
    sent_far = 0

    def begin(item, now):
        ready.append((send(*ways[item][0], now), item, 1))

    now = 0.0
    for point, time in enumerate(POINTS):
        now = max(now, time)
        last = point == len(POINTS) - 1
        if point == OUTPUT_POINT:
            for item in range(3):
                begin(item, now)
        if point in QUERY_POINTS:
            begin(3 + QUERY_POINTS.index(point), now)
        if point == SMALL_POINT:
            begin(6, now)
        while True:
            ready.sort()
            if sent_far < far_chunks and far_ready[sent_far] <= now and free["y"] <= now + 1.0:
                plan[point].append((-1, sent_far))
                now += 0.2
                send("y", chunk_bytes, now)
                sent_far += 1
                continue
            if ready and (last or ready[0][0] <= now):
                if last and sent_far < far_chunks and max(free["y"] - 1.0, far_ready[sent_far]) < ready[0][0]:
                    now = max(now, free["y"] - 1.0, far_ready[sent_far])
                    continue
                time, item, stage = ready.pop(0)
                now = max(now, time) + (0.3 if stage == 1 else 0.15)
                plan[point].append((item, stage))
                if stage < 8:
                    ready.append((send(*ways[item][stage], now), item, stage + 1))
                continue
            if last and sent_far < far_chunks:
                now = max(now, free["y"] - 1.0, far_ready[sent_far])
                continue
            break
    return plan, now


def backward_and_sums(block_rows, *refs):
    inputs, terms = refs[:22], refs[22]
    count = len(ORDERS)
    tokens_grad, terms_final, finals = refs[23], refs[24], refs[25 : 25 + count]
    wide, narrow, own_terms, near_terms, far_terms = refs[25 + count : 30 + count]
    fulls, lands = refs[30 + count : 30 + 2 * count], refs[30 + 2 * count : 30 + 6 * count]
    send, recv, load_sem, term_send, term_recv, near_send, near_recv = refs[30 + 6 * count :]
    units, width = terms.shape[0], terms.shape[3]
    line, group = lax.axis_index("expert"), lax.axis_index("dp")
    z, x, y, c = line // 2, line % 2, group // 2, group % 2
    to_core, to_y = {"dp": y * 2 + 1 - c}, {"dp": (1 - y) * 2 + c}
    to_x = {"expert": z * 2 + 1 - x}

    def to_z(hop):
        return {"expert": (z + hop) % 4 * 2 + x}

    barrier = pltpu.get_barrier_semaphore()
    for device in (to_core, to_x, to_y, to_z(1), to_z(2), to_z(3)):
        pl.semaphore_signal(barrier, inc=1, device_id=device, device_id_type=MESH)
    far, near = (1 - y) * 2 + c, y * 2 + c
    loads = [
        [
            pltpu.make_async_copy(terms.at[u, quarter], own_terms.at[u, side], load_sem.at[u, side])
            for side, quarter in enumerate((far, near))
        ]
        for u in range(units)
    ]
    for side in range(2):
        for u in range(units):
            loads[u][side].start()
    pl.semaphore_wait(barrier, 6)

    split_rows = width // 2

    def term_copy(u, half, stage):
        rows = pl.ds(half * split_rows, split_rows)
        if stage == 0:
            source = terms.at[u, (1 - y) * 2 + 1 - c, rows]
            target, device = near_terms.at[u, 0, rows], to_core
        else:
            source, target, device = own_terms.at[u, 0, rows], far_terms.at[u, rows], to_y
        return pltpu.make_async_remote_copy(
            src_ref=source, dst_ref=target, send_sem=term_send.at[u, half, stage],
            recv_sem=term_recv.at[u, half, stage], device_id=device, device_id_type=MESH,
        )

    def near_copy(u):
        return pltpu.make_async_remote_copy(
            src_ref=terms.at[u, y * 2 + 1 - c], dst_ref=near_terms.at[u, 1], send_sem=near_send.at[u],
            recv_sem=near_recv.at[u], device_id=to_core, device_id_type=MESH,
        )

    for chunk in range(2 * units):
        term_copy(chunk // 2, chunk % 2, 0).start()

    def send_far(chunk):
        u, half = chunk // 2, chunk % 2
        if half == 0:
            loads[u][0].wait()
        term_copy(u, half, 0).wait_recv()
        rows = pl.ds(half * split_rows, split_rows)
        total = own_terms[u, 0, rows].astype(f32) + near_terms[u, 0, rows].astype(f32)
        own_terms[u, 0, rows] = total.astype(bf16)
        term_copy(u, half, 1).start()

    def finish_near(u):
        loads[u][1].wait()
        near_copy(u).wait_recv()
        for half in range(2):
            term_copy(u, half, 1).wait_recv()
        total = own_terms[u, 1].astype(f32) + near_terms[u, 1].astype(f32) + far_terms[u].astype(f32)
        terms_final[u] = total.astype(bf16)
        near_copy(u).wait_send()
        for half in range(2):
            term_copy(u, half, 0).wait_send()
            term_copy(u, half, 1).wait_send()

    axes = {
        "x": (x, [(1 - x, to_x)]),
        "y": (y, [(1 - y, to_y)]),
        "z": (z, [((z + hop) % 4, to_z(hop)) for hop in (2, 1, 3)]),
    }
    items = [
        SumOverAll(
            index, [(c, [(1 - c, to_core)])] + [axes[axis] for axis in order], send, recv, fulls[index],
            finals[index], lands[4 * index : 4 * index + 4],
        )
        for index, order in enumerate(ORDERS)
    ]
    small_full = fulls[-1]
    third = math.prod(fulls[0].shape[:-1])
    block_bytes = math.prod(small_full.shape) * 4
    plan, _ = plan_steps(block_bytes, ORDERS, 2 * units, split_rows * width * 2)

    def take(index, term):
        part = index % 3
        value = term(slice(part * third, (part + 1) * third))
        fulls[index][...] = value.astype(bf16).reshape(fulls[index].shape)
        items[index].step(0)

    def take_output(term):
        for part in range(3):
            take(part, term)

    def take_query(term, pause):
        for part in range(3):
            take(3 + part, term)
            pause(QUERY_POINTS[part])

    def take_small(pieces):
        rows = math.prod(small_full.shape[:-1])
        small_full[...] = stack_small(pieces, rows).reshape(small_full.shape)
        items[6].step(0)

    def pause(point):
        for item, stage in plan[point]:
            if item < 0:
                send_far(stage)
            else:
                items[item].step(stage)

    attention_back(block_rows, (take_output, take_query, take_small, pause), *inputs, tokens_grad, wide, narrow)
    for u in range(units):
        near_copy(u).start()
    pause(SMALL_POINT)
    for u in range(units):
        finish_near(u)


def expert_exchange(
    capacity, chunks, lane,
    ffn_in, slots, tokens, hidden_one, state_cotan, accum_cotan, columns, vectors, first_hbm, second_hbm,
    new_state, accum_part, lines_out, grad_hidden, grad_rows, grad_logits_t, halt_sum, terms, out_final,
    first, second, column, gathered, grads_in, cross, act, slope, produced, crossed, grad_out, grad_crossed,
    partial, landed, keys, shares, share_out, out_core, out_y,
    weight_sem, key_send, key_recv, gather_send, gather_recv, cross_send, cross_recv, back_send, back_recv,
    reduce_send, reduce_recv, share_send, share_recv, stage_sem, own_send, own_recv, out_send, out_recv,
):
    rows, width = ffn_in.shape
    local, _, hidden_size = first.shape
    tile = width
    tiles = hidden_size // tile
    piece = rows // chunks
    me = lax.axis_index("expert")
    z, x = me // 2, me % 2
    other = 1 - x
    low = z < 2
    middle = (z == 1) | (z == 2)
    edge = jnp.logical_not(middle)

    def real(mirrored):
        return jnp.where(low, mirrored, 3 - mirrored)

    def along(depth):
        return {"expert": depth * 2 + x}

    across = {"expert": z * 2 + other}
    group = lax.axis_index("dp")
    y, c = group // 2, group % 2
    to_core, to_y = {"dp": y * 2 + 1 - c}, {"dp": (1 - y) * 2 + c}

    def order(j):
        return real(jnp.where(middle, jnp.where(j < 2, 1 - j, j), j))

    barrier = pltpu.get_barrier_semaphore()
    for step in range(1, 4):
        pl.semaphore_signal(barrier, inc=1, device_id=along((z + step) % 4), device_id_type=MESH)
    for device in (across, to_core, to_y):
        pl.semaphore_signal(barrier, inc=1, device_id=device, device_id_type=MESH)
    loads = [
        pltpu.make_async_copy(first_hbm, first, weight_sem.at[0]),
        pltpu.make_async_copy(second_hbm, second, weight_sem.at[1]),
    ]
    for load in loads:
        load.start()
    column[0, z] = ffn_in[...]
    keys[z] = slots[z]
    pl.semaphore_wait(barrier, 6)

    def key_copy(step):
        there = (z + step) % 4
        return pltpu.make_async_remote_copy(
            src_ref=slots.at[there], dst_ref=keys.at[z], send_sem=key_send.at[step], recv_sem=key_recv.at[z],
            device_id=along(there), device_id_type=MESH,
        )

    def key_arrival(shard):
        return pltpu.make_async_remote_copy(
            src_ref=slots.at[0], dst_ref=keys.at[shard], send_sem=key_send.at[0], recv_sem=key_recv.at[shard],
            device_id=across, device_id_type=MESH,
        )

    def gather_copy(phase, source, shard, depth, index):
        return pltpu.make_async_remote_copy(
            src_ref=source, dst_ref=column.at[phase, shard], send_sem=gather_send.at[phase, index],
            recv_sem=gather_recv.at[phase, shard], device_id=along(depth), device_id_type=MESH,
        )

    def send_own():
        @pl.when(edge)
        def _():
            gather_copy(0, ffn_in, z, real(1), 0).start()

        @pl.when(middle)
        def _():
            gather_copy(0, ffn_in, z, real(0), 0).start()
            gather_copy(0, ffn_in, z, real(2), 1).start()

    def chunk_copy(shard, chunk, depth, index):
        part = pl.ds(pl.multiple_of(chunk * piece, piece), piece)
        return pltpu.make_async_remote_copy(
            src_ref=column.at[1, shard, part], dst_ref=column.at[1, shard, part],
            send_sem=own_send.at[index, chunk], recv_sem=own_recv.at[shard, chunk], device_id=along(depth),
            device_id_type=MESH,
        )

    def send_chunk(chunk):
        @pl.when(edge)
        def _():
            chunk_copy(z, chunk, real(1), 0).start()

        @pl.when(middle)
        def _():
            chunk_copy(z, chunk, real(0), 0).start()
            chunk_copy(z, chunk, real(2), 1).start()

    def forward(phase, mirrored, target, index):
        shard = real(mirrored)
        return gather_copy(phase, column.at[phase, shard], shard, real(target), index)

    def finish_gather(phase):
        if phase == 0:
            gather_copy(0, ffn_in, z, real(1), 0).wait_send()
        else:
            for chunk in range(chunks):
                chunk_copy(z, chunk, real(1), 0).wait_send()

        @pl.when(middle)
        def _():
            if phase == 0:
                gather_copy(0, ffn_in, z, real(2), 1).wait_send()
            else:
                for chunk in range(chunks):
                    chunk_copy(z, chunk, real(2), 1).wait_send()
            forward(phase, 0, 2, 2).wait_send()
            forward(phase, 2, 0, 3).wait_send()
            forward(phase, 3, 0, 4).wait_send()

    def await_shard(phase, mirrored, next_to):
        shard = real(mirrored)
        if phase == 0:
            key_arrival(shard).wait_recv()
        if phase == 1 and next_to:
            for chunk in range(chunks):
                chunk_copy(shard, chunk, z, 0).wait_recv()
        else:
            gather_copy(phase, column.at[phase, shard], shard, z, 0).wait_recv()

    def await_shards(phase, j):
        @pl.when(edge & (j == 1))
        def _():
            await_shard(phase, 1, True)

        @pl.when(edge & (j > 1))
        def _():
            await_shard(phase, j, False)

        @pl.when(middle & (j == 1))
        def _():
            await_shard(phase, 0, True)
            forward(phase, 0, 2, 2).start()
            await_shard(phase, 2, True)
            forward(phase, 2, 0, 3).start()

        @pl.when(middle & (j == 2))
        def _():
            await_shard(phase, 3, False)
            forward(phase, 3, 0, 4).start()

    def experts_of(shard):
        table = keys[shard]
        found = []
        for own in (True, False):
            for r in range(local):
                here, there = (r, local + r) if own else (local + r, r)
                line = jnp.where(x == 0, table[here : here + 1], table[there : there + 1])
                gate = jnp.where(x == 0, table[4 + here : 5 + here], table[4 + there : 5 + there])
                mask = iota((capacity, rows), 0).astype(f32) == line
                found.append((mask, jnp.sum(jnp.where(mask, gate, 0.0), axis=1, keepdims=True)))
        return found

    def hot_rows(found):
        return jnp.concatenate([jnp.where(mask, 1.0, 0.0).astype(bf16) for mask, _ in found], axis=0)

    def cross_copy(phase, shard, r):
        target = gathered if phase == 0 else grads_in
        return pltpu.make_async_remote_copy(
            src_ref=cross.at[shard, r], dst_ref=target.at[4 + shard, r], send_sem=cross_send.at[phase, shard, r],
            recv_sem=cross_recv.at[phase, shard, r], device_id=across, device_id_type=MESH,
        )

    def back_copy(phase, shard, r):
        source, target = (produced, crossed) if phase == 0 else (grad_out, grad_crossed)
        return pltpu.make_async_remote_copy(
            src_ref=source.at[4 + shard, r], dst_ref=target.at[shard, r], send_sem=back_send.at[phase, shard, r],
            recv_sem=back_recv.at[phase, shard, r], device_id=across, device_id_type=MESH,
        )

    def share_copy(shard):
        return pltpu.make_async_remote_copy(
            src_ref=share_out.at[shard], dst_ref=shares.at[z], send_sem=share_send.at[shard],
            recv_sem=share_recv.at[z], device_id=along(shard), device_id_type=MESH,
        )

    def dispatch(phase, shard):
        found = experts_of(shard)
        taken = dot_nn(hot_rows(found), column[phase, shard])
        lines = []
        for index, (mask, gate) in enumerate(found):
            part = taken[index * capacity : (index + 1) * capacity]
            if phase == 1:
                part = gate * part
            r = index % local
            if index < local:
                (gathered if phase == 0 else grads_in)[shard, r] = part.astype(bf16)
            else:
                cross[shard, r] = part.astype(bf16)
                cross_copy(phase, shard, r).start()
            if phase == 1:
                value = (produced if index < local else crossed)[shard, r].astype(f32)
                inner = jnp.sum(part * value, axis=1, keepdims=True)
                lines.append(jnp.sum(jnp.where(mask, inner, 0.0), axis=0, keepdims=True))
        if phase == 1:
            own, far = lines[:local], lines[local:]
            stack = [jnp.where(x == 0, a, b) for a, b in zip(own + far, far + own)]
            share_out[shard] = jnp.concatenate(stack + [jnp.zeros((4, rows), f32)], axis=0)

            @pl.when(shard == z)
            def _():
                shares[z] = share_out[z]

            @pl.when(shard != z)
            def _():
                share_copy(shard).start()

    def expert_forward(shard):
        def one(r, carry):
            cross_copy(0, shard, r).wait_recv()
            taken = jnp.concatenate([gathered[shard, r], gathered[4 + shard, r]], axis=0)
            total = jnp.zeros((2 * capacity, width), f32)
            for n in range(tiles):
                part = slice(n * tile, (n + 1) * tile)
                pre = dot_nn(taken, first[r, :, part])
                cumulative = 0.5 * (1.0 + lax.erf(pre * (1.0 / math.sqrt(2.0))))
                density = jnp.exp(-0.5 * pre * pre) * (1.0 / math.sqrt(2.0 * math.pi))
                inner = (pre * cumulative).astype(bf16)
                steep = (cumulative + pre * density).astype(bf16)
                act[shard, r, :, part] = inner[:capacity]
                act[4 + shard, r, :, part] = inner[capacity:]
                slope[shard, r, :, part] = steep[:capacity]
                slope[4 + shard, r, :, part] = steep[capacity:]
                total = total + dot_nn(inner, second[r, part, :])
            produced[shard, r] = total[:capacity].astype(bf16)
            produced[4 + shard, r] = total[capacity:].astype(bf16)
            back_copy(0, shard, r).start()
            return carry

        lax.fori_loop(0, local, one, 0)

    def expert_backward(shard):
        def one(r, carry):
            cross_copy(1, shard, r).wait_recv()
            taken = jnp.concatenate([grads_in[shard, r], grads_in[4 + shard, r]], axis=0)
            total = jnp.zeros((2 * capacity, width), f32)
            for n in range(tiles):
                part = slice(n * tile, (n + 1) * tile)
                grad = dot_nt(taken, second[r, part, :])
                steep = jnp.concatenate([slope[shard, r, :, part], slope[4 + shard, r, :, part]], axis=0)
                grad_pre = (grad * steep.astype(f32)).astype(bf16)
                slope[shard, r, :, part] = grad_pre[:capacity]
                slope[4 + shard, r, :, part] = grad_pre[capacity:]
                total = total + dot_nt(grad_pre, first[r, :, part])
            grad_out[shard, r] = total[:capacity].astype(bf16)
            grad_out[4 + shard, r] = total[capacity:].astype(bf16)
            back_copy(1, shard, r).start()
            return carry

        lax.fori_loop(0, local, one, 0)

    def reduce_copy(phase, shard, index, chunk, depth):
        part = pl.ds(pl.multiple_of(chunk * piece, piece), piece)
        return pltpu.make_async_remote_copy(
            src_ref=partial.at[shard, part], dst_ref=landed.at[phase, index, part],
            send_sem=reduce_send.at[phase, index, chunk], recv_sem=reduce_recv.at[phase, index, chunk],
            device_id=along(depth), device_id_type=MESH,
        )

    def combine(phase, j):
        shard = order(j)
        for r in range(local):
            back_copy(phase, shard, r).wait_recv()
        found = experts_of(shard)
        if phase == 0:
            pieces = [
                gate * (produced if index < local else crossed)[shard, index % local].astype(f32)
                for index, (_, gate) in enumerate(found)
            ]
            pieces = [value.astype(bf16) for value in pieces]
        else:
            pieces = [
                (grad_out if index < local else grad_crossed)[shard, index % local]
                for index in range(2 * local)
            ]
        partial[shard] = dot_tn(hot_rows(found), jnp.concatenate(pieces, axis=0)).astype(bf16)

        @pl.when(edge & (j > 0))
        def _():
            for chunk in range(chunks):
                reduce_copy(phase, shard, j - 1, chunk, real(1)).start()

    def pass_on(phase, chunk, source, mirrored, index, depth):
        shard = real(mirrored)
        reduce_copy(phase, shard, source, chunk, z).wait_recv()
        part = pl.ds(pl.multiple_of(chunk * piece, piece), piece)
        partial[shard, part] = (
            partial[shard, part].astype(f32) + landed[phase, source, part].astype(f32)
        ).astype(bf16)
        reduce_copy(phase, shard, index, chunk, depth).start()

    def reduce_rows(phase, filler):
        def step(i, carry):
            @pl.when(middle & (i < chunks))
            def _():
                pass_on(phase, i, 1, 2, 3, real(2))

            @pl.when(middle & (i >= chunks))
            def _():
                pass_on(phase, i - chunks, 2, 3, 4, real(2))
                pass_on(phase, i - chunks, 4, 0, 0, real(0))

            filler(i)
            return carry

        lax.fori_loop(0, 2 * chunks, step, 0)

    def reduced_chunk(phase, chunk):
        reduce_copy(phase, z, 0, chunk, z).wait_recv()

        @pl.when(middle)
        def _():
            reduce_copy(phase, z, 3, chunk, z).wait_recv()

        part = pl.ds(pl.multiple_of(chunk * piece, piece), piece)
        total = partial[z, part].astype(f32) + landed[phase, 0, part].astype(f32)
        return total + jnp.where(middle, landed[phase, 3, part].astype(f32), 0.0)

    def reduced(phase):
        return jnp.concatenate([reduced_chunk(phase, chunk) for chunk in range(chunks)], axis=0)

    def finish_reduce(phase):
        @pl.when(edge)
        def _():
            for index in range(3):
                for chunk in range(chunks):
                    reduce_copy(phase, real(index + 1), index, chunk, real(1)).wait_send()

        @pl.when(middle)
        def _():
            for chunk in range(chunks):
                reduce_copy(phase, real(2), 3, chunk, real(2)).wait_send()
                reduce_copy(phase, real(3), 4, chunk, real(2)).wait_send()
                reduce_copy(phase, real(0), 0, chunk, real(0)).wait_send()

    def finish_cross(phase):
        for shard in range(4):
            for r in range(local):
                cross_copy(phase, shard, r).wait_send()
                back_copy(phase, shard, r).wait_send()

    out_terms = [column.at[0], landed.at[0]]

    def out_copy(r, stage):
        source, target, device = (
            (out_terms[r].at[0], out_core.at[r, 0], to_core),
            (out_terms[r].at[2], out_core.at[r, 1], to_core),
            (out_terms[r].at[1], out_y.at[r], to_y),
        )[stage]
        return pltpu.make_async_remote_copy(
            src_ref=source, dst_ref=target, send_sem=out_send.at[r, stage], recv_sem=out_recv.at[r, stage],
            device_id=device, device_id_type=MESH,
        )

    def make_out_terms():
        total = local * 4 * capacity

        def one(index, carry):
            k, r = index // local, index % local
            quarter = jnp.where(k < 2, 1 - y, y) * 2 + jnp.where(k % 2 == 0, 1 - c, c)
            part = pl.ds(pl.multiple_of(quarter * tile, tile), tile)
            left = act[:, r, :, part].reshape(total, tile)
            right = grads_in[:, r].reshape(total, width)
            value = dot_tn(left, right).astype(bf16)
            for here in range(local):

                @pl.when(r == here)
                def _():
                    out_terms[here][k] = value

                for stage in range(2):

                    @pl.when((r == here) & (k == 2 * stage))
                    def _():
                        out_copy(here, stage).start()

            return carry

        lax.fori_loop(0, 4 * local, one, 0)

    def send_out_terms():
        for r in range(local):
            out_copy(r, 0).wait_recv()
            out_terms[r][1] = (out_terms[r][1].astype(f32) + out_core[r, 0].astype(f32)).astype(bf16)
            out_copy(r, 2).start()

    def finish_out_terms():
        for r in range(local):
            out_copy(r, 1).wait_recv()
            out_copy(r, 2).wait_recv()
            total = out_terms[r][3].astype(f32) + out_core[r, 1].astype(f32) + out_y[r].astype(f32)
            out_final[r] = total.astype(bf16)
            for stage in range(3):
                out_copy(r, stage).wait_send()

    def run(phase, experts):
        def step(j, carry):
            if phase == 1:

                @pl.when(j == 5)
                def _():
                    make_out_terms()

            @pl.when(j >= 2)
            def _():
                combine(phase, j - 2)

            @pl.when((j >= 1) & (j <= 4))
            def _():
                experts(order(j - 1))

            @pl.when(j <= 3)
            def _():
                await_shards(phase, j)
                dispatch(phase, order(j))

            return carry

        lax.fori_loop(0, 6, step, 0)

    for step in range(1, 4):
        key_copy(step).start()
    send_own()
    for load in loads:
        load.wait()
    run(0, expert_forward)
    reduce_rows(0, lambda i: None)
    halt_vector = vectors[4:5, :]
    halt_sum[...] = jnp.zeros((8, width), f32)

    def halt(chunk, carry):
        part = pl.ds(pl.multiple_of(chunk * piece, piece), piece)
        hidden = hidden_one[part, :] + reduced_chunk(0, chunk)
        remain, active, remain_cotan = [columns[part, lane + index : lane + index + 1] for index in range(3)]
        halt_prob = jax.nn.sigmoid(jnp.sum(hidden * halt_vector, axis=1, keepdims=True))
        halt_share = active * remain * halt_prob
        grad_accum = accum_cotan[part, :].astype(f32)
        grad_share = jnp.sum(grad_accum * hidden, axis=1, keepdims=True)
        grad_logit = active * remain * (grad_share - remain_cotan) * halt_prob * (1.0 - halt_prob)
        grad_here = active * state_cotan[part, :].astype(f32) + halt_share * grad_accum + grad_logit * halt_vector
        column[1, z, part, :] = grad_here.astype(bf16)
        send_chunk(chunk)
        grad_hidden[part, :] = grad_here
        new_state[part, :] = jnp.where(active > 0.5, hidden, tokens[part, :].astype(f32)).astype(bf16)
        accum_part[part, :] = halt_share * hidden
        pair = lanes_of(
            [
                remain * (1.0 - active * halt_prob),
                active * halt_prob * grad_share + (1.0 - active * halt_prob) * remain_cotan,
            ]
        )
        lines_out[:, part] = pair.T[:8]
        halt_sum[0:1, :] = halt_sum[0:1, :] + jnp.sum(grad_logit * hidden, axis=0, keepdims=True)
        return carry

    lax.fori_loop(0, chunks, halt, 0)
    for step in range(1, 4):
        key_copy(step).wait_send()
    finish_gather(0)
    finish_cross(0)
    finish_reduce(0)
    run(1, expert_backward)

    def stage(r, n):
        return pltpu.make_async_copy(landed.at[0, 4], terms.at[r, n], stage_sem)

    def weight_terms(i):
        r, n = i // tiles, i % tiles
        part = pl.ds(pl.multiple_of(n * tile, tile), tile)
        total = local * 4 * capacity

        @pl.when(i > 0)
        def _():
            stage(0, 0).wait()

        left = gathered[:, r].reshape(total, width)
        right = slope[:, r, :, part].reshape(total, tile)
        landed[0, 4] = dot_tn(left, right).astype(bf16)
        stage(r, n).start()

    send_out_terms()
    reduce_rows(1, weight_terms)
    stage(0, 0).wait()
    for step in range(1, 4):
        shard = (z + step) % 4
        pltpu.make_async_remote_copy(
            src_ref=share_out.at[0], dst_ref=shares.at[shard], send_sem=share_send.at[0],
            recv_sem=share_recv.at[shard], device_id=across, device_id_type=MESH,
        ).wait_recv()
        share_copy(shard).wait_send()
    share = jnp.concatenate([shares[s, 0:4] for s in range(4)], axis=0)
    gate = jnp.concatenate([slots[s, 4:8] for s in range(4)], axis=0)
    grad_logits_t[...] = share - gate * jnp.sum(share, axis=0, keepdims=True)
    finish_out_terms()
    grad_rows[...] = reduced(1)
    finish_gather(1)
    finish_cross(1)
    finish_reduce(1)


def slot_targets(routes, experts, room_rows):
    flattened = routes.reshape(-1)
    hot_rows = (flattened[:, None] == jnp.arange(experts, dtype=jnp.int32)[None, :]).astype(jnp.int32)
    before = jnp.cumsum(hot_rows, axis=0) - hot_rows
    return flattened * room_rows + jnp.sum(hot_rows * before, axis=1)


def experts_by_all_to_all(
    capacity, tokens, remain, halting, expert_routes, halt_weight, expert_router, expert_in, expert_out,
    state_cotan, accum_cotan, remain_cotan, hidden_one, ffn_in,
):
    rows, width = tokens.shape
    experts = expert_router.shape[1]
    top = expert_routes.shape[1]
    highest = lax.Precision.HIGHEST
    inputs = tokens.astype(f32)
    active = halting.astype(f32)
    expert_logits = jnp.dot(ffn_in, expert_router, preferred_element_type=f32)
    expert_gate = jax.nn.softmax(jnp.take_along_axis(expert_logits, expert_routes, axis=1), axis=1)
    targets = slot_targets(expert_routes, experts, capacity)

    def spread(values):
        placed = jnp.zeros((experts * capacity, width), bf16).at[targets].set(values)
        return lax.all_to_all(
            placed.reshape(experts, capacity, width), "expert", split_axis=0, concat_axis=1, tiled=True
        )

    def collect(values):
        back = lax.all_to_all(values, "expert", split_axis=1, concat_axis=0, tiled=True)
        back = back.reshape(experts * capacity, width)
        return back[targets].astype(f32).reshape(rows, top, width)

    arrived = spread(jnp.repeat(ffn_in, top, axis=0))
    pre_act = jnp.einsum("erd,edf->erf", arrived, expert_in, preferred_element_type=f32)
    inner_act = jax.nn.gelu(pre_act, approximate=False).astype(bf16)
    produced = jnp.einsum("erf,efd->erd", inner_act, expert_out, preferred_element_type=f32).astype(bf16)
    picked = collect(produced)
    hidden = hidden_one + jnp.sum(expert_gate[:, :, None] * picked, axis=1)
    halt_vector = halt_weight.astype(f32)
    halt_prob = jax.nn.sigmoid(jnp.dot(hidden, halt_vector, precision=highest))
    halt_share = active * remain * halt_prob
    new_state = jnp.where(active[:, None] > 0.5, hidden, inputs).astype(bf16)
    accum_part = halt_share[:, None] * hidden
    remain_left = remain * (1.0 - active * halt_prob)
    grad_accum = accum_cotan.astype(f32)
    grad_share = jnp.sum(grad_accum * hidden, axis=1)
    grad_logit = active * remain * (grad_share - remain_cotan) * halt_prob * (1.0 - halt_prob)
    remain_grad = active * halt_prob * grad_share + (1.0 - active * halt_prob) * remain_cotan
    grad_hidden = (
        active[:, None] * state_cotan.astype(f32)
        + halt_share[:, None] * grad_accum
        + grad_logit[:, None] * halt_vector[None, :]
    )
    halt_sum = jnp.dot(grad_logit, hidden, precision=highest)
    grad_gate = jnp.sum(grad_hidden[:, None, :] * picked, axis=2)
    grad_chosen = expert_gate * (grad_gate - jnp.sum(expert_gate * grad_gate, axis=1, keepdims=True))
    expert_hot = (expert_routes[:, :, None] == jnp.arange(experts, dtype=jnp.int32)[None, None, :]).astype(f32)
    grad_logits = jnp.einsum("tk,tke->te", grad_chosen, expert_hot, precision=highest)
    grad_prod = (expert_gate[:, :, None] * grad_hidden[:, None, :]).astype(bf16)
    grad_arrived = spread(grad_prod.reshape(rows * top, width))
    grad_inner = jnp.einsum("erd,efd->erf", grad_arrived, expert_out, preferred_element_type=f32)
    cumulative = 0.5 * (1.0 + lax.erf(pre_act * (1.0 / math.sqrt(2.0))))
    density = jnp.exp(-0.5 * pre_act * pre_act) * (1.0 / math.sqrt(2.0 * math.pi))
    grad_pre = (grad_inner * (cumulative + pre_act * density)).astype(bf16)
    grad_rows = jnp.einsum("erf,edf->erd", grad_pre, expert_in, preferred_element_type=f32).astype(bf16)
    in_terms = jnp.einsum("erd,erf->edf", arrived, grad_pre, preferred_element_type=f32)
    out_terms = jnp.einsum("erf,erd->efd", inner_act, grad_arrived, preferred_element_type=f32)
    return (
        new_state, accum_part, jnp.stack([remain_left, remain_grad]), grad_hidden,
        jnp.sum(collect(grad_rows), axis=1),
        grad_logits.T, jnp.broadcast_to(halt_sum, (8, width)), (in_terms.astype(bf16), out_terms.astype(bf16)),
    )


def vmem(count):
    return [pl.BlockSpec(memory_space=pltpu.VMEM)] * count


def hbm(count):
    return [pl.BlockSpec(memory_space=pl.ANY)] * count


def experts_on_lines(
    capacity, chunks, lane, tokens, columns, vectors, expert_in, expert_out, state_cotan, accum_cotan, hidden_one, ffn_in,
    slots,
):
    rows, width = tokens.shape
    local, _, hidden_size = expert_in.shape
    shape, buffer, flags = jax.ShapeDtypeStruct, pltpu.VMEM, pltpu.SemaphoreType.DMA
    results = pl.pallas_call(
        functools.partial(expert_exchange, capacity, chunks, lane),
        out_shape=[
            shape((rows, width), bf16),
            shape((rows, width), f32),
            shape((8, rows), f32),
            shape((rows, width), f32),
            shape((rows, width), f32),
            shape((8 * local, rows), f32),
            shape((8, width), f32),
            shape((local, hidden_size // width, width, width), bf16),
            shape((local, width, width), bf16),
        ],
        in_specs=vmem(8) + hbm(2),
        out_specs=vmem(7) + hbm(1) + vmem(1),
        scratch_shapes=[
            buffer((local, width, hidden_size), bf16),
            buffer((local, hidden_size, width), bf16),
            buffer((2, 4, rows, width), bf16),
            buffer((8, local, capacity, width), bf16),
            buffer((8, local, capacity, width), bf16),
            buffer((4, local, capacity, width), bf16),
            buffer((8, local, capacity, hidden_size), bf16),
            buffer((8, local, capacity, hidden_size), bf16),
            buffer((8, local, capacity, width), bf16),
            buffer((4, local, capacity, width), bf16),
            buffer((8, local, capacity, width), bf16),
            buffer((4, local, capacity, width), bf16),
            buffer((4, rows, width), bf16),
            buffer((2, 5, rows, width), bf16),
            buffer((4, 8, rows), f32),
            buffer((4, 8, rows), f32),
            buffer((4, 8, rows), f32),
            buffer((local, 2, width, width), bf16),
            buffer((local, width, width), bf16),
            flags((2,)),
            flags((4,)),
            flags((4,)),
            flags((2, 5)),
            flags((2, 4)),
            flags((2, 4, local)),
            flags((2, 4, local)),
            flags((2, 4, local)),
            flags((2, 4, local)),
            flags((2, 5, chunks)),
            flags((2, 5, chunks)),
            flags((4,)),
            flags((4,)),
            flags(()),
            flags((2, chunks)),
            flags((4, chunks)),
            flags((local, 3)),
            flags((local, 3)),
        ],
        compiler_params=pltpu.CompilerParams(
            vmem_limit_bytes=VMEM_LIMIT, collective_id=1, has_side_effects=True
        ),
        name="expert_exchange",
    )(ffn_in, slots, tokens, hidden_one, state_cotan, accum_cotan, columns, vectors, expert_in, expert_out)
    *most, terms, out_final = results
    return *most, (terms, out_final)


def sums_on_links(operands, terms, small_rows, wides):
    rows, width = operands[0].shape
    wide_size = wides[0].shape[1]
    units = terms.shape[0]
    shape, buffer, flags = jax.ShapeDtypeStruct, pltpu.VMEM, pltpu.SemaphoreType.DMA
    parts = [wide_size // 3] * (len(ORDERS) - 1) + [small_rows]
    kinds = [bf16] * (len(ORDERS) - 1) + [f32]
    hops = {"x": 1, "y": 1, "z": 3}
    splits, landings = [], []
    for order, part, kind in zip(ORDERS, parts, kinds):
        split = (2,) + tuple(hops[axis] + 1 for axis in order) + (part // 32, width)
        splits.append((split, kind))
        for stage, size in enumerate((1, *[hops[axis] for axis in order])):
            landings.append(buffer((size,) + split[stage + 1 :], kind))
    tokens_grad, terms_final, *finals = pl.pallas_call(
        functools.partial(backward_and_sums, 128),
        out_shape=[
            shape((rows, width), f32),
            shape((units, width, width), bf16),
            *[shape(*split) for split in splits],
        ],
        in_specs=vmem(22) + hbm(1),
        out_specs=vmem(2 + len(splits)),
        scratch_shapes=[
            *wides,
            buffer((units, 2, width, width), bf16),
            buffer((units, 2, width, width), bf16),
            buffer((units, width, width), bf16),
            *[buffer(*split) for split in splits],
            *landings,
            flags((len(ORDERS), 12)),
            flags((len(ORDERS), 12)),
            flags((units, 2)),
            flags((units, 2, 2)),
            flags((units, 2, 2)),
            flags((units,)),
            flags((units,)),
        ],
        compiler_params=pltpu.CompilerParams(
            vmem_limit_bytes=VMEM_LIMIT, collective_id=2, has_side_effects=True
        ),
        name="backward_and_sums",
    )(*operands, terms)
    return tokens_grad, terms_final, [value.reshape(part, width) for value, part in zip(finals, parts)]


def write_results(edges, *refs):
    thirds, (in_low, out_low, small, lines, new_state_in, accum_in, tokens_in) = refs[:6], refs[6:13]
    output_grad, query_grad, in_grad, out_grad, new_state, accum_part, tokens_grad, *rest = refs[13:]
    width = small.shape[1]
    for index in range(3):
        output_grad[index] = thirds[index][...].astype(f32)
        query_grad[:, index * width : (index + 1) * width] = thirds[3 + index][...].astype(f32)
    in_grad[...] = in_low[...].astype(f32)
    out_grad[...] = out_low[...].astype(f32)
    new_state[...] = new_state_in[...]
    accum_part[...] = accum_in[...]
    tokens_grad[...] = tokens_in[...]
    for ref, start, stop in zip(rest, edges[:-1], edges[1:]):
        ref[...] = small[start:stop, :]
    rest[-2][...] = lines[0:1, :]
    rest[-1][...] = lines[1:2, :]


def results(edges, thirds, in_low, out_low, small, lines, new_state, accum_part, tokens_grad):
    shape, steps = jax.ShapeDtypeStruct, 4
    rows, width = new_state.shape
    units = in_low.shape[0]

    def by_rows(lanes):
        return pl.BlockSpec((width // steps, lanes), lambda i: (i, 0))

    def by_units(count):
        return pl.BlockSpec((count, width // steps, width), lambda i: (0, i, 0))

    def whole(count):
        return pl.BlockSpec((count, width), lambda i: (0, 0))

    def by_tokens():
        return pl.BlockSpec((rows // steps, width), lambda i: (i, 0))

    parts = [stop - start for start, stop in zip(edges[:-1], edges[1:])] + [1, 1]
    return pl.pallas_call(
        functools.partial(write_results, edges),
        grid=(steps,),
        out_shape=[
            shape((3, width, width), f32),
            shape((width, 3 * width), f32),
            shape((units, width, width), f32),
            shape((units, width, width), f32),
            shape((rows, width), bf16),
            shape((rows, width), f32),
            shape((rows, width), f32),
            *[shape((count, width), f32) for count in parts],
        ],
        in_specs=[
            *[by_rows(width) for _ in range(6)], by_units(units), by_units(units), whole(small.shape[0]), whole(lines.shape[0]),
            by_tokens(), by_tokens(), by_tokens(),
        ],
        out_specs=[
            by_units(3), by_rows(3 * width), by_units(units), by_units(units), by_tokens(), by_tokens(),
            by_tokens(), *[whole(count) for count in parts],
        ],
        compiler_params=pltpu.CompilerParams(vmem_limit_bytes=VMEM_LIMIT),
        name="results",
    )(*thirds, in_low, out_low, small, lines, new_state, accum_part, tokens_grad)


def body(
    mesh_sizes, tokens, remain, halting, head_routes, expert_routes, first_gain, first_bias, query_weight,
    key_weight, value_weight, output_weight, head_router, second_gain, second_bias, expert_router, expert_in,
    expert_out, halt_weight, state_cotan, accum_cotan, remain_cotan,
):
    rows, width = tokens.shape
    head_size = key_weight.shape[1]
    top = head_routes.shape[1]
    wide_size = query_weight.shape[1]
    experts = expert_router.shape[1]
    heads = head_router.shape[1]
    capacity = 4 * rows // experts
    shape = jax.ShapeDtypeStruct
    attn_in, query, keys, values, heads_out, spread_out, hidden_one, ffn_in, columns, slots, vectors = pl.pallas_call(
        functools.partial(attend_forward, 128),
        out_shape=[
            shape((rows, width), bf16),
            shape((top, rows, head_size), bf16),
            shape((rows, head_size), bf16),
            shape((rows, head_size), bf16),
            shape((top, rows, head_size), f32),
            shape((rows, wide_size), bf16),
            shape((rows, width), f32),
            shape((rows, width), bf16),
            shape((rows, 128), f32),
            shape((experts // 4, 8, rows), f32),
            shape((8, width), f32),
        ],
        in_specs=vmem(17),
        out_specs=vmem(11),
        scratch_shapes=[pltpu.VMEM((rows, wide_size), f32)],
        compiler_params=pltpu.CompilerParams(vmem_limit_bytes=VMEM_LIMIT),
        name="attend_forward",
    )(
        tokens, head_routes.T, expert_routes.T, remain[None], halting[None], remain_cotan[None], first_gain,
        first_bias, second_gain, second_bias, halt_weight, query_weight, key_weight.T,
        value_weight.T, output_weight, head_router.T, expert_router.T,
    )
    if mesh_sizes == (4, 8):
        stage = experts_on_lines(
            capacity, 4, 2 * top, tokens, columns, vectors, expert_in, expert_out, state_cotan, accum_cotan, hidden_one,
            ffn_in, slots,
        )
    else:
        stage = experts_by_all_to_all(
            capacity, tokens, remain, halting, expert_routes, halt_weight, expert_router, expert_in, expert_out,
            state_cotan, accum_cotan, remain_cotan, hidden_one, ffn_in,
        )
    new_state, accum_part, lines, grad_hidden, grad_rows, grad_logits_t, halt_sum, terms = stage
    operands = (
        tokens, vectors, query_weight, key_weight.T, value_weight.T, output_weight,
        head_router.T, expert_router.T, attn_in, query, keys, values, heads_out, spread_out, hidden_one, ffn_in,
        columns, grad_rows, grad_logits_t, grad_hidden, state_cotan, halt_sum,
    )
    edges = [0, head_size, 2 * head_size, 2 * head_size + heads, 2 * head_size + heads + experts]
    small_rows = 256
    wides = [pltpu.VMEM((rows, wide_size), f32), pltpu.VMEM((rows, wide_size), bf16)]
    if mesh_sizes == (4, 8):
        in_terms, out_final = terms
        tokens_grad, in_final, (*thirds, small) = sums_on_links(operands, in_terms, small_rows, wides)
        (output_grad, query_grad, expert_in_grad, expert_out_grad, new_state, accum_part, tokens_grad, *rest) = results(
            [*edges, *range(edges[-1] + 1, edges[-1] + 6)], thirds, in_final, out_final, small, lines, new_state,
            accum_part, tokens_grad,
        )
        output_grad = output_grad.reshape(wide_size, width)
        key_grad, value_grad, head_router_grad, expert_router_grad = [value.T for value in rest[:4]]
        first_gain_grad, first_bias_grad, second_gain_grad, second_bias_grad, halt_grad, remain_left, remain_grad = [
            value.reshape(width) for value in rest[4:]
        ]
    else:
        in_terms, out_terms = terms
        expert_in_grad = lax.psum_scatter(in_terms, "dp", scatter_dimension=2, tiled=True).astype(f32)
        expert_out_grad = lax.psum_scatter(out_terms, "dp", scatter_dimension=1, tiled=True).astype(f32)
        small_rows = -(-(2 * head_size + heads + experts + 5) // 8) * 8
        tokens_grad, query_sum, output_sum, small_sum = pl.pallas_call(
            functools.partial(attend_backward, 128),
            out_shape=[
                shape((rows, width), f32),
                shape((width, wide_size), f32),
                shape((wide_size, width), f32),
                shape((small_rows, width), f32),
            ],
            in_specs=vmem(22),
            out_specs=vmem(4),
            scratch_shapes=wides,
            compiler_params=pltpu.CompilerParams(vmem_limit_bytes=VMEM_LIMIT),
            name="attend_backward",
        )(*operands)
        query_grad, output_grad, small = lax.psum((query_sum, output_sum, small_sum), ("dp", "expert"))
        key_grad, value_grad, head_router_grad, expert_router_grad = [
            small[start:stop].T for start, stop in zip(edges[:-1], edges[1:])
        ]
        first_gain_grad, first_bias_grad, second_gain_grad, second_bias_grad, halt_grad = [
            small[edges[-1] + index] for index in range(5)
        ]
        remain_left, remain_grad = lines[0], lines[1]
    return (
        new_state, accum_part, remain_left, tokens_grad, remain_grad, first_gain_grad, first_bias_grad, query_grad,
        key_grad, value_grad, output_grad, head_router_grad, second_gain_grad, second_bias_grad,
        expert_router_grad, expert_in_grad, expert_out_grad, halt_grad,
    )


def solution(mesh):
    in_specs = (
        P(("dp", "expert"), None),
        P(("dp", "expert")),
        P(("dp", "expert")),
        P(("dp", "expert"), None),
        P(("dp", "expert"), None),
        P(),
        P(),
        P(),
        P(),
        P(),
        P(),
        P(),
        P(),
        P(),
        P(),
        P("expert", None, None),
        P("expert", None, None),
        P(),
        P(("dp", "expert"), None),
        P(("dp", "expert"), None),
        P(("dp", "expert")),
    )
    out_specs = (
        P(("dp", "expert"), None),
        P(("dp", "expert"), None),
        P(("dp", "expert")),
        P(("dp", "expert"), None),
        P(("dp", "expert")),
        P(),
        P(),
        P(),
        P(),
        P(),
        P(),
        P(),
        P(),
        P(),
        P(),
        P("expert", None, "dp"),
        P("expert", "dp", None),
        P(),
    )
    sizes = (mesh.shape["dp"], mesh.shape["expert"])
    run = functools.partial(body, sizes)
    return jax.shard_map(run, mesh=mesh, in_specs=in_specs, out_specs=out_specs, check_vma=False)
```
